32 devices in a mesh: dp: 16 (over z, y, core), seq: 2 (over x).
Axes of the slice: x: 2, y: 2, z: 4, core: 2. Of those that a mesh axis runs over, the one named last changes fastest.
Arguments:
- token_ids: int32 [16, 1024], P('dp'), may hold values from 0 to 31999
- segment_ids: int32 [16, 1024], P('dp'), may hold values from 0 to 7, never falling along the last dimension, each value on 1 to 512 neighbouring positions
- time_steps: int32 [16], P('dp'), may hold values from 0 to 999
- row_seeds: int32 [16], P('dp'), may hold values from 0 to 65520
- loss_weights: float32 [16, 1024], P('dp', 'seq'), may hold values from -6 to 6
- embed_table: bfloat16 [32000, 256], P(('dp', 'seq')), may hold values from -6 to 6
- input_proj: bfloat16 [256, 1024], P(('dp', 'seq')), may hold values from -0.375 to 0.375
- attn_gain: bfloat16 [1024], P(('dp', 'seq')), may hold values from 0.5 to 1.5
- attn_bias: bfloat16 [1024], P(('dp', 'seq')), may hold values from -1.796875 to 1.796875
- qkv_proj: bfloat16 [1024, 3072], P(('dp', 'seq')), may hold values from -0.1875 to 0.1875
- attn_proj: bfloat16 [1024, 1024], P(('dp', 'seq')), may hold values from -0.75 to 0.75
- mlp_gain: bfloat16 [1024], P(('dp', 'seq')), may hold values from 0.5 to 1.5
- mlp_bias: bfloat16 [1024], P(('dp', 'seq')), may hold values from -1.796875 to 1.796875
- up_proj: bfloat16 [1024, 4096], P(('dp', 'seq')), may hold values from -0.1875 to 0.1875
- up_bias: bfloat16 [4096], P(('dp', 'seq')), may hold values from -1.796875 to 1.796875
- down_proj: bfloat16 [4096, 1024], P(('dp', 'seq')), may hold values from -0.09375 to 0.09375
- output_proj: bfloat16 [1024, 256], P(('dp', 'seq')), may hold values from -0.1875 to 0.1875
Outputs:
- token_loss: float32 [16, 1024], P('dp', 'seq')
- table_grad: float32 [32000, 256], P(('dp', 'seq'))
- input_proj_grad: float32 [256, 1024], P(('dp', 'seq'))
- attn_gain_grad: float32 [1024], P(('dp', 'seq'))
- attn_bias_grad: float32 [1024], P(('dp', 'seq'))
- qkv_proj_grad: float32 [1024, 3072], P(('dp', 'seq'))
- attn_proj_grad: float32 [1024, 1024], P(('dp', 'seq'))
- mlp_gain_grad: float32 [1024], P(('dp', 'seq'))
- mlp_bias_grad: float32 [1024], P(('dp', 'seq'))
- up_proj_grad: float32 [1024, 4096], P(('dp', 'seq'))
- up_bias_grad: float32 [4096], P(('dp', 'seq'))
- down_proj_grad: float32 [4096, 1024], P(('dp', 'seq'))
- output_proj_grad: float32 [1024, 256], P(('dp', 'seq'))
The draws below stay inside these ranges and needn't reach their ends.
Inputs may be any that keep to these rules, and one draw needn't show every extreme that they name: `token_ids`: token ids over the vocabulary; a few of them are very common. `segment_ids`: within a row the ids never fall, so each document is one run of positions of at most 512; the longest run in a draw has exactly 512 positions.
All inputs are finite; a program needn't handle non-finite values.
Results may differ from the reference program's by a relative error of at most 0.015.
Values may be sent and summed in bfloat16 or wider, within the bound.
No kernel may reach another device: no remote copies, remote signals or barrier semaphores. Data moves between devices by JAX's collectives and lax.ppermute only.
A program may use at most 256 MiB of HBM per device.

```python
import math
import jax
import jax.numpy as jnp
import numpy as np
from jax import lax

D = 1024
HEADS = 16
HEAD_DIM = 64
FF = 4096
E = 256
V = 32000
LEN = 1024
DOCS = 8
TSTEPS = 1000
ROWS = 16


def with_ends(entries, key, low, largest):
    spot = [jax.random.randint(jax.random.fold_in(key, axis), (), 0, length) for axis, length in enumerate(entries.shape)]
    widest = entries.shape.index(max(entries.shape))
    next_to = spot[:widest] + [(spot[widest] + 1) % entries.shape[widest]] + spot[widest + 1:]
    return entries.at[tuple(spot)].set(low).at[tuple(next_to)].set(largest)


def steps_of(stream_key, shape, cuts, least, largest):
    loudness = 1.0
    for position, shards_of in cuts:
        heights = jax.random.uniform(jax.random.fold_in(jax.random.fold_in(stream_key, 6), position), (shards_of,), jnp.float32, least / len(cuts), largest / len(cuts))
        loudness = loudness * jnp.repeat(jnp.exp(heights), shape[position] // shards_of).reshape((-1,) + (1,) * (len(shape) - 1 - position))
    return loudness


def rank_table(amount, skew):
    loads = [(1 << 20) // math.isqrt(grade ** skew) + 1 for grade in range(1, amount + 1)]
    deviation = 1 + sum(loads) // (1 << 30)
    return np.cumsum(np.array([max(1, weight // deviation) for weight in loads]))


def skewed_ids(stream_key, shape, amount, skew):
    grid = rank_table(amount, skew)
    lot = jax.random.randint(jax.random.fold_in(stream_key, 1), shape, 0, int(grid[amount - 1]))
    standing = jnp.searchsorted(jnp.asarray(grid, jnp.int32), lot, side="right")
    return jax.random.permutation(jax.random.fold_in(stream_key, 2), amount)[standing].astype(jnp.int32)


def profile(amount, total, limit, slope):
    weights = [(1 << 20) // math.isqrt(rank ** slope) + 1 for rank in range(2, amount + 1)]
    surplus, counts = total - limit - (amount - 1), [1] * (amount - 1)
    while surplus > 0:
        free = [i for i in range(amount - 1) if counts[i] < limit]
        pool, remaining = sum([weights[i] for i in free]), surplus
        for i in free:
            extra = min(limit - counts[i], max(1, remaining * weights[i] // pool), surplus)
            counts[i] = counts[i] + extra
            surplus = surplus - extra
    return np.array([limit] + counts)


def ragged(key, count, total, bound, lean):
    if count == 2:
        one = jax.random.randint(key, (), max(1, total - bound), min(bound, total - 1) + 1)
        return jnp.stack([one, total - one])
    sizes = jnp.asarray(profile(count, total, bound, lean), jnp.int32)
    pairs = (count - 1) // 2
    donor, taker = sizes[1:1 + 2 * pairs:2], sizes[2:2 + 2 * pairs:2]
    slack = jnp.minimum(donor - 1, bound - taker)
    shifted = jax.random.randint(jax.random.fold_in(key, 1), (pairs,), 0, 1 << 20) % (slack + 1)
    sizes = sizes.at[1:1 + 2 * pairs:2].set(donor - shifted).at[2:2 + 2 * pairs:2].set(taker + shifted)
    return sizes[jax.random.permutation(jax.random.fold_in(key, 2), count)]


def gaussian(key, extent, deviation, most, shards=(), dtype=jnp.bfloat16):
    values = jax.random.normal(key, extent, jnp.float32) * deviation
    if len(shards) > 0:
        values = steps_of(key, extent, shards, -0.22, 0.18) * values
    return jnp.clip(values, min=-most, max=most).astype(dtype)


def setup_inputs(seed: int = 0) -> dict:
    arg_keys = jax.random.split(jax.random.key(seed), 18)
    token_ids = with_ends(skewed_ids(arg_keys[0], (ROWS, LEN), V, 2), jax.random.fold_in(arg_keys[0], 3), 0, V - 1).astype(jnp.int32)
    segment_ids = jax.vmap(lambda own: jnp.searchsorted(jnp.cumsum(ragged(own, DOCS, LEN, LEN // 2, 1)), jnp.arange(LEN), side="right"))(jax.random.split(arg_keys[1], ROWS)).reshape((ROWS, LEN)).astype(jnp.int32)
    time_steps = with_ends(jax.random.randint(arg_keys[2], (ROWS,), 0, TSTEPS), jax.random.fold_in(arg_keys[2], 1), 0, TSTEPS - 1).astype(jnp.int32)
    row_seeds = with_ends(jax.random.randint(arg_keys[3], (ROWS,), 0, 65521), jax.random.fold_in(arg_keys[3], 1), 0, 65520).astype(jnp.int32)
    loss_weights = gaussian(arg_keys[4], (ROWS, LEN), 1.0, 6.0, ((0, 16), (1, 2)), jnp.float32)
    embed_table = gaussian(arg_keys[5], (V, E), 1.0, 6.0, ((0, 32),))
    input_proj = gaussian(arg_keys[6], (E, D), E ** -0.5, 0.375, ((0, 32),))
    attn_gain = jnp.clip(1.0 + 0.1 * jax.random.normal(arg_keys[7], (D,), jnp.float32), 0.5, 1.5).astype(jnp.bfloat16)
    attn_bias = gaussian(arg_keys[8], (D,), 0.3, 1.796875, ((0, 32),))
    qkv_proj = gaussian(arg_keys[9], (D, 3 * D), D ** -0.5, 0.1875, ((0, 32),))
    attn_proj = gaussian(arg_keys[10], (D, D), (D // 16) ** -0.5, 0.75, ((0, 32),))
    mlp_gain = jnp.clip(1.0 + 0.1 * jax.random.normal(arg_keys[11], (D,), jnp.float32), 0.5, 1.5).astype(jnp.bfloat16)
    mlp_bias = gaussian(arg_keys[12], (D,), 0.3, 1.796875, ((0, 32),))
    up_proj = gaussian(arg_keys[13], (D, FF), D ** -0.5, 0.1875, ((0, 32),))
    up_bias = gaussian(arg_keys[14], (FF,), 0.3, 1.796875, ((0, 32),))
    down_proj = gaussian(arg_keys[15], (FF, D), FF ** -0.5, 0.09375, ((0, 32),))
    output_proj = gaussian(arg_keys[16], (D, E), D ** -0.5, 0.1875, ((0, 32),))
    return dict(token_ids=token_ids, segment_ids=segment_ids, time_steps=time_steps, row_seeds=row_seeds, loss_weights=loss_weights, embed_table=embed_table, input_proj=input_proj, attn_gain=attn_gain, attn_bias=attn_bias, qkv_proj=qkv_proj, attn_proj=attn_proj, mlp_gain=mlp_gain, mlp_bias=mlp_bias, up_proj=up_proj, up_bias=up_bias, down_proj=down_proj, output_proj=output_proj)


HIGH = lax.Precision.HIGHEST

@jax.custom_vjp
def low(v):
    return lax.optimization_barrier(v.astype(jnp.bfloat16)).astype(jnp.float32)

@jax.custom_vjp
def low_back(v):
    return v

def low_keep(v):
    return (low(v), None)

def low_pass(kept, grad):
    return (grad,)

def back_keep(v):
    return (v, None)

def back_low(kept, grad):
    return (low(grad),)
low.defvjp(low_keep, low_pass)
low_back.defvjp(back_keep, back_low)

def product(left, right):
    return jnp.dot(left, right, precision=HIGH, preferred_element_type=jnp.float32)

def normalize_rows(matrix):
    return matrix * lax.rsqrt(lax.optimization_barrier(jnp.mean(matrix * matrix, axis=1, keepdims=True)) + 1e-06)

def layer_norm(hidden, norm_gain, norm_bias):
    centre = hidden - lax.optimization_barrier(jnp.mean(hidden, axis=-1, keepdims=True))
    spread = lax.optimization_barrier(jnp.mean(centre * centre, axis=-1, keepdims=True))
    return centre * lax.rsqrt(spread + 1e-05) * norm_gain + norm_bias

def exact_gelu(pre_act):
    return jax.nn.gelu(pre_act, approximate=False)

def noise_field(row_seeds, positions, channel_count):
    channel = lax.iota(jnp.int32, channel_count)
    mixed_once = (row_seeds[:, None, None] + 7919 * positions[None, :, None] + 104729 * channel[None, None, :]) % 65521
    mixed_twice = (mixed_once * (mixed_once % 32719) + 31 * channel[None, None, :]) % 65521
    return (mixed_twice.astype(jnp.float32) / 32760.5 - 1.0) * 1.7320508

def time_terms(time_steps):
    fraction = time_steps.astype(jnp.float32) / (TSTEPS - 1)
    noise_level = 0.3 * jnp.exp(fraction * math.log(30.0))
    return (noise_level, lax.rsqrt(1.0 + noise_level * noise_level), 0.5 + fraction)

def attend(operands):
    queries, key_rows, value_rows, segment_row = operands
    scores = low_back(jnp.einsum('qhd,khd->hqk', queries, key_rows, precision=HIGH))
    same_doc = segment_row[:, None] == segment_row[None, :]
    scores = jnp.where(same_doc[None], scores, -1e+30)
    probs = jax.nn.softmax(scores, axis=-1)
    return jnp.einsum('hqk,khd->qhd', low(probs), value_rows, precision=HIGH)

def forward(params, token_ids, segment_ids, time_steps, row_seeds):
    embed_table, input_proj, attn_gain, attn_bias, qkv_proj, attn_proj, mlp_gain, mlp_bias, up_proj, up_bias, down_proj, output_proj = params
    group_rows = token_ids.shape[0]
    unit = normalize_rows(embed_table)
    noise_level, input_scale, residual_scale = time_terms(time_steps)
    noise = noise_field(row_seeds, lax.iota(jnp.int32, LEN), E)
    embedded = jnp.take(unit, token_ids, axis=0)
    inputs = input_scale[:, None, None] * (embedded + noise_level[:, None, None] * noise)
    hidden_zero = low_back(product(low(inputs), input_proj))
    first_in = low(layer_norm(hidden_zero, attn_gain, attn_bias))
    qkv = product(first_in, qkv_proj)
    head_shape = (group_rows, LEN, HEADS, HEAD_DIM)
    queries = low_back(low(qkv[..., :D] * HEAD_DIM ** (-0.5))).reshape(head_shape)
    key_rows = low_back(low(qkv[..., D:2 * D])).reshape(head_shape)
    value_rows = low_back(low(qkv[..., 2 * D:])).reshape(head_shape)
    attended = lax.map(jax.checkpoint(attend), (queries, key_rows, value_rows, segment_ids))
    attended = low_back(low(attended.reshape(group_rows, LEN, D)))
    row_scale = residual_scale[:, None, None]
    hidden_one = hidden_zero + row_scale * low_back(product(attended, attn_proj))
    second_in = low(layer_norm(hidden_one, mlp_gain, mlp_bias))
    pre_act = low_back(product(second_in, up_proj) + up_bias)
    activated = low(exact_gelu(pre_act))
    hidden_two = hidden_one + row_scale * low_back(product(activated, down_proj))
    outputs = low_back(low(product(low(hidden_two), output_proj)))
    scaled = low(unit * E ** (-0.5))
    flat_out = outputs.reshape(group_rows * LEN, E)
    flat_ids = token_ids.reshape(group_rows * LEN)
    tile_rows = math.gcd(group_rows * LEN, 512)
    tile_count = group_rows * LEN // tile_rows

    def score_tile(pieces):
        out_block, target_block = pieces
        logits = low_back(product(out_block, scaled.T))
        picked = jnp.take_along_axis(logits, target_block[:, None], axis=1)[:, 0]
        return jax.nn.logsumexp(logits, axis=1) - picked
    losses = lax.map(jax.checkpoint(score_tile), (flat_out.reshape(tile_count, tile_rows, E), flat_ids.reshape(tile_count, tile_rows)))
    return losses.reshape(group_rows, LEN)

def reference(token_ids, segment_ids, time_steps, row_seeds, loss_weights, embed_table, input_proj, attn_gain, attn_bias, qkv_proj, attn_proj, mlp_gain, mlp_bias, up_proj, up_bias, down_proj, output_proj):
    params = tuple((weight.astype(jnp.float32) for weight in (embed_table, input_proj, attn_gain, attn_bias, qkv_proj, attn_proj, mlp_gain, mlp_bias, up_proj, up_bias, down_proj, output_proj)))
    group_rows = math.gcd(ROWS, max(1, 4096 // LEN))
    group_count = ROWS // group_rows

    def group_step(totals, operands):
        group_ids, group_segs, group_times, group_seeds, group_weights = operands

        def group_loss(*values):
            return forward(values, group_ids, group_segs, group_times, group_seeds)
        losses, pullback = jax.vjp(group_loss, *params)
        gradients = pullback(group_weights)
        return (tuple((total + part for total, part in zip(totals, gradients))), losses)
    data = tuple((array.reshape((group_count, group_rows) + array.shape[1:]) for array in (token_ids, segment_ids, time_steps, row_seeds, loss_weights)))
    totals, losses = lax.scan(group_step, tuple((jnp.zeros_like(weight) for weight in params)), data)
    return (losses.reshape(ROWS, LEN),) + tuple(totals)
```

```python
import math

import jax
import jax.numpy as jnp
from jax import lax
from jax.experimental import pallas as pl
from jax.experimental.pallas import tpu as pltpu
from jax.sharding import Mesh
from jax.sharding import PartitionSpec as P

D = 1024
HEAD_DIM = 64
TSTEPS = 1000
SWAP = ((0, 1), (1, 0))
BF = jnp.bfloat16
F32 = jnp.float32
NEG = -1e30
MIB = 1 << 20


def dot_nn(left, right):
    return lax.dot_general(left, right, (((1,), (0,)), ((), ())), preferred_element_type=F32)


def dot_nt(left, right):
    return lax.dot_general(left, right, (((1,), (1,)), ((), ())), preferred_element_type=F32)


def dot_tn(left, right):
    return lax.dot_general(left, right, (((0,), (0,)), ((), ())), preferred_element_type=F32)


def swap(value, axis):
    return lax.ppermute(value, axis, SWAP)


def ring_down(value, axis):
    n = lax.axis_size(axis)
    return lax.ppermute(value, axis, [(i, (i - 1) % n) for i in range(n)])


def ring_up(value, axis):
    n = lax.axis_size(axis)
    return lax.ppermute(value, axis, [(i, (i + 1) % n) for i in range(n)])


def ordered(own, other, place, axis):
    return jnp.where(
        place == 0, jnp.stack([own, other], axis), jnp.stack([other, own], axis)
    )


def pick(value, index, axis):
    return lax.dynamic_index_in_dim(value, index, axis, keepdims=False)


def gather_axes(value, order):
    held = value[None]
    for axis in order:
        n = lax.axis_size(axis)
        parts, moving = [held], held
        for _ in range(n - 1):
            moving = swap(moving, axis) if n == 2 else ring_down(moving, axis)
            parts.append(moving)
        held = jnp.concatenate(parts, 0)
    return held


def relative_slots(order, targets):
    flat = 0
    for axis in reversed(order):
        n = lax.axis_size(axis)
        flat = flat * n + (targets[axis] - lax.axis_index(axis)) % n
    return flat


def reduce_axes(value, dims, order):
    dims = list(dims)
    last = order[-1]
    for axis in order:
        n, here, at = lax.axis_size(axis), lax.axis_index(axis), dims.index(axis)
        if n == 2:
            moved = swap(pick(value, 1 - here, at), axis)
            total = pick(value, here, at).astype(F32) + moved.astype(F32)
        else:
            total = pick(value, (here - 1) % n, at)
            for step in range(1, n):
                moved = ring_up(total.astype(BF), axis)
                total = pick(value, (here - 1 - step) % n, at).astype(F32) + moved.astype(F32)
        value = total if axis == last else total.astype(BF)
        dims.pop(at)
    return value


def block_copy(slots, blocks, out_shape, out_block, out_map):
    n, rows, cols = blocks.shape

    def body(slots_ref, in_ref, out_ref):
        out_ref[...] = in_ref[...].reshape(out_ref.shape)

    return pl.pallas_call(
        body,
        out_shape=jax.ShapeDtypeStruct(out_shape, blocks.dtype),
        grid_spec=pltpu.PrefetchScalarGridSpec(
            num_scalar_prefetch=1,
            grid=(n,),
            in_specs=[pl.BlockSpec((1, rows, cols), lambda i, slots_ref: (slots_ref[i], 0, 0))],
            out_specs=pl.BlockSpec(out_block, out_map),
        ),
        name="block_copy",
    )(slots, blocks)


def attend_body(lo_ref, hi_ref, q_ref, k_ref, v_ref, seg_col_ref, seg_row_ref, o_ref, lse_ref):
    length = q_ref.shape[0]
    blk = min(256, length)
    lane = lax.broadcasted_iota(jnp.int32, (1, 128), 1)
    masks = (lane < HEAD_DIM, lane >= HEAD_DIM)
    for qi in range(length // blk):
        rows = pl.ds(qi * blk, blk)
        q = q_ref[rows, :]
        heads = [jnp.where(m, q, jnp.zeros_like(q)) for m in masks]
        seg_q = seg_col_ref[rows, :]

        def step(kb, carry):
            at = pl.ds(pl.multiple_of(kb * blk, blk), blk)
            k, v = k_ref[at, :], v_ref[at, :]
            same = seg_q == seg_row_ref[:, at]
            out = []
            for h in range(2):
                top, total, acc = carry[h]
                s = jnp.where(same, dot_nt(heads[h], k), NEG)
                new_top = jnp.maximum(top, jnp.max(s, axis=1, keepdims=True))
                keep = jnp.exp(top - new_top)
                e = jnp.where(same, jnp.exp(s - new_top), 0.0)
                total = total * keep + jnp.sum(e, axis=1, keepdims=True)
                acc = acc * keep + dot_nn(e.astype(BF), v)
                out.append((new_top, total, acc))
            return tuple(out)

        start = tuple(
            (
                jnp.full((blk, 1), NEG, F32),
                jnp.zeros((blk, 1), F32),
                jnp.zeros((blk, 128), F32),
            )
            for _ in range(2)
        )
        done = lax.fori_loop(lo_ref[qi], hi_ref[qi], step, start)
        outs = [acc / total for _, total, acc in done]
        o_ref[rows, :] = jnp.where(masks[0], outs[0], outs[1]).astype(BF)
        lse = [jnp.broadcast_to(top + jnp.log(total), (blk, 128)) for top, total, _ in done]
        both = jnp.where(masks[0], lse[0], lse[1]).T
        lse_ref[0, 0:1, rows] = both[0:1, :]
        lse_ref[0, 1:2, rows] = both[HEAD_DIM : HEAD_DIM + 1, :]


def attend(q, k, v, seg_col, seg_row, lo, hi):
    length, width = q.shape
    pairs = width // 128
    spec = pl.BlockSpec((length, 128), lambda i, *_: (0, i))
    return pl.pallas_call(
        attend_body,
        out_shape=(
            jax.ShapeDtypeStruct((length, width), BF),
            jax.ShapeDtypeStruct((pairs, 2, length), F32),
        ),
        grid_spec=pltpu.PrefetchScalarGridSpec(
            num_scalar_prefetch=2,
            grid=(pairs,),
            in_specs=[
                spec,
                spec,
                spec,
                pl.BlockSpec((length, 1), lambda i, *_: (0, 0)),
                pl.BlockSpec((1, length), lambda i, *_: (0, 0)),
            ],
            out_specs=(spec, pl.BlockSpec((1, 2, length), lambda i, *_: (i, 0, 0))),
        ),
        compiler_params=pltpu.CompilerParams(vmem_limit_bytes=32 * MIB),
        name="attend",
    )(lo, hi, q, k, v, seg_col, seg_row)


def attend_back_body(
    lo_ref,
    hi_ref,
    q_ref,
    k_ref,
    v_ref,
    o_ref,
    g_ref,
    lse_ref,
    seg_col_ref,
    seg_row_ref,
    dq_ref,
    dk_ref,
    dv_ref,
    dk_sum,
    dv_sum,
):
    length = q_ref.shape[0]
    blk = min(256, length)
    lane = lax.broadcasted_iota(jnp.int32, (1, 128), 1)
    masks = (lane < HEAD_DIM, lane >= HEAD_DIM)
    dk_sum[...] = jnp.zeros_like(dk_sum)
    dv_sum[...] = jnp.zeros_like(dv_sum)
    for qi in range(length // blk):
        rows = pl.ds(qi * blk, blk)
        q, g = q_ref[rows, :], g_ref[rows, :]
        zero = jnp.zeros_like(q)
        q_heads = [jnp.where(m, q, zero) for m in masks]
        g_heads = [jnp.where(m, g, zero) for m in masks]
        mixed = (g.astype(F32) * o_ref[rows, :].astype(F32)).T
        delta = [
            jnp.sum(mixed[:HEAD_DIM], axis=0, keepdims=True),
            jnp.sum(mixed[HEAD_DIM:], axis=0, keepdims=True),
        ]
        lse = [lse_ref[0, h : h + 1, rows] for h in range(2)]
        seg_q = seg_row_ref[:, rows]

        def step(kb, dq):
            at = pl.ds(pl.multiple_of(kb * blk, blk), blk)
            k, v = k_ref[at, :], v_ref[at, :]
            same = seg_col_ref[at, :] == seg_q
            dk, dv = dk_sum[at, :], dv_sum[at, :]
            for h in range(2):
                s = dot_nt(k, q_heads[h])
                p = jnp.where(same, jnp.exp(jnp.where(same, s - lse[h], NEG)), 0.0)
                dp = dot_nt(v, g_heads[h])
                ds = (p * (dp - delta[h])).astype(BF)
                dv = dv + dot_nn(p.astype(BF), g_heads[h])
                dk = dk + dot_nn(ds, q_heads[h])
                dq = dq + dot_tn(ds, jnp.where(masks[h], k, jnp.zeros_like(k)))
            dk_sum[at, :] = dk
            dv_sum[at, :] = dv
            return dq

        dq = lax.fori_loop(lo_ref[qi], hi_ref[qi], step, jnp.zeros((blk, 128), F32))
        dq_ref[rows, :] = dq.astype(BF)
    dk_ref[...] = dk_sum[...].astype(BF)
    dv_ref[...] = dv_sum[...].astype(BF)


def attend_back(q, k, v, o, g, lse, seg_col, seg_row, lo, hi):
    length, width = q.shape
    pairs = width // 128
    spec = pl.BlockSpec((length, 128), lambda i, *_: (0, i))
    shape = jax.ShapeDtypeStruct((length, width), BF)
    return pl.pallas_call(
        attend_back_body,
        out_shape=(shape, shape, shape),
        grid_spec=pltpu.PrefetchScalarGridSpec(
            num_scalar_prefetch=2,
            grid=(pairs,),
            in_specs=[
                spec,
                spec,
                spec,
                spec,
                spec,
                pl.BlockSpec((1, 2, length), lambda i, *_: (i, 0, 0)),
                pl.BlockSpec((length, 1), lambda i, *_: (0, 0)),
                pl.BlockSpec((1, length), lambda i, *_: (0, 0)),
            ],
            out_specs=(spec, spec, spec),
            scratch_shapes=[pltpu.VMEM((length, 128), F32), pltpu.VMEM((length, 128), F32)],
        ),
        compiler_params=pltpu.CompilerParams(vmem_limit_bytes=32 * MIB),
        name="attend_back",
    )(lo, hi, q, k, v, o, g, lse, seg_col, seg_row)


def score_body(out_ref, table_ref, raised_ref, tops_ref, ends_ref, acc_ref, scaled, scaled_t):
    i, j = pl.program_id(0), pl.program_id(1)

    @pl.when(i == 0)
    def _():
        rows = table_ref[0].astype(F32)
        width = rows.shape[1]
        unit = rows * lax.rsqrt(jnp.mean(rows * rows, axis=1, keepdims=True) + 1e-06)
        low = (unit * width ** (-0.5)).astype(BF)
        scaled[j] = low
        scaled_t[j] = low.astype(F32).T.astype(BF)

    @pl.when(j == 0)
    def _():
        ends_ref[...] = jnp.full_like(ends_ref, NEG)
        acc_ref[...] = jnp.zeros_like(acc_ref)

    logits = dot_nt(scaled[j], out_ref[...])
    top = ends_ref[0:1, :]
    total = jnp.where(j == 0, 0.0, ends_ref[1:2, :])
    new_top = jnp.maximum(top, jnp.max(logits, axis=0, keepdims=True))
    keep = jnp.exp(top - new_top)
    e = jnp.exp(logits - new_top)
    low = e.astype(BF)
    raised_ref[0] = low
    ends_ref[0:1, :] = new_top
    ends_ref[1:2, :] = total * keep + jnp.sum(e, axis=0, keepdims=True)
    acc_ref[...] = acc_ref[...] * keep + dot_nn(scaled_t[j], low)
    tops_ref[0] = new_top


def score(outputs, table):
    tokens, width = outputs.shape
    blocks, rows, _ = table.shape
    tile = math.gcd(tokens, 512)
    return pl.pallas_call(
        score_body,
        out_shape=(
            jax.ShapeDtypeStruct((blocks, rows, tokens), BF),
            jax.ShapeDtypeStruct((blocks, 1, tokens), F32),
            jax.ShapeDtypeStruct((8, tokens), F32),
            jax.ShapeDtypeStruct((width, tokens), F32),
        ),
        grid=(tokens // tile, blocks),
        in_specs=[
            pl.BlockSpec((tile, width), lambda i, j: (i, 0)),
            pl.BlockSpec(
                (1, rows, width), lambda i, j: (jnp.where(i == 0, j, blocks - 1), 0, 0)
            ),
        ],
        out_specs=(
            pl.BlockSpec((1, rows, tile), lambda i, j: (j, 0, i)),
            pl.BlockSpec((1, 1, tile), lambda i, j: (j, 0, i)),
            pl.BlockSpec((8, tile), lambda i, j: (0, i)),
            pl.BlockSpec((width, tile), lambda i, j: (0, i)),
        ),
        scratch_shapes=[
            pltpu.VMEM((blocks, rows, width), BF),
            pltpu.VMEM((blocks, width, rows), BF),
        ],
        compiler_params=pltpu.CompilerParams(vmem_limit_bytes=48 * MIB),
        name="score",
    )(outputs, table)


def table_product_body(raised_ref, out_ref, coef_ref, sum_ref):
    j = pl.program_id(0)
    lane = lax.broadcasted_iota(jnp.int32, coef_ref.shape, 1)
    coef = jnp.sum(jnp.where(lane == j, coef_ref[...], 0.0), axis=1, keepdims=True)
    weighted = (out_ref[...].astype(F32) * coef).astype(BF)
    sum_ref[0] = dot_nn(raised_ref[0], weighted)


def table_product(raised, outputs, coef):
    blocks, rows, tokens = raised.shape
    width = outputs.shape[1]
    return pl.pallas_call(
        table_product_body,
        out_shape=jax.ShapeDtypeStruct((blocks, rows, width), F32),
        grid=(blocks,),
        in_specs=[
            pl.BlockSpec((1, rows, tokens), lambda j: (j, 0, 0)),
            pl.BlockSpec((tokens, width), lambda j: (0, 0)),
            pl.BlockSpec((tokens, blocks), lambda j: (0, 0)),
        ],
        out_specs=pl.BlockSpec((1, rows, width), lambda j: (j, 0, 0)),
        compiler_params=pltpu.CompilerParams(vmem_limit_bytes=48 * MIB),
        name="table_product",
    )(raised, outputs, coef)


def table_add_body(sum_ref, slot_ref, grad_ref, out_ref):
    j = pl.program_id(0)
    rows = sum_ref.shape[1]
    row = lax.broadcasted_iota(jnp.int32, (rows, 1), 0) + j * rows
    chosen = (row == slot_ref[...]).astype(F32).astype(BF)
    out_ref[0] = (sum_ref[0] + dot_nn(chosen, grad_ref[...])).astype(BF)


def table_add(sums, slots, grads):
    blocks, rows, width = sums.shape
    tokens = grads.shape[0]
    return pl.pallas_call(
        table_add_body,
        out_shape=jax.ShapeDtypeStruct(sums.shape, BF),
        grid=(blocks,),
        in_specs=[
            pl.BlockSpec((1, rows, width), lambda j: (j, 0, 0)),
            pl.BlockSpec((1, tokens), lambda j: (0, 0)),
            pl.BlockSpec((tokens, width), lambda j: (0, 0)),
        ],
        out_specs=pl.BlockSpec((1, rows, width), lambda j: (j, 0, 0)),
        compiler_params=pltpu.CompilerParams(vmem_limit_bytes=48 * MIB),
        name="table_add",
    )(sums, slots, grads)


def norm_parts(hidden):
    centre = hidden - jnp.mean(hidden, axis=-1, keepdims=True)
    spread = jnp.mean(centre * centre, axis=-1, keepdims=True)
    inverse = lax.rsqrt(spread + 1e-05)
    return centre * inverse, inverse


def norm_back(grad, gain, normed, inverse):
    grad_normed = grad * gain
    first = jnp.mean(grad_normed, axis=-1, keepdims=True)
    second = jnp.mean(grad_normed * normed, axis=-1, keepdims=True)
    return inverse * (grad_normed - first - normed * second)


def noise_field(row_seed, length, channel_count):
    position = lax.iota(jnp.int32, length)[:, None]
    channel = lax.iota(jnp.int32, channel_count)[None, :]
    mixed_once = (row_seed + 7919 * position + 104729 * channel) % 65521
    mixed_twice = (mixed_once * (mixed_once % 32719) + 31 * channel) % 65521
    return (mixed_twice.astype(F32) / 32760.5 - 1.0) * 1.7320508


def paired(
    token_ids,
    segment_ids,
    time_steps,
    row_seeds,
    loss_weights,
    embed_table,
    input_proj,
    attn_gain,
    attn_bias,
    qkv_proj,
    attn_proj,
    mlp_gain,
    mlp_bias,
    up_proj,
    up_bias,
    down_proj,
    output_proj,
):
    z, y, c, x = (lax.axis_index(a) for a in ("z", "y", "c", "x"))
    groups = lax.axis_size("z") * lax.axis_size("y")
    length = token_ids.shape[1]
    half = length // 2
    block_len, width = embed_table.shape
    ff = up_proj.shape[1]
    rows_here = qkv_proj.shape[0]
    heads = D // HEAD_DIM
    ff_block = down_proj.shape[0] * 2

    cut = block_len // 32 * 16
    table_a = gather_axes(embed_table[:cut], ("z", "y"))
    table_b = gather_axes(embed_table[cut:], ("y", "z"))

    meta = jnp.concatenate([token_ids[0], segment_ids[0], time_steps, row_seeds])
    meta_two = ordered(meta, swap(meta, "c"), c, 0)
    weight_c = ordered(loss_weights[0], swap(loss_weights[0], "c"), c, 0)
    weight_two = ordered(weight_c, swap(weight_c, "x"), x, 1).reshape(2, length)
    ids_two = meta_two[:, :length]
    own_meta = pick(meta_two, x, 0)
    segments = own_meta[length : 2 * length]
    weight_row = pick(weight_two, x, 0)
    fraction = own_meta[2 * length].astype(F32) / (TSTEPS - 1)
    noise_level = 0.3 * jnp.exp(fraction * math.log(30.0))
    input_scale = lax.rsqrt(1.0 + noise_level * noise_level)
    residual_scale = 0.5 + fraction
    noise = noise_field(own_meta[2 * length + 1], length, width)

    small = jnp.concatenate(
        [
            input_proj.reshape(-1, width),
            output_proj,
            jnp.concatenate([attn_gain, attn_bias, mlp_gain, mlp_bias, up_bias]).reshape(1, width),
            jnp.zeros((15, width), BF),
        ]
    )
    small_pair = ordered(small, swap(small, "c"), c, 0)
    small_rows = small.shape[0]
    small_all = gather_axes(small_pair.reshape(2 * small_rows, width), ("z", "y", "x"))

    qkv_split = qkv_proj.reshape(rows_here, 3, heads // 2, 2, HEAD_DIM)
    qkv_pair = ordered(
        pick(qkv_split, c, 3).reshape(rows_here, -1),
        swap(pick(qkv_split, 1 - c, 3).reshape(rows_here, -1), "c"),
        c,
        0,
    ).reshape(2 * rows_here, 3 * D // 2)
    up_split = up_proj.reshape(rows_here, groups, 2, ff_block)
    up_pair = ordered(
        pick(up_split, c, 2).reshape(rows_here, -1),
        swap(pick(up_split, 1 - c, 2).reshape(rows_here, -1), "c"),
        c,
        0,
    ).reshape(2 * rows_here, ff // 2)

    block = jnp.arange(2 * groups, dtype=jnp.int32)
    place = {"z": block // 4, "y": block // 2 % 2, "x": block % 2}

    def gathered_rows(shard, order):
        held = gather_axes(shard, order)
        n, rows, cols = held.shape
        return block_copy(
            relative_slots(order, place),
            held,
            (n, rows, cols),
            (1, rows, cols),
            lambda i, slots_ref: (i, 0, 0),
        ).reshape(n * rows, cols)

    def gathered_pairs(shard, order):
        held = gather_axes(shard, order)
        n, rows, cols = held.shape
        return block_copy(
            relative_slots(order, place),
            held,
            (groups, 2, 2, rows // 2, cols),
            (1, 2, 1, rows // 2, cols),
            lambda i, slots_ref: (i // 2, 0, i % 2, 0, 0),
        ).reshape(n * rows, cols)

    small_full = block_copy(
        relative_slots(("z", "y", "x"), place),
        small_all,
        small_all.shape,
        (1,) + small_all.shape[1:],
        lambda i, slots_ref: (i, 0, 0),
    ).reshape(groups, 2, 2, small_rows, width)
    small_full = small_full.transpose(0, 2, 1, 3, 4)
    input_count = input_proj.shape[0] * D // width
    input_full = small_full[..., :input_count, :].reshape(width, D)
    output_full = small_full[..., input_count : input_count + rows_here, :].reshape(D, width)
    vectors = small_full[..., input_count + rows_here, :]
    gain_one, bias_one, gain_two, bias_two = (
        vectors[..., k * rows_here : (k + 1) * rows_here].reshape(1, D).astype(F32)
        for k in range(4)
    )
    up_bias_half = pick(vectors[..., 4 * rows_here :], c, 1).reshape(1, ff // 2).astype(F32)

    qkv_half = gathered_pairs(qkv_pair, ("z", "y", "x"))
    attn_half = gathered_rows(attn_proj, ("z", "x", "y"))
    up_half = gathered_pairs(up_pair, ("z", "x", "y"))
    down_half = gathered_rows(down_proj, ("z", "y", "x"))

    flat_ids = ids_two.reshape(-1)
    owner = flat_ids // block_len
    within = flat_ids % block_len
    home = {"z": owner // 8, "y": owner // 4 % 2}
    mine = owner % 4 == c * 2 + x
    table_rows = jnp.concatenate(
        [
            table_a,
            table_b.reshape(2 * groups // 4, 2, block_len - cut, width)
            .transpose(1, 0, 2, 3)
            .reshape(groups, block_len - cut, width),
        ],
        axis=1,
    )
    slot = relative_slots(("z", "y"), home) * block_len + within
    found = jnp.take(
        table_rows.reshape(groups * block_len, width), jnp.where(mine, slot, 0), axis=0
    )
    found = jnp.where(mine[:, None], found, jnp.zeros_like(found)).reshape(2, length, width)

    def to_rows(terms, kind):
        split = terms.reshape(2, 2, half, width)
        moved = swap(pick(split, 1 - c, 1).astype(kind), "c")
        both = pick(split, c, 1).astype(F32) + moved.astype(F32)
        moved = swap(pick(both, 1 - x, 0).astype(kind), "x")
        own = (pick(both, x, 0).astype(F32) + moved.astype(F32)).astype(kind)
        return ordered(own, swap(own, "c"), c, 0).reshape(length, width)

    def to_pair(row):
        own = pick(row.reshape(2, half, width), c, 0)
        moved = swap(own, "x")
        other = ordered(moved, swap(moved, "c"), c, 0).reshape(length, width)
        return ordered(row, other, x, 0)

    raw = to_rows(found, BF).astype(F32)
    unit = raw * lax.rsqrt(jnp.mean(raw * raw, axis=1, keepdims=True) + 1e-06)
    target = (unit * width ** (-0.5)).astype(BF)
    inputs = (input_scale * (unit + noise_level * noise)).astype(BF)

    hidden_zero = dot_nn(inputs, input_full)
    normed_one, inverse_one = norm_parts(hidden_zero)
    first_in = (normed_one * gain_one + bias_one).astype(BF)
    qkv = dot_nn(first_in, qkv_half)
    split = D // 2
    queries = (qkv[:, :split] * HEAD_DIM ** (-0.5)).astype(BF)
    keys = qkv[:, split : 2 * split].astype(BF)
    values = qkv[:, 2 * split :].astype(BF)
    seg_col, seg_row = segments[:, None], segments[None, :]
    blk = min(256, length)
    edges = segments.reshape(length // blk, blk)
    before = jnp.sum(seg_row < edges[:, :1], axis=1, dtype=jnp.int32)
    through = jnp.sum(seg_row <= edges[:, -1:], axis=1, dtype=jnp.int32)
    low_block, high_block = before // blk, (through + blk - 1) // blk
    attended, log_total = attend(queries, keys, values, seg_col, seg_row, low_block, high_block)

    def both_cores(part):
        return part + swap(part.astype(BF), "c").astype(F32)

    hidden_one = hidden_zero + residual_scale * both_cores(dot_nn(attended, attn_half))
    normed_two, inverse_two = norm_parts(hidden_one)
    second_in = (normed_two * gain_two + bias_two).astype(BF)
    pre_act = dot_nn(second_in, up_half) + up_bias_half
    below = 0.5 * (1.0 + lax.erf(pre_act * math.sqrt(0.5)))
    activated = (pre_act * below).astype(BF)
    slope = (
        below + pre_act * (jnp.exp(-0.5 * pre_act * pre_act) * (1.0 / math.sqrt(2.0 * math.pi)))
    ).astype(BF)
    hidden_two = hidden_one + residual_scale * both_cores(dot_nn(activated, down_half))
    final_in = hidden_two.astype(BF)
    outputs = dot_nn(final_in, output_full).astype(BF)

    outputs_two = to_pair(outputs).reshape(2 * length, width)
    raised, tops, ends, reached = score(outputs_two, table_rows)
    ends = ends[:2]

    def joined(first, second):
        top = jnp.maximum(first[0], second[0])
        return jnp.stack(
            [top, first[1] * jnp.exp(first[0] - top) + second[1] * jnp.exp(second[0] - top)]
        )

    all_ends = joined(ends, swap(ends, "c"))
    all_ends = joined(all_ends, swap(all_ends, "x"))
    log_sum = all_ends[0] + jnp.log(all_ends[1])
    share = (reached * jnp.exp(ends[0] - log_sum)[None, :]).T
    expected = to_rows(share.reshape(2, length, width), BF).astype(F32)
    log_row = pick(log_sum.reshape(2, length), x, 0)
    chosen = jnp.sum(outputs.astype(F32) * target.astype(F32), axis=1)
    loss_row = log_row - chosen
    loss_two = ordered(loss_row, swap(loss_row, "x"), x, 0)
    token_loss = pick(pick(loss_two, c, 0).reshape(2, half), x, 0)[None]

    out_grad = (weight_row[:, None] * (expected - target.astype(F32))).astype(BF)
    coef = (
        (weight_two.reshape(-1) * width ** (-0.5))[None, :] * jnp.exp(tops[:, 0] - log_sum[None, :])
    ).T
    table_sums = table_product(raised, outputs_two, coef)

    xyz, yxz = ("x", "y", "z"), ("y", "x", "z")
    row_dims = ("z", "y", "x", None, None)
    pair_dims = ("z", "y", None, "x", None, None)
    zy = (lax.axis_size("z"), lax.axis_size("y"))

    def reduced_rows(grad, order):
        rows = grad.shape[0] // (2 * groups)
        shaped = grad.astype(BF).reshape(zy + (2, rows, grad.shape[1]))
        return reduce_axes(shaped, row_dims, order)

    def reduced_pairs(grad, order):
        rows = grad.shape[0] // (4 * groups)
        shaped = grad.astype(BF).reshape(zy + (2, 2, rows, grad.shape[1]))
        return reduce_axes(shaped, pair_dims, order)

    output_w_grad = dot_tn(final_in, out_grad)
    hidden_two_grad = dot_nt(out_grad, output_full)
    branch_grad = (residual_scale * hidden_two_grad).astype(BF)
    down_own = reduced_rows(dot_tn(activated, branch_grad), xyz)
    pre_grad = (dot_nt(branch_grad, down_half) * slope.astype(F32)).astype(BF)
    up_sum = reduced_pairs(dot_tn(second_in, pre_grad), yxz)
    up_bias_part = jnp.sum(pre_grad, axis=0, dtype=F32)
    second_grad = both_cores(dot_nt(pre_grad, up_half))
    gain_two_part = jnp.sum(second_grad * normed_two, axis=0)
    bias_two_part = jnp.sum(second_grad, axis=0)
    hidden_one_grad = hidden_two_grad + norm_back(second_grad, gain_two, normed_two, inverse_two)
    attn_grad = (residual_scale * hidden_one_grad).astype(BF)
    attn_own = reduced_rows(dot_tn(attended, attn_grad), yxz)
    attended_grad = dot_nt(attn_grad, attn_half).astype(BF)
    query_grad, key_grad, value_grad = attend_back(
        queries,
        keys,
        values,
        attended,
        attended_grad,
        log_total,
        seg_col,
        seg_row,
        low_block,
        high_block,
    )
    qkv_grad = jnp.concatenate(
        [query_grad * jnp.asarray(HEAD_DIM ** (-0.5), BF), key_grad, value_grad], axis=1
    )
    qkv_sum = reduced_pairs(dot_tn(first_in, qkv_grad), xyz)
    first_grad = both_cores(dot_nt(qkv_grad, qkv_half))
    gain_one_part = jnp.sum(first_grad * normed_one, axis=0)
    bias_one_part = jnp.sum(first_grad, axis=0)
    hidden_zero_grad = (
        hidden_one_grad + norm_back(first_grad, gain_one, normed_one, inverse_one)
    ).astype(BF)
    input_w_grad = dot_tn(inputs, hidden_zero_grad)
    embed_grad = input_scale * dot_nt(hidden_zero_grad, input_full)
    token_grad = (
        embed_grad - (weight_row * width ** (-0.5))[:, None] * outputs.astype(F32)
    ).astype(BF)

    token_grad_two = to_pair(token_grad).reshape(2 * length, width)
    slots_here = jnp.where(mine, slot, -1)[None, :]
    table_terms = table_add(table_sums, slots_here, token_grad_two)
    relative = (2, zy[0], block_len, width)

    def reduced_table(terms, order):
        for axis in order:
            at = 0 if axis == "y" or terms.ndim == 3 else 1
            n = lax.axis_size(axis)
            if n == 2:
                keep, send = jnp.take(terms, 0, at), jnp.take(terms, 1, at)
                terms = keep.astype(F32) + swap(send, axis).astype(F32)
            else:
                total = jnp.take(terms, n - 1, at)
                for k in range(n - 2, -1, -1):
                    total = jnp.take(terms, k, at).astype(F32) + ring_down_from(
                        total.astype(BF), axis
                    ).astype(F32)
                terms = total
            if axis != order[-1]:
                terms = terms.astype(BF)
        return terms

    def ring_down_from(value, axis):
        return ring_up(value, axis)

    shaped = table_terms.reshape(relative)
    unit_grad = jnp.concatenate(
        [
            reduced_table(shaped[:, :, :cut], ("y", "z")),
            reduced_table(shaped[:, :, cut:], ("z", "y")),
        ],
        axis=0,
    )
    own_rows = embed_table.astype(F32)
    inverse = lax.rsqrt(jnp.mean(own_rows * own_rows, axis=1, keepdims=True) + 1e-06)
    along = jnp.mean(own_rows * unit_grad, axis=1, keepdims=True)
    table_grad = inverse * unit_grad - own_rows * (inverse * inverse * inverse * along)

    input_rows = input_proj.shape[0]
    small_grad = jnp.concatenate(
        [
            pick(input_w_grad.reshape(zy + (2, 2, input_rows, D)), c, 2).reshape(
                zy + (2, -1, width)
            ),
            pick(output_w_grad.reshape(zy + (2, 2, rows_here, width)), c, 2),
            jnp.concatenate(
                [
                    pick(part.reshape(zy + (2, 2, rows_here)), c, 2)
                    for part in (gain_one_part, bias_one_part, gain_two_part, bias_two_part)
                ]
                + [up_bias_part.reshape(zy + (2, -1))],
                axis=-1,
            )[..., None, :],
            jnp.zeros(zy + (2, 15, width), F32),
        ],
        axis=-2,
    )
    small_own = reduce_axes(small_grad.astype(BF), row_dims, xyz)
    input_own = small_own[:input_count].reshape(input_rows, D)
    output_own = small_own[input_count : input_count + rows_here]
    vector_own = small_own[input_count + rows_here]
    gains = [vector_own[k * rows_here : (k + 1) * rows_here] for k in range(4)]

    def columns_back(sums, split_shape, axis):
        mine_rows, other_rows = pick(sums, c, 0), pick(sums, 1 - c, 0)
        other_cols = swap(other_rows, "c")
        return ordered(
            mine_rows.reshape(split_shape), other_cols.reshape(split_shape), c, axis
        ).reshape(rows_here, -1)

    qkv_own = columns_back(qkv_sum, (rows_here, 3 * heads // 2, HEAD_DIM), 2)
    up_own = columns_back(up_sum, (rows_here, groups, ff_block), 2)
    return (
        token_loss,
        table_grad,
        input_own,
        gains[0],
        gains[1],
        qkv_own,
        attn_own,
        gains[2],
        gains[3],
        up_own,
        vector_own[4 * rows_here :],
        down_own,
        output_own,
    )


def combined_all(shard, axis, combine):
    everything = jax.tree.map(lambda part: lax.all_gather(part, axis), shard)
    first = jax.tree.map(lambda part: part[0], everything)

    def step(k, so_far):
        return combine(so_far, jax.tree.map(lambda part: part[k], everything))

    return lax.fori_loop(1, lax.axis_size(axis), step, first)


def product(left, right):
    return jnp.dot(left, right, preferred_element_type=jnp.float32)


def product_left(left, right):
    return lax.dot_general(
        left, right, (((0,), (0,)), ((), ())), preferred_element_type=jnp.float32
    )


def product_right(left, right):
    return lax.dot_general(
        left, right, (((1,), (1,)), ((), ())), preferred_element_type=jnp.float32
    )


def normalize_rows(matrix):
    return matrix * lax.rsqrt(jnp.mean(matrix * matrix, axis=1, keepdims=True) + 1e-06)


def layer_norm(hidden, norm_gain, norm_bias):
    centre = hidden - jnp.mean(hidden, axis=-1, keepdims=True)
    spread = jnp.mean(centre * centre, axis=-1, keepdims=True)
    return centre * lax.rsqrt(spread + 1e-05) * norm_gain + norm_bias


def exact_gelu(pre_act):
    return jax.nn.gelu(pre_act, approximate=False)


def noise_rows(row_seeds, positions, channel_count):
    channel = lax.iota(jnp.int32, channel_count)
    mixed_once = (
        row_seeds[:, None, None] + 7919 * positions[None, :, None] + 104729 * channel[None, None, :]
    ) % 65521
    mixed_twice = (mixed_once * (mixed_once % 32719) + 31 * channel[None, None, :]) % 65521
    return (mixed_twice.astype(jnp.float32) / 32760.5 - 1.0) * 1.7320508


def time_terms(time_steps):
    fraction = time_steps.astype(jnp.float32) / (TSTEPS - 1)
    noise_level = 0.3 * jnp.exp(fraction * math.log(30.0))
    return (noise_level, lax.rsqrt(1.0 + noise_level * noise_level), 0.5 + fraction)


def masked_scores(query_block, key_rows, segment_block, segment_row):
    scores = jnp.einsum("qhd,khd->hqk", query_block, key_rows, preferred_element_type=jnp.float32)
    same_doc = segment_block[:, None] == segment_row[None, :]
    return jnp.where(same_doc[None], scores, -1e30)


def attend_row(operands):
    queries, key_rows, value_rows, segment_row = operands
    length = queries.shape[0]
    block_rows = math.gcd(length, 512)
    block_count = length // block_rows

    def attend_block(pieces):
        query_block, segment_block = pieces
        scores = masked_scores(query_block, key_rows, segment_block, segment_row)
        row_max = jnp.max(scores, axis=-1, keepdims=True)
        raised = jnp.exp(scores - row_max)
        summed = jnp.sum(raised, axis=-1, keepdims=True)
        probs_low = (raised / summed).astype(jnp.bfloat16)
        attended = jnp.einsum(
            "hqk,khd->qhd", probs_low, value_rows, preferred_element_type=jnp.float32
        )
        return (attended.astype(jnp.bfloat16), (row_max + jnp.log(summed))[..., 0])

    attended, log_total = lax.map(
        attend_block,
        (
            queries.reshape((block_count, block_rows) + queries.shape[1:]),
            segment_row.reshape(block_count, block_rows),
        ),
    )
    return (attended.reshape(queries.shape), log_total)


def attend_back_row(operands):
    queries, key_rows, value_rows, segment_row, grad_rows, log_total = operands
    length = queries.shape[0]
    block_rows = math.gcd(length, 512)
    block_count = length // block_rows

    def back_block(carry, pieces):
        key_sum, value_sum = carry
        query_block, segment_block, grad_block, total_block = pieces
        scores = masked_scores(query_block, key_rows, segment_block, segment_row)
        probs = jnp.exp(scores - total_block[:, :, None])
        prob_grad = jnp.einsum(
            "qhd,khd->hqk", grad_block, value_rows, preferred_element_type=jnp.float32
        )
        score_grad = (
            probs * (prob_grad - jnp.sum(probs * prob_grad, axis=-1, keepdims=True))
        ).astype(jnp.bfloat16)
        query_grad = jnp.einsum(
            "hqk,khd->qhd", score_grad, key_rows, preferred_element_type=jnp.float32
        )
        key_sum = key_sum + jnp.einsum(
            "hqk,qhd->khd", score_grad, query_block, preferred_element_type=jnp.float32
        )
        value_sum = value_sum + jnp.einsum(
            "hqk,qhd->khd",
            probs.astype(jnp.bfloat16),
            grad_block,
            preferred_element_type=jnp.float32,
        )
        return ((key_sum, value_sum), query_grad.astype(jnp.bfloat16))

    block_shape = (block_count, block_rows) + queries.shape[1:]
    start_sums = (jnp.zeros(key_rows.shape, jnp.float32), jnp.zeros(value_rows.shape, jnp.float32))
    (key_sum, value_sum), query_grad = lax.scan(
        back_block,
        start_sums,
        (
            queries.reshape(block_shape),
            segment_row.reshape(block_count, block_rows),
            grad_rows.reshape(block_shape),
            log_total,
        ),
    )
    return (
        query_grad.reshape(queries.shape),
        key_sum.astype(jnp.bfloat16),
        value_sum.astype(jnp.bfloat16),
    )


def join_parts(first, second):
    top = jnp.maximum(first[0], second[0])
    total = first[1] * jnp.exp(first[0] - top) + second[1] * jnp.exp(second[0] - top)
    return (top, total, first[2] + second[2], first[3] + second[3])


def local(
    token_ids,
    segment_ids,
    time_steps,
    row_seeds,
    loss_weights,
    embed_table,
    input_proj,
    attn_gain,
    attn_bias,
    qkv_proj,
    attn_proj,
    mlp_gain,
    mlp_bias,
    up_proj,
    up_bias,
    down_proj,
    output_proj,
):
    seq_count = lax.axis_size("seq")
    seq_place = lax.axis_index("seq")
    dp_count = lax.axis_size("dp")
    row_count, length = token_ids.shape
    local_len = length // seq_count
    tok_count = row_count * local_len
    start_pos = seq_place * local_len
    own_ids = lax.dynamic_slice_in_dim(token_ids, start_pos, local_len, 1)
    positions = start_pos + lax.iota(jnp.int32, local_len)
    gathered = (
        lax.all_gather(embed_table, ("dp", "seq"), axis=0, tiled=True),
        lax.all_gather(input_proj, ("dp", "seq"), axis=0, tiled=True),
        lax.all_gather(attn_gain, ("dp", "seq"), axis=0, tiled=True),
        lax.all_gather(attn_bias, ("dp", "seq"), axis=0, tiled=True),
        lax.all_gather(qkv_proj, ("dp", "seq"), axis=0, tiled=True),
        lax.all_gather(attn_proj, ("dp", "seq"), axis=0, tiled=True),
        lax.all_gather(mlp_gain, ("dp", "seq"), axis=0, tiled=True),
        lax.all_gather(mlp_bias, ("dp", "seq"), axis=0, tiled=True),
        lax.all_gather(up_proj, ("dp", "seq"), axis=0, tiled=True),
        lax.all_gather(up_bias, ("dp", "seq"), axis=0, tiled=True),
        lax.all_gather(down_proj, ("dp", "seq"), axis=0, tiled=True),
        lax.all_gather(output_proj, ("dp", "seq"), axis=0, tiled=True),
    )
    (
        table_full,
        input_full,
        gain_one,
        bias_one,
        qkv_full,
        attn_full,
        gain_two,
        bias_two,
        up_full,
        upbias_full,
        down_full,
        output_full,
    ) = gathered
    vocab_size, embed_width = table_full.shape
    block_len = vocab_size // (dp_count * seq_count)
    unit, unit_back = jax.vjp(normalize_rows, table_full.astype(jnp.float32))
    sub_table = lax.dynamic_slice_in_dim(
        table_full.reshape(dp_count, seq_count, block_len, embed_width), seq_place, 1, 1
    ).reshape(dp_count * block_len, embed_width)
    sub_unit = lax.dynamic_slice_in_dim(
        unit.reshape(dp_count, seq_count, block_len, embed_width), seq_place, 1, 1
    ).reshape(dp_count * block_len, embed_width)
    scaled = (sub_unit * embed_width ** (-0.5)).astype(jnp.bfloat16)
    local_rows = lax.iota(jnp.int32, dp_count * block_len)
    vocab_index = (
        local_rows // block_len * seq_count + seq_place
    ) * block_len + local_rows % block_len
    noise_level, input_scale, residual_scale = time_terms(time_steps)
    noise = noise_rows(row_seeds, positions, embed_width)
    embedded = jnp.take(unit, own_ids, axis=0)
    inputs = (
        (input_scale[:, None, None] * (embedded + noise_level[:, None, None] * noise))
        .astype(jnp.bfloat16)
        .reshape(tok_count, embed_width)
    )
    token_scale = jnp.repeat(residual_scale, local_len)[:, None]
    token_input_scale = jnp.repeat(input_scale, local_len)[:, None]
    hidden_zero = product(inputs, input_full)
    first_norm, first_back = jax.vjp(
        layer_norm, hidden_zero, gain_one.astype(jnp.float32), bias_one.astype(jnp.float32)
    )
    first_in = first_norm.astype(jnp.bfloat16)
    qkv = product(first_in, qkv_full)
    query_tok = (
        (qkv[:, :D] * HEAD_DIM ** (-0.5)).astype(jnp.bfloat16).reshape(row_count, local_len, D)
    )
    key_tok = qkv[:, D : 2 * D].astype(jnp.bfloat16).reshape(row_count, local_len, D)
    value_tok = qkv[:, 2 * D :].astype(jnp.bfloat16).reshape(row_count, local_len, D)
    head_q, head_k, head_v = (
        lax.all_to_all(query_tok, "seq", split_axis=2, concat_axis=1, tiled=True),
        lax.all_to_all(key_tok, "seq", split_axis=2, concat_axis=1, tiled=True),
        lax.all_to_all(value_tok, "seq", split_axis=2, concat_axis=1, tiled=True),
    )
    heads_here = head_q.shape[2] // HEAD_DIM
    head_shape = (row_count, length, heads_here, HEAD_DIM)
    head_q = head_q.reshape(head_shape)
    head_k = head_k.reshape(head_shape)
    head_v = head_v.reshape(head_shape)
    attended, log_total = lax.map(attend_row, (head_q, head_k, head_v, segment_ids))
    attended = attended.reshape(row_count, length, heads_here * HEAD_DIM)
    mixed = lax.all_to_all(attended, "seq", split_axis=1, concat_axis=2, tiled=True).reshape(
        tok_count, D
    )
    hidden_one = hidden_zero + token_scale * product(mixed, attn_full)
    second_norm, second_back = jax.vjp(
        layer_norm, hidden_one, gain_two.astype(jnp.float32), bias_two.astype(jnp.float32)
    )
    second_in = second_norm.astype(jnp.bfloat16)
    pre_act = product(second_in, up_full) + upbias_full.astype(jnp.float32)
    activated, gelu_back = jax.vjp(exact_gelu, pre_act)
    act_low = activated.astype(jnp.bfloat16)
    hidden_two = hidden_one + token_scale * product(act_low, down_full)
    final_in = hidden_two.astype(jnp.bfloat16)
    outputs = product(final_in, output_full).astype(jnp.bfloat16)
    group_tok = seq_count * tok_count
    group_out = lax.all_gather(outputs, "seq", axis=0, tiled=True)
    group_ids = (
        token_ids.reshape(row_count, seq_count, local_len).transpose(1, 0, 2).reshape(group_tok)
    )
    spread = jnp.where(
        lax.iota(jnp.int32, seq_count)[:, None] == seq_place,
        loss_weights.reshape(1, tok_count),
        0.0,
    )
    tile_rows = math.gcd(group_tok, 512)
    tile_count = group_tok // tile_rows
    out_tiles = group_out.reshape(tile_count, tile_rows, embed_width)
    id_tiles = group_ids.reshape(tile_count, tile_rows)

    def part_tile(pieces):
        out_block, target_block = pieces
        logits = product_right(out_block, scaled)
        row_max = jnp.max(logits, axis=1)
        exp_sum = jnp.sum(jnp.exp(logits - row_max[:, None]), axis=1)
        picked = jnp.sum(
            jnp.where(vocab_index[None, :] == target_block[:, None], logits, 0.0), axis=1
        )
        return (row_max, exp_sum, picked)

    part_max, part_sum, part_pick = lax.map(part_tile, (out_tiles, id_tiles))
    top, total, pick, weight_tiles = combined_all(
        (part_max, part_sum, part_pick, spread), "seq", join_parts
    )
    log_tiles = top + jnp.log(total)
    all_loss = log_tiles - pick
    token_loss = lax.dynamic_slice_in_dim(all_loss, seq_place, 1, 0)

    def back_tile(scaled_sum, pieces):
        out_block, target_block, log_block, weight_block = pieces
        logits = product_right(out_block, scaled)
        probs = jnp.exp(logits - log_block[:, None])
        onehot = (vocab_index[None, :] == target_block[:, None]).astype(jnp.float32)
        grad_logits = (weight_block[:, None] * (probs - onehot)).astype(jnp.bfloat16)
        scaled_sum = scaled_sum + product_left(grad_logits, out_block)
        return (scaled_sum, product(grad_logits, scaled))

    scaled_grad, out_terms = lax.scan(
        back_tile,
        jnp.zeros(scaled.shape, jnp.float32),
        (out_tiles, id_tiles, log_tiles, weight_tiles),
    )
    out_terms = out_terms.reshape(tile_count * tile_rows, embed_width)
    out_grad = lax.psum_scatter(out_terms, "seq", scatter_dimension=0, tiled=True).astype(
        jnp.bfloat16
    )
    output_w_grad = product_left(final_in, out_grad)
    hidden_two_grad = product_right(out_grad, output_full)
    branch_grad = (token_scale * hidden_two_grad).astype(jnp.bfloat16)
    down_w_grad = product_left(act_low, branch_grad)
    pre_grad = gelu_back(product_right(branch_grad, down_full))[0].astype(jnp.bfloat16)
    up_w_grad = product_left(second_in, pre_grad)
    upbias_grad = jnp.sum(pre_grad, axis=0, dtype=jnp.float32)
    hidden_one_part, gain_two_grad, bias_two_grad = second_back(product_right(pre_grad, up_full))
    hidden_one_grad = hidden_two_grad + hidden_one_part
    attn_grad = (token_scale * hidden_one_grad).astype(jnp.bfloat16)
    attn_w_grad = product_left(mixed, attn_grad)
    mixed_grad = (
        product_right(attn_grad, attn_full).astype(jnp.bfloat16).reshape(row_count, local_len, D)
    )
    head_grad = lax.all_to_all(mixed_grad, "seq", split_axis=2, concat_axis=1, tiled=True).reshape(
        head_shape
    )
    query_grad, key_grad, value_grad = lax.map(
        attend_back_row, (head_q, head_k, head_v, segment_ids, head_grad, log_total)
    )
    merged_shape = (row_count, length, heads_here * HEAD_DIM)
    query_back, key_back, value_back = (
        lax.all_to_all(
            query_grad.reshape(merged_shape), "seq", split_axis=1, concat_axis=2, tiled=True
        ),
        lax.all_to_all(
            key_grad.reshape(merged_shape), "seq", split_axis=1, concat_axis=2, tiled=True
        ),
        lax.all_to_all(
            value_grad.reshape(merged_shape), "seq", split_axis=1, concat_axis=2, tiled=True
        ),
    )
    qkv_grad = jnp.concatenate(
        [query_back * HEAD_DIM ** (-0.5), key_back, value_back], axis=2
    ).reshape(tok_count, 3 * D)
    qkv_w_grad = product_left(first_in, qkv_grad)
    hidden_zero_part, gain_one_grad, bias_one_grad = first_back(product_right(qkv_grad, qkv_full))
    hidden_zero_grad = (hidden_one_grad + hidden_zero_part).astype(jnp.bfloat16)
    input_w_grad = product_left(inputs, hidden_zero_grad)
    embedded_grad = token_input_scale * product_right(hidden_zero_grad, input_full)
    scaled_part = scaled_grad * embed_width ** (-0.5)
    group_grad = lax.all_gather(
        embedded_grad.astype(jnp.bfloat16), "seq", axis=0, tiled=True
    ).astype(embedded_grad.dtype)
    block_id = group_ids // block_len
    owned = block_id % seq_count == seq_place
    local_slot = jnp.where(
        owned, block_id // seq_count * block_len + group_ids % block_len, scaled.shape[0]
    )
    unit_grad = scaled_part.at[local_slot].add(group_grad, mode="drop")
    table_term = jax.vjp(normalize_rows, sub_table.astype(jnp.float32))[1](unit_grad)[0]
    table_grad = lax.psum_scatter(
        table_term.astype(jnp.bfloat16), "dp", scatter_dimension=0, tiled=True
    ).astype(jnp.float32)
    summed = (
        lax.psum_scatter(input_w_grad, ("dp", "seq"), scatter_dimension=0, tiled=True),
        lax.psum_scatter(gain_one_grad, ("dp", "seq"), scatter_dimension=0, tiled=True),
        lax.psum_scatter(bias_one_grad, ("dp", "seq"), scatter_dimension=0, tiled=True),
        lax.psum_scatter(qkv_w_grad, ("dp", "seq"), scatter_dimension=0, tiled=True),
        lax.psum_scatter(attn_w_grad, ("dp", "seq"), scatter_dimension=0, tiled=True),
        lax.psum_scatter(gain_two_grad, ("dp", "seq"), scatter_dimension=0, tiled=True),
        lax.psum_scatter(bias_two_grad, ("dp", "seq"), scatter_dimension=0, tiled=True),
        lax.psum_scatter(up_w_grad, ("dp", "seq"), scatter_dimension=0, tiled=True),
        lax.psum_scatter(upbias_grad, ("dp", "seq"), scatter_dimension=0, tiled=True),
        lax.psum_scatter(down_w_grad, ("dp", "seq"), scatter_dimension=0, tiled=True),
        lax.psum_scatter(output_w_grad, ("dp", "seq"), scatter_dimension=0, tiled=True),
    )
    return (token_loss.reshape(row_count, local_len), table_grad) + tuple(summed)


def solution(mesh):
    dp, seq = mesh.shape["dp"], mesh.shape["seq"]
    if (dp, seq) == (16, 2):
        inner = Mesh(mesh.devices.reshape(dp // 4, 2, 2, seq), ("z", "y", "c", "x"))
        dp_names, seq_names, body = ("z", "y", "c"), ("x",), paired
    else:
        inner, dp_names, seq_names, body = mesh, ("dp",), ("seq",), local
    every = dp_names + seq_names
    in_specs = (
        P(dp_names, None),
        P(dp_names, None),
        P(dp_names),
        P(dp_names),
        P(dp_names, seq_names),
        P(every, None),
        P(every, None),
        P(every),
        P(every),
        P(every, None),
        P(every, None),
        P(every),
        P(every),
        P(every, None),
        P(every),
        P(every, None),
        P(every, None),
    )
    out_specs = (
        P(dp_names, seq_names),
        P(every, None),
        P(every, None),
        P(every),
        P(every),
        P(every, None),
        P(every, None),
        P(every),
        P(every),
        P(every, None),
        P(every),
        P(every, None),
        P(every, None),
    )
    return jax.shard_map(body, mesh=inner, in_specs=in_specs, out_specs=out_specs, check_vma=False)
```

```python
import math

import jax
import jax.numpy as jnp
from jax import lax
from jax.experimental import pallas as pl
from jax.experimental.pallas import tpu as pltpu
from jax.sharding import Mesh
from jax.sharding import PartitionSpec as P

D = 1024
HEAD_DIM = 64
TSTEPS = 1000
SWAP = ((0, 1), (1, 0))
BF = jnp.bfloat16
F32 = jnp.float32
NEG = -1e30
LIMIT = 70.0
MIB = 1 << 20


def dot_nn(left, right):
    return lax.dot_general(left, right, (((1,), (0,)), ((), ())), preferred_element_type=F32)


def dot_nt(left, right):
    return lax.dot_general(left, right, (((1,), (1,)), ((), ())), preferred_element_type=F32)


def dot_tn(left, right):
    return lax.dot_general(left, right, (((0,), (0,)), ((), ())), preferred_element_type=F32)


def swap(value, axis):
    return lax.ppermute(value, axis, SWAP)


def ring_down(value, axis):
    n = lax.axis_size(axis)
    return lax.ppermute(value, axis, [(i, (i - 1) % n) for i in range(n)])


def ring_up(value, axis):
    n = lax.axis_size(axis)
    return lax.ppermute(value, axis, [(i, (i + 1) % n) for i in range(n)])


def ordered(own, other, place, axis):
    return jnp.where(
        place == 0, jnp.stack([own, other], axis), jnp.stack([other, own], axis)
    )


def pick(value, index, axis):
    return lax.dynamic_index_in_dim(value, index, axis, keepdims=False)


def after(value, *others):
    return lax.optimization_barrier((value,) + others)[0]


def ring_blocks(value, axis):
    parts = [value]
    for _ in range(lax.axis_size(axis) - 1):
        parts.append(ring_down(parts[-1], axis))
    return parts


def joined_swap(held, axis):
    return jnp.concatenate([held, swap(held, axis)], 0)


def apart(value, axis, distance):
    n = lax.axis_size(axis)
    return lax.ppermute(value, axis, [(i, i ^ distance) for i in range(n)])


def joined_apart(value, axis):
    held, distance = value[None], 1
    while distance < lax.axis_size(axis):
        held = jnp.concatenate([held, apart(held, axis, distance)], 0)
        distance *= 2
    return held


def halve(value, axis, at):
    here = lax.axis_index(axis)
    return pick(value, here, at), swap(pick(value, 1 - here, at), axis)


def added(kept, moved):
    return (kept.astype(F32) + moved.astype(F32)).astype(BF)


def ring_start(value, axis):
    n, here = lax.axis_size(axis), lax.axis_index(axis)
    return ring_up(pick(value, (here - 1) % n, 0), axis)


def ring_next(value, moved, step, axis):
    n, here = lax.axis_size(axis), lax.axis_index(axis)
    return pick(value, (here - 1 - step) % n, 0).astype(F32) + moved.astype(F32)


def place_blocks(places, halves, outs):
    flat = halves[0] + halves[1]
    count = sum(piece.shape[0] for piece in flat) * len(outs)

    def body(places_ref, *refs):
        ins, results, sems = refs[: len(flat)], refs[len(flat) : -1], refs[-1]
        copies, block = [], 0
        for number, piece in enumerate(ins):
            for k in range(piece.shape[0]):
                p, h = places_ref[block], number // len(halves[0])
                block += 1
                for (low, high, _, index), result in zip(outs, results):
                    copies.append(
                        pltpu.make_async_copy(
                            piece.at[k, :, low:high],
                            result.at[index(p, h)],
                            sems.at[len(copies)],
                        )
                    )
        for copy in copies:
            copy.start()
        for copy in copies:
            copy.wait()

    return pl.pallas_call(
        body,
        out_shape=tuple(jax.ShapeDtypeStruct(shape, BF) for _, _, shape, _ in outs),
        grid=(1,),
        in_specs=[pl.BlockSpec(memory_space=pltpu.SMEM)]
        + [pl.BlockSpec(memory_space=pl.ANY)] * len(flat),
        out_specs=tuple(
            pl.BlockSpec(shape, lambda i, n=len(shape): (0,) * n) for _, _, shape, _ in outs
        ),
        scratch_shapes=[pltpu.SemaphoreType.DMA((count,))],
        compiler_params=pltpu.CompilerParams(vmem_limit_bytes=24 * MIB),
        name="place_blocks",
    )(places, *flat)


def for_each_window(lo, hi, blocks, run):
    for count in range(1, blocks + 1):

        @pl.when(hi - lo == count)
        def _():
            run(lo, count)


def attend_body(
    lo_ref, hi_ref, q_ref, k_ref, v_ref, seg_col_ref, seg_row_ref, o_ref, lse_ref, v_ones
):
    length = q_ref.shape[0]
    blk = min(256, length)
    lane = lax.broadcasted_iota(jnp.int32, (1, 128), 1)
    masks = (lane < HEAD_DIM, lane >= HEAD_DIM)
    v = v_ref[...]
    for h in range(2):
        v_ones[h] = jnp.where(masks[h], v, jnp.ones_like(v))

    def largest(ref):
        rows = ref[...].astype(F32)
        return jnp.max(jnp.sum(rows * rows, axis=1, keepdims=True))

    small = largest(q_ref) * largest(k_ref) <= LIMIT * LIMIT

    def finish(rows, accs):
        totals = [pltpu.roll(acc, HEAD_DIM, axis=1) for acc in accs]
        o_ref[rows, :] = (
            jnp.where(masks[0], accs[0], accs[1]) / jnp.where(masks[0], totals[0], totals[1])
        ).astype(BF)
        return [accs[0].T[HEAD_DIM : HEAD_DIM + 1], accs[1].T[0:1]]

    def each(qi, _):
        rows = pl.ds(pl.multiple_of(qi * blk, blk), blk)
        q = q_ref[rows, :]
        q_heads = [jnp.where(m, q, jnp.zeros_like(q)) for m in masks]

        def run(first, count):
            at = pl.ds(pl.multiple_of(first * blk, blk), count * blk)
            k = k_ref[at, :]
            same = seg_col_ref[at, :] == seg_row_ref[:, rows]
            accs = []
            for h in range(2):
                e = jnp.exp(jnp.where(same, dot_nt(k, q_heads[h]), NEG)).astype(BF)
                accs.append(dot_tn(e, v_ones[h, at, :]))
            for h, total in enumerate(finish(rows, accs)):
                lse_ref[0, h : h + 1, rows] = jnp.log(total)

        @pl.when(small)
        def _():
            for_each_window(lo_ref[qi], hi_ref[qi], length // blk, run)

        @pl.when(jnp.logical_not(small))
        def _():
            def scores(kb, h):
                at = pl.ds(pl.multiple_of(kb * blk, blk), blk)
                same = seg_col_ref[at, :] == seg_row_ref[:, rows]
                return jnp.where(same, dot_nt(k_ref[at, :], q_heads[h]), NEG)

            def highest(kb, tops):
                return tuple(
                    jnp.maximum(tops[h], jnp.max(scores(kb, h), axis=0, keepdims=True))
                    for h in range(2)
                )

            tops = lax.fori_loop(
                lo_ref[qi], hi_ref[qi], highest, (jnp.full((1, blk), NEG, F32),) * 2
            )

            def gather(kb, accs):
                at = pl.ds(pl.multiple_of(kb * blk, blk), blk)
                return tuple(
                    accs[h]
                    + dot_tn(jnp.exp(scores(kb, h) - tops[h]).astype(BF), v_ones[h, at, :])
                    for h in range(2)
                )

            accs = lax.fori_loop(
                lo_ref[qi], hi_ref[qi], gather, (jnp.zeros((blk, 128), F32),) * 2
            )
            for h, total in enumerate(finish(rows, accs)):
                lse_ref[0, h : h + 1, rows] = tops[h] + jnp.log(total)

        return 0

    lax.fori_loop(0, length // blk, each, 0)


def attend(q, k, v, seg_col, seg_row, lo, hi):
    length, width = q.shape
    pairs = width // 128
    spec = pl.BlockSpec((length, 128), lambda i, *_: (0, i))
    return pl.pallas_call(
        attend_body,
        out_shape=(
            jax.ShapeDtypeStruct((length, width), BF),
            jax.ShapeDtypeStruct((pairs, 2, length), F32),
        ),
        grid_spec=pltpu.PrefetchScalarGridSpec(
            num_scalar_prefetch=2,
            grid=(pairs,),
            in_specs=[
                spec,
                spec,
                spec,
                pl.BlockSpec((length, 1), lambda i, *_: (0, 0)),
                pl.BlockSpec((1, length), lambda i, *_: (0, 0)),
            ],
            out_specs=(spec, pl.BlockSpec((1, 2, length), lambda i, *_: (i, 0, 0))),
            scratch_shapes=[pltpu.VMEM((2, length, 128), BF)],
        ),
        compiler_params=pltpu.CompilerParams(vmem_limit_bytes=32 * MIB),
        cost_estimate=pl.CostEstimate(
            flops=16 * length * length * width, bytes_accessed=8 * length * width, transcendentals=length * length * width // HEAD_DIM
        ),
        name="attend",
    )(lo, hi, q, k, v, seg_col, seg_row)


def attend_back_body(
    lo_ref,
    hi_ref,
    q_ref,
    k_ref,
    v_ref,
    o_ref,
    g_ref,
    lse_ref,
    seg_col_ref,
    seg_row_ref,
    dq_ref,
    dk_ref,
    dv_ref,
    dk_sum,
    dv_sum,
):
    length = q_ref.shape[0]
    blk = min(256, length)
    lane = lax.broadcasted_iota(jnp.int32, (1, 128), 1)
    masks = (lane < HEAD_DIM, lane >= HEAD_DIM)
    dk_sum[...] = jnp.zeros_like(dk_sum)
    dv_sum[...] = jnp.zeros_like(dv_sum)
    def each(qi, _):
        rows = pl.ds(pl.multiple_of(qi * blk, blk), blk)

        def run(first, count):
            q, g = q_ref[rows, :], g_ref[rows, :]
            mixed = (g.astype(F32) * o_ref[rows, :].astype(F32)).T
            at = pl.ds(pl.multiple_of(first * blk, blk), count * blk)
            k, v = k_ref[at, :], v_ref[at, :]
            same = seg_col_ref[at, :] == seg_row_ref[:, rows]
            dq = jnp.zeros((blk, 128), F32)
            dk, dv = dk_sum[at, :], dv_sum[at, :]
            for h in range(2):
                q_head = jnp.where(masks[h], q, jnp.zeros_like(q))
                g_head = jnp.where(masks[h], g, jnp.zeros_like(g))
                k_head = jnp.where(masks[h], k, jnp.zeros_like(k))
                delta = jnp.sum(mixed[h * HEAD_DIM : (h + 1) * HEAD_DIM], axis=0, keepdims=True)
                s = dot_nt(k, q_head)
                p = jnp.exp(jnp.where(same, s - lse_ref[0, h : h + 1, rows], NEG))
                dp = dot_nt(v, g_head)
                ds = (p * (dp - delta)).astype(BF)
                dv = dv + dot_nn(p.astype(BF), g_head)
                dk = dk + dot_nn(ds, q_head)
                dq = dq + dot_tn(ds, k_head)
            dk_sum[at, :] = dk
            dv_sum[at, :] = dv
            dq_ref[rows, :] = dq.astype(BF)

        for_each_window(lo_ref[qi], hi_ref[qi], length // blk, run)
        return 0

    lax.fori_loop(0, length // blk, each, 0)
    dk_ref[...] = dk_sum[...].astype(BF)
    dv_ref[...] = dv_sum[...].astype(BF)


def attend_back(q, k, v, o, g, lse, seg_col, seg_row, lo, hi):
    length, width = q.shape
    pairs = width // 128
    spec = pl.BlockSpec((length, 128), lambda i, *_: (0, i))
    shape = jax.ShapeDtypeStruct((length, width), BF)
    return pl.pallas_call(
        attend_back_body,
        out_shape=(shape, shape, shape),
        grid_spec=pltpu.PrefetchScalarGridSpec(
            num_scalar_prefetch=2,
            grid=(pairs,),
            in_specs=[
                spec,
                spec,
                spec,
                spec,
                spec,
                pl.BlockSpec((1, 2, length), lambda i, *_: (i, 0, 0)),
                pl.BlockSpec((length, 1), lambda i, *_: (0, 0)),
                pl.BlockSpec((1, length), lambda i, *_: (0, 0)),
            ],
            out_specs=(spec, spec, spec),
            scratch_shapes=[pltpu.VMEM((length, 128), F32), pltpu.VMEM((length, 128), F32)],
        ),
        compiler_params=pltpu.CompilerParams(vmem_limit_bytes=32 * MIB),
        cost_estimate=pl.CostEstimate(
            flops=32 * length * length * width, bytes_accessed=16 * length * width, transcendentals=length * length * width // HEAD_DIM
        ),
        name="attend_back",
    )(lo, hi, q, k, v, o, g, lse, seg_col, seg_row)


def score_body(
    small_ref, out_ref, table_ref, slot_ref, raised_ref, tops_ref, acc_ref, total_ref, top
):
    j = pl.program_id(0)
    tokens, width = out_ref.shape
    count = table_ref.shape[1]
    rows = table_ref[0].astype(F32)
    unit = rows * lax.rsqrt(jnp.mean(rows * rows, axis=1, keepdims=True) + 1e-06)
    low = unit * width ** (-0.5)
    scaled, scaled_t = low.astype(BF), low.T.astype(BF)
    row = lax.broadcasted_iota(jnp.int32, (count, 1), 0) + j * count

    @pl.when(j == 0)
    def _():
        acc_ref[...] = jnp.zeros_like(acc_ref)
        total_ref[...] = jnp.zeros_like(total_ref)
        top[...] = jnp.full_like(top, NEG)

    @pl.when(small_ref[0] == 1)
    def _():
        e = jnp.exp(dot_nt(scaled, out_ref[...]))
        total_ref[...] += jnp.sum(e, axis=0, keepdims=True)
        raised_ref[0] = jnp.where(row == slot_ref[...], 0.0, e).astype(BF)
        acc_ref[...] += dot_nn(scaled_t, raised_ref[0])
        tops_ref[0] = jnp.zeros_like(tops_ref[0])

    @pl.when(small_ref[0] == 0)
    def _():
        part = math.gcd(tokens, 512)

        def each(n, _):
            at = pl.ds(pl.multiple_of(n * part, part), part)
            logits = dot_nt(scaled, out_ref[at, :])
            new_top = jnp.maximum(top[:, at], jnp.max(logits, axis=0, keepdims=True))
            keep = jnp.exp(top[:, at] - new_top)
            e = jnp.exp(logits - new_top)
            total_ref[:, at] = total_ref[:, at] * keep + jnp.sum(e, axis=0, keepdims=True)
            raised_ref[0, :, at] = jnp.where(row == slot_ref[:, at], 0.0, e).astype(BF)
            acc_ref[:, at] = acc_ref[:, at] * keep + dot_nn(scaled_t, raised_ref[0, :, at])
            tops_ref[0, :, at] = new_top
            top[:, at] = new_top
            return 0

        lax.fori_loop(0, tokens // part, each, 0)


def score(outputs, table, slots):
    tokens, width = outputs.shape
    blocks, rows, _ = table.shape
    norms = jnp.sum(jnp.square(outputs.astype(F32)), axis=1)
    small = (jnp.max(norms) <= LIMIT * LIMIT).astype(jnp.int32).reshape(1)
    return pl.pallas_call(
        score_body,
        out_shape=(
            jax.ShapeDtypeStruct((blocks, rows, tokens), BF),
            jax.ShapeDtypeStruct((blocks, 1, tokens), F32),
            jax.ShapeDtypeStruct((width, tokens), F32),
            jax.ShapeDtypeStruct((1, tokens), F32),
        ),
        grid_spec=pltpu.PrefetchScalarGridSpec(
            num_scalar_prefetch=1,
            grid=(blocks,),
            in_specs=[
                pl.BlockSpec((tokens, width), lambda j, *_: (0, 0)),
                pl.BlockSpec((1, rows, width), lambda j, *_: (j, 0, 0)),
                pl.BlockSpec((1, tokens), lambda j, *_: (0, 0)),
            ],
            out_specs=(
                pl.BlockSpec((1, rows, tokens), lambda j, *_: (j, 0, 0)),
                pl.BlockSpec((1, 1, tokens), lambda j, *_: (j, 0, 0)),
                pl.BlockSpec((width, tokens), lambda j, *_: (0, 0)),
                pl.BlockSpec((1, tokens), lambda j, *_: (0, 0)),
            ),
            scratch_shapes=[pltpu.VMEM((1, tokens), F32)],
        ),
        compiler_params=pltpu.CompilerParams(vmem_limit_bytes=48 * MIB),
        cost_estimate=pl.CostEstimate(
            flops=4 * blocks * rows * tokens * width,
            bytes_accessed=2 * blocks * rows * tokens,
            transcendentals=blocks * rows * tokens,
        ),
        name="score",
    )(small, outputs, table, slots)


def table_product_body(raised_ref, out_ref, coef_ref, sum_ref):
    j = pl.program_id(0)
    lane = lax.broadcasted_iota(jnp.int32, coef_ref.shape, 1)
    coef = jnp.sum(jnp.where(lane == j, coef_ref[...], 0.0), axis=1, keepdims=True)
    weighted = (out_ref[...].astype(F32) * coef).astype(BF)
    sum_ref[0] = dot_nn(raised_ref[0], weighted)


def table_product(raised, outputs, coef):
    blocks, rows, tokens = raised.shape
    width = outputs.shape[1]
    return pl.pallas_call(
        table_product_body,
        out_shape=jax.ShapeDtypeStruct((blocks, rows, width), F32),
        grid=(blocks,),
        in_specs=[
            pl.BlockSpec((1, rows, tokens), lambda j: (j, 0, 0)),
            pl.BlockSpec((tokens, width), lambda j: (0, 0)),
            pl.BlockSpec((tokens, blocks), lambda j: (0, 0)),
        ],
        out_specs=pl.BlockSpec((1, rows, width), lambda j: (j, 0, 0)),
        compiler_params=pltpu.CompilerParams(vmem_limit_bytes=48 * MIB),
        cost_estimate=pl.CostEstimate(
            flops=2 * blocks * rows * tokens * width, bytes_accessed=2 * blocks * rows * tokens, transcendentals=0
        ),
        name="table_product",
    )(raised, outputs, coef)


def table_add_body(sum_ref, slot_ref, grad_ref, out_ref):
    j = pl.program_id(0)
    rows = sum_ref.shape[1]
    row = lax.broadcasted_iota(jnp.int32, (rows, 1), 0) + j * rows
    chosen = (row == slot_ref[...]).astype(F32).astype(BF)
    out_ref[0] = (sum_ref[0] + dot_nn(chosen, grad_ref[...])).astype(BF)


def table_add(sums, slots, grads):
    blocks, rows, width = sums.shape
    tokens = grads.shape[0]
    return pl.pallas_call(
        table_add_body,
        out_shape=jax.ShapeDtypeStruct(sums.shape, BF),
        grid=(blocks,),
        in_specs=[
            pl.BlockSpec((1, rows, width), lambda j: (j, 0, 0)),
            pl.BlockSpec((1, tokens), lambda j: (0, 0)),
            pl.BlockSpec((tokens, width), lambda j: (0, 0)),
        ],
        out_specs=pl.BlockSpec((1, rows, width), lambda j: (j, 0, 0)),
        compiler_params=pltpu.CompilerParams(vmem_limit_bytes=48 * MIB),
        cost_estimate=pl.CostEstimate(
            flops=2 * blocks * rows * tokens * width, bytes_accessed=6 * blocks * rows * width, transcendentals=0
        ),
        name="table_add",
    )(sums, slots, grads)


def norm_parts(hidden):
    centre = hidden - jnp.mean(hidden, axis=-1, keepdims=True)
    spread = jnp.mean(centre * centre, axis=-1, keepdims=True)
    inverse = lax.rsqrt(spread + 1e-05)
    return centre * inverse, inverse


def norm_back(grad, gain, normed, inverse):
    grad_normed = grad * gain
    first = jnp.mean(grad_normed, axis=-1, keepdims=True)
    second = jnp.mean(grad_normed * normed, axis=-1, keepdims=True)
    return inverse * (grad_normed - first - normed * second)


def noise_field(row_seed, length, channel_count):
    position = lax.iota(jnp.int32, length)[:, None]
    channel = lax.iota(jnp.int32, channel_count)[None, :]
    mixed_once = (row_seed + 7919 * position + 104729 * channel) % 65521
    mixed_twice = (mixed_once * (mixed_once % 32719) + 31 * channel) % 65521
    return (mixed_twice.astype(F32) / 32760.5 - 1.0) * 1.7320508


def paired(
    token_ids,
    segment_ids,
    time_steps,
    row_seeds,
    loss_weights,
    embed_table,
    input_proj,
    attn_gain,
    attn_bias,
    qkv_proj,
    attn_proj,
    mlp_gain,
    mlp_bias,
    up_proj,
    up_bias,
    down_proj,
    output_proj,
):
    z, y, c, x = (lax.axis_index(a) for a in ("z", "y", "c", "x"))
    groups = lax.axis_size("z") * lax.axis_size("y")
    length = token_ids.shape[1]
    half = length // 2
    block_len, width = embed_table.shape
    ff = up_proj.shape[1]
    rows_here = qkv_proj.shape[0]
    heads = D // HEAD_DIM
    ff_block = down_proj.shape[0] * 2

    meta = jnp.concatenate([token_ids[0], segment_ids[0], time_steps, row_seeds])
    meta_two = ordered(meta, swap(meta, "c"), c, 0)
    weight_c = ordered(loss_weights[0], swap(loss_weights[0], "c"), c, 0)
    weight_two = ordered(weight_c, swap(weight_c, "x"), x, 1).reshape(2, length)
    ids_two = meta_two[:, :length]
    own_meta = pick(meta_two, x, 0)
    segments = own_meta[length : 2 * length]
    weight_row = pick(weight_two, x, 0)
    fraction = own_meta[2 * length].astype(F32) / (TSTEPS - 1)
    noise_level = 0.3 * jnp.exp(fraction * math.log(30.0))
    input_scale = lax.rsqrt(1.0 + noise_level * noise_level)
    residual_scale = 0.5 + fraction
    noise = noise_field(own_meta[2 * length + 1], length, width)

    small_width = 2 * width + 128
    vector = jnp.concatenate([attn_gain, attn_bias, mlp_gain, mlp_bias, up_bias])
    small = jnp.concatenate(
        [
            input_proj.reshape(rows_here, width),
            output_proj,
            jnp.pad(vector.reshape(-1, 128), ((0, rows_here - vector.size // 128), (0, 0))),
        ],
        axis=1,
    )
    qkv_split = qkv_proj.reshape(rows_here, 3 * heads // 2, 2, HEAD_DIM)
    up_split = up_proj.reshape(rows_here, groups, 2, ff_block)

    def packed(core):
        return jnp.concatenate(
            [
                pick(qkv_split, core, 2).reshape(rows_here, -1),
                small,
                pick(up_split, core, 2).reshape(rows_here, -1),
            ],
            axis=1,
        )

    pair = ordered(packed(c), swap(packed(1 - c), "c"), c, 0).reshape(2 * rows_here, -1)
    qkv_cols, small_cols = 3 * D // 2, 3 * D // 2 + small_width
    first_cols = small_cols + D // 2
    first_shard = jnp.concatenate(
        [
            pair[:, :small_cols],
            jnp.concatenate([attn_proj[:, : D // 2], attn_proj[:, D // 2 :]], axis=0),
        ],
        axis=1,
    )
    up_shard = pair[:, small_cols:]

    def places(order, ring):
        block, found = jnp.arange(2 * groups, dtype=jnp.int32), {}
        for axis in order:
            n, here = lax.axis_size(axis), lax.axis_index(axis)
            found[axis] = (block + here) % n if ring else (block % n) ^ here
            block = block // n
        return (found["z"] * 2 + found["y"]) * 2 + found["x"]

    def both_places(ring):
        return jnp.concatenate([places(("z", "y", "x"), ring), places(("z", "x", "y"), ring)])

    def over_one(blocks):
        rows = blocks.shape[1] // 2
        return joined_swap(blocks[:, :rows], "y"), joined_swap(blocks[:, rows:], "x")

    def over_other(held):
        return [[held[0], swap(held[0], "x")], [held[1], swap(held[1], "y")]]

    cut = block_len // 32 * 16
    with jax.named_scope("gather_table"):
        table_a = ring_blocks(embed_table[None, :cut], "z")
        table_b = ring_blocks(joined_swap(embed_table[None, cut:], "y"), "z")
        table_z = table_b[-1]
        table_a = joined_swap(jnp.concatenate(table_a, 0), "y")
        table_b = jnp.stack(table_b, 1).reshape(groups, block_len - cut, width)
    with jax.named_scope("gather_first"):
        first_z = ring_blocks(first_shard[None], "z")
        first_pieces = over_other(over_one(jnp.concatenate(first_z, 0)))
    with jax.named_scope("gather_up"):
        up_z = joined_apart(after(up_shard, table_z, first_z[-1]), "z")
    with jax.named_scope("gather_down"):
        down_z = joined_apart(after(down_proj, table_z, first_z[-1]), "z")

    flat_ids = ids_two.reshape(-1)
    owner = flat_ids // block_len
    within = flat_ids % block_len
    home = {"z": owner // 8, "y": owner // 4 % 2}
    mine = owner % 4 == c * 2 + x
    table_rows = jnp.concatenate([table_a, table_b], axis=1)
    zn = lax.axis_size("z")
    relative_y, relative_z = (home["y"] - y) % 2, (home["z"] - z) % zn
    slot = (relative_y * zn + relative_z) * block_len + within
    found = jnp.take(
        table_rows.reshape(groups * block_len, width), jnp.where(mine, slot, 0), axis=0
    )
    found = jnp.where(mine[:, None], found, jnp.zeros_like(found)).reshape(2, length, width)

    def to_rows(terms, kind):
        split = terms.reshape(2, 2, half, width)
        moved = swap(pick(split, 1 - c, 1).astype(kind), "c")
        both = pick(split, c, 1).astype(F32) + moved.astype(F32)
        moved = swap(pick(both, 1 - x, 0).astype(kind), "x")
        own = (pick(both, x, 0).astype(F32) + moved.astype(F32)).astype(kind)
        return ordered(own, swap(own, "c"), c, 0).reshape(length, width)

    def to_pair(row):
        own = pick(row.reshape(2, half, width), c, 0)
        moved = swap(own, "x")
        other = ordered(moved, swap(moved, "c"), c, 0).reshape(length, width)
        return ordered(row, other, x, 0)

    raw = to_rows(found, BF).astype(F32)
    paired_shape = (groups, 2, 2, rows_here)

    def in_pairs(p, h):
        return (p // 2, h, p % 2)

    def held_back(pieces, *values):
        return [[after(piece, *values) for piece in half_pieces] for half_pieces in pieces]

    qkv_half, small_full, attn_half = place_blocks(
        both_places(True),
        held_back(first_pieces, found),
        [
            (0, qkv_cols, paired_shape + (qkv_cols,), in_pairs),
            (qkv_cols, small_cols, paired_shape + (small_width,), in_pairs),
            (
                small_cols,
                first_cols,
                (2 * groups, rows_here, D),
                lambda p, h: (p, slice(None), slice(h * D // 2, (h + 1) * D // 2)),
            ),
        ],
    )
    qkv_half, small_full = qkv_half.reshape(D, qkv_cols), small_full.reshape(D, small_width)
    attn_half = attn_half.reshape(D // 2, D)
    input_full = small_full[:, :width].reshape(width, D)
    output_full = small_full[:, width : 2 * width]
    vectors = small_full[:, 2 * width :].reshape(groups, 2, 2, rows_here, 128)
    vectors = vectors[..., : vector.size // 128, :].reshape(groups, 2, 2, vector.size)
    gain_one, bias_one, gain_two, bias_two = (
        vectors[..., k * rows_here : (k + 1) * rows_here].reshape(1, D).astype(F32)
        for k in range(4)
    )
    up_bias_half = pick(vectors[..., 4 * rows_here :], c, 1).reshape(1, ff // 2).astype(F32)
    unit = raw * lax.rsqrt(jnp.mean(raw * raw, axis=1, keepdims=True) + 1e-06)
    target = (unit * width ** (-0.5)).astype(BF)
    inputs = (input_scale * (unit + noise_level * noise)).astype(BF)

    hidden_zero = dot_nn(inputs, input_full)
    normed_one, inverse_one = norm_parts(hidden_zero)
    first_in = (normed_one * gain_one + bias_one).astype(BF)
    qkv = dot_nn(first_in, qkv_half)
    split = D // 2
    queries = (qkv[:, :split] * HEAD_DIM ** (-0.5)).astype(BF)
    keys = qkv[:, split : 2 * split].astype(BF)
    values = qkv[:, 2 * split :].astype(BF)
    seg_col, seg_row = segments[:, None], segments[None, :]
    blk = min(256, length)
    edges = segments.reshape(length // blk, blk)
    before = jnp.sum(seg_row < edges[:, :1], axis=1, dtype=jnp.int32)
    through = jnp.sum(seg_row <= edges[:, -1:], axis=1, dtype=jnp.int32)
    low_block, high_block = before // blk, (through + blk - 1) // blk
    with jax.named_scope("gather_up"):
        up_held = over_one(after(up_z, first_in))
        up_pieces = over_other(up_held)
    with jax.named_scope("gather_down"):
        down_held = over_one(after(down_z, first_in))
    attended, log_total = attend(
        after(queries, *up_held, *down_held),
        keys,
        values,
        seg_col,
        seg_row,
        low_block,
        high_block,
    )
    with jax.named_scope("gather_down"):
        down_pieces = over_other(down_held)

    (up_half,) = place_blocks(
        both_places(False),
        held_back(up_pieces, attended),
        [(0, ff // 2, paired_shape + (ff // 2,), in_pairs)],
    )
    up_half = up_half.reshape(D, ff // 2)
    (down_half,) = place_blocks(
        both_places(False),
        held_back(down_pieces, attended),
        [
            (
                0,
                D,
                (2 * groups, 2, down_proj.shape[0] // 2, D),
                lambda p, h: (p, h),
            )
        ],
    )
    down_half = down_half.reshape(ff // 2, D)

    def both_cores(part):
        return part + swap(part.astype(BF), "c").astype(F32)

    hidden_one = hidden_zero + residual_scale * both_cores(dot_nn(attended, attn_half))
    normed_two, inverse_two = norm_parts(hidden_one)
    second_in = (normed_two * gain_two + bias_two).astype(BF)
    pre_act = dot_nn(second_in, up_half) + up_bias_half
    below = 0.5 * (1.0 + lax.erf(pre_act * math.sqrt(0.5)))
    activated = (pre_act * below).astype(BF)
    slope = (
        below + pre_act * (jnp.exp(-0.5 * pre_act * pre_act) * (1.0 / math.sqrt(2.0 * math.pi)))
    ).astype(BF)
    hidden_two = hidden_one + residual_scale * both_cores(dot_nn(activated, down_half))
    final_in = hidden_two.astype(BF)
    outputs = dot_nn(final_in, output_full).astype(BF)

    outputs_two = to_pair(outputs).reshape(2 * length, width)
    slots_here = jnp.where(mine, slot, -1)[None, :]
    raised, tops, reached, total = score(outputs_two, table_rows, slots_here)
    ends = jnp.concatenate([tops[-1], total])

    def joined(first, second):
        top = jnp.maximum(first[0], second[0])
        return jnp.stack(
            [top, first[1] * jnp.exp(first[0] - top) + second[1] * jnp.exp(second[0] - top)]
        )

    all_ends = joined(ends, swap(ends, "c"))
    all_ends = joined(all_ends, swap(all_ends, "x"))
    log_sum = all_ends[0] + jnp.log(all_ends[1])
    share = (reached * jnp.exp(ends[0] - log_sum)[None, :]).astype(BF)
    parts = [share[:, k * half : (k + 1) * half] for k in range(4)]
    kept = jnp.concatenate([jnp.where(c == 0, parts[0], parts[1]), jnp.where(c == 0, parts[2], parts[3])], 1)
    sent = jnp.concatenate([jnp.where(c == 0, parts[1], parts[0]), jnp.where(c == 0, parts[3], parts[2])], 1)
    both = kept.astype(F32) + swap(sent, "c").astype(F32)
    own, other = jnp.where(x == 0, both[:, :half], both[:, half:]), jnp.where(x == 0, both[:, half:], both[:, :half])
    own = (own + swap(other.astype(BF), "x").astype(F32)).astype(BF)
    moved = swap(own, "c")
    expected = jnp.concatenate(
        [jnp.where(c == 0, own, moved), jnp.where(c == 0, moved, own)], 1
    ).astype(F32).T
    log_row = pick(log_sum.reshape(2, length), x, 0)
    chosen = jnp.sum(outputs.astype(F32) * target.astype(F32), axis=1)
    loss_row = log_row - chosen
    loss_two = ordered(loss_row, swap(loss_row, "x"), x, 0)
    token_loss = pick(pick(loss_two, c, 0).reshape(2, half), x, 0)[None]

    own_term = weight_row * (jnp.exp(chosen - log_row) - 1.0)
    out_grad = (
        weight_row[:, None] * expected + own_term[:, None] * target.astype(F32)
    ).astype(BF)
    coef = (
        (weight_two.reshape(-1) * width ** (-0.5))[None, :] * jnp.exp(tops[:, 0] - log_sum[None, :])
    ).T
    table_sums = table_product(raised, outputs_two, coef)

    zy = (zn, lax.axis_size("y"))
    table_cut = cut

    def rows_of(grad):
        rows = grad.shape[0] // (2 * groups)
        return grad.astype(BF).reshape(zy + (2, rows, grad.shape[1]))

    def pairs_of(grad):
        rows = grad.shape[0] // (4 * groups)
        shaped = grad.astype(BF).reshape(zy + (2, 2, rows, grad.shape[1]))
        return shaped[:, :, 0], shaped[:, :, 1]

    output_w_grad = dot_tn(final_in, out_grad)
    hidden_two_grad = dot_nt(out_grad, output_full)
    branch_grad = (residual_scale * hidden_two_grad).astype(BF)
    with jax.named_scope("reduce_down"):
        down_terms = rows_of(dot_tn(activated, branch_grad))
        rows = down_terms.shape[3] // 2
        down_a = halve(down_terms[..., :rows, :], "x", 2)
        down_b = halve(down_terms[..., rows:, :], "y", 1)
    pre_grad = (
        dot_nt(after(branch_grad, down_terms), down_half) * slope.astype(F32)
    ).astype(BF)
    with jax.named_scope("reduce_up"):
        up_terms = dot_tn(second_in, pre_grad).astype(BF)
        up_a, up_b = pairs_of(up_terms)
        up_a, up_b = halve(up_a, "y", 1), halve(up_b, "x", 2)
    up_bias_part = jnp.sum(pre_grad, axis=0, dtype=F32)
    second_grad = both_cores(dot_nt(after(pre_grad, up_terms), up_half))
    gain_two_part = jnp.sum(second_grad * normed_two, axis=0)
    bias_two_part = jnp.sum(second_grad, axis=0)
    hidden_one_grad = hidden_two_grad + norm_back(second_grad, gain_two, normed_two, inverse_two)
    attn_grad = (residual_scale * hidden_one_grad).astype(BF)
    with jax.named_scope("reduce_attn"):
        attn_terms = halve(rows_of(dot_tn(attended, attn_grad)), "y", 1)
    attended_grad = dot_nt(attn_grad, attn_half).astype(BF)
    with jax.named_scope("reduce_down"):
        down_a = added(down_a[0], after(down_a[1], attn_grad))
        down_b = added(down_b[0], after(down_b[1], attn_grad))
        down_next_a, down_next_b = halve(down_a, "y", 1), halve(down_b, "x", 1)
    with jax.named_scope("reduce_up"):
        up_a = added(up_a[0], after(up_a[1], attended_grad))
        up_b = added(up_b[0], after(up_b[1], attended_grad))
        up_next_a, up_next_b = halve(up_a, "x", 1), halve(up_b, "y", 1)
    query_grad, key_grad, value_grad = attend_back(
        queries,
        keys,
        values,
        attended,
        after(attended_grad, down_a, down_b, up_a, up_b, attn_terms[0]),
        log_total,
        seg_col,
        seg_row,
        low_block,
        high_block,
    )
    with jax.named_scope("reduce_mlp"):
        mlp_sum = jnp.concatenate(
            [
                jnp.concatenate(
                    [
                        added(up_next_a[0], after(up_next_a[1], query_grad)),
                        added(up_next_b[0], after(up_next_b[1], query_grad)),
                    ],
                    1,
                ),
                added(down_next_a[0], after(down_next_a[1], query_grad)),
                added(down_next_b[0], after(down_next_b[1], query_grad)),
            ],
            2,
        )
        mlp_ring = ring_start(mlp_sum, "z")
    with jax.named_scope("reduce_attn"):
        attn_terms = halve(added(attn_terms[0], after(attn_terms[1], query_grad)), "x", 1)
    qkv_grad = jnp.concatenate(
        [query_grad * jnp.asarray(HEAD_DIM ** (-0.5), BF), key_grad, value_grad], axis=1
    )
    first_part = dot_nt(qkv_grad, qkv_half)
    with jax.named_scope("reduce_qkv"):
        qkv_a, qkv_b = pairs_of(dot_tn(first_in, qkv_grad))
        qkv_a = halve(qkv_a, "y", 1)
    first_grad = both_cores(first_part)
    gain_one_part = jnp.sum(first_grad * normed_one, axis=0)
    bias_one_part = jnp.sum(first_grad, axis=0)
    hidden_zero_grad = (
        hidden_one_grad + norm_back(first_grad, gain_one, normed_one, inverse_one)
    ).astype(BF)
    embed_grad = input_scale * dot_nt(hidden_zero_grad, input_full)
    token_grad = (
        embed_grad + (own_term * width ** (-0.5))[:, None] * outputs.astype(F32)
    ).astype(BF)
    token_own = pick(token_grad.reshape(2, half, width), c, 0)
    with jax.named_scope("token_pair"):
        token_moved = swap(token_own, "x")
    with jax.named_scope("reduce_mlp"):
        mlp_ring = ring_up(ring_next(mlp_sum, after(mlp_ring, token_own), 1, "z").astype(BF), "z")
    with jax.named_scope("token_pair"):
        token_other = ordered(token_moved, swap(token_moved, "c"), c, 0).reshape(length, width)
        token_grad_two = ordered(token_grad, token_other, x, 0).reshape(2 * length, width)
    with jax.named_scope("reduce_qkv"):
        qkv_b = halve(after(qkv_b, token_moved), "x", 2)

    input_w_grad = dot_tn(inputs, hidden_zero_grad)
    input_rows = input_proj.shape[0]
    with jax.named_scope("reduce_small"):
        vector_grad = jnp.concatenate(
            [
                pick(part.reshape(zy + (2, 2, rows_here)), c, 2)
                for part in (gain_one_part, bias_one_part, gain_two_part, bias_two_part)
            ]
            + [up_bias_part.reshape(zy + (2, -1))],
            axis=-1,
        ).reshape(zy + (2, -1, 128))
        small_grad = jnp.concatenate(
            [
                pick(input_w_grad.reshape(zy + (2, 2, input_rows, D)), c, 2).reshape(
                    zy + (2, rows_here, width)
                ),
                pick(output_w_grad.reshape(zy + (2, 2, rows_here, width)), c, 2),
                jnp.pad(
                    vector_grad,
                    ((0, 0),) * 3 + ((0, rows_here - vector_grad.shape[3]), (0, 128)),
                ),
            ],
            axis=-1,
        ).astype(BF)
        small_terms = halve(small_grad, "y", 1)

    table_terms = table_add(table_sums, slots_here, token_grad_two)
    with jax.named_scope("reduce_table"):
        terms = table_terms.reshape(2, zn, block_len, width)
        terms_a, terms_b = terms[:, :, :table_cut], terms[:, :, table_cut:]
        moved_a = swap(terms_a[1], "y")
        moved_b = ring_up(terms_b[:, zn - 1], "z")
    with jax.named_scope("reduce_mlp"):
        mlp_ring = ring_up(
            ring_next(mlp_sum, after(mlp_ring, table_terms), 2, "z").astype(BF), "z"
        )
    with jax.named_scope("reduce_small"):
        small_terms = halve(added(small_terms[0], after(small_terms[1], token_moved)), "x", 1)
    with jax.named_scope("reduce_qkv"):
        qkv_a = halve(added(qkv_a[0], after(qkv_a[1], table_terms)), "x", 1)
        qkv_b = halve(added(qkv_b[0], after(qkv_b[1], table_terms)), "y", 1)
    with jax.named_scope("reduce_table"):
        sums_b = [terms_b[:, zn - 2].astype(F32) + moved_b.astype(F32)]
        moved_b = ring_up(sums_b[-1].astype(BF), "z")
    with jax.named_scope("reduce_rest"):
        attn_sum = added(attn_terms[0], after(attn_terms[1], table_terms))
        rest_sum = jnp.concatenate(
            [
                jnp.concatenate(
                    [
                        added(qkv_a[0], after(qkv_a[1], sums_b[-1])),
                        added(qkv_b[0], after(qkv_b[1], sums_b[-1])),
                    ],
                    1,
                ),
                jnp.concatenate(
                    [small_terms[0].astype(F32) + after(small_terms[1], sums_b[-1]).astype(F32)], 0
                )
                .astype(BF)
                .reshape(zn, rows_here, 2, -1)
                .transpose(0, 2, 1, 3)
                .reshape(zn, 2 * rows_here, -1),
                attn_sum.reshape(zn, rows_here, 2, D // 2)
                .transpose(0, 2, 1, 3)
                .reshape(zn, 2 * rows_here, D // 2),
            ],
            2,
        )
        rest_ring = ring_start(rest_sum, "z")
    with jax.named_scope("reduce_table"):
        sum_a = added(terms_a[0], after(moved_a, rest_sum))
        ring_a = ring_up(sum_a[zn - 1], "z")
        for step in range(2, zn):
            sums_b.append(terms_b[:, zn - 1 - step].astype(F32) + after(moved_b, sum_a).astype(F32))
            if step < zn - 1:
                moved_b = ring_up(sums_b[-1].astype(BF), "z")
        last_b = sums_b[-1] if zn > 2 else sums_b[0]
        swap_b = swap(last_b[1].astype(BF), "y")
    with jax.named_scope("reduce_rest"):
        rest_ring = ring_up(
            ring_next(rest_sum, after(rest_ring, last_b), 1, "z").astype(BF), "z"
        )
    with jax.named_scope("reduce_table"):
        total_a = sum_a[zn - 2].astype(F32) + ring_a.astype(F32)
        for k in range(zn - 3, -1, -1):
            total_a = sum_a[k].astype(F32) + ring_up(total_a.astype(BF), "z").astype(F32)
        total_b = last_b[0] + swap_b.astype(F32)
    with jax.named_scope("reduce_mlp"):
        mlp_own = ring_next(mlp_sum, after(mlp_ring, rest_sum), 3, "z")
    with jax.named_scope("reduce_rest"):
        rest_ring = ring_up(ring_next(rest_sum, rest_ring, 2, "z").astype(BF), "z")
        rest_own = ring_next(rest_sum, rest_ring, 3, "z")

    up_total = mlp_own[:, : ff // 2].reshape(2, rows_here, ff // 2)
    down_own = jnp.concatenate([mlp_own[:, ff // 2 : ff // 2 + D], mlp_own[:, ff // 2 + D :]], 0)
    qkv_total = rest_own[:, :qkv_cols].reshape(2, rows_here, qkv_cols)
    small_end = rest_own.shape[1] - D // 2
    small_own = rest_own[:, qkv_cols:small_end]
    small_own = jnp.concatenate([small_own[:rows_here], small_own[rows_here:]], 1)
    attn_own = rest_own[:, small_end:]
    attn_own = jnp.concatenate([attn_own[:rows_here], attn_own[rows_here:]], 1)

    unit_grad = jnp.concatenate([total_a, total_b], axis=0)
    own_rows = embed_table.astype(F32)
    inverse = lax.rsqrt(jnp.mean(own_rows * own_rows, axis=1, keepdims=True) + 1e-06)
    along = jnp.mean(own_rows * unit_grad, axis=1, keepdims=True)
    table_grad = inverse * unit_grad - own_rows * (inverse * inverse * inverse * along)

    input_own = small_own[:, :width].reshape(input_rows, D)
    output_own = small_own[:, width : 2 * width]
    vector_own = small_own[: vector.size // 128, 2 * width : 2 * width + 128].reshape(-1)
    gains = [vector_own[k * rows_here : (k + 1) * rows_here] for k in range(4)]

    def columns_back(sums, split_shape, axis):
        mine_rows, other_rows = pick(sums, c, 0), pick(sums, 1 - c, 0)
        other_cols = swap(other_rows, "c")
        return ordered(
            mine_rows.reshape(split_shape), other_cols.reshape(split_shape), c, axis
        ).reshape(rows_here, -1)

    qkv_own = columns_back(qkv_total, (rows_here, 3 * heads // 2, HEAD_DIM), 2)
    up_own = columns_back(up_total, (rows_here, groups, ff_block), 2)
    return (
        token_loss,
        table_grad,
        input_own,
        gains[0],
        gains[1],
        qkv_own,
        attn_own,
        gains[2],
        gains[3],
        up_own,
        vector_own[4 * rows_here :],
        down_own,
        output_own,
    )


def combined_all(shard, axis, combine):
    everything = jax.tree.map(lambda part: lax.all_gather(part, axis), shard)
    first = jax.tree.map(lambda part: part[0], everything)

    def step(k, so_far):
        return combine(so_far, jax.tree.map(lambda part: part[k], everything))

    return lax.fori_loop(1, lax.axis_size(axis), step, first)


def product(left, right):
    return jnp.dot(left, right, preferred_element_type=jnp.float32)


def product_left(left, right):
    return lax.dot_general(
        left, right, (((0,), (0,)), ((), ())), preferred_element_type=jnp.float32
    )


def product_right(left, right):
    return lax.dot_general(
        left, right, (((1,), (1,)), ((), ())), preferred_element_type=jnp.float32
    )


def normalize_rows(matrix):
    return matrix * lax.rsqrt(jnp.mean(matrix * matrix, axis=1, keepdims=True) + 1e-06)


def layer_norm(hidden, norm_gain, norm_bias):
    centre = hidden - jnp.mean(hidden, axis=-1, keepdims=True)
    spread = jnp.mean(centre * centre, axis=-1, keepdims=True)
    return centre * lax.rsqrt(spread + 1e-05) * norm_gain + norm_bias


def exact_gelu(pre_act):
    return jax.nn.gelu(pre_act, approximate=False)


def noise_rows(row_seeds, positions, channel_count):
    channel = lax.iota(jnp.int32, channel_count)
    mixed_once = (
        row_seeds[:, None, None] + 7919 * positions[None, :, None] + 104729 * channel[None, None, :]
    ) % 65521
    mixed_twice = (mixed_once * (mixed_once % 32719) + 31 * channel[None, None, :]) % 65521
    return (mixed_twice.astype(jnp.float32) / 32760.5 - 1.0) * 1.7320508


def time_terms(time_steps):
    fraction = time_steps.astype(jnp.float32) / (TSTEPS - 1)
    noise_level = 0.3 * jnp.exp(fraction * math.log(30.0))
    return (noise_level, lax.rsqrt(1.0 + noise_level * noise_level), 0.5 + fraction)


def masked_scores(query_block, key_rows, segment_block, segment_row):
    scores = jnp.einsum("qhd,khd->hqk", query_block, key_rows, preferred_element_type=jnp.float32)
    same_doc = segment_block[:, None] == segment_row[None, :]
    return jnp.where(same_doc[None], scores, -1e30)


def attend_row(operands):
    queries, key_rows, value_rows, segment_row = operands
    length = queries.shape[0]
    block_rows = math.gcd(length, 512)
    block_count = length // block_rows

    def attend_block(pieces):
        query_block, segment_block = pieces
        scores = masked_scores(query_block, key_rows, segment_block, segment_row)
        row_max = jnp.max(scores, axis=-1, keepdims=True)
        raised = jnp.exp(scores - row_max)
        summed = jnp.sum(raised, axis=-1, keepdims=True)
        probs_low = (raised / summed).astype(jnp.bfloat16)
        attended = jnp.einsum(
            "hqk,khd->qhd", probs_low, value_rows, preferred_element_type=jnp.float32
        )
        return (attended.astype(jnp.bfloat16), (row_max + jnp.log(summed))[..., 0])

    attended, log_total = lax.map(
        attend_block,
        (
            queries.reshape((block_count, block_rows) + queries.shape[1:]),
            segment_row.reshape(block_count, block_rows),
        ),
    )
    return (attended.reshape(queries.shape), log_total)


def attend_back_row(operands):
    queries, key_rows, value_rows, segment_row, grad_rows, log_total = operands
    length = queries.shape[0]
    block_rows = math.gcd(length, 512)
    block_count = length // block_rows

    def back_block(carry, pieces):
        key_sum, value_sum = carry
        query_block, segment_block, grad_block, total_block = pieces
        scores = masked_scores(query_block, key_rows, segment_block, segment_row)
        probs = jnp.exp(scores - total_block[:, :, None])
        prob_grad = jnp.einsum(
            "qhd,khd->hqk", grad_block, value_rows, preferred_element_type=jnp.float32
        )
        score_grad = (
            probs * (prob_grad - jnp.sum(probs * prob_grad, axis=-1, keepdims=True))
        ).astype(jnp.bfloat16)
        query_grad = jnp.einsum(
            "hqk,khd->qhd", score_grad, key_rows, preferred_element_type=jnp.float32
        )
        key_sum = key_sum + jnp.einsum(
            "hqk,qhd->khd", score_grad, query_block, preferred_element_type=jnp.float32
        )
        value_sum = value_sum + jnp.einsum(
            "hqk,qhd->khd",
            probs.astype(jnp.bfloat16),
            grad_block,
            preferred_element_type=jnp.float32,
        )
        return ((key_sum, value_sum), query_grad.astype(jnp.bfloat16))

    block_shape = (block_count, block_rows) + queries.shape[1:]
    start_sums = (jnp.zeros(key_rows.shape, jnp.float32), jnp.zeros(value_rows.shape, jnp.float32))
    (key_sum, value_sum), query_grad = lax.scan(
        back_block,
        start_sums,
        (
            queries.reshape(block_shape),
            segment_row.reshape(block_count, block_rows),
            grad_rows.reshape(block_shape),
            log_total,
        ),
    )
    return (
        query_grad.reshape(queries.shape),
        key_sum.astype(jnp.bfloat16),
        value_sum.astype(jnp.bfloat16),
    )


def join_parts(first, second):
    top = jnp.maximum(first[0], second[0])
    total = first[1] * jnp.exp(first[0] - top) + second[1] * jnp.exp(second[0] - top)
    return (top, total, first[2] + second[2], first[3] + second[3])


def local(
    token_ids,
    segment_ids,
    time_steps,
    row_seeds,
    loss_weights,
    embed_table,
    input_proj,
    attn_gain,
    attn_bias,
    qkv_proj,
    attn_proj,
    mlp_gain,
    mlp_bias,
    up_proj,
    up_bias,
    down_proj,
    output_proj,
):
    seq_count = lax.axis_size("seq")
    seq_place = lax.axis_index("seq")
    dp_count = lax.axis_size("dp")
    row_count, length = token_ids.shape
    local_len = length // seq_count
    tok_count = row_count * local_len
    start_pos = seq_place * local_len
    own_ids = lax.dynamic_slice_in_dim(token_ids, start_pos, local_len, 1)
    positions = start_pos + lax.iota(jnp.int32, local_len)
    gathered = (
        lax.all_gather(embed_table, ("dp", "seq"), axis=0, tiled=True),
        lax.all_gather(input_proj, ("dp", "seq"), axis=0, tiled=True),
        lax.all_gather(attn_gain, ("dp", "seq"), axis=0, tiled=True),
        lax.all_gather(attn_bias, ("dp", "seq"), axis=0, tiled=True),
        lax.all_gather(qkv_proj, ("dp", "seq"), axis=0, tiled=True),
        lax.all_gather(attn_proj, ("dp", "seq"), axis=0, tiled=True),
        lax.all_gather(mlp_gain, ("dp", "seq"), axis=0, tiled=True),
        lax.all_gather(mlp_bias, ("dp", "seq"), axis=0, tiled=True),
        lax.all_gather(up_proj, ("dp", "seq"), axis=0, tiled=True),
        lax.all_gather(up_bias, ("dp", "seq"), axis=0, tiled=True),
        lax.all_gather(down_proj, ("dp", "seq"), axis=0, tiled=True),
        lax.all_gather(output_proj, ("dp", "seq"), axis=0, tiled=True),
    )
    (
        table_full,
        input_full,
        gain_one,
        bias_one,
        qkv_full,
        attn_full,
        gain_two,
        bias_two,
        up_full,
        upbias_full,
        down_full,
        output_full,
    ) = gathered
    vocab_size, embed_width = table_full.shape
    block_len = vocab_size // (dp_count * seq_count)
    unit, unit_back = jax.vjp(normalize_rows, table_full.astype(jnp.float32))
    sub_table = lax.dynamic_slice_in_dim(
        table_full.reshape(dp_count, seq_count, block_len, embed_width), seq_place, 1, 1
    ).reshape(dp_count * block_len, embed_width)
    sub_unit = lax.dynamic_slice_in_dim(
        unit.reshape(dp_count, seq_count, block_len, embed_width), seq_place, 1, 1
    ).reshape(dp_count * block_len, embed_width)
    scaled = (sub_unit * embed_width ** (-0.5)).astype(jnp.bfloat16)
    local_rows = lax.iota(jnp.int32, dp_count * block_len)
    vocab_index = (
        local_rows // block_len * seq_count + seq_place
    ) * block_len + local_rows % block_len
    noise_level, input_scale, residual_scale = time_terms(time_steps)
    noise = noise_rows(row_seeds, positions, embed_width)
    embedded = jnp.take(unit, own_ids, axis=0)
    inputs = (
        (input_scale[:, None, None] * (embedded + noise_level[:, None, None] * noise))
        .astype(jnp.bfloat16)
        .reshape(tok_count, embed_width)
    )
    token_scale = jnp.repeat(residual_scale, local_len)[:, None]
    token_input_scale = jnp.repeat(input_scale, local_len)[:, None]
    hidden_zero = product(inputs, input_full)
    first_norm, first_back = jax.vjp(
        layer_norm, hidden_zero, gain_one.astype(jnp.float32), bias_one.astype(jnp.float32)
    )
    first_in = first_norm.astype(jnp.bfloat16)
    qkv = product(first_in, qkv_full)
    query_tok = (
        (qkv[:, :D] * HEAD_DIM ** (-0.5)).astype(jnp.bfloat16).reshape(row_count, local_len, D)
    )
    key_tok = qkv[:, D : 2 * D].astype(jnp.bfloat16).reshape(row_count, local_len, D)
    value_tok = qkv[:, 2 * D :].astype(jnp.bfloat16).reshape(row_count, local_len, D)
    head_q, head_k, head_v = (
        lax.all_to_all(query_tok, "seq", split_axis=2, concat_axis=1, tiled=True),
        lax.all_to_all(key_tok, "seq", split_axis=2, concat_axis=1, tiled=True),
        lax.all_to_all(value_tok, "seq", split_axis=2, concat_axis=1, tiled=True),
    )
    heads_here = head_q.shape[2] // HEAD_DIM
    head_shape = (row_count, length, heads_here, HEAD_DIM)
    head_q = head_q.reshape(head_shape)
    head_k = head_k.reshape(head_shape)
    head_v = head_v.reshape(head_shape)
    attended, log_total = lax.map(attend_row, (head_q, head_k, head_v, segment_ids))
    attended = attended.reshape(row_count, length, heads_here * HEAD_DIM)
    mixed = lax.all_to_all(attended, "seq", split_axis=1, concat_axis=2, tiled=True).reshape(
        tok_count, D
    )
    hidden_one = hidden_zero + token_scale * product(mixed, attn_full)
    second_norm, second_back = jax.vjp(
        layer_norm, hidden_one, gain_two.astype(jnp.float32), bias_two.astype(jnp.float32)
    )
    second_in = second_norm.astype(jnp.bfloat16)
    pre_act = product(second_in, up_full) + upbias_full.astype(jnp.float32)
    activated, gelu_back = jax.vjp(exact_gelu, pre_act)
    act_low = activated.astype(jnp.bfloat16)
    hidden_two = hidden_one + token_scale * product(act_low, down_full)
    final_in = hidden_two.astype(jnp.bfloat16)
    outputs = product(final_in, output_full).astype(jnp.bfloat16)
    group_tok = seq_count * tok_count
    group_out = lax.all_gather(outputs, "seq", axis=0, tiled=True)
    group_ids = (
        token_ids.reshape(row_count, seq_count, local_len).transpose(1, 0, 2).reshape(group_tok)
    )
    spread = jnp.where(
        lax.iota(jnp.int32, seq_count)[:, None] == seq_place,
        loss_weights.reshape(1, tok_count),
        0.0,
    )
    tile_rows = math.gcd(group_tok, 512)
    tile_count = group_tok // tile_rows
    out_tiles = group_out.reshape(tile_count, tile_rows, embed_width)
    id_tiles = group_ids.reshape(tile_count, tile_rows)

    def part_tile(pieces):
        out_block, target_block = pieces
        logits = product_right(out_block, scaled)
        row_max = jnp.max(logits, axis=1)
        exp_sum = jnp.sum(jnp.exp(logits - row_max[:, None]), axis=1)
        picked = jnp.sum(
            jnp.where(vocab_index[None, :] == target_block[:, None], logits, 0.0), axis=1
        )
        return (row_max, exp_sum, picked)

    part_max, part_sum, part_pick = lax.map(part_tile, (out_tiles, id_tiles))
    top, total, pick, weight_tiles = combined_all(
        (part_max, part_sum, part_pick, spread), "seq", join_parts
    )
    log_tiles = top + jnp.log(total)
    all_loss = log_tiles - pick
    token_loss = lax.dynamic_slice_in_dim(all_loss, seq_place, 1, 0)

    def back_tile(scaled_sum, pieces):
        out_block, target_block, log_block, weight_block = pieces
        logits = product_right(out_block, scaled)
        probs = jnp.exp(logits - log_block[:, None])
        onehot = (vocab_index[None, :] == target_block[:, None]).astype(jnp.float32)
        grad_logits = (weight_block[:, None] * (probs - onehot)).astype(jnp.bfloat16)
        scaled_sum = scaled_sum + product_left(grad_logits, out_block)
        return (scaled_sum, product(grad_logits, scaled))

    scaled_grad, out_terms = lax.scan(
        back_tile,
        jnp.zeros(scaled.shape, jnp.float32),
        (out_tiles, id_tiles, log_tiles, weight_tiles),
    )
    out_terms = out_terms.reshape(tile_count * tile_rows, embed_width)
    out_grad = lax.psum_scatter(out_terms, "seq", scatter_dimension=0, tiled=True).astype(
        jnp.bfloat16
    )
    output_w_grad = product_left(final_in, out_grad)
    hidden_two_grad = product_right(out_grad, output_full)
    branch_grad = (token_scale * hidden_two_grad).astype(jnp.bfloat16)
    down_w_grad = product_left(act_low, branch_grad)
    pre_grad = gelu_back(product_right(branch_grad, down_full))[0].astype(jnp.bfloat16)
    up_w_grad = product_left(second_in, pre_grad)
    upbias_grad = jnp.sum(pre_grad, axis=0, dtype=jnp.float32)
    hidden_one_part, gain_two_grad, bias_two_grad = second_back(product_right(pre_grad, up_full))
    hidden_one_grad = hidden_two_grad + hidden_one_part
    attn_grad = (token_scale * hidden_one_grad).astype(jnp.bfloat16)
    attn_w_grad = product_left(mixed, attn_grad)
    mixed_grad = (
        product_right(attn_grad, attn_full).astype(jnp.bfloat16).reshape(row_count, local_len, D)
    )
    head_grad = lax.all_to_all(mixed_grad, "seq", split_axis=2, concat_axis=1, tiled=True).reshape(
        head_shape
    )
    query_grad, key_grad, value_grad = lax.map(
        attend_back_row, (head_q, head_k, head_v, segment_ids, head_grad, log_total)
    )
    merged_shape = (row_count, length, heads_here * HEAD_DIM)
    query_back, key_back, value_back = (
        lax.all_to_all(
            query_grad.reshape(merged_shape), "seq", split_axis=1, concat_axis=2, tiled=True
        ),
        lax.all_to_all(
            key_grad.reshape(merged_shape), "seq", split_axis=1, concat_axis=2, tiled=True
        ),
        lax.all_to_all(
            value_grad.reshape(merged_shape), "seq", split_axis=1, concat_axis=2, tiled=True
        ),
    )
    qkv_grad = jnp.concatenate(
        [query_back * HEAD_DIM ** (-0.5), key_back, value_back], axis=2
    ).reshape(tok_count, 3 * D)
    qkv_w_grad = product_left(first_in, qkv_grad)
    hidden_zero_part, gain_one_grad, bias_one_grad = first_back(product_right(qkv_grad, qkv_full))
    hidden_zero_grad = (hidden_one_grad + hidden_zero_part).astype(jnp.bfloat16)
    input_w_grad = product_left(inputs, hidden_zero_grad)
    embedded_grad = token_input_scale * product_right(hidden_zero_grad, input_full)
    scaled_part = scaled_grad * embed_width ** (-0.5)
    group_grad = lax.all_gather(
        embedded_grad.astype(jnp.bfloat16), "seq", axis=0, tiled=True
    ).astype(embedded_grad.dtype)
    block_id = group_ids // block_len
    owned = block_id % seq_count == seq_place
    local_slot = jnp.where(
        owned, block_id // seq_count * block_len + group_ids % block_len, scaled.shape[0]
    )
    unit_grad = scaled_part.at[local_slot].add(group_grad, mode="drop")
    table_term = jax.vjp(normalize_rows, sub_table.astype(jnp.float32))[1](unit_grad)[0]
    table_grad = lax.psum_scatter(
        table_term.astype(jnp.bfloat16), "dp", scatter_dimension=0, tiled=True
    ).astype(jnp.float32)
    summed = (
        lax.psum_scatter(input_w_grad, ("dp", "seq"), scatter_dimension=0, tiled=True),
        lax.psum_scatter(gain_one_grad, ("dp", "seq"), scatter_dimension=0, tiled=True),
        lax.psum_scatter(bias_one_grad, ("dp", "seq"), scatter_dimension=0, tiled=True),
        lax.psum_scatter(qkv_w_grad, ("dp", "seq"), scatter_dimension=0, tiled=True),
        lax.psum_scatter(attn_w_grad, ("dp", "seq"), scatter_dimension=0, tiled=True),
        lax.psum_scatter(gain_two_grad, ("dp", "seq"), scatter_dimension=0, tiled=True),
        lax.psum_scatter(bias_two_grad, ("dp", "seq"), scatter_dimension=0, tiled=True),
        lax.psum_scatter(up_w_grad, ("dp", "seq"), scatter_dimension=0, tiled=True),
        lax.psum_scatter(upbias_grad, ("dp", "seq"), scatter_dimension=0, tiled=True),
        lax.psum_scatter(down_w_grad, ("dp", "seq"), scatter_dimension=0, tiled=True),
        lax.psum_scatter(output_w_grad, ("dp", "seq"), scatter_dimension=0, tiled=True),
    )
    return (token_loss.reshape(row_count, local_len), table_grad) + tuple(summed)


def solution(mesh):
    dp, seq = mesh.shape["dp"], mesh.shape["seq"]
    if (dp, seq) == (16, 2):
        inner = Mesh(mesh.devices.reshape(dp // 4, 2, 2, seq), ("z", "y", "c", "x"))
        dp_names, seq_names, body = ("z", "y", "c"), ("x",), paired
    else:
        inner, dp_names, seq_names, body = mesh, ("dp",), ("seq",), local
    every = dp_names + seq_names
    in_specs = (
        P(dp_names, None),
        P(dp_names, None),
        P(dp_names),
        P(dp_names),
        P(dp_names, seq_names),
        P(every, None),
        P(every, None),
        P(every),
        P(every),
        P(every, None),
        P(every, None),
        P(every),
        P(every),
        P(every, None),
        P(every),
        P(every, None),
        P(every, None),
    )
    out_specs = (
        P(dp_names, seq_names),
        P(every, None),
        P(every, None),
        P(every),
        P(every),
        P(every, None),
        P(every, None),
        P(every),
        P(every),
        P(every, None),
        P(every),
        P(every, None),
        P(every, None),
    )
    return jax.shard_map(body, mesh=inner, in_specs=in_specs, out_specs=out_specs, check_vma=False)
```

```python
import math

import jax
import jax.numpy as jnp
from jax import lax
from jax.experimental import pallas as pl
from jax.experimental.pallas import tpu as pltpu
from jax.sharding import Mesh
from jax.sharding import PartitionSpec as P

D = 1024
HEAD_DIM = 64
TSTEPS = 1000
SWAP = ((0, 1), (1, 0))
BF = jnp.bfloat16
F32 = jnp.float32
NEG = -1e30
LIMIT = 70.0
MIB = 1 << 20


def dot_nn(left, right):
    return lax.dot_general(left, right, (((1,), (0,)), ((), ())), preferred_element_type=F32)


def dot_nt(left, right):
    return lax.dot_general(left, right, (((1,), (1,)), ((), ())), preferred_element_type=F32)


def dot_tn(left, right):
    return lax.dot_general(left, right, (((0,), (0,)), ((), ())), preferred_element_type=F32)


def swap(value, axis):
    return lax.ppermute(value, axis, SWAP)


def ring_down(value, axis):
    n = lax.axis_size(axis)
    return lax.ppermute(value, axis, [(i, (i - 1) % n) for i in range(n)])


def ring_up(value, axis):
    n = lax.axis_size(axis)
    return lax.ppermute(value, axis, [(i, (i + 1) % n) for i in range(n)])


def ordered(own, other, place, axis):
    return jnp.where(
        place == 0, jnp.stack([own, other], axis), jnp.stack([other, own], axis)
    )


def pick(value, index, axis):
    return lax.dynamic_index_in_dim(value, index, axis, keepdims=False)


def after(value, *others):
    return lax.optimization_barrier((value,) + others)[0]


def ring_blocks(value, axis):
    parts = [value]
    for _ in range(lax.axis_size(axis) - 1):
        parts.append(ring_down(parts[-1], axis))
    return parts


def joined_swap(held, axis):
    return jnp.concatenate([held, swap(held, axis)], 0)


def apart(value, axis, distance):
    n = lax.axis_size(axis)
    return lax.ppermute(value, axis, [(i, i ^ distance) for i in range(n)])


def joined_apart(value, axis):
    held, distance = value[None], 1
    while distance < lax.axis_size(axis):
        held = jnp.concatenate([held, apart(held, axis, distance)], 0)
        distance *= 2
    return held


def halve(value, axis, at):
    here = lax.axis_index(axis)
    return pick(value, here, at), swap(pick(value, 1 - here, at), axis)


def added(kept, moved):
    return (kept.astype(F32) + moved.astype(F32)).astype(BF)


def ring_start(value, axis):
    n, here = lax.axis_size(axis), lax.axis_index(axis)
    return ring_up(pick(value, (here - 1) % n, 0), axis)


def ring_next(value, moved, step, axis):
    n, here = lax.axis_size(axis), lax.axis_index(axis)
    return pick(value, (here - 1 - step) % n, 0).astype(F32) + moved.astype(F32)


def place_blocks(places, halves, outs):
    flat = halves[0] + halves[1]
    count = sum(piece.shape[0] for piece in flat) * len(outs)

    def body(places_ref, *refs):
        ins, results, sems = refs[: len(flat)], refs[len(flat) : -1], refs[-1]
        copies, block = [], 0
        for number, piece in enumerate(ins):
            for k in range(piece.shape[0]):
                p, h = places_ref[block], number // len(halves[0])
                block += 1
                for (low, high, _, index), result in zip(outs, results):
                    copies.append(
                        pltpu.make_async_copy(
                            piece.at[k, :, low:high],
                            result.at[index(p, h)],
                            sems.at[len(copies)],
                        )
                    )
        for copy in copies:
            copy.start()
        for copy in copies:
            copy.wait()

    return pl.pallas_call(
        body,
        out_shape=tuple(jax.ShapeDtypeStruct(shape, BF) for _, _, shape, _ in outs),
        grid=(1,),
        in_specs=[pl.BlockSpec(memory_space=pltpu.SMEM)]
        + [pl.BlockSpec(memory_space=pl.ANY)] * len(flat),
        out_specs=tuple(
            pl.BlockSpec(shape, lambda i, n=len(shape): (0,) * n) for _, _, shape, _ in outs
        ),
        scratch_shapes=[pltpu.SemaphoreType.DMA((count,))],
        compiler_params=pltpu.CompilerParams(vmem_limit_bytes=24 * MIB),
        name="place_blocks",
    )(places, *flat)


def for_each_window(lo, hi, blocks, run):
    for count in range(1, blocks + 1):

        @pl.when(hi - lo == count)
        def _():
            run(lo, count)


def attend_body(
    lo_ref, hi_ref, q_ref, k_ref, v_ref, seg_col_ref, seg_row_ref, o_ref, lse_ref, v_ones
):
    length = q_ref.shape[0]
    blk = min(256, length)
    lane = lax.broadcasted_iota(jnp.int32, (1, 128), 1)
    masks = (lane < HEAD_DIM, lane >= HEAD_DIM)
    v = v_ref[...]
    for h in range(2):
        v_ones[h] = jnp.where(masks[h], v, jnp.ones_like(v))

    def largest(ref):
        rows = ref[...].astype(F32)
        return jnp.max(jnp.sum(rows * rows, axis=1, keepdims=True))

    small = largest(q_ref) * largest(k_ref) <= LIMIT * LIMIT

    def finish(rows, accs):
        totals = [pltpu.roll(acc, HEAD_DIM, axis=1) for acc in accs]
        o_ref[rows, :] = (
            jnp.where(masks[0], accs[0], accs[1]) / jnp.where(masks[0], totals[0], totals[1])
        ).astype(BF)
        return [accs[0].T[HEAD_DIM : HEAD_DIM + 1], accs[1].T[0:1]]

    def each(qi, _):
        rows = pl.ds(pl.multiple_of(qi * blk, blk), blk)
        q = q_ref[rows, :]
        q_heads = [jnp.where(m, q, jnp.zeros_like(q)) for m in masks]

        def run(first, count):
            at = pl.ds(pl.multiple_of(first * blk, blk), count * blk)
            k = k_ref[at, :]
            same = seg_col_ref[at, :] == seg_row_ref[:, rows]
            accs = []
            for h in range(2):
                e = jnp.exp(jnp.where(same, dot_nt(k, q_heads[h]), NEG)).astype(BF)
                accs.append(dot_tn(e, v_ones[h, at, :]))
            for h, total in enumerate(finish(rows, accs)):
                lse_ref[0, h : h + 1, rows] = jnp.log(total)

        @pl.when(small)
        def _():
            for_each_window(lo_ref[qi], hi_ref[qi], length // blk, run)

        @pl.when(jnp.logical_not(small))
        def _():
            def scores(kb, h):
                at = pl.ds(pl.multiple_of(kb * blk, blk), blk)
                same = seg_col_ref[at, :] == seg_row_ref[:, rows]
                return jnp.where(same, dot_nt(k_ref[at, :], q_heads[h]), NEG)

            def highest(kb, tops):
                return tuple(
                    jnp.maximum(tops[h], jnp.max(scores(kb, h), axis=0, keepdims=True))
                    for h in range(2)
                )

            tops = lax.fori_loop(
                lo_ref[qi], hi_ref[qi], highest, (jnp.full((1, blk), NEG, F32),) * 2
            )

            def gather(kb, accs):
                at = pl.ds(pl.multiple_of(kb * blk, blk), blk)
                return tuple(
                    accs[h]
                    + dot_tn(jnp.exp(scores(kb, h) - tops[h]).astype(BF), v_ones[h, at, :])
                    for h in range(2)
                )

            accs = lax.fori_loop(
                lo_ref[qi], hi_ref[qi], gather, (jnp.zeros((blk, 128), F32),) * 2
            )
            for h, total in enumerate(finish(rows, accs)):
                lse_ref[0, h : h + 1, rows] = tops[h] + jnp.log(total)

        return 0

    lax.fori_loop(0, length // blk, each, 0)


def attend(q, k, v, seg_col, seg_row, lo, hi):
    length, width = q.shape
    pairs = width // 128
    spec = pl.BlockSpec((length, 128), lambda i, *_: (0, i))
    return pl.pallas_call(
        attend_body,
        out_shape=(
            jax.ShapeDtypeStruct((length, width), BF),
            jax.ShapeDtypeStruct((pairs, 2, length), F32),
        ),
        grid_spec=pltpu.PrefetchScalarGridSpec(
            num_scalar_prefetch=2,
            grid=(pairs,),
            in_specs=[
                spec,
                spec,
                spec,
                pl.BlockSpec((length, 1), lambda i, *_: (0, 0)),
                pl.BlockSpec((1, length), lambda i, *_: (0, 0)),
            ],
            out_specs=(spec, pl.BlockSpec((1, 2, length), lambda i, *_: (i, 0, 0))),
            scratch_shapes=[pltpu.VMEM((2, length, 128), BF)],
        ),
        compiler_params=pltpu.CompilerParams(vmem_limit_bytes=32 * MIB),
        cost_estimate=pl.CostEstimate(
            flops=16 * length * length * width,
            bytes_accessed=8 * length * width,
            transcendentals=length * length * width // HEAD_DIM,
        ),
        name="attend",
    )(lo, hi, q, k, v, seg_col, seg_row)


def attend_back_body(
    lo_ref,
    hi_ref,
    q_ref,
    k_ref,
    v_ref,
    o_ref,
    g_ref,
    lse_ref,
    seg_col_ref,
    seg_row_ref,
    dq_ref,
    dk_ref,
    dv_ref,
    dk_sum,
    dv_sum,
):
    length = q_ref.shape[0]
    blk = min(256, length)
    lane = lax.broadcasted_iota(jnp.int32, (1, 128), 1)
    masks = (lane < HEAD_DIM, lane >= HEAD_DIM)
    dk_sum[...] = jnp.zeros_like(dk_sum)
    dv_sum[...] = jnp.zeros_like(dv_sum)
    def each(qi, _):
        rows = pl.ds(pl.multiple_of(qi * blk, blk), blk)

        def run(first, count):
            q, g = q_ref[rows, :], g_ref[rows, :]
            mixed = (g.astype(F32) * o_ref[rows, :].astype(F32)).T
            at = pl.ds(pl.multiple_of(first * blk, blk), count * blk)
            k, v = k_ref[at, :], v_ref[at, :]
            same = seg_col_ref[at, :] == seg_row_ref[:, rows]
            dq = jnp.zeros((blk, 128), F32)
            dk, dv = dk_sum[at, :], dv_sum[at, :]
            for h in range(2):
                q_head = jnp.where(masks[h], q, jnp.zeros_like(q))
                g_head = jnp.where(masks[h], g, jnp.zeros_like(g))
                k_head = jnp.where(masks[h], k, jnp.zeros_like(k))
                delta = jnp.sum(mixed[h * HEAD_DIM : (h + 1) * HEAD_DIM], axis=0, keepdims=True)
                s = dot_nt(k, q_head)
                p = jnp.exp(jnp.where(same, s - lse_ref[0, h : h + 1, rows], NEG))
                dp = dot_nt(v, g_head)
                ds = (p * (dp - delta)).astype(BF)
                dv = dv + dot_nn(p.astype(BF), g_head)
                dk = dk + dot_nn(ds, q_head)
                dq = dq + dot_tn(ds, k_head)
            dk_sum[at, :] = dk
            dv_sum[at, :] = dv
            dq_ref[rows, :] = dq.astype(BF)

        for_each_window(lo_ref[qi], hi_ref[qi], length // blk, run)
        return 0

    lax.fori_loop(0, length // blk, each, 0)
    dk_ref[...] = dk_sum[...].astype(BF)
    dv_ref[...] = dv_sum[...].astype(BF)


def attend_back(q, k, v, o, g, lse, seg_col, seg_row, lo, hi):
    length, width = q.shape
    pairs = width // 128
    spec = pl.BlockSpec((length, 128), lambda i, *_: (0, i))
    shape = jax.ShapeDtypeStruct((length, width), BF)
    return pl.pallas_call(
        attend_back_body,
        out_shape=(shape, shape, shape),
        grid_spec=pltpu.PrefetchScalarGridSpec(
            num_scalar_prefetch=2,
            grid=(pairs,),
            in_specs=[
                spec,
                spec,
                spec,
                spec,
                spec,
                pl.BlockSpec((1, 2, length), lambda i, *_: (i, 0, 0)),
                pl.BlockSpec((length, 1), lambda i, *_: (0, 0)),
                pl.BlockSpec((1, length), lambda i, *_: (0, 0)),
            ],
            out_specs=(spec, spec, spec),
            scratch_shapes=[pltpu.VMEM((length, 128), F32), pltpu.VMEM((length, 128), F32)],
        ),
        compiler_params=pltpu.CompilerParams(vmem_limit_bytes=32 * MIB),
        cost_estimate=pl.CostEstimate(
            flops=32 * length * length * width,
            bytes_accessed=16 * length * width,
            transcendentals=length * length * width // HEAD_DIM,
        ),
        name="attend_back",
    )(lo, hi, q, k, v, o, g, lse, seg_col, seg_row)


def score_body(
    norm_ref, out_ref, table_ref, slot_ref, raised_ref, tops_ref, acc_ref, total_ref, top, fast
):
    j = pl.program_id(0)
    tokens, width = out_ref.shape
    count = table_ref.shape[1]
    rows = table_ref[0].astype(F32)
    unit = rows * lax.rsqrt(jnp.mean(rows * rows, axis=1, keepdims=True) + 1e-06)
    low = unit * width ** (-0.5)
    scaled, scaled_t = low.astype(BF), low.T.astype(BF)
    row = lax.broadcasted_iota(jnp.int32, (count, 1), 0) + j * count

    @pl.when(j == 0)
    def _():
        acc_ref[...] = jnp.zeros_like(acc_ref)
        total_ref[...] = jnp.zeros_like(total_ref)
        some = scaled[: min(count, 128)]
        first = jnp.max(dot_nt(some, out_ref[...]), axis=0, keepdims=True)
        floor = norm_ref[...] - LIMIT
        kept = jnp.max(floor - first) <= LIMIT
        top[...] = jnp.where(kept, jnp.maximum(first, floor), NEG)
        fast[0] = kept.astype(jnp.int32)

    @pl.when(fast[0] == 1)
    def _():
        e = jnp.exp(dot_nt(scaled, out_ref[...]) - top[...])
        total_ref[...] += jnp.sum(e, axis=0, keepdims=True)
        raised_ref[0] = jnp.where(row == slot_ref[...], 0.0, e).astype(BF)
        acc_ref[...] += dot_nn(scaled_t, raised_ref[0])
        tops_ref[0] = top[...]

    @pl.when(fast[0] == 0)
    def _():
        part = math.gcd(tokens, 512)

        def each(n, _):
            at = pl.ds(pl.multiple_of(n * part, part), part)
            logits = dot_nt(scaled, out_ref[at, :])
            new_top = jnp.maximum(top[:, at], jnp.max(logits, axis=0, keepdims=True))
            keep = jnp.exp(top[:, at] - new_top)
            e = jnp.exp(logits - new_top)
            total_ref[:, at] = total_ref[:, at] * keep + jnp.sum(e, axis=0, keepdims=True)
            raised_ref[0, :, at] = jnp.where(row == slot_ref[:, at], 0.0, e).astype(BF)
            acc_ref[:, at] = acc_ref[:, at] * keep + dot_nn(scaled_t, raised_ref[0, :, at])
            tops_ref[0, :, at] = new_top
            top[:, at] = new_top
            return 0

        lax.fori_loop(0, tokens // part, each, 0)


def score(outputs, table, slots):
    tokens, width = outputs.shape
    blocks, rows, _ = table.shape
    squares = jnp.square(outputs.astype(F32))
    norms = 1.01 * jnp.sqrt(dot_nt(jnp.ones((8, width), BF), squares.astype(BF))[:1])
    return pl.pallas_call(
        score_body,
        out_shape=(
            jax.ShapeDtypeStruct((blocks, rows, tokens), BF),
            jax.ShapeDtypeStruct((blocks, 1, tokens), F32),
            jax.ShapeDtypeStruct((width, tokens), F32),
            jax.ShapeDtypeStruct((1, tokens), F32),
        ),
        grid=(blocks,),
        in_specs=[
            pl.BlockSpec((1, tokens), lambda j: (0, 0)),
            pl.BlockSpec((tokens, width), lambda j: (0, 0)),
            pl.BlockSpec((1, rows, width), lambda j: (j, 0, 0)),
            pl.BlockSpec((1, tokens), lambda j: (0, 0)),
        ],
        out_specs=(
            pl.BlockSpec((1, rows, tokens), lambda j: (j, 0, 0)),
            pl.BlockSpec((1, 1, tokens), lambda j: (j, 0, 0)),
            pl.BlockSpec((width, tokens), lambda j: (0, 0)),
            pl.BlockSpec((1, tokens), lambda j: (0, 0)),
        ),
        scratch_shapes=[pltpu.VMEM((1, tokens), F32), pltpu.SMEM((1,), jnp.int32)],
        compiler_params=pltpu.CompilerParams(vmem_limit_bytes=48 * MIB),
        cost_estimate=pl.CostEstimate(
            flops=4 * blocks * rows * tokens * width,
            bytes_accessed=2 * blocks * rows * tokens,
            transcendentals=blocks * rows * tokens,
        ),
        name="score",
    )(norms, outputs, table, slots)


def table_product_body(raised_ref, out_ref, coef_ref, sum_ref):
    j = pl.program_id(0)
    lane = lax.broadcasted_iota(jnp.int32, coef_ref.shape, 1)
    coef = jnp.sum(jnp.where(lane == j, coef_ref[...], 0.0), axis=1, keepdims=True)
    weighted = (out_ref[...].astype(F32) * coef).astype(BF)
    sum_ref[0] = dot_nn(raised_ref[0], weighted)


def table_product(raised, outputs, coef):
    blocks, rows, tokens = raised.shape
    width = outputs.shape[1]
    return pl.pallas_call(
        table_product_body,
        out_shape=jax.ShapeDtypeStruct((blocks, rows, width), F32),
        grid=(blocks,),
        in_specs=[
            pl.BlockSpec((1, rows, tokens), lambda j: (j, 0, 0)),
            pl.BlockSpec((tokens, width), lambda j: (0, 0)),
            pl.BlockSpec((tokens, blocks), lambda j: (0, 0)),
        ],
        out_specs=pl.BlockSpec((1, rows, width), lambda j: (j, 0, 0)),
        compiler_params=pltpu.CompilerParams(vmem_limit_bytes=48 * MIB),
        cost_estimate=pl.CostEstimate(
            flops=2 * blocks * rows * tokens * width,
            bytes_accessed=2 * blocks * rows * tokens,
            transcendentals=0,
        ),
        name="table_product",
    )(raised, outputs, coef)


def table_add_body(sum_ref, slot_ref, grad_ref, out_ref):
    j = pl.program_id(0)
    rows = sum_ref.shape[1]
    row = lax.broadcasted_iota(jnp.int32, (rows, 1), 0) + j * rows
    chosen = (row == slot_ref[...]).astype(F32).astype(BF)
    out_ref[0] = (sum_ref[0] + dot_nn(chosen, grad_ref[...])).astype(BF)


def table_add(sums, slots, grads):
    blocks, rows, width = sums.shape
    tokens = grads.shape[0]
    return pl.pallas_call(
        table_add_body,
        out_shape=jax.ShapeDtypeStruct(sums.shape, BF),
        grid=(blocks,),
        in_specs=[
            pl.BlockSpec((1, rows, width), lambda j: (j, 0, 0)),
            pl.BlockSpec((1, tokens), lambda j: (0, 0)),
            pl.BlockSpec((tokens, width), lambda j: (0, 0)),
        ],
        out_specs=pl.BlockSpec((1, rows, width), lambda j: (j, 0, 0)),
        compiler_params=pltpu.CompilerParams(vmem_limit_bytes=48 * MIB),
        cost_estimate=pl.CostEstimate(
            flops=2 * blocks * rows * tokens * width,
            bytes_accessed=6 * blocks * rows * width,
            transcendentals=0,
        ),
        name="table_add",
    )(sums, slots, grads)


def norm_parts(hidden):
    centre = hidden - jnp.mean(hidden, axis=-1, keepdims=True)
    spread = jnp.mean(centre * centre, axis=-1, keepdims=True)
    inverse = lax.rsqrt(spread + 1e-05)
    return centre * inverse, inverse


def norm_back(grad, gain, normed, inverse):
    grad_normed = grad * gain
    first = jnp.mean(grad_normed, axis=-1, keepdims=True)
    second = jnp.mean(grad_normed * normed, axis=-1, keepdims=True)
    return inverse * (grad_normed - first - normed * second)


def noise_field(row_seed, length, channel_count):
    position = lax.iota(jnp.int32, length)[:, None]
    channel = lax.iota(jnp.int32, channel_count)[None, :]
    mixed_once = (row_seed + 7919 * position + 104729 * channel) % 65521
    mixed_twice = (mixed_once * (mixed_once % 32719) + 31 * channel) % 65521
    return (mixed_twice.astype(F32) / 32760.5 - 1.0) * 1.7320508


def paired(
    token_ids,
    segment_ids,
    time_steps,
    row_seeds,
    loss_weights,
    embed_table,
    input_proj,
    attn_gain,
    attn_bias,
    qkv_proj,
    attn_proj,
    mlp_gain,
    mlp_bias,
    up_proj,
    up_bias,
    down_proj,
    output_proj,
):
    z, y, c, x = (lax.axis_index(a) for a in ("z", "y", "c", "x"))
    groups = lax.axis_size("z") * lax.axis_size("y")
    length = token_ids.shape[1]
    half = length // 2
    block_len, width = embed_table.shape
    ff = up_proj.shape[1]
    rows_here = qkv_proj.shape[0]
    heads = D // HEAD_DIM
    ff_block = down_proj.shape[0] * 2

    meta = jnp.concatenate([token_ids[0], segment_ids[0], time_steps, row_seeds])
    meta_two = ordered(meta, swap(meta, "c"), c, 0)
    weight_c = ordered(loss_weights[0], swap(loss_weights[0], "c"), c, 0)
    weight_two = ordered(weight_c, swap(weight_c, "x"), x, 1).reshape(2, length)
    ids_two = meta_two[:, :length]
    own_meta = pick(meta_two, x, 0)
    segments = own_meta[length : 2 * length]
    weight_row = pick(weight_two, x, 0)
    fraction = own_meta[2 * length].astype(F32) / (TSTEPS - 1)
    noise_level = 0.3 * jnp.exp(fraction * math.log(30.0))
    input_scale = lax.rsqrt(1.0 + noise_level * noise_level)
    residual_scale = 0.5 + fraction
    noise = noise_field(own_meta[2 * length + 1], length, width)

    small_width = 2 * width + 128
    vector = jnp.concatenate([attn_gain, attn_bias, mlp_gain, mlp_bias, up_bias])
    small = jnp.concatenate(
        [
            input_proj.reshape(rows_here, width),
            output_proj,
            jnp.pad(vector.reshape(-1, 128), ((0, rows_here - vector.size // 128), (0, 0))),
        ],
        axis=1,
    )
    qkv_split = qkv_proj.reshape(rows_here, 3 * heads // 2, 2, HEAD_DIM)
    up_split = up_proj.reshape(rows_here, groups, 2, ff_block)

    def packed(core):
        return jnp.concatenate(
            [
                pick(qkv_split, core, 2).reshape(rows_here, -1),
                small,
                pick(up_split, core, 2).reshape(rows_here, -1),
            ],
            axis=1,
        )

    pair = ordered(packed(c), swap(packed(1 - c), "c"), c, 0).reshape(2 * rows_here, -1)
    qkv_cols, small_cols = 3 * D // 2, 3 * D // 2 + small_width
    first_cols = small_cols + D // 2
    first_shard = jnp.concatenate(
        [
            pair[:, :small_cols],
            jnp.concatenate([attn_proj[:, : D // 2], attn_proj[:, D // 2 :]], axis=0),
        ],
        axis=1,
    )
    up_shard = pair[:, small_cols:]

    def places(order, ring):
        block, found = jnp.arange(2 * groups, dtype=jnp.int32), {}
        for axis in order:
            n, here = lax.axis_size(axis), lax.axis_index(axis)
            found[axis] = (block + here) % n if ring else (block % n) ^ here
            block = block // n
        return (found["z"] * 2 + found["y"]) * 2 + found["x"]

    def both_places(ring):
        return jnp.concatenate([places(("z", "y", "x"), ring), places(("z", "x", "y"), ring)])

    def over_one(blocks):
        rows = blocks.shape[1] // 2
        return joined_swap(blocks[:, :rows], "y"), joined_swap(blocks[:, rows:], "x")

    def over_one_start(blocks):
        rows = blocks.shape[1] // 2
        first, second = blocks[:, :rows], blocks[:, rows:]
        return (first, swap(first, "y")), (second, swap(second, "x"))

    def over_other(held):
        return [[held[0], swap(held[0], "x")], [held[1], swap(held[1], "y")]]

    cut = block_len // 32 * 16
    with jax.named_scope("gather_table"):
        table_a = ring_blocks(embed_table[None, :cut], "z")
        table_b = ring_blocks(joined_swap(embed_table[None, cut:], "y"), "z")
        table_z = table_b[-1]
        table_a = joined_swap(jnp.concatenate(table_a, 0), "y")
        table_b = jnp.stack(table_b, 1).reshape(groups, block_len - cut, width)
    with jax.named_scope("gather_first"):
        first_z = ring_blocks(first_shard[None], "z")
        first_held = over_one(jnp.concatenate(first_z, 0))
        first_pieces = over_other(first_held)
    with jax.named_scope("gather_up"):
        up_first = after(up_shard[None], table_z, first_z[-1])
        up_moved = apart(up_first, "z", 1)
        up_two = jnp.concatenate([up_first, up_moved], 0)
        up_z = jnp.concatenate([up_two, apart(up_two, "z", 2)], 0)
        up_held = over_one(after(up_z, first_pieces[0][1], first_pieces[1][1]))
        up_pieces = over_other(up_held)
    with jax.named_scope("gather_down"):
        down_z = joined_apart(after(down_proj, up_two), "z")

    flat_ids = ids_two.reshape(-1)
    owner = flat_ids // block_len
    within = flat_ids % block_len
    home = {"z": owner // 8, "y": owner // 4 % 2}
    mine = owner % 4 == c * 2 + x
    table_rows = jnp.concatenate([after(table_a, *first_held), table_b], axis=1)
    zn = lax.axis_size("z")
    relative_y, relative_z = (home["y"] - y) % 2, (home["z"] - z) % zn
    slot = (relative_y * zn + relative_z) * block_len + within
    found = jnp.take(
        table_rows.reshape(groups * block_len, width), jnp.where(mine, slot, 0), axis=0
    )
    found = after(found, up_moved)
    found = jnp.where(mine[:, None], found, jnp.zeros_like(found)).reshape(2, length, width)

    def to_rows(terms, kind):
        split = terms.reshape(2, 2, half, width)
        moved = swap(pick(split, 1 - c, 1).astype(kind), "c")
        both = pick(split, c, 1).astype(F32) + moved.astype(F32)
        moved = swap(pick(both, 1 - x, 0).astype(kind), "x")
        own = (pick(both, x, 0).astype(F32) + moved.astype(F32)).astype(kind)
        return ordered(own, swap(own, "c"), c, 0).reshape(length, width)

    def to_pair(row):
        own = pick(row.reshape(2, half, width), c, 0)
        moved = swap(own, "x")
        other = ordered(moved, swap(moved, "c"), c, 0).reshape(length, width)
        return ordered(row, other, x, 0)

    raw = to_rows(found, BF).astype(F32)
    paired_shape = (groups, 2, 2, rows_here)

    def in_pairs(p, h):
        return (p // 2, h, p % 2)

    def held_back(pieces, *values):
        return [[after(piece, *values) for piece in half_pieces] for half_pieces in pieces]

    qkv_half, small_full, attn_half = place_blocks(
        both_places(True),
        held_back(first_pieces, found),
        [
            (0, qkv_cols, paired_shape + (qkv_cols,), in_pairs),
            (qkv_cols, small_cols, paired_shape + (small_width,), in_pairs),
            (
                small_cols,
                first_cols,
                (2 * groups, rows_here, D),
                lambda p, h: (p, slice(None), slice(h * D // 2, (h + 1) * D // 2)),
            ),
        ],
    )
    qkv_half, small_full = qkv_half.reshape(D, qkv_cols), small_full.reshape(D, small_width)
    attn_half = attn_half.reshape(D // 2, D)
    input_full = small_full[:, :width].reshape(width, D)
    output_full = small_full[:, width : 2 * width]
    vectors = small_full[:, 2 * width :].reshape(groups, 2, 2, rows_here, 128)
    vectors = vectors[..., : vector.size // 128, :].reshape(groups, 2, 2, vector.size)
    gain_one, bias_one, gain_two, bias_two = (
        vectors[..., k * rows_here : (k + 1) * rows_here].reshape(1, D).astype(F32)
        for k in range(4)
    )
    up_bias_half = pick(vectors[..., 4 * rows_here :], c, 1).reshape(1, ff // 2).astype(F32)
    unit = raw * lax.rsqrt(jnp.mean(raw * raw, axis=1, keepdims=True) + 1e-06)
    target = (unit * width ** (-0.5)).astype(BF)
    inputs = (input_scale * (unit + noise_level * noise)).astype(BF)

    hidden_zero = dot_nn(inputs, input_full)
    normed_one, inverse_one = norm_parts(hidden_zero)
    first_in = (normed_one * gain_one + bias_one).astype(BF)
    qkv = dot_nn(first_in, qkv_half)
    split = D // 2
    queries = (qkv[:, :split] * HEAD_DIM ** (-0.5)).astype(BF)
    keys = qkv[:, split : 2 * split].astype(BF)
    values = qkv[:, 2 * split :].astype(BF)
    seg_col, seg_row = segments[:, None], segments[None, :]
    blk = min(256, length)
    edges = segments.reshape(length // blk, blk)
    before = jnp.sum(seg_row < edges[:, :1], axis=1, dtype=jnp.int32)
    through = jnp.sum(seg_row <= edges[:, -1:], axis=1, dtype=jnp.int32)
    low_block, high_block = before // blk, (through + blk - 1) // blk
    with jax.named_scope("gather_down"):
        down_z = after(down_z, inputs)
        down_moved = over_one_start(down_z)
    attended, log_total = attend(
        after(queries, down_z), keys, values, seg_col, seg_row, low_block, high_block
    )
    attended = after(
        attended, up_pieces[0][1], up_pieces[1][1], down_moved[0][1], down_moved[1][1]
    )
    with jax.named_scope("gather_down"):
        down_held = [jnp.concatenate([own, after(got, attended)], 0) for own, got in down_moved]
        down_pieces = over_other(down_held)

    def both_cores(part):
        return part + swap(part.astype(BF), "c").astype(F32)

    hidden_one = hidden_zero + residual_scale * both_cores(dot_nn(attended, attn_half))
    normed_two, inverse_two = norm_parts(hidden_one)
    second_in = (normed_two * gain_two + bias_two).astype(BF)
    (up_half,) = place_blocks(
        both_places(False),
        held_back(up_pieces, queries),
        [(0, ff // 2, paired_shape + (ff // 2,), in_pairs)],
    )
    up_half = up_half.reshape(D, ff // 2)
    pre_act = dot_nn(second_in, up_half) + up_bias_half
    below = 0.5 * (1.0 + lax.erf(pre_act * math.sqrt(0.5)))
    activated = (pre_act * below).astype(BF)
    slope = (
        below + pre_act * (jnp.exp(-0.5 * pre_act * pre_act) * (1.0 / math.sqrt(2.0 * math.pi)))
    ).astype(BF)
    (down_half,) = place_blocks(
        both_places(False),
        held_back(down_pieces, activated),
        [
            (
                0,
                D,
                (2 * groups, 2, down_proj.shape[0] // 2, D),
                lambda p, h: (p, h),
            )
        ],
    )
    down_half = down_half.reshape(ff // 2, D)
    hidden_two = hidden_one + residual_scale * both_cores(dot_nn(activated, down_half))
    final_in = hidden_two.astype(BF)
    outputs = dot_nn(final_in, output_full).astype(BF)

    outputs_two = to_pair(outputs).reshape(2 * length, width)
    slots_here = jnp.where(mine, slot, -1)[None, :]
    raised, tops, reached, total = score(outputs_two, table_rows, slots_here)
    ends = jnp.concatenate([tops[-1], total])

    def joined(first, second):
        top = jnp.maximum(first[0], second[0])
        return jnp.stack(
            [top, first[1] * jnp.exp(first[0] - top) + second[1] * jnp.exp(second[0] - top)]
        )

    all_ends = joined(ends, swap(ends, "c"))
    all_ends = joined(all_ends, swap(all_ends, "x"))
    log_sum = all_ends[0] + jnp.log(all_ends[1])
    share = (reached * jnp.exp(ends[0] - log_sum)[None, :]).astype(BF)
    parts = [share[:, k * half : (k + 1) * half] for k in range(4)]
    kept = jnp.concatenate([jnp.where(c == 0, parts[0], parts[1]), jnp.where(c == 0, parts[2], parts[3])], 1)
    sent = jnp.concatenate([jnp.where(c == 0, parts[1], parts[0]), jnp.where(c == 0, parts[3], parts[2])], 1)
    both = kept.astype(F32) + swap(sent, "c").astype(F32)
    own, other = jnp.where(x == 0, both[:, :half], both[:, half:]), jnp.where(x == 0, both[:, half:], both[:, :half])
    own = (own + swap(other.astype(BF), "x").astype(F32)).astype(BF)
    moved = swap(own, "c")
    expected = jnp.concatenate(
        [jnp.where(c == 0, own, moved), jnp.where(c == 0, moved, own)], 1
    ).astype(F32).T
    log_row = pick(log_sum.reshape(2, length), x, 0)
    chosen = jnp.sum(outputs.astype(F32) * target.astype(F32), axis=1)
    loss_row = log_row - chosen
    loss_two = ordered(loss_row, swap(loss_row, "x"), x, 0)
    token_loss = pick(pick(loss_two, c, 0).reshape(2, half), x, 0)[None]

    own_term = weight_row * (jnp.exp(chosen - log_row) - 1.0)
    out_grad = (
        weight_row[:, None] * expected + own_term[:, None] * target.astype(F32)
    ).astype(BF)
    coef = (
        (weight_two.reshape(-1) * width ** (-0.5))[None, :] * jnp.exp(tops[:, 0] - log_sum[None, :])
    ).T
    table_sums = table_product(raised, outputs_two, coef)

    zy = (zn, lax.axis_size("y"))
    table_cut = block_len * 5 // 128 * 16

    def rows_of(grad):
        rows = grad.shape[0] // (2 * groups)
        return grad.astype(BF).reshape(zy + (2, rows, grad.shape[1]))

    def pairs_of(grad):
        rows = grad.shape[0] // (4 * groups)
        shaped = grad.astype(BF).reshape(zy + (2, 2, rows, grad.shape[1]))
        return shaped[:, :, 0], shaped[:, :, 1]

    output_w_grad = dot_tn(final_in, out_grad)
    hidden_two_grad = dot_nt(out_grad, output_full)
    branch_grad = (residual_scale * hidden_two_grad).astype(BF)
    with jax.named_scope("reduce_down"):
        down_terms = rows_of(dot_tn(activated, branch_grad))
        rows = down_terms.shape[3] // 2
        down_a = halve(down_terms[..., :rows, :], "x", 2)
        down_b = halve(down_terms[..., rows:, :], "y", 1)
    pre_grad = (
        dot_nt(after(branch_grad, down_terms), down_half) * slope.astype(F32)
    ).astype(BF)
    with jax.named_scope("reduce_up"):
        up_terms = dot_tn(second_in, pre_grad).astype(BF)
        up_a, up_b = pairs_of(up_terms)
        up_a, up_b = halve(up_a, "y", 1), halve(up_b, "x", 2)
    up_bias_part = jnp.sum(pre_grad, axis=0, dtype=F32)
    second_grad = both_cores(
        dot_nt(after(pre_grad, up_terms, down_a[1], down_b[1]), up_half)
    )
    gain_two_part = jnp.sum(second_grad * normed_two, axis=0)
    bias_two_part = jnp.sum(second_grad, axis=0)
    hidden_one_grad = hidden_two_grad + norm_back(second_grad, gain_two, normed_two, inverse_two)
    attn_grad = after((residual_scale * hidden_one_grad).astype(BF), up_a[1], up_b[1])
    with jax.named_scope("reduce_attn"):
        attn_terms = halve(rows_of(dot_tn(attended, attn_grad)), "y", 1)
    attended_grad = dot_nt(attn_grad, attn_half).astype(BF)
    with jax.named_scope("reduce_down"):
        down_a = added(down_a[0], after(down_a[1], up_terms))
        down_b = added(down_b[0], after(down_b[1], up_terms))
        down_next_a, down_next_b = halve(down_a, "y", 1), halve(down_b, "x", 1)
    with jax.named_scope("reduce_up"):
        up_a = added(up_a[0], after(up_a[1], attn_grad))
        up_b = added(up_b[0], after(up_b[1], attn_grad))
        up_next_a, up_next_b = halve(up_a, "x", 1), halve(up_b, "y", 1)
    query_grad, key_grad, value_grad = attend_back(
        queries,
        keys,
        values,
        attended,
        after(attended_grad, down_a, down_b, up_a, up_b, attn_terms[0]),
        log_total,
        seg_col,
        seg_row,
        low_block,
        high_block,
    )
    query_grad = after(
        query_grad,
        up_next_a[1],
        up_next_b[1],
        down_next_a[1],
        down_next_b[1],
        attn_terms[1],
    )
    with jax.named_scope("reduce_mlp"):
        mlp_sum = jnp.concatenate(
            [
                jnp.concatenate(
                    [
                        added(up_next_a[0], after(up_next_a[1], query_grad)),
                        added(up_next_b[0], after(up_next_b[1], query_grad)),
                    ],
                    1,
                ),
                added(down_next_a[0], after(down_next_a[1], query_grad)),
                added(down_next_b[0], after(down_next_b[1], query_grad)),
            ],
            2,
        )
        mlp_ring = ring_start(mlp_sum, "z")
    with jax.named_scope("reduce_attn"):
        attn_terms = halve(added(attn_terms[0], after(attn_terms[1], query_grad)), "x", 1)
    qkv_grad = jnp.concatenate(
        [query_grad * jnp.asarray(HEAD_DIM ** (-0.5), BF), key_grad, value_grad], axis=1
    )
    with jax.named_scope("reduce_qkv"):
        qkv_terms = dot_tn(first_in, after(qkv_grad, mlp_sum)).astype(BF)
        qkv_a, qkv_b = pairs_of(qkv_terms)
        qkv_a, qkv_b = halve(qkv_a, "y", 1), halve(qkv_b, "x", 2)
    first_grad = both_cores(dot_nt(after(qkv_grad, qkv_terms), qkv_half))
    gain_one_part = jnp.sum(first_grad * normed_one, axis=0)
    bias_one_part = jnp.sum(first_grad, axis=0)
    hidden_zero_grad = (
        hidden_one_grad + norm_back(first_grad, gain_one, normed_one, inverse_one)
    ).astype(BF)
    embed_grad = input_scale * dot_nt(hidden_zero_grad, input_full)
    token_grad = (
        embed_grad + (own_term * width ** (-0.5))[:, None] * outputs.astype(F32)
    ).astype(BF)
    token_own = pick(token_grad.reshape(2, half, width), c, 0)
    with jax.named_scope("token_pair"):
        token_moved = swap(token_own, "x")
    with jax.named_scope("reduce_mlp"):
        mlp_ring = ring_up(ring_next(mlp_sum, after(mlp_ring, token_own), 1, "z").astype(BF), "z")
    with jax.named_scope("token_pair"):
        token_other = ordered(token_moved, swap(token_moved, "c"), c, 0).reshape(length, width)
        token_grad_two = ordered(token_grad, token_other, x, 0).reshape(2 * length, width)
    with jax.named_scope("reduce_qkv"):
        qkv_a = halve(added(qkv_a[0], after(qkv_a[1], token_moved)), "x", 1)
        qkv_b = halve(added(qkv_b[0], after(qkv_b[1], token_moved)), "y", 1)

    input_w_grad = dot_tn(inputs, hidden_zero_grad)
    input_rows = input_proj.shape[0]
    with jax.named_scope("reduce_small"):
        vector_grad = jnp.concatenate(
            [
                pick(part.reshape(zy + (2, 2, rows_here)), c, 2)
                for part in (gain_one_part, bias_one_part, gain_two_part, bias_two_part)
            ]
            + [up_bias_part.reshape(zy + (2, -1))],
            axis=-1,
        ).reshape(zy + (2, -1, 128))
        small_grad = jnp.concatenate(
            [
                pick(input_w_grad.reshape(zy + (2, 2, input_rows, D)), c, 2).reshape(
                    zy + (2, rows_here, width)
                ),
                pick(output_w_grad.reshape(zy + (2, 2, rows_here, width)), c, 2),
                jnp.pad(
                    vector_grad,
                    ((0, 0),) * 3 + ((0, rows_here - vector_grad.shape[3]), (0, 128)),
                ),
            ],
            axis=-1,
        ).astype(BF)
        small_terms = halve(small_grad, "y", 1)

    with jax.named_scope("reduce_small"):
        small_terms = halve(added(small_terms[0], after(small_terms[1], token_moved)), "x", 1)
    with jax.named_scope("reduce_attn"):
        attn_sum = added(attn_terms[0], after(attn_terms[1], token_moved))
    with jax.named_scope("reduce_mlp"):
        mlp_ring = ring_up(ring_next(mlp_sum, after(mlp_ring, token_moved), 2, "z").astype(BF), "z")
    table_terms = table_add(table_sums, slots_here, token_grad_two)
    table_terms = after(table_terms, qkv_a[1], qkv_b[1], small_terms[1], mlp_ring)
    with jax.named_scope("reduce_table"):
        terms = table_terms.reshape(2, zn, block_len, width)
        terms_a, terms_b = terms[:, :, :table_cut], terms[:, :, table_cut:]
        moved_a = swap(terms_a[1], "y")
        moved_b = ring_up(terms_b[:, zn - 1], "z")
    with jax.named_scope("reduce_rest"):
        rest_sum = jnp.concatenate(
            [
                jnp.concatenate(
                    [
                        added(qkv_a[0], after(qkv_a[1], table_terms)),
                        added(qkv_b[0], after(qkv_b[1], table_terms)),
                    ],
                    1,
                ),
                added(small_terms[0], after(small_terms[1], table_terms))
                .reshape(zn, rows_here, 2, -1)
                .transpose(0, 2, 1, 3)
                .reshape(zn, 2 * rows_here, -1),
                attn_sum.reshape(zn, rows_here, 2, D // 2)
                .transpose(0, 2, 1, 3)
                .reshape(zn, 2 * rows_here, D // 2),
            ],
            2,
        )
        rest_ring = ring_start(rest_sum, "z")
    moved_b, rest_ring = lax.optimization_barrier((moved_b, rest_ring))
    for step in range(1, zn):
        with jax.named_scope("reduce_table"):
            total_b = terms_b[:, zn - 1 - step].astype(F32) + moved_b.astype(F32)
            if step < zn - 1:
                moved_b = ring_up(total_b.astype(BF), "z")
            else:
                moved_b = swap(total_b[1].astype(BF), "y")
        with jax.named_scope("reduce_rest"):
            rest_own = ring_next(rest_sum, rest_ring, step, "z")
            if step < zn - 1:
                rest_ring = ring_up(rest_own.astype(BF), "z")
        with jax.named_scope("reduce_table"):
            if step == 1:
                sum_a = added(terms_a[0], moved_a)
                moving_a = ring_up(sum_a[zn - 1], "z")
            else:
                total_a = sum_a[zn - step].astype(F32) + moving_a.astype(F32)
                moving_a = ring_up(total_a.astype(BF), "z")
        moved_b, rest_ring, moving_a = lax.optimization_barrier((moved_b, rest_ring, moving_a))
    with jax.named_scope("reduce_table"):
        total_b = total_b[0] + moved_b.astype(F32)
        total_a = sum_a[0].astype(F32) + moving_a.astype(F32)
    with jax.named_scope("reduce_mlp"):
        mlp_own = ring_next(mlp_sum, after(mlp_ring, rest_sum), 3, "z")

    up_total = mlp_own[:, : ff // 2].reshape(2, rows_here, ff // 2)
    down_own = jnp.concatenate([mlp_own[:, ff // 2 : ff // 2 + D], mlp_own[:, ff // 2 + D :]], 0)
    qkv_total = rest_own[:, :qkv_cols].reshape(2, rows_here, qkv_cols)
    small_end = rest_own.shape[1] - D // 2
    small_own = rest_own[:, qkv_cols:small_end]
    small_own = jnp.concatenate([small_own[:rows_here], small_own[rows_here:]], 1)
    attn_own = rest_own[:, small_end:]
    attn_own = jnp.concatenate([attn_own[:rows_here], attn_own[rows_here:]], 1)

    unit_grad = jnp.concatenate([total_a, total_b], axis=0)
    own_rows = embed_table.astype(F32)
    inverse = lax.rsqrt(jnp.mean(own_rows * own_rows, axis=1, keepdims=True) + 1e-06)
    along = jnp.mean(own_rows * unit_grad, axis=1, keepdims=True)
    table_grad = inverse * unit_grad - own_rows * (inverse * inverse * inverse * along)

    input_own = small_own[:, :width].reshape(input_rows, D)
    output_own = small_own[:, width : 2 * width]
    vector_own = small_own[: vector.size // 128, 2 * width : 2 * width + 128].reshape(-1)
    gains = [vector_own[k * rows_here : (k + 1) * rows_here] for k in range(4)]

    def columns_back(sums, split_shape, axis):
        mine_rows, other_rows = pick(sums, c, 0), pick(sums, 1 - c, 0)
        other_cols = swap(other_rows, "c")
        return ordered(
            mine_rows.reshape(split_shape), other_cols.reshape(split_shape), c, axis
        ).reshape(rows_here, -1)

    qkv_own = columns_back(qkv_total, (rows_here, 3 * heads // 2, HEAD_DIM), 2)
    up_own = columns_back(up_total, (rows_here, groups, ff_block), 2)
    return (
        token_loss,
        table_grad,
        input_own,
        gains[0],
        gains[1],
        qkv_own,
        attn_own,
        gains[2],
        gains[3],
        up_own,
        vector_own[4 * rows_here :],
        down_own,
        output_own,
    )


def combined_all(shard, axis, combine):
    everything = jax.tree.map(lambda part: lax.all_gather(part, axis), shard)
    first = jax.tree.map(lambda part: part[0], everything)

    def step(k, so_far):
        return combine(so_far, jax.tree.map(lambda part: part[k], everything))

    return lax.fori_loop(1, lax.axis_size(axis), step, first)


def product(left, right):
    return jnp.dot(left, right, preferred_element_type=jnp.float32)


def product_left(left, right):
    return lax.dot_general(
        left, right, (((0,), (0,)), ((), ())), preferred_element_type=jnp.float32
    )


def product_right(left, right):
    return lax.dot_general(
        left, right, (((1,), (1,)), ((), ())), preferred_element_type=jnp.float32
    )


def normalize_rows(matrix):
    return matrix * lax.rsqrt(jnp.mean(matrix * matrix, axis=1, keepdims=True) + 1e-06)


def layer_norm(hidden, norm_gain, norm_bias):
    centre = hidden - jnp.mean(hidden, axis=-1, keepdims=True)
    spread = jnp.mean(centre * centre, axis=-1, keepdims=True)
    return centre * lax.rsqrt(spread + 1e-05) * norm_gain + norm_bias


def exact_gelu(pre_act):
    return jax.nn.gelu(pre_act, approximate=False)


def noise_rows(row_seeds, positions, channel_count):
    channel = lax.iota(jnp.int32, channel_count)
    mixed_once = (
        row_seeds[:, None, None] + 7919 * positions[None, :, None] + 104729 * channel[None, None, :]
    ) % 65521
    mixed_twice = (mixed_once * (mixed_once % 32719) + 31 * channel[None, None, :]) % 65521
    return (mixed_twice.astype(jnp.float32) / 32760.5 - 1.0) * 1.7320508


def time_terms(time_steps):
    fraction = time_steps.astype(jnp.float32) / (TSTEPS - 1)
    noise_level = 0.3 * jnp.exp(fraction * math.log(30.0))
    return (noise_level, lax.rsqrt(1.0 + noise_level * noise_level), 0.5 + fraction)


def masked_scores(query_block, key_rows, segment_block, segment_row):
    scores = jnp.einsum("qhd,khd->hqk", query_block, key_rows, preferred_element_type=jnp.float32)
    same_doc = segment_block[:, None] == segment_row[None, :]
    return jnp.where(same_doc[None], scores, -1e30)


def attend_row(operands):
    queries, key_rows, value_rows, segment_row = operands
    length = queries.shape[0]
    block_rows = math.gcd(length, 512)
    block_count = length // block_rows

    def attend_block(pieces):
        query_block, segment_block = pieces
        scores = masked_scores(query_block, key_rows, segment_block, segment_row)
        row_max = jnp.max(scores, axis=-1, keepdims=True)
        raised = jnp.exp(scores - row_max)
        summed = jnp.sum(raised, axis=-1, keepdims=True)
        probs_low = (raised / summed).astype(jnp.bfloat16)
        attended = jnp.einsum(
            "hqk,khd->qhd", probs_low, value_rows, preferred_element_type=jnp.float32
        )
        return (attended.astype(jnp.bfloat16), (row_max + jnp.log(summed))[..., 0])

    attended, log_total = lax.map(
        attend_block,
        (
            queries.reshape((block_count, block_rows) + queries.shape[1:]),
            segment_row.reshape(block_count, block_rows),
        ),
    )
    return (attended.reshape(queries.shape), log_total)


def attend_back_row(operands):
    queries, key_rows, value_rows, segment_row, grad_rows, log_total = operands
    length = queries.shape[0]
    block_rows = math.gcd(length, 512)
    block_count = length // block_rows

    def back_block(carry, pieces):
        key_sum, value_sum = carry
        query_block, segment_block, grad_block, total_block = pieces
        scores = masked_scores(query_block, key_rows, segment_block, segment_row)
        probs = jnp.exp(scores - total_block[:, :, None])
        prob_grad = jnp.einsum(
            "qhd,khd->hqk", grad_block, value_rows, preferred_element_type=jnp.float32
        )
        score_grad = (
            probs * (prob_grad - jnp.sum(probs * prob_grad, axis=-1, keepdims=True))
        ).astype(jnp.bfloat16)
        query_grad = jnp.einsum(
            "hqk,khd->qhd", score_grad, key_rows, preferred_element_type=jnp.float32
        )
        key_sum = key_sum + jnp.einsum(
            "hqk,qhd->khd", score_grad, query_block, preferred_element_type=jnp.float32
        )
        value_sum = value_sum + jnp.einsum(
            "hqk,qhd->khd",
            probs.astype(jnp.bfloat16),
            grad_block,
            preferred_element_type=jnp.float32,
        )
        return ((key_sum, value_sum), query_grad.astype(jnp.bfloat16))

    block_shape = (block_count, block_rows) + queries.shape[1:]
    start_sums = (jnp.zeros(key_rows.shape, jnp.float32), jnp.zeros(value_rows.shape, jnp.float32))
    (key_sum, value_sum), query_grad = lax.scan(
        back_block,
        start_sums,
        (
            queries.reshape(block_shape),
            segment_row.reshape(block_count, block_rows),
            grad_rows.reshape(block_shape),
            log_total,
        ),
    )
    return (
        query_grad.reshape(queries.shape),
        key_sum.astype(jnp.bfloat16),
        value_sum.astype(jnp.bfloat16),
    )


def join_parts(first, second):
    top = jnp.maximum(first[0], second[0])
    total = first[1] * jnp.exp(first[0] - top) + second[1] * jnp.exp(second[0] - top)
    return (top, total, first[2] + second[2], first[3] + second[3])


def local(
    token_ids,
    segment_ids,
    time_steps,
    row_seeds,
    loss_weights,
    embed_table,
    input_proj,
    attn_gain,
    attn_bias,
    qkv_proj,
    attn_proj,
    mlp_gain,
    mlp_bias,
    up_proj,
    up_bias,
    down_proj,
    output_proj,
):
    seq_count = lax.axis_size("seq")
    seq_place = lax.axis_index("seq")
    dp_count = lax.axis_size("dp")
    row_count, length = token_ids.shape
    local_len = length // seq_count
    tok_count = row_count * local_len
    start_pos = seq_place * local_len
    own_ids = lax.dynamic_slice_in_dim(token_ids, start_pos, local_len, 1)
    positions = start_pos + lax.iota(jnp.int32, local_len)
    gathered = (
        lax.all_gather(embed_table, ("dp", "seq"), axis=0, tiled=True),
        lax.all_gather(input_proj, ("dp", "seq"), axis=0, tiled=True),
        lax.all_gather(attn_gain, ("dp", "seq"), axis=0, tiled=True),
        lax.all_gather(attn_bias, ("dp", "seq"), axis=0, tiled=True),
        lax.all_gather(qkv_proj, ("dp", "seq"), axis=0, tiled=True),
        lax.all_gather(attn_proj, ("dp", "seq"), axis=0, tiled=True),
        lax.all_gather(mlp_gain, ("dp", "seq"), axis=0, tiled=True),
        lax.all_gather(mlp_bias, ("dp", "seq"), axis=0, tiled=True),
        lax.all_gather(up_proj, ("dp", "seq"), axis=0, tiled=True),
        lax.all_gather(up_bias, ("dp", "seq"), axis=0, tiled=True),
        lax.all_gather(down_proj, ("dp", "seq"), axis=0, tiled=True),
        lax.all_gather(output_proj, ("dp", "seq"), axis=0, tiled=True),
    )
    (
        table_full,
        input_full,
        gain_one,
        bias_one,
        qkv_full,
        attn_full,
        gain_two,
        bias_two,
        up_full,
        upbias_full,
        down_full,
        output_full,
    ) = gathered
    vocab_size, embed_width = table_full.shape
    block_len = vocab_size // (dp_count * seq_count)
    unit, unit_back = jax.vjp(normalize_rows, table_full.astype(jnp.float32))
    sub_table = lax.dynamic_slice_in_dim(
        table_full.reshape(dp_count, seq_count, block_len, embed_width), seq_place, 1, 1
    ).reshape(dp_count * block_len, embed_width)
    sub_unit = lax.dynamic_slice_in_dim(
        unit.reshape(dp_count, seq_count, block_len, embed_width), seq_place, 1, 1
    ).reshape(dp_count * block_len, embed_width)
    scaled = (sub_unit * embed_width ** (-0.5)).astype(jnp.bfloat16)
    local_rows = lax.iota(jnp.int32, dp_count * block_len)
    vocab_index = (
        local_rows // block_len * seq_count + seq_place
    ) * block_len + local_rows % block_len
    noise_level, input_scale, residual_scale = time_terms(time_steps)
    noise = noise_rows(row_seeds, positions, embed_width)
    embedded = jnp.take(unit, own_ids, axis=0)
    inputs = (
        (input_scale[:, None, None] * (embedded + noise_level[:, None, None] * noise))
        .astype(jnp.bfloat16)
        .reshape(tok_count, embed_width)
    )
    token_scale = jnp.repeat(residual_scale, local_len)[:, None]
    token_input_scale = jnp.repeat(input_scale, local_len)[:, None]
    hidden_zero = product(inputs, input_full)
    first_norm, first_back = jax.vjp(
        layer_norm, hidden_zero, gain_one.astype(jnp.float32), bias_one.astype(jnp.float32)
    )
    first_in = first_norm.astype(jnp.bfloat16)
    qkv = product(first_in, qkv_full)
    query_tok = (
        (qkv[:, :D] * HEAD_DIM ** (-0.5)).astype(jnp.bfloat16).reshape(row_count, local_len, D)
    )
    key_tok = qkv[:, D : 2 * D].astype(jnp.bfloat16).reshape(row_count, local_len, D)
    value_tok = qkv[:, 2 * D :].astype(jnp.bfloat16).reshape(row_count, local_len, D)
    head_q, head_k, head_v = (
        lax.all_to_all(query_tok, "seq", split_axis=2, concat_axis=1, tiled=True),
        lax.all_to_all(key_tok, "seq", split_axis=2, concat_axis=1, tiled=True),
        lax.all_to_all(value_tok, "seq", split_axis=2, concat_axis=1, tiled=True),
    )
    heads_here = head_q.shape[2] // HEAD_DIM
    head_shape = (row_count, length, heads_here, HEAD_DIM)
    head_q = head_q.reshape(head_shape)
    head_k = head_k.reshape(head_shape)
    head_v = head_v.reshape(head_shape)
    attended, log_total = lax.map(attend_row, (head_q, head_k, head_v, segment_ids))
    attended = attended.reshape(row_count, length, heads_here * HEAD_DIM)
    mixed = lax.all_to_all(attended, "seq", split_axis=1, concat_axis=2, tiled=True).reshape(
        tok_count, D
    )
    hidden_one = hidden_zero + token_scale * product(mixed, attn_full)
    second_norm, second_back = jax.vjp(
        layer_norm, hidden_one, gain_two.astype(jnp.float32), bias_two.astype(jnp.float32)
    )
    second_in = second_norm.astype(jnp.bfloat16)
    pre_act = product(second_in, up_full) + upbias_full.astype(jnp.float32)
    activated, gelu_back = jax.vjp(exact_gelu, pre_act)
    act_low = activated.astype(jnp.bfloat16)
    hidden_two = hidden_one + token_scale * product(act_low, down_full)
    final_in = hidden_two.astype(jnp.bfloat16)
    outputs = product(final_in, output_full).astype(jnp.bfloat16)
    group_tok = seq_count * tok_count
    group_out = lax.all_gather(outputs, "seq", axis=0, tiled=True)
    group_ids = (
        token_ids.reshape(row_count, seq_count, local_len).transpose(1, 0, 2).reshape(group_tok)
    )
    spread = jnp.where(
        lax.iota(jnp.int32, seq_count)[:, None] == seq_place,
        loss_weights.reshape(1, tok_count),
        0.0,
    )
    tile_rows = math.gcd(group_tok, 512)
    tile_count = group_tok // tile_rows
    out_tiles = group_out.reshape(tile_count, tile_rows, embed_width)
    id_tiles = group_ids.reshape(tile_count, tile_rows)

    def part_tile(pieces):
        out_block, target_block = pieces
        logits = product_right(out_block, scaled)
        row_max = jnp.max(logits, axis=1)
        exp_sum = jnp.sum(jnp.exp(logits - row_max[:, None]), axis=1)
        picked = jnp.sum(
            jnp.where(vocab_index[None, :] == target_block[:, None], logits, 0.0), axis=1
        )
        return (row_max, exp_sum, picked)

    part_max, part_sum, part_pick = lax.map(part_tile, (out_tiles, id_tiles))
    top, total, pick, weight_tiles = combined_all(
        (part_max, part_sum, part_pick, spread), "seq", join_parts
    )
    log_tiles = top + jnp.log(total)
    all_loss = log_tiles - pick
    token_loss = lax.dynamic_slice_in_dim(all_loss, seq_place, 1, 0)

    def back_tile(scaled_sum, pieces):
        out_block, target_block, log_block, weight_block = pieces
        logits = product_right(out_block, scaled)
        probs = jnp.exp(logits - log_block[:, None])
        onehot = (vocab_index[None, :] == target_block[:, None]).astype(jnp.float32)
        grad_logits = (weight_block[:, None] * (probs - onehot)).astype(jnp.bfloat16)
        scaled_sum = scaled_sum + product_left(grad_logits, out_block)
        return (scaled_sum, product(grad_logits, scaled))

    scaled_grad, out_terms = lax.scan(
        back_tile,
        jnp.zeros(scaled.shape, jnp.float32),
        (out_tiles, id_tiles, log_tiles, weight_tiles),
    )
    out_terms = out_terms.reshape(tile_count * tile_rows, embed_width)
    out_grad = lax.psum_scatter(out_terms, "seq", scatter_dimension=0, tiled=True).astype(
        jnp.bfloat16
    )
    output_w_grad = product_left(final_in, out_grad)
    hidden_two_grad = product_right(out_grad, output_full)
    branch_grad = (token_scale * hidden_two_grad).astype(jnp.bfloat16)
    down_w_grad = product_left(act_low, branch_grad)
    pre_grad = gelu_back(product_right(branch_grad, down_full))[0].astype(jnp.bfloat16)
    up_w_grad = product_left(second_in, pre_grad)
    upbias_grad = jnp.sum(pre_grad, axis=0, dtype=jnp.float32)
    hidden_one_part, gain_two_grad, bias_two_grad = second_back(product_right(pre_grad, up_full))
    hidden_one_grad = hidden_two_grad + hidden_one_part
    attn_grad = (token_scale * hidden_one_grad).astype(jnp.bfloat16)
    attn_w_grad = product_left(mixed, attn_grad)
    mixed_grad = (
        product_right(attn_grad, attn_full).astype(jnp.bfloat16).reshape(row_count, local_len, D)
    )
    head_grad = lax.all_to_all(mixed_grad, "seq", split_axis=2, concat_axis=1, tiled=True).reshape(
        head_shape
    )
    query_grad, key_grad, value_grad = lax.map(
        attend_back_row, (head_q, head_k, head_v, segment_ids, head_grad, log_total)
    )
    merged_shape = (row_count, length, heads_here * HEAD_DIM)
    query_back, key_back, value_back = (
        lax.all_to_all(
            query_grad.reshape(merged_shape), "seq", split_axis=1, concat_axis=2, tiled=True
        ),
        lax.all_to_all(
            key_grad.reshape(merged_shape), "seq", split_axis=1, concat_axis=2, tiled=True
        ),
        lax.all_to_all(
            value_grad.reshape(merged_shape), "seq", split_axis=1, concat_axis=2, tiled=True
        ),
    )
    qkv_grad = jnp.concatenate(
        [query_back * HEAD_DIM ** (-0.5), key_back, value_back], axis=2
    ).reshape(tok_count, 3 * D)
    qkv_w_grad = product_left(first_in, qkv_grad)
    hidden_zero_part, gain_one_grad, bias_one_grad = first_back(product_right(qkv_grad, qkv_full))
    hidden_zero_grad = (hidden_one_grad + hidden_zero_part).astype(jnp.bfloat16)
    input_w_grad = product_left(inputs, hidden_zero_grad)
    embedded_grad = token_input_scale * product_right(hidden_zero_grad, input_full)
    scaled_part = scaled_grad * embed_width ** (-0.5)
    group_grad = lax.all_gather(
        embedded_grad.astype(jnp.bfloat16), "seq", axis=0, tiled=True
    ).astype(embedded_grad.dtype)
    block_id = group_ids // block_len
    owned = block_id % seq_count == seq_place
    local_slot = jnp.where(
        owned, block_id // seq_count * block_len + group_ids % block_len, scaled.shape[0]
    )
    unit_grad = scaled_part.at[local_slot].add(group_grad, mode="drop")
    table_term = jax.vjp(normalize_rows, sub_table.astype(jnp.float32))[1](unit_grad)[0]
    table_grad = lax.psum_scatter(
        table_term.astype(jnp.bfloat16), "dp", scatter_dimension=0, tiled=True
    ).astype(jnp.float32)
    summed = (
        lax.psum_scatter(input_w_grad, ("dp", "seq"), scatter_dimension=0, tiled=True),
        lax.psum_scatter(gain_one_grad, ("dp", "seq"), scatter_dimension=0, tiled=True),
        lax.psum_scatter(bias_one_grad, ("dp", "seq"), scatter_dimension=0, tiled=True),
        lax.psum_scatter(qkv_w_grad, ("dp", "seq"), scatter_dimension=0, tiled=True),
        lax.psum_scatter(attn_w_grad, ("dp", "seq"), scatter_dimension=0, tiled=True),
        lax.psum_scatter(gain_two_grad, ("dp", "seq"), scatter_dimension=0, tiled=True),
        lax.psum_scatter(bias_two_grad, ("dp", "seq"), scatter_dimension=0, tiled=True),
        lax.psum_scatter(up_w_grad, ("dp", "seq"), scatter_dimension=0, tiled=True),
        lax.psum_scatter(upbias_grad, ("dp", "seq"), scatter_dimension=0, tiled=True),
        lax.psum_scatter(down_w_grad, ("dp", "seq"), scatter_dimension=0, tiled=True),
        lax.psum_scatter(output_w_grad, ("dp", "seq"), scatter_dimension=0, tiled=True),
    )
    return (token_loss.reshape(row_count, local_len), table_grad) + tuple(summed)


def solution(mesh):
    dp, seq = mesh.shape["dp"], mesh.shape["seq"]
    if (dp, seq) == (16, 2):
        inner = Mesh(mesh.devices.reshape(dp // 4, 2, 2, seq), ("z", "y", "c", "x"))
        dp_names, seq_names, body = ("z", "y", "c"), ("x",), paired
    else:
        inner, dp_names, seq_names, body = mesh, ("dp",), ("seq",), local
    every = dp_names + seq_names
    in_specs = (
        P(dp_names, None),
        P(dp_names, None),
        P(dp_names),
        P(dp_names),
        P(dp_names, seq_names),
        P(every, None),
        P(every, None),
        P(every),
        P(every),
        P(every, None),
        P(every, None),
        P(every),
        P(every),
        P(every, None),
        P(every),
        P(every, None),
        P(every, None),
    )
    out_specs = (
        P(dp_names, seq_names),
        P(every, None),
        P(every, None),
        P(every),
        P(every),
        P(every, None),
        P(every, None),
        P(every),
        P(every),
        P(every, None),
        P(every),
        P(every, None),
        P(every, None),
    )
    return jax.shard_map(body, mesh=inner, in_specs=in_specs, out_specs=out_specs, check_vma=False)
```

```python
import math

import jax
import jax.numpy as jnp
from jax import lax
from jax.experimental import pallas as pl
from jax.experimental.pallas import tpu as pltpu
from jax.sharding import Mesh
from jax.sharding import PartitionSpec as P

D = 1024
HEAD_DIM = 64
TSTEPS = 1000
SWAP = ((0, 1), (1, 0))
BF = jnp.bfloat16
F32 = jnp.float32
NEG = -1e30
LIMIT = 70.0
MIB = 1 << 20


def dot_nn(left, right):
    return lax.dot_general(left, right, (((1,), (0,)), ((), ())), preferred_element_type=F32)


def dot_nt(left, right):
    return lax.dot_general(left, right, (((1,), (1,)), ((), ())), preferred_element_type=F32)


def dot_tn(left, right):
    return lax.dot_general(left, right, (((0,), (0,)), ((), ())), preferred_element_type=F32)


def swap(value, axis):
    return lax.ppermute(value, axis, SWAP)


def ring_down(value, axis):
    n = lax.axis_size(axis)
    return lax.ppermute(value, axis, [(i, (i - 1) % n) for i in range(n)])


def ring_up(value, axis):
    n = lax.axis_size(axis)
    return lax.ppermute(value, axis, [(i, (i + 1) % n) for i in range(n)])


def ordered(own, other, place, axis):
    return jnp.where(
        place == 0, jnp.stack([own, other], axis), jnp.stack([other, own], axis)
    )


def pick(value, index, axis):
    return lax.dynamic_index_in_dim(value, index, axis, keepdims=False)


def after(value, *others):
    return lax.optimization_barrier((value,) + others)[0]


def ring_blocks(value, axis):
    parts = [value]
    for _ in range(lax.axis_size(axis) - 1):
        parts.append(ring_down(parts[-1], axis))
    return parts


def joined_swap(held, axis):
    return jnp.concatenate([held, swap(held, axis)], 0)


def apart(value, axis, distance):
    n = lax.axis_size(axis)
    return lax.ppermute(value, axis, [(i, i ^ distance) for i in range(n)])


def joined_apart(value, axis):
    held, distance = value[None], 1
    while distance < lax.axis_size(axis):
        held = jnp.concatenate([held, apart(held, axis, distance)], 0)
        distance *= 2
    return held


def halve(value, axis, at):
    here = lax.axis_index(axis)
    return pick(value, here, at), swap(pick(value, 1 - here, at), axis)


def added(kept, moved):
    return (kept.astype(F32) + moved.astype(F32)).astype(BF)


def ring_start(value, axis):
    n, here = lax.axis_size(axis), lax.axis_index(axis)
    return ring_up(pick(value, (here - 1) % n, 0), axis)


def ring_next(value, moved, step, axis):
    n, here = lax.axis_size(axis), lax.axis_index(axis)
    return pick(value, (here - 1 - step) % n, 0).astype(F32) + moved.astype(F32)


def place_blocks(places, halves, outs):
    flat = halves[0] + halves[1]
    count = sum(piece.shape[0] for piece in flat) * len(outs)

    def body(places_ref, *refs):
        ins, results, sems = refs[: len(flat)], refs[len(flat) : -1], refs[-1]
        copies, block = [], 0
        for number, piece in enumerate(ins):
            for k in range(piece.shape[0]):
                p, h = places_ref[block], number // len(halves[0])
                block += 1
                for (low, high, _, index), result in zip(outs, results):
                    copies.append(
                        pltpu.make_async_copy(
                            piece.at[k, :, low:high],
                            result.at[index(p, h)],
                            sems.at[len(copies)],
                        )
                    )
        for copy in copies:
            copy.start()
        for copy in copies:
            copy.wait()

    return pl.pallas_call(
        body,
        out_shape=tuple(jax.ShapeDtypeStruct(shape, BF) for _, _, shape, _ in outs),
        grid=(1,),
        in_specs=[pl.BlockSpec(memory_space=pltpu.SMEM)]
        + [pl.BlockSpec(memory_space=pl.ANY)] * len(flat),
        out_specs=tuple(
            pl.BlockSpec(shape, lambda i, n=len(shape): (0,) * n) for _, _, shape, _ in outs
        ),
        scratch_shapes=[pltpu.SemaphoreType.DMA((count,))],
        compiler_params=pltpu.CompilerParams(vmem_limit_bytes=24 * MIB),
        name="place_blocks",
    )(places, *flat)


def for_each_window(lo, hi, blocks, run):
    for count in range(1, blocks + 1):

        @pl.when(hi - lo == count)
        def _():
            run(lo, count)


def attend_body(
    lo_ref, hi_ref, q_ref, k_ref, v_ref, seg_col_ref, seg_row_ref, o_ref, lse_ref, v_ones
):
    length = q_ref.shape[0]
    blk = min(256, length)
    lane = lax.broadcasted_iota(jnp.int32, (1, 128), 1)
    masks = (lane < HEAD_DIM, lane >= HEAD_DIM)
    v = v_ref[...]
    for h in range(2):
        v_ones[h] = jnp.where(masks[h], v, jnp.ones_like(v))

    def largest(ref):
        rows = ref[...].astype(F32)
        return jnp.max(jnp.sum(rows * rows, axis=1, keepdims=True))

    small = largest(q_ref) * largest(k_ref) <= LIMIT * LIMIT

    def finish(rows, accs):
        totals = [pltpu.roll(acc, HEAD_DIM, axis=1) for acc in accs]
        o_ref[rows, :] = (
            jnp.where(masks[0], accs[0], accs[1]) / jnp.where(masks[0], totals[0], totals[1])
        ).astype(BF)
        return [accs[0].T[HEAD_DIM : HEAD_DIM + 1], accs[1].T[0:1]]

    def each(qi, _):
        rows = pl.ds(pl.multiple_of(qi * blk, blk), blk)
        q = q_ref[rows, :]
        q_heads = [jnp.where(m, q, jnp.zeros_like(q)) for m in masks]

        def run(first, count):
            at = pl.ds(pl.multiple_of(first * blk, blk), count * blk)
            k = k_ref[at, :]
            same = seg_col_ref[rows, :] == seg_row_ref[:, at]
            accs = []
            for h in range(2):
                e = jnp.exp(jnp.where(same, dot_nt(q_heads[h], k), NEG)).astype(BF)
                accs.append(dot_nn(e, v_ones[h, at, :]))
            for h, total in enumerate(finish(rows, accs)):
                lse_ref[0, h : h + 1, rows] = jnp.log(total)

        @pl.when(small)
        def _():
            for_each_window(lo_ref[qi], hi_ref[qi], length // blk, run)

        @pl.when(jnp.logical_not(small))
        def _():
            def scores(kb, h):
                at = pl.ds(pl.multiple_of(kb * blk, blk), blk)
                same = seg_col_ref[at, :] == seg_row_ref[:, rows]
                return jnp.where(same, dot_nt(k_ref[at, :], q_heads[h]), NEG)

            def highest(kb, tops):
                return tuple(
                    jnp.maximum(tops[h], jnp.max(scores(kb, h), axis=0, keepdims=True))
                    for h in range(2)
                )

            tops = lax.fori_loop(
                lo_ref[qi], hi_ref[qi], highest, (jnp.full((1, blk), NEG, F32),) * 2
            )

            def gather(kb, accs):
                at = pl.ds(pl.multiple_of(kb * blk, blk), blk)
                return tuple(
                    accs[h]
                    + dot_tn(jnp.exp(scores(kb, h) - tops[h]).astype(BF), v_ones[h, at, :])
                    for h in range(2)
                )

            accs = lax.fori_loop(
                lo_ref[qi], hi_ref[qi], gather, (jnp.zeros((blk, 128), F32),) * 2
            )
            for h, total in enumerate(finish(rows, accs)):
                lse_ref[0, h : h + 1, rows] = tops[h] + jnp.log(total)

        return 0

    lax.fori_loop(0, length // blk, each, 0)


def attend(q, k, v, seg_col, seg_row, lo, hi):
    length, width = q.shape
    pairs = width // 128
    spec = pl.BlockSpec((length, 128), lambda i, *_: (0, i))
    return pl.pallas_call(
        attend_body,
        out_shape=(
            jax.ShapeDtypeStruct((length, width), BF),
            jax.ShapeDtypeStruct((pairs, 2, length), F32),
        ),
        grid_spec=pltpu.PrefetchScalarGridSpec(
            num_scalar_prefetch=2,
            grid=(pairs,),
            in_specs=[
                spec,
                spec,
                spec,
                pl.BlockSpec((length, 1), lambda i, *_: (0, 0)),
                pl.BlockSpec((1, length), lambda i, *_: (0, 0)),
            ],
            out_specs=(spec, pl.BlockSpec((1, 2, length), lambda i, *_: (i, 0, 0))),
            scratch_shapes=[pltpu.VMEM((2, length, 128), BF)],
        ),
        compiler_params=pltpu.CompilerParams(vmem_limit_bytes=32 * MIB),
        cost_estimate=pl.CostEstimate(
            flops=16 * length * length * width,
            bytes_accessed=8 * length * width,
            transcendentals=length * length * width // HEAD_DIM,
        ),
        name="attend",
    )(lo, hi, q, k, v, seg_col, seg_row)


def attend_back_body(
    lo_ref,
    hi_ref,
    q_ref,
    k_ref,
    v_ref,
    o_ref,
    g_ref,
    lse_ref,
    seg_col_ref,
    seg_row_ref,
    dq_ref,
    dk_ref,
    dv_ref,
    dk_sum,
    dv_sum,
    k_t,
):
    length = q_ref.shape[0]
    blk = min(256, length)
    lane = lax.broadcasted_iota(jnp.int32, (1, 128), 1)
    masks = (lane < HEAD_DIM, lane >= HEAD_DIM)
    dk_sum[...] = jnp.zeros_like(dk_sum)
    dv_sum[...] = jnp.zeros_like(dv_sum)
    k_t[...] = k_ref[...].astype(F32).T.astype(BF)
    def each(qi, _):
        rows = pl.ds(pl.multiple_of(qi * blk, blk), blk)

        def run(first, count):
            q, g = q_ref[rows, :], g_ref[rows, :]
            mixed = (g.astype(F32) * o_ref[rows, :].astype(F32)).T
            at = pl.ds(pl.multiple_of(first * blk, blk), count * blk)
            k, v = k_ref[at, :], v_ref[at, :]
            same = seg_col_ref[at, :] == seg_row_ref[:, rows]
            dq = []
            dk, dv = dk_sum[at, :], dv_sum[at, :]
            for h in range(2):
                q_head = jnp.where(masks[h], q, jnp.zeros_like(q))
                g_head = jnp.where(masks[h], g, jnp.zeros_like(g))
                delta = jnp.sum(mixed[h * HEAD_DIM : (h + 1) * HEAD_DIM], axis=0, keepdims=True)
                s = dot_nt(k, q_head)
                p = jnp.exp(jnp.where(same, s - lse_ref[0, h : h + 1, rows], NEG))
                dp = dot_nt(v, g_head)
                ds = (p * (dp - delta)).astype(BF)
                dv = dv + dot_nn(p.astype(BF), g_head)
                dk = dk + dot_nn(ds, q_head)
                dq.append(dot_nn(k_t[h * HEAD_DIM : (h + 1) * HEAD_DIM, at], ds))
            dk_sum[at, :] = dk
            dv_sum[at, :] = dv
            dq_ref[rows, :] = jnp.concatenate(dq, axis=0).T.astype(BF)

        for_each_window(lo_ref[qi], hi_ref[qi], length // blk, run)
        return 0

    lax.fori_loop(0, length // blk, each, 0)
    dk_ref[...] = dk_sum[...].astype(BF)
    dv_ref[...] = dv_sum[...].astype(BF)


def attend_back(q, k, v, o, g, lse, seg_col, seg_row, lo, hi):
    length, width = q.shape
    pairs = width // 128
    spec = pl.BlockSpec((length, 128), lambda i, *_: (0, i))
    shape = jax.ShapeDtypeStruct((length, width), BF)
    return pl.pallas_call(
        attend_back_body,
        out_shape=(shape, shape, shape),
        grid_spec=pltpu.PrefetchScalarGridSpec(
            num_scalar_prefetch=2,
            grid=(pairs,),
            in_specs=[
                spec,
                spec,
                spec,
                spec,
                spec,
                pl.BlockSpec((1, 2, length), lambda i, *_: (i, 0, 0)),
                pl.BlockSpec((length, 1), lambda i, *_: (0, 0)),
                pl.BlockSpec((1, length), lambda i, *_: (0, 0)),
            ],
            out_specs=(spec, spec, spec),
            scratch_shapes=[
                pltpu.VMEM((length, 128), F32),
                pltpu.VMEM((length, 128), F32),
                pltpu.VMEM((128, length), BF),
            ],
        ),
        compiler_params=pltpu.CompilerParams(vmem_limit_bytes=32 * MIB),
        cost_estimate=pl.CostEstimate(
            flops=32 * length * length * width,
            bytes_accessed=16 * length * width,
            transcendentals=length * length * width // HEAD_DIM,
        ),
        name="attend_back",
    )(lo, hi, q, k, v, o, g, lse, seg_col, seg_row)


def score_body(
    norm_ref, out_ref, table_ref, slot_ref, raised_ref, tops_ref, acc_ref, total_ref, top, fast
):
    j = pl.program_id(0)
    tokens, width = out_ref.shape
    count = table_ref.shape[1]
    rows = table_ref[0].astype(F32)
    unit = rows * lax.rsqrt(jnp.mean(rows * rows, axis=1, keepdims=True) + 1e-06)
    low = unit * width ** (-0.5)
    scaled, scaled_t = low.astype(BF), low.T.astype(BF)
    row = lax.broadcasted_iota(jnp.int32, (count, 1), 0) + j * count

    @pl.when(j == 0)
    def _():
        acc_ref[...] = jnp.zeros_like(acc_ref)
        total_ref[...] = jnp.zeros_like(total_ref)
        some = scaled[: min(count, 128)]
        first = jnp.max(dot_nt(some, out_ref[...]), axis=0, keepdims=True)
        floor = norm_ref[...] - LIMIT
        kept = jnp.max(floor - first) <= LIMIT
        top[...] = jnp.where(kept, jnp.maximum(first, floor), NEG)
        fast[0] = kept.astype(jnp.int32)

    @pl.when(fast[0] == 1)
    def _():
        e = jnp.exp(dot_nt(scaled, out_ref[...]) - top[...])
        total_ref[...] += jnp.sum(e, axis=0, keepdims=True)
        raised_ref[0] = jnp.where(row == slot_ref[...], 0.0, e).astype(BF)
        acc_ref[...] += dot_nn(scaled_t, raised_ref[0])
        tops_ref[0] = top[...]

    @pl.when(fast[0] == 0)
    def _():
        part = math.gcd(tokens, 512)

        def each(n, _):
            at = pl.ds(pl.multiple_of(n * part, part), part)
            logits = dot_nt(scaled, out_ref[at, :])
            new_top = jnp.maximum(top[:, at], jnp.max(logits, axis=0, keepdims=True))
            keep = jnp.exp(top[:, at] - new_top)
            e = jnp.exp(logits - new_top)
            total_ref[:, at] = total_ref[:, at] * keep + jnp.sum(e, axis=0, keepdims=True)
            raised_ref[0, :, at] = jnp.where(row == slot_ref[:, at], 0.0, e).astype(BF)
            acc_ref[:, at] = acc_ref[:, at] * keep + dot_nn(scaled_t, raised_ref[0, :, at])
            tops_ref[0, :, at] = new_top
            top[:, at] = new_top
            return 0

        lax.fori_loop(0, tokens // part, each, 0)


def score(outputs, table, slots):
    tokens, width = outputs.shape
    blocks, rows, _ = table.shape
    squares = jnp.square(outputs.astype(F32))
    norms = 1.01 * jnp.sqrt(dot_nt(jnp.ones((8, width), BF), squares.astype(BF))[:1])
    return pl.pallas_call(
        score_body,
        out_shape=(
            jax.ShapeDtypeStruct((blocks, rows, tokens), BF),
            jax.ShapeDtypeStruct((blocks, 1, tokens), F32),
            jax.ShapeDtypeStruct((width, tokens), F32),
            jax.ShapeDtypeStruct((1, tokens), F32),
        ),
        grid=(blocks,),
        in_specs=[
            pl.BlockSpec((1, tokens), lambda j: (0, 0)),
            pl.BlockSpec((tokens, width), lambda j: (0, 0)),
            pl.BlockSpec((1, rows, width), lambda j: (j, 0, 0)),
            pl.BlockSpec((1, tokens), lambda j: (0, 0)),
        ],
        out_specs=(
            pl.BlockSpec((1, rows, tokens), lambda j: (j, 0, 0)),
            pl.BlockSpec((1, 1, tokens), lambda j: (j, 0, 0)),
            pl.BlockSpec((width, tokens), lambda j: (0, 0)),
            pl.BlockSpec((1, tokens), lambda j: (0, 0)),
        ),
        scratch_shapes=[pltpu.VMEM((1, tokens), F32), pltpu.SMEM((1,), jnp.int32)],
        compiler_params=pltpu.CompilerParams(vmem_limit_bytes=48 * MIB),
        cost_estimate=pl.CostEstimate(
            flops=4 * blocks * rows * tokens * width,
            bytes_accessed=2 * blocks * rows * tokens,
            transcendentals=blocks * rows * tokens,
        ),
        name="score",
    )(norms, outputs, table, slots)


def table_product_body(raised_ref, out_ref, coef_ref, sum_ref):
    j = pl.program_id(0)
    lane = lax.broadcasted_iota(jnp.int32, coef_ref.shape, 1)
    coef = jnp.sum(jnp.where(lane == j, coef_ref[...], 0.0), axis=1, keepdims=True)
    weighted = (out_ref[...].astype(F32) * coef).astype(BF)
    sum_ref[0] = dot_nn(raised_ref[0], weighted)


def table_product(raised, outputs, coef):
    blocks, rows, tokens = raised.shape
    width = outputs.shape[1]
    return pl.pallas_call(
        table_product_body,
        out_shape=jax.ShapeDtypeStruct((blocks, rows, width), F32),
        grid=(blocks,),
        in_specs=[
            pl.BlockSpec((1, rows, tokens), lambda j: (j, 0, 0)),
            pl.BlockSpec((tokens, width), lambda j: (0, 0)),
            pl.BlockSpec((tokens, blocks), lambda j: (0, 0)),
        ],
        out_specs=pl.BlockSpec((1, rows, width), lambda j: (j, 0, 0)),
        compiler_params=pltpu.CompilerParams(vmem_limit_bytes=48 * MIB),
        cost_estimate=pl.CostEstimate(
            flops=2 * blocks * rows * tokens * width,
            bytes_accessed=2 * blocks * rows * tokens,
            transcendentals=0,
        ),
        name="table_product",
    )(raised, outputs, coef)


def table_add_body(sum_ref, slot_ref, grad_ref, out_ref):
    j = pl.program_id(0)
    rows = sum_ref.shape[1]
    row = lax.broadcasted_iota(jnp.int32, (rows, 1), 0) + j * rows
    chosen = (row == slot_ref[...]).astype(F32).astype(BF)
    out_ref[0] = (sum_ref[0] + dot_nn(chosen, grad_ref[...])).astype(BF)


def table_add(sums, slots, grads):
    blocks, rows, width = sums.shape
    tokens = grads.shape[0]
    return pl.pallas_call(
        table_add_body,
        out_shape=jax.ShapeDtypeStruct(sums.shape, BF),
        grid=(blocks,),
        in_specs=[
            pl.BlockSpec((1, rows, width), lambda j: (j, 0, 0)),
            pl.BlockSpec((1, tokens), lambda j: (0, 0)),
            pl.BlockSpec((tokens, width), lambda j: (0, 0)),
        ],
        out_specs=pl.BlockSpec((1, rows, width), lambda j: (j, 0, 0)),
        compiler_params=pltpu.CompilerParams(vmem_limit_bytes=48 * MIB),
        cost_estimate=pl.CostEstimate(
            flops=2 * blocks * rows * tokens * width,
            bytes_accessed=6 * blocks * rows * width,
            transcendentals=0,
        ),
        name="table_add",
    )(sums, slots, grads)


def norm_parts(hidden):
    centre = hidden - jnp.mean(hidden, axis=-1, keepdims=True)
    spread = jnp.mean(centre * centre, axis=-1, keepdims=True)
    inverse = lax.rsqrt(spread + 1e-05)
    return centre * inverse, inverse


def norm_back(grad, gain, normed, inverse):
    grad_normed = grad * gain
    first = jnp.mean(grad_normed, axis=-1, keepdims=True)
    second = jnp.mean(grad_normed * normed, axis=-1, keepdims=True)
    return inverse * (grad_normed - first - normed * second)


def noise_field(row_seed, length, channel_count):
    position = lax.iota(jnp.int32, length)[:, None]
    channel = lax.iota(jnp.int32, channel_count)[None, :]
    mixed_once = (row_seed + 7919 * position + 104729 * channel) % 65521
    mixed_twice = (mixed_once * (mixed_once % 32719) + 31 * channel) % 65521
    return (mixed_twice.astype(F32) / 32760.5 - 1.0) * 1.7320508


def paired(
    token_ids,
    segment_ids,
    time_steps,
    row_seeds,
    loss_weights,
    embed_table,
    input_proj,
    attn_gain,
    attn_bias,
    qkv_proj,
    attn_proj,
    mlp_gain,
    mlp_bias,
    up_proj,
    up_bias,
    down_proj,
    output_proj,
):
    z, y, c, x = (lax.axis_index(a) for a in ("z", "y", "c", "x"))
    groups = lax.axis_size("z") * lax.axis_size("y")
    length = token_ids.shape[1]
    half = length // 2
    block_len, width = embed_table.shape
    ff = up_proj.shape[1]
    rows_here = qkv_proj.shape[0]
    heads = D // HEAD_DIM
    ff_block = down_proj.shape[0] * 2

    meta = jnp.concatenate([token_ids[0], segment_ids[0], time_steps, row_seeds])
    meta_two = ordered(meta, swap(meta, "c"), c, 0)
    weight_c = ordered(loss_weights[0], swap(loss_weights[0], "c"), c, 0)
    weight_two = ordered(weight_c, swap(weight_c, "x"), x, 1).reshape(2, length)
    ids_two = meta_two[:, :length]
    own_meta = pick(meta_two, x, 0)
    segments = own_meta[length : 2 * length]
    weight_row = pick(weight_two, x, 0)
    fraction = own_meta[2 * length].astype(F32) / (TSTEPS - 1)
    noise_level = 0.3 * jnp.exp(fraction * math.log(30.0))
    input_scale = lax.rsqrt(1.0 + noise_level * noise_level)
    residual_scale = 0.5 + fraction
    noise = noise_field(own_meta[2 * length + 1], length, width)

    small_width = 2 * width + 128
    vector = jnp.concatenate([attn_gain, attn_bias, mlp_gain, mlp_bias, up_bias])
    small = jnp.concatenate(
        [
            input_proj.reshape(rows_here, width),
            output_proj,
            jnp.pad(vector.reshape(-1, 128), ((0, rows_here - vector.size // 128), (0, 0))),
        ],
        axis=1,
    )
    qkv_split = qkv_proj.reshape(rows_here, 3 * heads // 2, 2, HEAD_DIM)
    up_split = up_proj.reshape(rows_here, groups, 2, ff_block)

    def packed(core):
        return jnp.concatenate(
            [
                pick(qkv_split, core, 2).reshape(rows_here, -1),
                small,
                pick(up_split, core, 2).reshape(rows_here, -1),
            ],
            axis=1,
        )

    pair = ordered(packed(c), swap(packed(1 - c), "c"), c, 0).reshape(2 * rows_here, -1)
    qkv_cols, small_cols = 3 * D // 2, 3 * D // 2 + small_width
    first_cols = small_cols + D // 2
    first_shard = jnp.concatenate(
        [
            pair[:, :small_cols],
            jnp.concatenate([attn_proj[:, : D // 2], attn_proj[:, D // 2 :]], axis=0),
        ],
        axis=1,
    )
    up_shard = pair[:, small_cols:]

    def places(order, ring):
        block, found = jnp.arange(2 * groups, dtype=jnp.int32), {}
        for axis in order:
            n, here = lax.axis_size(axis), lax.axis_index(axis)
            found[axis] = (block + here) % n if ring else (block % n) ^ here
            block = block // n
        return (found["z"] * 2 + found["y"]) * 2 + found["x"]

    def both_places(ring):
        return jnp.concatenate([places(("z", "y", "x"), ring), places(("z", "x", "y"), ring)])

    def over_one(blocks):
        rows = blocks.shape[1] // 2
        return joined_swap(blocks[:, :rows], "y"), joined_swap(blocks[:, rows:], "x")

    def over_one_start(blocks):
        rows = blocks.shape[1] // 2
        first, second = blocks[:, :rows], blocks[:, rows:]
        return (first, swap(first, "y")), (second, swap(second, "x"))

    def over_other(held):
        return [[held[0], swap(held[0], "x")], [held[1], swap(held[1], "y")]]

    cut = block_len // 32 * 16
    with jax.named_scope("gather_table"):
        table_a = ring_blocks(embed_table[None, :cut], "z")
        table_b = ring_blocks(joined_swap(embed_table[None, cut:], "y"), "z")
        table_z = table_b[-1]
        table_a = joined_swap(jnp.concatenate(table_a, 0), "y")
        table_b = jnp.stack(table_b, 1).reshape(groups, block_len - cut, width)
    with jax.named_scope("gather_first"):
        first_z = ring_blocks(first_shard[None], "z")
        first_held = over_one(jnp.concatenate(first_z, 0))
        first_pieces = over_other(first_held)
    with jax.named_scope("gather_up"):
        up_first = after(up_shard[None], table_z, first_z[-1])
        up_moved = apart(up_first, "z", 1)
        up_two = jnp.concatenate([up_first, up_moved], 0)
        up_far = apart(up_two, "z", 2)
    with jax.named_scope("gather_down"):
        down_first = after(down_proj[None], up_far)
        down_moved = apart(down_first, "z", 1)
        down_two = jnp.concatenate([down_first, down_moved], 0)

    flat_ids = ids_two.reshape(-1)
    owner = flat_ids // block_len
    within = flat_ids % block_len
    home = {"z": owner // 8, "y": owner // 4 % 2}
    mine = owner % 4 == c * 2 + x
    table_rows = jnp.concatenate([after(table_a, *first_held, up_moved), table_b], axis=1)
    zn = lax.axis_size("z")
    relative_y, relative_z = (home["y"] - y) % 2, (home["z"] - z) % zn
    slot = (relative_y * zn + relative_z) * block_len + within
    found = jnp.take(
        table_rows.reshape(groups * block_len, width), jnp.where(mine, slot, 0), axis=0
    )
    found = jnp.where(mine[:, None], found, jnp.zeros_like(found)).reshape(2, length, width)

    def to_rows(terms, kind, others):
        split = terms.reshape(2, 2, half, width)
        moved = swap(pick(split, 1 - c, 1).astype(kind), "c")
        both = pick(split, c, 1).astype(F32) + moved.astype(F32)
        both = after(both, *others)
        moved = swap(pick(both, 1 - x, 0).astype(kind), "x")
        own = (pick(both, x, 0).astype(F32) + moved.astype(F32)).astype(kind)
        return ordered(own, swap(own, "c"), c, 0).reshape(length, width)

    def to_pair(row):
        own = pick(row.reshape(2, half, width), c, 0)
        moved = swap(own, "x")
        other = ordered(moved, swap(moved, "c"), c, 0).reshape(length, width)
        return ordered(row, other, x, 0)

    raw = to_rows(found, BF, (first_pieces[0][1], first_pieces[1][1], up_far))
    raw_low = after(raw, down_moved)
    raw = raw_low.astype(F32)
    with jax.named_scope("gather_up"):
        up_z = after(jnp.concatenate([up_two, up_far], 0), first_pieces[0][1], first_pieces[1][1])
        up_moved = over_one_start(up_z)
    paired_shape = (groups, 2, 2, rows_here)

    def in_pairs(p, h):
        return (p // 2, h, p % 2)

    def held_back(pieces, *values):
        return [[after(piece, *values) for piece in half_pieces] for half_pieces in pieces]

    qkv_half, small_full, attn_half = place_blocks(
        both_places(True),
        held_back(first_pieces, found),
        [
            (0, qkv_cols, paired_shape + (qkv_cols,), in_pairs),
            (qkv_cols, small_cols, paired_shape + (small_width,), in_pairs),
            (
                small_cols,
                first_cols,
                (2 * groups, rows_here, D),
                lambda p, h: (p, slice(None), slice(h * D // 2, (h + 1) * D // 2)),
            ),
        ],
    )
    qkv_half, small_full = qkv_half.reshape(D, qkv_cols), small_full.reshape(D, small_width)
    attn_half = attn_half.reshape(D // 2, D)
    input_full = small_full[:, :width].reshape(width, D)
    output_full = small_full[:, width : 2 * width]
    vectors = small_full[:, 2 * width :].reshape(groups, 2, 2, rows_here, 128)
    vectors = vectors[..., : vector.size // 128, :].reshape(groups, 2, 2, vector.size)
    gain_one, bias_one, gain_two, bias_two = (
        vectors[..., k * rows_here : (k + 1) * rows_here].reshape(1, D).astype(F32)
        for k in range(4)
    )
    up_bias_half = pick(vectors[..., 4 * rows_here :], c, 1).reshape(1, ff // 2).astype(F32)
    unit = raw * lax.rsqrt(jnp.mean(raw * raw, axis=1, keepdims=True) + 1e-06)
    target = (unit * width ** (-0.5)).astype(BF)
    inputs = (input_scale * (unit + noise_level * noise)).astype(BF)

    hidden_zero = dot_nn(inputs, input_full)
    normed_one, inverse_one = norm_parts(hidden_zero)
    first_in = (normed_one * gain_one + bias_one).astype(BF)
    first_in = after(first_in, up_moved[0][1], up_moved[1][1])
    with jax.named_scope("gather_up"):
        up_held = [
            jnp.concatenate([own, after(got, first_in)], 0) for own, got in up_moved
        ]
        up_pieces = over_other(up_held)
    with jax.named_scope("gather_down"):
        down_far = apart(after(down_two, raw_low), "z", 2)
    qkv = dot_nn(first_in, qkv_half)
    split = D // 2
    queries = (qkv[:, :split] * HEAD_DIM ** (-0.5)).astype(BF)
    keys = qkv[:, split : 2 * split].astype(BF)
    values = qkv[:, 2 * split :].astype(BF)
    seg_col, seg_row = segments[:, None], segments[None, :]
    blk = min(256, length)
    edges = segments.reshape(length // blk, blk)
    before = jnp.sum(seg_row < edges[:, :1], axis=1, dtype=jnp.int32)
    through = jnp.sum(seg_row <= edges[:, -1:], axis=1, dtype=jnp.int32)
    low_block, high_block = before // blk, (through + blk - 1) // blk
    with jax.named_scope("gather_down"):
        down_z = jnp.concatenate([down_two, down_far], 0)
        down_moved = over_one_start(down_z)
    attended, log_total = attend(
        after(queries, down_z, *up_held), keys, values, seg_col, seg_row, low_block, high_block
    )
    attended = after(
        attended, up_pieces[0][1], up_pieces[1][1], down_moved[0][1], down_moved[1][1]
    )
    with jax.named_scope("gather_down"):
        down_held = [jnp.concatenate([own, after(got, attended)], 0) for own, got in down_moved]
        down_pieces = over_other(down_held)

    def both_cores(part):
        return part + swap(part.astype(BF), "c").astype(F32)

    hidden_one = hidden_zero + residual_scale * both_cores(dot_nn(attended, attn_half))
    normed_two, inverse_two = norm_parts(hidden_one)
    second_in = (normed_two * gain_two + bias_two).astype(BF)
    (up_half,) = place_blocks(
        both_places(False),
        held_back(up_pieces, queries),
        [(0, ff // 2, paired_shape + (ff // 2,), in_pairs)],
    )
    up_half = up_half.reshape(D, ff // 2)
    pre_act = dot_nn(second_in, up_half) + up_bias_half
    below = 0.5 * (1.0 + lax.erf(pre_act * math.sqrt(0.5)))
    activated = (pre_act * below).astype(BF)
    slope = (
        below + pre_act * (jnp.exp(-0.5 * pre_act * pre_act) * (1.0 / math.sqrt(2.0 * math.pi)))
    ).astype(BF)
    (down_half,) = place_blocks(
        both_places(False),
        held_back(down_pieces, activated),
        [
            (
                0,
                D,
                (2 * groups, 2, down_proj.shape[0] // 2, D),
                lambda p, h: (p, h),
            )
        ],
    )
    down_half = down_half.reshape(ff // 2, D)
    hidden_two = hidden_one + residual_scale * both_cores(dot_nn(activated, down_half))
    final_in = hidden_two.astype(BF)
    outputs = dot_nn(final_in, output_full).astype(BF)

    outputs_two = to_pair(outputs).reshape(2 * length, width)
    slots_here = jnp.where(mine, slot, -1)[None, :]
    raised, tops, reached, total = score(outputs_two, table_rows, slots_here)
    ends = jnp.concatenate([tops[-1], total])

    def joined(first, second):
        top = jnp.maximum(first[0], second[0])
        scale_first, scale_second = jnp.exp(first[0] - top), jnp.exp(second[0] - top)
        return jnp.stack([top, first[1] * scale_first + second[1] * scale_second])

    def own_half(value):
        parts = [value[:, k * half : (k + 1) * half] for k in range(4)]
        low, high = jnp.concatenate(parts[::2], 1), jnp.concatenate(parts[1::2], 1)
        return jnp.where(c == 0, low, high), jnp.where(c == 0, high, low)

    def own_row(value):
        first, second = value[:, :half], value[:, half:]
        return jnp.where(x == 0, first, second), jnp.where(x == 0, second, first)

    ends_c = swap(ends, "c")
    kept, sent = own_half(reached)
    moved = swap(sent.astype(BF), "c").astype(F32)
    all_ends = joined(ends, ends_c)
    ends_x = swap(all_ends, "x")
    kept_top, _ = own_half(all_ends[:1])
    both = kept * jnp.exp(own_half(ends[:1])[0] - kept_top) + moved * jnp.exp(
        own_half(ends_c[:1])[0] - kept_top
    )
    kept, sent = own_row(both)
    moved = swap(sent.astype(BF), "x").astype(F32)
    last_ends = joined(all_ends, ends_x)
    log_sum = last_ends[0] + jnp.log(last_ends[1])
    own_log = own_row(own_half(log_sum[None])[0])[0]
    here_top = own_row(own_half(all_ends[:1])[0])[0]
    there_top = own_row(own_half(ends_x[:1])[0])[0]
    own = (kept * jnp.exp(here_top - own_log) + moved * jnp.exp(there_top - own_log)).astype(BF)
    moved = swap(own, "c")
    expected = jnp.concatenate(
        [jnp.where(c == 0, own, moved), jnp.where(c == 0, moved, own)], 1
    ).astype(F32).T
    log_row = pick(log_sum.reshape(2, length), x, 0)
    chosen = jnp.sum(outputs.astype(F32) * target.astype(F32), axis=1)
    loss_row = log_row - chosen
    loss_two = ordered(loss_row, swap(loss_row, "x"), x, 0)
    token_loss = pick(pick(loss_two, c, 0).reshape(2, half), x, 0)[None]

    own_term = weight_row * (jnp.exp(chosen - log_row) - 1.0)
    out_grad = (
        weight_row[:, None] * expected + own_term[:, None] * target.astype(F32)
    ).astype(BF)
    coef = (
        (weight_two.reshape(-1) * width ** (-0.5))[None, :] * jnp.exp(tops[:, 0] - log_sum[None, :])
    ).T

    zy = (zn, lax.axis_size("y"))
    table_cut = block_len * 5 // 128 * 16

    def rows_of(grad):
        rows = grad.shape[0] // (2 * groups)
        return grad.astype(BF).reshape(zy + (2, rows, grad.shape[1]))

    def pairs_of(grad):
        rows = grad.shape[0] // (4 * groups)
        shaped = grad.astype(BF).reshape(zy + (2, 2, rows, grad.shape[1]))
        return shaped[:, :, 0], shaped[:, :, 1]

    output_w_grad = dot_tn(final_in, out_grad)
    hidden_two_grad = dot_nt(out_grad, output_full)
    branch_grad = (residual_scale * hidden_two_grad).astype(BF)
    with jax.named_scope("reduce_down"):
        down_terms = rows_of(dot_tn(activated, branch_grad))
        rows = down_terms.shape[3] // 2
        down_a = halve(down_terms[..., :rows, :], "x", 2)
        down_b = halve(down_terms[..., rows:, :], "y", 1)
    pre_grad = (
        dot_nt(after(branch_grad, down_terms), down_half) * slope.astype(F32)
    ).astype(BF)
    with jax.named_scope("reduce_up"):
        up_terms = dot_tn(second_in, pre_grad).astype(BF)
        up_a, up_b = pairs_of(up_terms)
        up_a, up_b = halve(up_a, "y", 1), halve(up_b, "x", 2)
    up_bias_part = jnp.sum(pre_grad, axis=0, dtype=F32)
    second_part = dot_nt(after(pre_grad, up_terms, down_a[1], down_b[1]), up_half)
    table_sums = table_product(raised, after(outputs_two, second_part), coef)
    second_grad = after(both_cores(second_part), table_sums)
    gain_two_part = jnp.sum(second_grad * normed_two, axis=0)
    bias_two_part = jnp.sum(second_grad, axis=0)
    hidden_one_grad = hidden_two_grad + norm_back(second_grad, gain_two, normed_two, inverse_two)
    attn_grad = after((residual_scale * hidden_one_grad).astype(BF), up_a[1], up_b[1])
    with jax.named_scope("reduce_attn"):
        attn_terms = halve(rows_of(dot_tn(attended, attn_grad)), "y", 1)
    attended_grad = dot_nt(attn_grad, attn_half).astype(BF)
    with jax.named_scope("reduce_down"):
        down_a = added(down_a[0], after(down_a[1], up_terms))
        down_b = added(down_b[0], after(down_b[1], up_terms))
        down_next_a, down_next_b = halve(down_a, "y", 1), halve(down_b, "x", 1)
    with jax.named_scope("reduce_up"):
        up_a = added(up_a[0], after(up_a[1], attn_grad))
        up_b = added(up_b[0], after(up_b[1], attn_grad))
        up_next_a, up_next_b = halve(up_a, "x", 1), halve(up_b, "y", 1)
    query_grad, key_grad, value_grad = attend_back(
        queries,
        keys,
        values,
        attended,
        after(attended_grad, down_a, down_b, up_a, up_b, attn_terms[0]),
        log_total,
        seg_col,
        seg_row,
        low_block,
        high_block,
    )
    query_grad = after(
        query_grad,
        up_next_a[1],
        up_next_b[1],
        down_next_a[1],
        down_next_b[1],
        attn_terms[1],
    )
    with jax.named_scope("reduce_mlp"):
        mlp_sum = jnp.concatenate(
            [
                jnp.concatenate(
                    [
                        added(up_next_a[0], after(up_next_a[1], query_grad)),
                        added(up_next_b[0], after(up_next_b[1], query_grad)),
                    ],
                    1,
                ),
                added(down_next_a[0], after(down_next_a[1], query_grad)),
                added(down_next_b[0], after(down_next_b[1], query_grad)),
            ],
            2,
        )
        mlp_ring = ring_start(mlp_sum, "z")
    with jax.named_scope("reduce_attn"):
        attn_terms = halve(added(attn_terms[0], after(attn_terms[1], query_grad)), "x", 1)
    qkv_grad = jnp.concatenate(
        [query_grad * jnp.asarray(HEAD_DIM ** (-0.5), BF), key_grad, value_grad], axis=1
    )
    with jax.named_scope("reduce_qkv"):
        qkv_terms = dot_tn(first_in, after(qkv_grad, mlp_sum)).astype(BF)
        qkv_a, qkv_b = pairs_of(qkv_terms)
        qkv_a, qkv_b = halve(qkv_a, "y", 1), halve(qkv_b, "x", 2)
    first_grad = both_cores(dot_nt(after(qkv_grad, qkv_terms), qkv_half))
    gain_one_part = jnp.sum(first_grad * normed_one, axis=0)
    bias_one_part = jnp.sum(first_grad, axis=0)
    hidden_zero_grad = (
        hidden_one_grad + norm_back(first_grad, gain_one, normed_one, inverse_one)
    ).astype(BF)
    embed_grad = input_scale * dot_nt(hidden_zero_grad, input_full)
    token_grad = (
        embed_grad + (own_term * width ** (-0.5))[:, None] * outputs.astype(F32)
    ).astype(BF)
    token_own = pick(token_grad.reshape(2, half, width), c, 0)
    with jax.named_scope("token_pair"):
        token_moved = swap(token_own, "x")
    with jax.named_scope("reduce_mlp"):
        mlp_ring = ring_up(ring_next(mlp_sum, after(mlp_ring, token_own), 1, "z").astype(BF), "z")
    with jax.named_scope("token_pair"):
        token_other = ordered(token_moved, swap(token_moved, "c"), c, 0).reshape(length, width)
        token_grad_two = ordered(token_grad, token_other, x, 0).reshape(2 * length, width)
    with jax.named_scope("reduce_qkv"):
        qkv_a = halve(added(qkv_a[0], after(qkv_a[1], token_moved)), "x", 1)
        qkv_b = halve(added(qkv_b[0], after(qkv_b[1], token_moved)), "y", 1)

    input_w_grad = dot_tn(inputs, hidden_zero_grad)
    input_rows = input_proj.shape[0]
    with jax.named_scope("reduce_small"):
        vector_grad = jnp.concatenate(
            [
                pick(part.reshape(zy + (2, 2, rows_here)), c, 2)
                for part in (gain_one_part, bias_one_part, gain_two_part, bias_two_part)
            ]
            + [up_bias_part.reshape(zy + (2, -1))],
            axis=-1,
        ).reshape(zy + (2, -1, 128))
        small_grad = jnp.concatenate(
            [
                pick(input_w_grad.reshape(zy + (2, 2, input_rows, D)), c, 2).reshape(
                    zy + (2, rows_here, width)
                ),
                pick(output_w_grad.reshape(zy + (2, 2, rows_here, width)), c, 2),
                jnp.pad(
                    vector_grad,
                    ((0, 0),) * 3 + ((0, rows_here - vector_grad.shape[3]), (0, 128)),
                ),
            ],
            axis=-1,
        ).astype(BF)
        small_terms = halve(small_grad, "y", 1)

    with jax.named_scope("reduce_small"):
        small_terms = halve(added(small_terms[0], after(small_terms[1], token_moved)), "x", 1)
    with jax.named_scope("reduce_attn"):
        attn_sum = added(attn_terms[0], after(attn_terms[1], token_moved))
    with jax.named_scope("reduce_mlp"):
        mlp_ring = ring_up(ring_next(mlp_sum, after(mlp_ring, token_moved), 2, "z").astype(BF), "z")
    with jax.named_scope("reduce_rest"):
        rest_sum = jnp.concatenate(
            [
                jnp.concatenate(
                    [
                        added(qkv_a[0], after(qkv_a[1], token_grad_two)),
                        added(qkv_b[0], after(qkv_b[1], token_grad_two)),
                    ],
                    1,
                ),
                added(small_terms[0], after(small_terms[1], token_grad_two))
                .reshape(zn, rows_here, 2, -1)
                .transpose(0, 2, 1, 3)
                .reshape(zn, 2 * rows_here, -1),
                attn_sum.reshape(zn, rows_here, 2, D // 2)
                .transpose(0, 2, 1, 3)
                .reshape(zn, 2 * rows_here, D // 2),
            ],
            2,
        )
        rest_ring = ring_start(rest_sum, "z")
    table_terms = table_add(table_sums, slots_here, after(token_grad_two, rest_sum))
    table_terms = after(table_terms, mlp_ring, rest_ring)
    with jax.named_scope("reduce_table"):
        terms = table_terms.reshape(2, zn, block_len, width)
        terms_a, terms_b = terms[:, :, :table_cut], terms[:, :, table_cut:]
        early = table_cut // 32 * 16
        moved_early = swap(terms_a[1, :, :early], "y")
        moved_late = swap(terms_a[1, :, early:], "y")
        moved_b = ring_up(terms_b[:, zn - 1], "z")
    with jax.named_scope("reduce_rest"):
        rest_own = ring_next(rest_sum, after(rest_ring, table_terms), 1, "z")
        rest_ring = ring_up(rest_own.astype(BF), "z")
    moved_b, rest_ring, moved_early = lax.optimization_barrier((moved_b, rest_ring, moved_early))
    for step in range(1, zn):
        with jax.named_scope("reduce_table"):
            total_b = terms_b[:, zn - 1 - step].astype(F32) + moved_b.astype(F32)
            if step < zn - 1:
                moved_b = ring_up(total_b.astype(BF), "z")
            else:
                moved_b = swap(total_b[1].astype(BF), "y")
        if step < zn - 1:
            with jax.named_scope("reduce_rest"):
                rest_own = ring_next(rest_sum, rest_ring, step + 1, "z")
                if step < zn - 2:
                    rest_ring = ring_up(rest_own.astype(BF), "z")
        if step == zn - 2:
            with jax.named_scope("reduce_table"):
                moved_a = jnp.concatenate([moved_early, moved_late], 1)
                sum_a = added(terms_a[0], after(moved_a, total_b))
                moving_a = ring_up(sum_a[zn - 1], "z")
            moved_b, moving_a = lax.optimization_barrier((moved_b, moving_a))
        elif step < zn - 2:
            moved_b, rest_ring, moved_late = lax.optimization_barrier(
                (moved_b, rest_ring, moved_late)
            )
    with jax.named_scope("reduce_table"):
        for step in range(2, zn):
            total_a = sum_a[zn - step].astype(F32) + moving_a.astype(F32)
            moving_a = ring_up(total_a.astype(BF), "z")
            if step == 2:
                moved_b, moving_a = lax.optimization_barrier((moved_b, moving_a))
        total_b = total_b[0] + moved_b.astype(F32)
        total_a = sum_a[0].astype(F32) + moving_a.astype(F32)
    with jax.named_scope("reduce_mlp"):
        mlp_own = ring_next(mlp_sum, after(mlp_ring, rest_sum), 3, "z")

    up_total = mlp_own[:, : ff // 2].reshape(2, rows_here, ff // 2)
    down_own = jnp.concatenate([mlp_own[:, ff // 2 : ff // 2 + D], mlp_own[:, ff // 2 + D :]], 0)
    qkv_total = rest_own[:, :qkv_cols].reshape(2, rows_here, qkv_cols)
    small_end = rest_own.shape[1] - D // 2
    small_own = rest_own[:, qkv_cols:small_end]
    small_own = jnp.concatenate([small_own[:rows_here], small_own[rows_here:]], 1)
    attn_own = rest_own[:, small_end:]
    attn_own = jnp.concatenate([attn_own[:rows_here], attn_own[rows_here:]], 1)

    unit_grad = jnp.concatenate([total_a, total_b], axis=0)
    own_rows = embed_table.astype(F32)
    inverse = lax.rsqrt(jnp.mean(own_rows * own_rows, axis=1, keepdims=True) + 1e-06)
    along = jnp.mean(own_rows * unit_grad, axis=1, keepdims=True)
    table_grad = inverse * unit_grad - own_rows * (inverse * inverse * inverse * along)

    input_own = small_own[:, :width].reshape(input_rows, D)
    output_own = small_own[:, width : 2 * width]
    vector_own = small_own[: vector.size // 128, 2 * width : 2 * width + 128].reshape(-1)
    gains = [vector_own[k * rows_here : (k + 1) * rows_here] for k in range(4)]

    def columns_back(sums, split_shape, axis):
        mine_rows, other_rows = pick(sums, c, 0), pick(sums, 1 - c, 0)
        other_cols = swap(other_rows, "c")
        return ordered(
            mine_rows.reshape(split_shape), other_cols.reshape(split_shape), c, axis
        ).reshape(rows_here, -1)

    qkv_own = columns_back(qkv_total, (rows_here, 3 * heads // 2, HEAD_DIM), 2)
    up_own = columns_back(up_total, (rows_here, groups, ff_block), 2)
    return (
        token_loss,
        table_grad,
        input_own,
        gains[0],
        gains[1],
        qkv_own,
        attn_own,
        gains[2],
        gains[3],
        up_own,
        vector_own[4 * rows_here :],
        down_own,
        output_own,
    )


def combined_all(shard, axis, combine):
    everything = jax.tree.map(lambda part: lax.all_gather(part, axis), shard)
    first = jax.tree.map(lambda part: part[0], everything)

    def step(k, so_far):
        return combine(so_far, jax.tree.map(lambda part: part[k], everything))

    return lax.fori_loop(1, lax.axis_size(axis), step, first)


def product(left, right):
    return jnp.dot(left, right, preferred_element_type=jnp.float32)


def product_left(left, right):
    return lax.dot_general(
        left, right, (((0,), (0,)), ((), ())), preferred_element_type=jnp.float32
    )


def product_right(left, right):
    return lax.dot_general(
        left, right, (((1,), (1,)), ((), ())), preferred_element_type=jnp.float32
    )


def normalize_rows(matrix):
    return matrix * lax.rsqrt(jnp.mean(matrix * matrix, axis=1, keepdims=True) + 1e-06)


def layer_norm(hidden, norm_gain, norm_bias):
    centre = hidden - jnp.mean(hidden, axis=-1, keepdims=True)
    spread = jnp.mean(centre * centre, axis=-1, keepdims=True)
    return centre * lax.rsqrt(spread + 1e-05) * norm_gain + norm_bias


def exact_gelu(pre_act):
    return jax.nn.gelu(pre_act, approximate=False)


def noise_rows(row_seeds, positions, channel_count):
    channel = lax.iota(jnp.int32, channel_count)
    mixed_once = (
        row_seeds[:, None, None] + 7919 * positions[None, :, None] + 104729 * channel[None, None, :]
    ) % 65521
    mixed_twice = (mixed_once * (mixed_once % 32719) + 31 * channel[None, None, :]) % 65521
    return (mixed_twice.astype(jnp.float32) / 32760.5 - 1.0) * 1.7320508


def time_terms(time_steps):
    fraction = time_steps.astype(jnp.float32) / (TSTEPS - 1)
    noise_level = 0.3 * jnp.exp(fraction * math.log(30.0))
    return (noise_level, lax.rsqrt(1.0 + noise_level * noise_level), 0.5 + fraction)


def masked_scores(query_block, key_rows, segment_block, segment_row):
    scores = jnp.einsum("qhd,khd->hqk", query_block, key_rows, preferred_element_type=jnp.float32)
    same_doc = segment_block[:, None] == segment_row[None, :]
    return jnp.where(same_doc[None], scores, -1e30)


def attend_row(operands):
    queries, key_rows, value_rows, segment_row = operands
    length = queries.shape[0]
    block_rows = math.gcd(length, 512)
    block_count = length // block_rows

    def attend_block(pieces):
        query_block, segment_block = pieces
        scores = masked_scores(query_block, key_rows, segment_block, segment_row)
        row_max = jnp.max(scores, axis=-1, keepdims=True)
        raised = jnp.exp(scores - row_max)
        summed = jnp.sum(raised, axis=-1, keepdims=True)
        probs_low = (raised / summed).astype(jnp.bfloat16)
        attended = jnp.einsum(
            "hqk,khd->qhd", probs_low, value_rows, preferred_element_type=jnp.float32
        )
        return (attended.astype(jnp.bfloat16), (row_max + jnp.log(summed))[..., 0])

    attended, log_total = lax.map(
        attend_block,
        (
            queries.reshape((block_count, block_rows) + queries.shape[1:]),
            segment_row.reshape(block_count, block_rows),
        ),
    )
    return (attended.reshape(queries.shape), log_total)


def attend_back_row(operands):
    queries, key_rows, value_rows, segment_row, grad_rows, log_total = operands
    length = queries.shape[0]
    block_rows = math.gcd(length, 512)
    block_count = length // block_rows

    def back_block(carry, pieces):
        key_sum, value_sum = carry
        query_block, segment_block, grad_block, total_block = pieces
        scores = masked_scores(query_block, key_rows, segment_block, segment_row)
        probs = jnp.exp(scores - total_block[:, :, None])
        prob_grad = jnp.einsum(
            "qhd,khd->hqk", grad_block, value_rows, preferred_element_type=jnp.float32
        )
        score_grad = (
            probs * (prob_grad - jnp.sum(probs * prob_grad, axis=-1, keepdims=True))
        ).astype(jnp.bfloat16)
        query_grad = jnp.einsum(
            "hqk,khd->qhd", score_grad, key_rows, preferred_element_type=jnp.float32
        )
        key_sum = key_sum + jnp.einsum(
            "hqk,qhd->khd", score_grad, query_block, preferred_element_type=jnp.float32
        )
        value_sum = value_sum + jnp.einsum(
            "hqk,qhd->khd",
            probs.astype(jnp.bfloat16),
            grad_block,
            preferred_element_type=jnp.float32,
        )
        return ((key_sum, value_sum), query_grad.astype(jnp.bfloat16))

    block_shape = (block_count, block_rows) + queries.shape[1:]
    start_sums = (jnp.zeros(key_rows.shape, jnp.float32), jnp.zeros(value_rows.shape, jnp.float32))
    (key_sum, value_sum), query_grad = lax.scan(
        back_block,
        start_sums,
        (
            queries.reshape(block_shape),
            segment_row.reshape(block_count, block_rows),
            grad_rows.reshape(block_shape),
            log_total,
        ),
    )
    return (
        query_grad.reshape(queries.shape),
        key_sum.astype(jnp.bfloat16),
        value_sum.astype(jnp.bfloat16),
    )


def join_parts(first, second):
    top = jnp.maximum(first[0], second[0])
    total = first[1] * jnp.exp(first[0] - top) + second[1] * jnp.exp(second[0] - top)
    return (top, total, first[2] + second[2], first[3] + second[3])


def local(
    token_ids,
    segment_ids,
    time_steps,
    row_seeds,
    loss_weights,
    embed_table,
    input_proj,
    attn_gain,
    attn_bias,
    qkv_proj,
    attn_proj,
    mlp_gain,
    mlp_bias,
    up_proj,
    up_bias,
    down_proj,
    output_proj,
):
    seq_count = lax.axis_size("seq")
    seq_place = lax.axis_index("seq")
    dp_count = lax.axis_size("dp")
    row_count, length = token_ids.shape
    local_len = length // seq_count
    tok_count = row_count * local_len
    start_pos = seq_place * local_len
    own_ids = lax.dynamic_slice_in_dim(token_ids, start_pos, local_len, 1)
    positions = start_pos + lax.iota(jnp.int32, local_len)
    gathered = (
        lax.all_gather(embed_table, ("dp", "seq"), axis=0, tiled=True),
        lax.all_gather(input_proj, ("dp", "seq"), axis=0, tiled=True),
        lax.all_gather(attn_gain, ("dp", "seq"), axis=0, tiled=True),
        lax.all_gather(attn_bias, ("dp", "seq"), axis=0, tiled=True),
        lax.all_gather(qkv_proj, ("dp", "seq"), axis=0, tiled=True),
        lax.all_gather(attn_proj, ("dp", "seq"), axis=0, tiled=True),
        lax.all_gather(mlp_gain, ("dp", "seq"), axis=0, tiled=True),
        lax.all_gather(mlp_bias, ("dp", "seq"), axis=0, tiled=True),
        lax.all_gather(up_proj, ("dp", "seq"), axis=0, tiled=True),
        lax.all_gather(up_bias, ("dp", "seq"), axis=0, tiled=True),
        lax.all_gather(down_proj, ("dp", "seq"), axis=0, tiled=True),
        lax.all_gather(output_proj, ("dp", "seq"), axis=0, tiled=True),
    )
    (
        table_full,
        input_full,
        gain_one,
        bias_one,
        qkv_full,
        attn_full,
        gain_two,
        bias_two,
        up_full,
        upbias_full,
        down_full,
        output_full,
    ) = gathered
    vocab_size, embed_width = table_full.shape
    block_len = vocab_size // (dp_count * seq_count)
    unit, unit_back = jax.vjp(normalize_rows, table_full.astype(jnp.float32))
    sub_table = lax.dynamic_slice_in_dim(
        table_full.reshape(dp_count, seq_count, block_len, embed_width), seq_place, 1, 1
    ).reshape(dp_count * block_len, embed_width)
    sub_unit = lax.dynamic_slice_in_dim(
        unit.reshape(dp_count, seq_count, block_len, embed_width), seq_place, 1, 1
    ).reshape(dp_count * block_len, embed_width)
    scaled = (sub_unit * embed_width ** (-0.5)).astype(jnp.bfloat16)
    local_rows = lax.iota(jnp.int32, dp_count * block_len)
    vocab_index = (
        local_rows // block_len * seq_count + seq_place
    ) * block_len + local_rows % block_len
    noise_level, input_scale, residual_scale = time_terms(time_steps)
    noise = noise_rows(row_seeds, positions, embed_width)
    embedded = jnp.take(unit, own_ids, axis=0)
    inputs = (
        (input_scale[:, None, None] * (embedded + noise_level[:, None, None] * noise))
        .astype(jnp.bfloat16)
        .reshape(tok_count, embed_width)
    )
    token_scale = jnp.repeat(residual_scale, local_len)[:, None]
    token_input_scale = jnp.repeat(input_scale, local_len)[:, None]
    hidden_zero = product(inputs, input_full)
    first_norm, first_back = jax.vjp(
        layer_norm, hidden_zero, gain_one.astype(jnp.float32), bias_one.astype(jnp.float32)
    )
    first_in = first_norm.astype(jnp.bfloat16)
    qkv = product(first_in, qkv_full)
    query_tok = (
        (qkv[:, :D] * HEAD_DIM ** (-0.5)).astype(jnp.bfloat16).reshape(row_count, local_len, D)
    )
    key_tok = qkv[:, D : 2 * D].astype(jnp.bfloat16).reshape(row_count, local_len, D)
    value_tok = qkv[:, 2 * D :].astype(jnp.bfloat16).reshape(row_count, local_len, D)
    head_q, head_k, head_v = (
        lax.all_to_all(query_tok, "seq", split_axis=2, concat_axis=1, tiled=True),
        lax.all_to_all(key_tok, "seq", split_axis=2, concat_axis=1, tiled=True),
        lax.all_to_all(value_tok, "seq", split_axis=2, concat_axis=1, tiled=True),
    )
    heads_here = head_q.shape[2] // HEAD_DIM
    head_shape = (row_count, length, heads_here, HEAD_DIM)
    head_q = head_q.reshape(head_shape)
    head_k = head_k.reshape(head_shape)
    head_v = head_v.reshape(head_shape)
    attended, log_total = lax.map(attend_row, (head_q, head_k, head_v, segment_ids))
    attended = attended.reshape(row_count, length, heads_here * HEAD_DIM)
    mixed = lax.all_to_all(attended, "seq", split_axis=1, concat_axis=2, tiled=True).reshape(
        tok_count, D
    )
    hidden_one = hidden_zero + token_scale * product(mixed, attn_full)
    second_norm, second_back = jax.vjp(
        layer_norm, hidden_one, gain_two.astype(jnp.float32), bias_two.astype(jnp.float32)
    )
    second_in = second_norm.astype(jnp.bfloat16)
    pre_act = product(second_in, up_full) + upbias_full.astype(jnp.float32)
    activated, gelu_back = jax.vjp(exact_gelu, pre_act)
    act_low = activated.astype(jnp.bfloat16)
    hidden_two = hidden_one + token_scale * product(act_low, down_full)
    final_in = hidden_two.astype(jnp.bfloat16)
    outputs = product(final_in, output_full).astype(jnp.bfloat16)
    group_tok = seq_count * tok_count
    group_out = lax.all_gather(outputs, "seq", axis=0, tiled=True)
    group_ids = (
        token_ids.reshape(row_count, seq_count, local_len).transpose(1, 0, 2).reshape(group_tok)
    )
    spread = jnp.where(
        lax.iota(jnp.int32, seq_count)[:, None] == seq_place,
        loss_weights.reshape(1, tok_count),
        0.0,
    )
    tile_rows = math.gcd(group_tok, 512)
    tile_count = group_tok // tile_rows
    out_tiles = group_out.reshape(tile_count, tile_rows, embed_width)
    id_tiles = group_ids.reshape(tile_count, tile_rows)

    def part_tile(pieces):
        out_block, target_block = pieces
        logits = product_right(out_block, scaled)
        row_max = jnp.max(logits, axis=1)
        exp_sum = jnp.sum(jnp.exp(logits - row_max[:, None]), axis=1)
        picked = jnp.sum(
            jnp.where(vocab_index[None, :] == target_block[:, None], logits, 0.0), axis=1
        )
        return (row_max, exp_sum, picked)

    part_max, part_sum, part_pick = lax.map(part_tile, (out_tiles, id_tiles))
    top, total, pick, weight_tiles = combined_all(
        (part_max, part_sum, part_pick, spread), "seq", join_parts
    )
    log_tiles = top + jnp.log(total)
    all_loss = log_tiles - pick
    token_loss = lax.dynamic_slice_in_dim(all_loss, seq_place, 1, 0)

    def back_tile(scaled_sum, pieces):
        out_block, target_block, log_block, weight_block = pieces
        logits = product_right(out_block, scaled)
        probs = jnp.exp(logits - log_block[:, None])
        onehot = (vocab_index[None, :] == target_block[:, None]).astype(jnp.float32)
        grad_logits = (weight_block[:, None] * (probs - onehot)).astype(jnp.bfloat16)
        scaled_sum = scaled_sum + product_left(grad_logits, out_block)
        return (scaled_sum, product(grad_logits, scaled))

    scaled_grad, out_terms = lax.scan(
        back_tile,
        jnp.zeros(scaled.shape, jnp.float32),
        (out_tiles, id_tiles, log_tiles, weight_tiles),
    )
    out_terms = out_terms.reshape(tile_count * tile_rows, embed_width)
    out_grad = lax.psum_scatter(out_terms, "seq", scatter_dimension=0, tiled=True).astype(
        jnp.bfloat16
    )
    output_w_grad = product_left(final_in, out_grad)
    hidden_two_grad = product_right(out_grad, output_full)
    branch_grad = (token_scale * hidden_two_grad).astype(jnp.bfloat16)
    down_w_grad = product_left(act_low, branch_grad)
    pre_grad = gelu_back(product_right(branch_grad, down_full))[0].astype(jnp.bfloat16)
    up_w_grad = product_left(second_in, pre_grad)
    upbias_grad = jnp.sum(pre_grad, axis=0, dtype=jnp.float32)
    hidden_one_part, gain_two_grad, bias_two_grad = second_back(product_right(pre_grad, up_full))
    hidden_one_grad = hidden_two_grad + hidden_one_part
    attn_grad = (token_scale * hidden_one_grad).astype(jnp.bfloat16)
    attn_w_grad = product_left(mixed, attn_grad)
    mixed_grad = (
        product_right(attn_grad, attn_full).astype(jnp.bfloat16).reshape(row_count, local_len, D)
    )
    head_grad = lax.all_to_all(mixed_grad, "seq", split_axis=2, concat_axis=1, tiled=True).reshape(
        head_shape
    )
    query_grad, key_grad, value_grad = lax.map(
        attend_back_row, (head_q, head_k, head_v, segment_ids, head_grad, log_total)
    )
    merged_shape = (row_count, length, heads_here * HEAD_DIM)
    query_back, key_back, value_back = (
        lax.all_to_all(
            query_grad.reshape(merged_shape), "seq", split_axis=1, concat_axis=2, tiled=True
        ),
        lax.all_to_all(
            key_grad.reshape(merged_shape), "seq", split_axis=1, concat_axis=2, tiled=True
        ),
        lax.all_to_all(
            value_grad.reshape(merged_shape), "seq", split_axis=1, concat_axis=2, tiled=True
        ),
    )
    qkv_grad = jnp.concatenate(
        [query_back * HEAD_DIM ** (-0.5), key_back, value_back], axis=2
    ).reshape(tok_count, 3 * D)
    qkv_w_grad = product_left(first_in, qkv_grad)
    hidden_zero_part, gain_one_grad, bias_one_grad = first_back(product_right(qkv_grad, qkv_full))
    hidden_zero_grad = (hidden_one_grad + hidden_zero_part).astype(jnp.bfloat16)
    input_w_grad = product_left(inputs, hidden_zero_grad)
    embedded_grad = token_input_scale * product_right(hidden_zero_grad, input_full)
    scaled_part = scaled_grad * embed_width ** (-0.5)
    group_grad = lax.all_gather(
        embedded_grad.astype(jnp.bfloat16), "seq", axis=0, tiled=True
    ).astype(embedded_grad.dtype)
    block_id = group_ids // block_len
    owned = block_id % seq_count == seq_place
    local_slot = jnp.where(
        owned, block_id // seq_count * block_len + group_ids % block_len, scaled.shape[0]
    )
    unit_grad = scaled_part.at[local_slot].add(group_grad, mode="drop")
    table_term = jax.vjp(normalize_rows, sub_table.astype(jnp.float32))[1](unit_grad)[0]
    table_grad = lax.psum_scatter(
        table_term.astype(jnp.bfloat16), "dp", scatter_dimension=0, tiled=True
    ).astype(jnp.float32)
    summed = (
        lax.psum_scatter(input_w_grad, ("dp", "seq"), scatter_dimension=0, tiled=True),
        lax.psum_scatter(gain_one_grad, ("dp", "seq"), scatter_dimension=0, tiled=True),
        lax.psum_scatter(bias_one_grad, ("dp", "seq"), scatter_dimension=0, tiled=True),
        lax.psum_scatter(qkv_w_grad, ("dp", "seq"), scatter_dimension=0, tiled=True),
        lax.psum_scatter(attn_w_grad, ("dp", "seq"), scatter_dimension=0, tiled=True),
        lax.psum_scatter(gain_two_grad, ("dp", "seq"), scatter_dimension=0, tiled=True),
        lax.psum_scatter(bias_two_grad, ("dp", "seq"), scatter_dimension=0, tiled=True),
        lax.psum_scatter(up_w_grad, ("dp", "seq"), scatter_dimension=0, tiled=True),
        lax.psum_scatter(upbias_grad, ("dp", "seq"), scatter_dimension=0, tiled=True),
        lax.psum_scatter(down_w_grad, ("dp", "seq"), scatter_dimension=0, tiled=True),
        lax.psum_scatter(output_w_grad, ("dp", "seq"), scatter_dimension=0, tiled=True),
    )
    return (token_loss.reshape(row_count, local_len), table_grad) + tuple(summed)


def solution(mesh):
    dp, seq = mesh.shape["dp"], mesh.shape["seq"]
    if (dp, seq) == (16, 2):
        inner = Mesh(mesh.devices.reshape(dp // 4, 2, 2, seq), ("z", "y", "c", "x"))
        dp_names, seq_names, body = ("z", "y", "c"), ("x",), paired
    else:
        inner, dp_names, seq_names, body = mesh, ("dp",), ("seq",), local
    every = dp_names + seq_names
    in_specs = (
        P(dp_names, None),
        P(dp_names, None),
        P(dp_names),
        P(dp_names),
        P(dp_names, seq_names),
        P(every, None),
        P(every, None),
        P(every),
        P(every),
        P(every, None),
        P(every, None),
        P(every),
        P(every),
        P(every, None),
        P(every),
        P(every, None),
        P(every, None),
    )
    out_specs = (
        P(dp_names, seq_names),
        P(every, None),
        P(every, None),
        P(every),
        P(every),
        P(every, None),
        P(every, None),
        P(every),
        P(every),
        P(every, None),
        P(every),
        P(every, None),
        P(every, None),
    )
    return jax.shard_map(body, mesh=inner, in_specs=in_specs, out_specs=out_specs, check_vma=False)
```

```python
import math

import jax
import jax.numpy as jnp
from jax import lax
from jax.experimental import pallas as pl
from jax.experimental.pallas import tpu as pltpu
from jax.sharding import Mesh
from jax.sharding import PartitionSpec as P

D = 1024
HEAD_DIM = 64
TSTEPS = 1000
SWAP = ((0, 1), (1, 0))
BF = jnp.bfloat16
F32 = jnp.float32
NEG = -1e30
LIMIT = 70.0
MIB = 1 << 20


def dot_nn(left, right):
    return lax.dot_general(left, right, (((1,), (0,)), ((), ())), preferred_element_type=F32)


def dot_nt(left, right):
    return lax.dot_general(left, right, (((1,), (1,)), ((), ())), preferred_element_type=F32)


def dot_tn(left, right):
    return lax.dot_general(left, right, (((0,), (0,)), ((), ())), preferred_element_type=F32)


def swap(value, axis):
    return lax.ppermute(value, axis, SWAP)


def ring_down(value, axis):
    n = lax.axis_size(axis)
    return lax.ppermute(value, axis, [(i, (i - 1) % n) for i in range(n)])


def ring_up(value, axis):
    n = lax.axis_size(axis)
    return lax.ppermute(value, axis, [(i, (i + 1) % n) for i in range(n)])


def ordered(own, other, place, axis):
    return jnp.where(
        place == 0, jnp.stack([own, other], axis), jnp.stack([other, own], axis)
    )


def pick(value, index, axis):
    return lax.dynamic_index_in_dim(value, index, axis, keepdims=False)


def after(value, *others):
    return lax.optimization_barrier((value,) + others)[0]


def ring_blocks(value, axis):
    parts = [value]
    for _ in range(lax.axis_size(axis) - 1):
        parts.append(ring_down(parts[-1], axis))
    return parts


def joined_swap(held, axis):
    return jnp.concatenate([held, swap(held, axis)], 0)


def apart(value, axis, distance):
    n = lax.axis_size(axis)
    return lax.ppermute(value, axis, [(i, i ^ distance) for i in range(n)])


def joined_apart(value, axis):
    held, distance = value[None], 1
    while distance < lax.axis_size(axis):
        held = jnp.concatenate([held, apart(held, axis, distance)], 0)
        distance *= 2
    return held


def halve(value, axis, at):
    here = lax.axis_index(axis)
    return pick(value, here, at), swap(pick(value, 1 - here, at), axis)


def added(kept, moved):
    return (kept.astype(F32) + moved.astype(F32)).astype(BF)


def ring_start(value, axis):
    n, here = lax.axis_size(axis), lax.axis_index(axis)
    return ring_up(pick(value, (here - 1) % n, 0), axis)


def ring_next(value, moved, step, axis):
    n, here = lax.axis_size(axis), lax.axis_index(axis)
    return pick(value, (here - 1 - step) % n, 0).astype(F32) + moved.astype(F32)


def place_blocks(places, halves, outs):
    flat = halves[0] + halves[1]

    def body(places_ref, *refs):
        ins, results, block = refs[: len(flat)], refs[len(flat) :], 0
        for number, piece in enumerate(ins):
            for k in range(piece.shape[0]):
                p, h = places_ref[block], number // len(halves[0])
                block += 1
                for (low, high, _, index), result in zip(outs, results):
                    result[index(p, h)] = piece[k, :, low:high]

    return pl.pallas_call(
        body,
        out_shape=tuple(jax.ShapeDtypeStruct(shape, BF) for _, _, shape, _ in outs),
        in_specs=[pl.BlockSpec(memory_space=pltpu.SMEM)]
        + [pl.BlockSpec(memory_space=pltpu.VMEM)] * len(flat),
        out_specs=tuple(pl.BlockSpec(memory_space=pltpu.VMEM) for _ in outs),
        compiler_params=pltpu.CompilerParams(vmem_limit_bytes=32 * MIB),
        name="place_blocks",
    )(places, *flat)


def for_each_window(lo, hi, blocks, run):
    for count in range(1, blocks + 1):

        @pl.when(hi - lo == count)
        def _():
            run(lo, count)


def attend_body(
    lo_ref, hi_ref, q_ref, k_ref, v_ref, seg_col_ref, seg_row_ref, o_ref, lse_ref, v_ones
):
    length = q_ref.shape[0]
    blk = min(256, length)
    lane = lax.broadcasted_iota(jnp.int32, (1, 128), 1)
    masks = (lane < HEAD_DIM, lane >= HEAD_DIM)
    v = v_ref[...]
    for h in range(2):
        v_ones[h] = jnp.where(masks[h], v, jnp.ones_like(v))

    def largest(ref):
        rows = ref[...].astype(F32)
        return jnp.max(jnp.sum(rows * rows, axis=1, keepdims=True))

    small = largest(q_ref) * largest(k_ref) <= LIMIT * LIMIT

    def finish(rows, accs):
        totals = [pltpu.roll(acc, HEAD_DIM, axis=1) for acc in accs]
        o_ref[rows, :] = (
            jnp.where(masks[0], accs[0], accs[1]) / jnp.where(masks[0], totals[0], totals[1])
        ).astype(BF)
        return [accs[0].T[HEAD_DIM : HEAD_DIM + 1], accs[1].T[0:1]]

    def each(qi, _):
        rows = pl.ds(pl.multiple_of(qi * blk, blk), blk)
        q = q_ref[rows, :]
        q_heads = [jnp.where(m, q, jnp.zeros_like(q)) for m in masks]

        def run(first, count):
            at = pl.ds(pl.multiple_of(first * blk, blk), count * blk)
            k = k_ref[at, :]
            same = seg_col_ref[rows, :] == seg_row_ref[:, at]
            accs = []
            for h in range(2):
                e = jnp.exp(jnp.where(same, dot_nt(q_heads[h], k), NEG)).astype(BF)
                accs.append(dot_nn(e, v_ones[h, at, :]))
            for h, total in enumerate(finish(rows, accs)):
                lse_ref[0, h : h + 1, rows] = jnp.log(total)

        @pl.when(small)
        def _():
            for_each_window(lo_ref[qi], hi_ref[qi], length // blk, run)

        @pl.when(jnp.logical_not(small))
        def _():
            def scores(kb, h):
                at = pl.ds(pl.multiple_of(kb * blk, blk), blk)
                same = seg_col_ref[at, :] == seg_row_ref[:, rows]
                return jnp.where(same, dot_nt(k_ref[at, :], q_heads[h]), NEG)

            def highest(kb, tops):
                return tuple(
                    jnp.maximum(tops[h], jnp.max(scores(kb, h), axis=0, keepdims=True))
                    for h in range(2)
                )

            tops = lax.fori_loop(
                lo_ref[qi], hi_ref[qi], highest, (jnp.full((1, blk), NEG, F32),) * 2
            )

            def gather(kb, accs):
                at = pl.ds(pl.multiple_of(kb * blk, blk), blk)
                return tuple(
                    accs[h]
                    + dot_tn(jnp.exp(scores(kb, h) - tops[h]).astype(BF), v_ones[h, at, :])
                    for h in range(2)
                )

            accs = lax.fori_loop(
                lo_ref[qi], hi_ref[qi], gather, (jnp.zeros((blk, 128), F32),) * 2
            )
            for h, total in enumerate(finish(rows, accs)):
                lse_ref[0, h : h + 1, rows] = tops[h] + jnp.log(total)

        return 0

    lax.fori_loop(0, length // blk, each, 0)


def attend(q, k, v, seg_col, seg_row, lo, hi):
    length, width = q.shape
    pairs = width // 128
    spec = pl.BlockSpec((length, 128), lambda i, *_: (0, i))
    return pl.pallas_call(
        attend_body,
        out_shape=(
            jax.ShapeDtypeStruct((length, width), BF),
            jax.ShapeDtypeStruct((pairs, 2, length), F32),
        ),
        grid_spec=pltpu.PrefetchScalarGridSpec(
            num_scalar_prefetch=2,
            grid=(pairs,),
            in_specs=[
                spec,
                spec,
                spec,
                pl.BlockSpec((length, 1), lambda i, *_: (0, 0)),
                pl.BlockSpec((1, length), lambda i, *_: (0, 0)),
            ],
            out_specs=(spec, pl.BlockSpec((1, 2, length), lambda i, *_: (i, 0, 0))),
            scratch_shapes=[pltpu.VMEM((2, length, 128), BF)],
        ),
        compiler_params=pltpu.CompilerParams(vmem_limit_bytes=32 * MIB),
        cost_estimate=pl.CostEstimate(
            flops=16 * length * length * width,
            bytes_accessed=8 * length * width,
            transcendentals=length * length * width // HEAD_DIM,
        ),
        name="attend",
    )(lo, hi, q, k, v, seg_col, seg_row)


def attend_back_body(
    lo_ref,
    hi_ref,
    q_ref,
    k_ref,
    v_ref,
    o_ref,
    g_ref,
    lse_ref,
    seg_col_ref,
    seg_row_ref,
    dq_ref,
    dk_ref,
    dv_ref,
    dk_sum,
    dv_sum,
    k_t,
):
    length = q_ref.shape[0]
    blk = min(256, length)
    lane = lax.broadcasted_iota(jnp.int32, (1, 128), 1)
    masks = (lane < HEAD_DIM, lane >= HEAD_DIM)
    dk_sum[...] = jnp.zeros_like(dk_sum)
    dv_sum[...] = jnp.zeros_like(dv_sum)
    k_t[...] = k_ref[...].astype(F32).T.astype(BF)
    def each(qi, _):
        rows = pl.ds(pl.multiple_of(qi * blk, blk), blk)

        def run(first, count):
            q, g = q_ref[rows, :], g_ref[rows, :]
            mixed = (g.astype(F32) * o_ref[rows, :].astype(F32)).T
            at = pl.ds(pl.multiple_of(first * blk, blk), count * blk)
            k, v = k_ref[at, :], v_ref[at, :]
            same = seg_col_ref[at, :] == seg_row_ref[:, rows]
            dq = []
            dk, dv = dk_sum[at, :], dv_sum[at, :]
            for h in range(2):
                q_head = jnp.where(masks[h], q, jnp.zeros_like(q))
                g_head = jnp.where(masks[h], g, jnp.zeros_like(g))
                delta = jnp.sum(mixed[h * HEAD_DIM : (h + 1) * HEAD_DIM], axis=0, keepdims=True)
                s = dot_nt(k, q_head)
                p = jnp.exp(jnp.where(same, s - lse_ref[0, h : h + 1, rows], NEG))
                dp = dot_nt(v, g_head)
                ds = (p * (dp - delta)).astype(BF)
                dv = dv + dot_nn(p.astype(BF), g_head)
                dk = dk + dot_nn(ds, q_head)
                dq.append(dot_nn(k_t[h * HEAD_DIM : (h + 1) * HEAD_DIM, at], ds))
            dk_sum[at, :] = dk
            dv_sum[at, :] = dv
            dq_ref[rows, :] = jnp.concatenate(dq, axis=0).T.astype(BF)

        for_each_window(lo_ref[qi], hi_ref[qi], length // blk, run)
        return 0

    lax.fori_loop(0, length // blk, each, 0)
    dk_ref[...] = dk_sum[...].astype(BF)
    dv_ref[...] = dv_sum[...].astype(BF)


def attend_back(q, k, v, o, g, lse, seg_col, seg_row, lo, hi):
    length, width = q.shape
    pairs = width // 128
    spec = pl.BlockSpec((length, 128), lambda i, *_: (0, i))
    shape = jax.ShapeDtypeStruct((length, width), BF)
    return pl.pallas_call(
        attend_back_body,
        out_shape=(shape, shape, shape),
        grid_spec=pltpu.PrefetchScalarGridSpec(
            num_scalar_prefetch=2,
            grid=(pairs,),
            in_specs=[
                spec,
                spec,
                spec,
                spec,
                spec,
                pl.BlockSpec((1, 2, length), lambda i, *_: (i, 0, 0)),
                pl.BlockSpec((length, 1), lambda i, *_: (0, 0)),
                pl.BlockSpec((1, length), lambda i, *_: (0, 0)),
            ],
            out_specs=(spec, spec, spec),
            scratch_shapes=[
                pltpu.VMEM((length, 128), F32),
                pltpu.VMEM((length, 128), F32),
                pltpu.VMEM((128, length), BF),
            ],
        ),
        compiler_params=pltpu.CompilerParams(vmem_limit_bytes=32 * MIB),
        cost_estimate=pl.CostEstimate(
            flops=32 * length * length * width,
            bytes_accessed=16 * length * width,
            transcendentals=length * length * width // HEAD_DIM,
        ),
        name="attend_back",
    )(lo, hi, q, k, v, o, g, lse, seg_col, seg_row)


def score_body(
    norm_ref, out_ref, table_ref, slot_ref, raised_ref, tops_ref, acc_ref, total_ref, top, fast
):
    j = pl.program_id(0)
    tokens, width = out_ref.shape
    count = table_ref.shape[1]
    rows = table_ref[0].astype(F32)
    unit = rows * lax.rsqrt(jnp.mean(rows * rows, axis=1, keepdims=True) + 1e-06)
    low = unit * width ** (-0.5)
    scaled, scaled_t = low.astype(BF), low.T.astype(BF)
    row = lax.broadcasted_iota(jnp.int32, (count, 1), 0) + j * count

    @pl.when(j == 0)
    def _():
        acc_ref[...] = jnp.zeros_like(acc_ref)
        total_ref[...] = jnp.zeros_like(total_ref)
        some = scaled[: min(count, 128)]
        first = jnp.max(dot_nt(some, out_ref[...]), axis=0, keepdims=True)
        floor = norm_ref[...] - LIMIT
        kept = jnp.max(floor - first) <= LIMIT
        top[...] = jnp.where(kept, jnp.maximum(first, floor), NEG)
        fast[0] = kept.astype(jnp.int32)

    @pl.when(fast[0] == 1)
    def _():
        e = jnp.exp(dot_nt(scaled, out_ref[...]) - top[...])
        total_ref[...] += jnp.sum(e, axis=0, keepdims=True)
        raised_ref[0] = jnp.where(row == slot_ref[...], 0.0, e).astype(BF)
        acc_ref[...] += dot_nn(scaled_t, raised_ref[0])
        tops_ref[0] = top[...]

    @pl.when(fast[0] == 0)
    def _():
        part = math.gcd(tokens, 512)

        def each(n, _):
            at = pl.ds(pl.multiple_of(n * part, part), part)
            logits = dot_nt(scaled, out_ref[at, :])
            new_top = jnp.maximum(top[:, at], jnp.max(logits, axis=0, keepdims=True))
            keep = jnp.exp(top[:, at] - new_top)
            e = jnp.exp(logits - new_top)
            total_ref[:, at] = total_ref[:, at] * keep + jnp.sum(e, axis=0, keepdims=True)
            raised_ref[0, :, at] = jnp.where(row == slot_ref[:, at], 0.0, e).astype(BF)
            acc_ref[:, at] = acc_ref[:, at] * keep + dot_nn(scaled_t, raised_ref[0, :, at])
            tops_ref[0, :, at] = new_top
            top[:, at] = new_top
            return 0

        lax.fori_loop(0, tokens // part, each, 0)


def score(outputs, table, slots):
    tokens, width = outputs.shape
    blocks, rows, _ = table.shape
    squares = jnp.square(outputs.astype(F32))
    norms = 1.01 * jnp.sqrt(dot_nt(jnp.ones((8, width), BF), squares.astype(BF))[:1])
    return pl.pallas_call(
        score_body,
        out_shape=(
            jax.ShapeDtypeStruct((blocks, rows, tokens), BF),
            jax.ShapeDtypeStruct((blocks, 1, tokens), F32),
            jax.ShapeDtypeStruct((width, tokens), F32),
            jax.ShapeDtypeStruct((1, tokens), F32),
        ),
        grid=(blocks,),
        in_specs=[
            pl.BlockSpec((1, tokens), lambda j: (0, 0)),
            pl.BlockSpec((tokens, width), lambda j: (0, 0)),
            pl.BlockSpec((1, rows, width), lambda j: (j, 0, 0)),
            pl.BlockSpec((1, tokens), lambda j: (0, 0)),
        ],
        out_specs=(
            pl.BlockSpec((1, rows, tokens), lambda j: (j, 0, 0)),
            pl.BlockSpec((1, 1, tokens), lambda j: (j, 0, 0)),
            pl.BlockSpec((width, tokens), lambda j: (0, 0)),
            pl.BlockSpec((1, tokens), lambda j: (0, 0)),
        ),
        scratch_shapes=[pltpu.VMEM((1, tokens), F32), pltpu.SMEM((1,), jnp.int32)],
        compiler_params=pltpu.CompilerParams(vmem_limit_bytes=48 * MIB),
        cost_estimate=pl.CostEstimate(
            flops=4 * blocks * rows * tokens * width,
            bytes_accessed=2 * blocks * rows * tokens,
            transcendentals=blocks * rows * tokens,
        ),
        name="score",
    )(norms, outputs, table, slots)


def table_product_body(raised_ref, out_ref, coef_ref, sum_ref):
    j = pl.program_id(0)
    lane = lax.broadcasted_iota(jnp.int32, coef_ref.shape, 1)
    coef = jnp.sum(jnp.where(lane == j, coef_ref[...], 0.0), axis=1, keepdims=True)
    weighted = (out_ref[...].astype(F32) * coef).astype(BF)
    sum_ref[0] = dot_nn(raised_ref[0], weighted)


def table_product(raised, outputs, coef):
    blocks, rows, tokens = raised.shape
    width = outputs.shape[1]
    return pl.pallas_call(
        table_product_body,
        out_shape=jax.ShapeDtypeStruct((blocks, rows, width), F32),
        grid=(blocks,),
        in_specs=[
            pl.BlockSpec((1, rows, tokens), lambda j: (j, 0, 0)),
            pl.BlockSpec((tokens, width), lambda j: (0, 0)),
            pl.BlockSpec((tokens, blocks), lambda j: (0, 0)),
        ],
        out_specs=pl.BlockSpec((1, rows, width), lambda j: (j, 0, 0)),
        compiler_params=pltpu.CompilerParams(vmem_limit_bytes=48 * MIB),
        cost_estimate=pl.CostEstimate(
            flops=2 * blocks * rows * tokens * width,
            bytes_accessed=2 * blocks * rows * tokens,
            transcendentals=0,
        ),
        name="table_product",
    )(raised, outputs, coef)


def table_add_body(sum_ref, slot_ref, grad_ref, out_ref):
    j = pl.program_id(0)
    rows = sum_ref.shape[1]
    row = lax.broadcasted_iota(jnp.int32, (rows, 1), 0) + j * rows
    chosen = (row == slot_ref[...]).astype(F32).astype(BF)
    out_ref[0] = (sum_ref[0] + dot_nn(chosen, grad_ref[...])).astype(BF)


def table_add(sums, slots, grads):
    blocks, rows, width = sums.shape
    tokens = grads.shape[0]
    return pl.pallas_call(
        table_add_body,
        out_shape=jax.ShapeDtypeStruct(sums.shape, BF),
        grid=(blocks,),
        in_specs=[
            pl.BlockSpec((1, rows, width), lambda j: (j, 0, 0)),
            pl.BlockSpec((1, tokens), lambda j: (0, 0)),
            pl.BlockSpec((tokens, width), lambda j: (0, 0)),
        ],
        out_specs=pl.BlockSpec((1, rows, width), lambda j: (j, 0, 0)),
        compiler_params=pltpu.CompilerParams(vmem_limit_bytes=48 * MIB),
        cost_estimate=pl.CostEstimate(
            flops=2 * blocks * rows * tokens * width,
            bytes_accessed=6 * blocks * rows * width,
            transcendentals=0,
        ),
        name="table_add",
    )(sums, slots, grads)


def norm_parts(hidden):
    centre = hidden - jnp.mean(hidden, axis=-1, keepdims=True)
    spread = jnp.mean(centre * centre, axis=-1, keepdims=True)
    inverse = lax.rsqrt(spread + 1e-05)
    return centre * inverse, inverse


def norm_back(grad, gain, normed, inverse):
    grad_normed = grad * gain
    first = jnp.mean(grad_normed, axis=-1, keepdims=True)
    second = jnp.mean(grad_normed * normed, axis=-1, keepdims=True)
    return inverse * (grad_normed - first - normed * second)


def noise_field(row_seed, length, channel_count):
    position = lax.iota(jnp.int32, length)[:, None]
    channel = lax.iota(jnp.int32, channel_count)[None, :]
    mixed_once = (row_seed + 7919 * position + 104729 * channel) % 65521
    mixed_twice = (mixed_once * (mixed_once % 32719) + 31 * channel) % 65521
    return (mixed_twice.astype(F32) / 32760.5 - 1.0) * 1.7320508


def paired(
    token_ids,
    segment_ids,
    time_steps,
    row_seeds,
    loss_weights,
    embed_table,
    input_proj,
    attn_gain,
    attn_bias,
    qkv_proj,
    attn_proj,
    mlp_gain,
    mlp_bias,
    up_proj,
    up_bias,
    down_proj,
    output_proj,
):
    z, y, c, x = (lax.axis_index(a) for a in ("z", "y", "c", "x"))
    zn = lax.axis_size("z")
    groups = zn * lax.axis_size("y")
    length = token_ids.shape[1]
    half = length // 2
    block_len, width = embed_table.shape
    ff = up_proj.shape[1]
    rows_here = qkv_proj.shape[0]
    heads = D // HEAD_DIM
    ff_block = down_proj.shape[0] * 2

    meta = jnp.concatenate([token_ids[0], segment_ids[0], time_steps, row_seeds])
    meta_two = ordered(meta, swap(meta, "c"), c, 0)
    weight_c = ordered(loss_weights[0], swap(loss_weights[0], "c"), c, 0)
    weight_two = ordered(weight_c, swap(weight_c, "x"), x, 1).reshape(2, length)
    ids_two = meta_two[:, :length]
    own_meta = pick(meta_two, x, 0)
    segments = own_meta[length : 2 * length]
    weight_row = pick(weight_two, x, 0)
    fraction = own_meta[2 * length].astype(F32) / (TSTEPS - 1)
    noise_level = 0.3 * jnp.exp(fraction * math.log(30.0))
    input_scale = lax.rsqrt(1.0 + noise_level * noise_level)
    residual_scale = 0.5 + fraction
    noise = noise_field(own_meta[2 * length + 1], length, width)

    small_width = 2 * width + 128
    vector = jnp.concatenate([attn_gain, attn_bias, mlp_gain, mlp_bias, up_bias])
    small = jnp.concatenate(
        [
            input_proj.reshape(rows_here, width),
            output_proj,
            jnp.pad(vector.reshape(-1, 128), ((0, rows_here - vector.size // 128), (0, 0))),
        ],
        axis=1,
    )
    qkv_split = qkv_proj.reshape(rows_here, 3 * heads // 2, 2, HEAD_DIM)
    up_split = up_proj.reshape(rows_here, groups, 2, ff_block)

    def packed(core):
        return jnp.concatenate(
            [
                pick(qkv_split, core, 2).reshape(rows_here, -1),
                small,
                pick(up_split, core, 2).reshape(rows_here, -1),
            ],
            axis=1,
        )

    pair = ordered(packed(c), swap(packed(1 - c), "c"), c, 0).reshape(2 * rows_here, -1)
    qkv_cols, small_cols = 3 * D // 2, 3 * D // 2 + small_width
    first_cols = small_cols + D // 2
    first_shard = jnp.concatenate(
        [
            pair[:, :small_cols],
            jnp.concatenate([attn_proj[:, : D // 2], attn_proj[:, D // 2 :]], axis=0),
        ],
        axis=1,
    )
    up_shard = pair[:, small_cols:]

    def places(order, ring):
        block, found = jnp.arange(2 * groups, dtype=jnp.int32), {}
        for axis in order:
            n, here = lax.axis_size(axis), lax.axis_index(axis)
            found[axis] = (block + here) % n if ring else (block % n) ^ here
            block = block // n
        return (found["z"] * 2 + found["y"]) * 2 + found["x"]

    def both_places(ring):
        return jnp.concatenate([places(("z", "y", "x"), ring), places(("z", "x", "y"), ring)])

    def over_one(blocks):
        rows = blocks.shape[1] // 2
        return joined_swap(blocks[:, :rows], "y"), joined_swap(blocks[:, rows:], "x")

    def over_one_start(blocks):
        rows = blocks.shape[1] // 2
        first, second = blocks[:, :rows], blocks[:, rows:]
        return (first, swap(first, "y")), (second, swap(second, "x"))

    def over_other(held):
        return [[held[0], swap(held[0], "x")], [held[1], swap(held[1], "y")]]

    cut = block_len // 32 * 16
    with jax.named_scope("gather_table"):
        table_a = [embed_table[None, :cut]]
        table_a.append(ring_down(table_a[-1], "z"))
        table_b = [joined_swap(embed_table[None, cut:], "y")]
        table_b.append(ring_down(table_b[-1], "z"))
    with jax.named_scope("gather_first"):
        first_z = [first_shard[None]]
        first_z.append(ring_down(first_z[-1], "z"))
    with jax.named_scope("gather_table"):
        for _ in range(2, zn):
            table_a.append(ring_down(table_a[-1], "z"))
    for step in range(2, zn):
        with jax.named_scope("gather_first"):
            first_z.append(ring_down(after(first_z[-1], table_a[step - 1]), "z"))
        with jax.named_scope("gather_table"):
            table_b.append(ring_down(after(table_b[-1], table_a[-1]), "z"))
    with jax.named_scope("gather_table"):
        table_z = table_b[-1]
        table_a = joined_swap(jnp.concatenate(table_a, 0), "y")
        table_b = jnp.stack(table_b, 1).reshape(groups, block_len - cut, width)
    with jax.named_scope("gather_first"):
        first_held = over_one(jnp.concatenate(first_z, 0))
        first_pieces = over_other(first_held)
    with jax.named_scope("gather_up"):
        up_first = after(up_shard[None], table_z, first_z[-1])
        up_moved = apart(up_first, "z", 1)
        up_two = jnp.concatenate([up_first, up_moved], 0)
        up_far = apart(up_two, "z", 2)
    with jax.named_scope("gather_down"):
        down_first = after(down_proj[None], up_far)
        down_moved = apart(down_first, "z", 1)
        down_two = jnp.concatenate([down_first, down_moved], 0)

    flat_ids = ids_two.reshape(-1)
    owner = flat_ids // block_len
    within = flat_ids % block_len
    home = {"z": owner // 8, "y": owner // 4 % 2}
    mine = owner % 4 == c * 2 + x
    table_rows = jnp.concatenate([after(table_a, *first_held, up_moved), table_b], axis=1)
    relative_y, relative_z = (home["y"] - y) % 2, (home["z"] - z) % zn
    slot = (relative_y * zn + relative_z) * block_len + within
    found = jnp.take(
        table_rows.reshape(groups * block_len, width), jnp.where(mine, slot, 0), axis=0
    )
    found = jnp.where(mine[:, None], found, jnp.zeros_like(found)).reshape(2, length, width)

    def to_rows(terms, kind, others):
        split = terms.reshape(2, 2, half, width)
        moved = swap(pick(split, 1 - c, 1).astype(kind), "c")
        both = pick(split, c, 1).astype(F32) + moved.astype(F32)
        both = after(both, *others)
        moved = swap(pick(both, 1 - x, 0).astype(kind), "x")
        own = (pick(both, x, 0).astype(F32) + moved.astype(F32)).astype(kind)
        return ordered(own, swap(own, "c"), c, 0).reshape(length, width)

    def to_pair(row):
        own = pick(row.reshape(2, half, width), c, 0)
        moved = swap(own, "x")
        other = ordered(moved, swap(moved, "c"), c, 0).reshape(length, width)
        return ordered(row, other, x, 0)

    raw = to_rows(found, BF, (first_pieces[0][1], first_pieces[1][1], up_far))
    raw_low = after(raw, down_moved)
    raw = raw_low.astype(F32)
    with jax.named_scope("gather_up"):
        up_z = after(jnp.concatenate([up_two, up_far], 0), first_pieces[0][1], first_pieces[1][1])
        up_moved = over_one_start(up_z)
    paired_shape = (groups, 2, 2, rows_here)

    def in_pairs(p, h):
        return (p // 2, h, p % 2)

    def held_back(pieces, *values):
        return [[after(piece, *values) for piece in half_pieces] for half_pieces in pieces]

    qkv_half, small_full, attn_half = place_blocks(
        both_places(True),
        held_back(first_pieces, found),
        [
            (0, qkv_cols, paired_shape + (qkv_cols,), in_pairs),
            (qkv_cols, small_cols, paired_shape + (small_width,), in_pairs),
            (
                small_cols,
                first_cols,
                (2 * groups, rows_here, D),
                lambda p, h: (p, slice(None), slice(h * D // 2, (h + 1) * D // 2)),
            ),
        ],
    )
    qkv_half, small_full = qkv_half.reshape(D, qkv_cols), small_full.reshape(D, small_width)
    attn_half = attn_half.reshape(D // 2, D)
    input_full = small_full[:, :width].reshape(width, D)
    output_full = small_full[:, width : 2 * width]
    vectors = small_full[:, 2 * width :].reshape(groups, 2, 2, rows_here, 128)
    vectors = vectors[..., : vector.size // 128, :].reshape(groups, 2, 2, vector.size)
    gain_one, bias_one, gain_two, bias_two = (
        vectors[..., k * rows_here : (k + 1) * rows_here].reshape(1, D).astype(F32)
        for k in range(4)
    )
    up_bias_half = pick(vectors[..., 4 * rows_here :], c, 1).reshape(1, ff // 2).astype(F32)
    unit = raw * lax.rsqrt(jnp.mean(raw * raw, axis=1, keepdims=True) + 1e-06)
    target = (unit * width ** (-0.5)).astype(BF)
    inputs = (input_scale * (unit + noise_level * noise)).astype(BF)

    hidden_zero = dot_nn(inputs, input_full)
    normed_one, inverse_one = norm_parts(hidden_zero)
    first_in = (normed_one * gain_one + bias_one).astype(BF)
    first_in = after(first_in, up_moved[0][1], up_moved[1][1])
    with jax.named_scope("gather_up"):
        up_held = [
            jnp.concatenate([own, after(got, first_in)], 0) for own, got in up_moved
        ]
        up_pieces = over_other(up_held)
    with jax.named_scope("gather_down"):
        down_far = apart(after(down_two, raw_low), "z", 2)
    qkv = dot_nn(first_in, qkv_half)
    split = D // 2
    queries = (qkv[:, :split] * HEAD_DIM ** (-0.5)).astype(BF)
    keys = qkv[:, split : 2 * split].astype(BF)
    values = qkv[:, 2 * split :].astype(BF)
    seg_col, seg_row = segments[:, None], segments[None, :]
    blk = min(256, length)
    edges = segments.reshape(length // blk, blk)
    before = jnp.sum(seg_row < edges[:, :1], axis=1, dtype=jnp.int32)
    through = jnp.sum(seg_row <= edges[:, -1:], axis=1, dtype=jnp.int32)
    low_block, high_block = before // blk, (through + blk - 1) // blk
    with jax.named_scope("gather_down"):
        down_z = jnp.concatenate([down_two, down_far], 0)
        down_moved = over_one_start(down_z)
    attended, log_total = attend(
        after(queries, down_z, *up_held), keys, values, seg_col, seg_row, low_block, high_block
    )
    attended = after(
        attended, up_pieces[0][1], up_pieces[1][1], down_moved[0][1], down_moved[1][1]
    )
    with jax.named_scope("gather_down"):
        down_held = [jnp.concatenate([own, after(got, attended)], 0) for own, got in down_moved]
        down_pieces = over_other(down_held)

    def both_cores(part):
        return part + swap(part.astype(BF), "c").astype(F32)

    hidden_one = hidden_zero + residual_scale * both_cores(dot_nn(attended, attn_half))
    normed_two, inverse_two = norm_parts(hidden_one)
    second_in = (normed_two * gain_two + bias_two).astype(BF)
    (up_half,) = place_blocks(
        both_places(False),
        held_back(up_pieces, queries),
        [(0, ff // 2, paired_shape + (ff // 2,), in_pairs)],
    )
    up_half = up_half.reshape(D, ff // 2)
    pre_act = dot_nn(second_in, up_half) + up_bias_half
    below = 0.5 * (1.0 + lax.erf(pre_act * math.sqrt(0.5)))
    activated = (pre_act * below).astype(BF)
    slope = (
        below + pre_act * (jnp.exp(-0.5 * pre_act * pre_act) * (1.0 / math.sqrt(2.0 * math.pi)))
    ).astype(BF)
    (down_half,) = place_blocks(
        both_places(False),
        held_back(down_pieces, activated),
        [
            (
                0,
                D,
                (2 * groups, 2, down_proj.shape[0] // 2, D),
                lambda p, h: (p, h),
            )
        ],
    )
    down_half = down_half.reshape(ff // 2, D)
    hidden_two = hidden_one + residual_scale * both_cores(dot_nn(activated, down_half))
    final_in = hidden_two.astype(BF)
    outputs = dot_nn(final_in, output_full).astype(BF)

    outputs_two = to_pair(outputs).reshape(2 * length, width)
    slots_here = jnp.where(mine, slot, -1)[None, :]
    raised, tops, reached, total = score(outputs_two, table_rows, slots_here)
    ends = jnp.concatenate([tops[-1], total])

    def joined(first, second):
        top = jnp.maximum(first[0], second[0])
        scale_first, scale_second = jnp.exp(first[0] - top), jnp.exp(second[0] - top)
        return jnp.stack([top, first[1] * scale_first + second[1] * scale_second])

    def own_half(value):
        parts = [value[:, k * half : (k + 1) * half] for k in range(4)]
        low, high = jnp.concatenate(parts[::2], 1), jnp.concatenate(parts[1::2], 1)
        return jnp.where(c == 0, low, high), jnp.where(c == 0, high, low)

    def own_row(value):
        first, second = value[:, :half], value[:, half:]
        return jnp.where(x == 0, first, second), jnp.where(x == 0, second, first)

    ends_c = swap(ends, "c")
    kept, sent = own_half(reached)
    moved = swap(sent.astype(BF), "c").astype(F32)
    all_ends = joined(ends, ends_c)
    ends_x = swap(all_ends, "x")
    kept_top, _ = own_half(all_ends[:1])
    both = kept * jnp.exp(own_half(ends[:1])[0] - kept_top) + moved * jnp.exp(
        own_half(ends_c[:1])[0] - kept_top
    )
    kept, sent = own_row(both)
    moved = swap(sent.astype(BF), "x").astype(F32)
    last_ends = joined(all_ends, ends_x)
    log_sum = last_ends[0] + jnp.log(last_ends[1])
    own_log = own_row(own_half(log_sum[None])[0])[0]
    here_top = own_row(own_half(all_ends[:1])[0])[0]
    there_top = own_row(own_half(ends_x[:1])[0])[0]
    own = (kept * jnp.exp(here_top - own_log) + moved * jnp.exp(there_top - own_log)).astype(BF)
    moved = swap(own, "c")
    expected = jnp.concatenate(
        [jnp.where(c == 0, own, moved), jnp.where(c == 0, moved, own)], 1
    ).astype(F32).T
    log_row = pick(log_sum.reshape(2, length), x, 0)
    chosen = jnp.sum(outputs.astype(F32) * target.astype(F32), axis=1)
    loss_row = log_row - chosen
    loss_two = ordered(loss_row, swap(loss_row, "x"), x, 0)
    token_loss = pick(pick(loss_two, c, 0).reshape(2, half), x, 0)[None]

    own_term = weight_row * (jnp.exp(chosen - log_row) - 1.0)
    out_grad = (
        weight_row[:, None] * expected + own_term[:, None] * target.astype(F32)
    ).astype(BF)
    coef = (
        (weight_two.reshape(-1) * width ** (-0.5))[None, :] * jnp.exp(tops[:, 0] - log_sum[None, :])
    ).T

    zy = (zn, lax.axis_size("y"))
    table_cut = block_len * 5 // 128 * 16

    def rows_of(grad):
        rows = grad.shape[0] // (2 * groups)
        return grad.astype(BF).reshape(zy + (2, rows, grad.shape[1]))

    def pairs_of(grad):
        rows = grad.shape[0] // (4 * groups)
        shaped = grad.astype(BF).reshape(zy + (2, 2, rows, grad.shape[1]))
        return shaped[:, :, 0], shaped[:, :, 1]

    output_w_grad = dot_tn(final_in, out_grad)
    hidden_two_grad = dot_nt(out_grad, output_full)
    branch_grad = (residual_scale * hidden_two_grad).astype(BF)
    with jax.named_scope("reduce_down"):
        down_terms = rows_of(dot_tn(activated, branch_grad))
        rows = down_terms.shape[3] // 2
        down_a = halve(down_terms[..., :rows, :], "x", 2)
        down_b = halve(down_terms[..., rows:, :], "y", 1)
    pre_grad = (
        dot_nt(after(branch_grad, down_terms), down_half) * slope.astype(F32)
    ).astype(BF)
    with jax.named_scope("reduce_up"):
        up_terms = dot_tn(second_in, pre_grad).astype(BF)
        up_a, up_b = pairs_of(up_terms)
        up_a, up_b = halve(up_a, "y", 1), halve(up_b, "x", 2)
    up_bias_part = jnp.sum(pre_grad, axis=0, dtype=F32)
    second_part = dot_nt(after(pre_grad, up_terms, down_a[1], down_b[1]), up_half)
    table_sums = table_product(raised, after(outputs_two, second_part), coef)
    second_grad = after(both_cores(second_part), table_sums)
    gain_two_part = jnp.sum(second_grad * normed_two, axis=0)
    bias_two_part = jnp.sum(second_grad, axis=0)
    hidden_one_grad = hidden_two_grad + norm_back(second_grad, gain_two, normed_two, inverse_two)
    attn_grad = after((residual_scale * hidden_one_grad).astype(BF), up_a[1], up_b[1])
    with jax.named_scope("reduce_attn"):
        attn_terms = halve(rows_of(dot_tn(attended, attn_grad)), "y", 1)
    attended_grad = dot_nt(attn_grad, attn_half).astype(BF)
    with jax.named_scope("reduce_down"):
        down_a = added(down_a[0], after(down_a[1], up_terms))
        down_b = added(down_b[0], after(down_b[1], up_terms))
        down_next_a, down_next_b = halve(down_a, "y", 1), halve(down_b, "x", 1)
    with jax.named_scope("reduce_up"):
        up_a = added(up_a[0], after(up_a[1], attn_grad))
        up_b = added(up_b[0], after(up_b[1], attn_grad))
        up_next_a, up_next_b = halve(up_a, "x", 1), halve(up_b, "y", 1)
    query_grad, key_grad, value_grad = attend_back(
        queries,
        keys,
        values,
        attended,
        after(attended_grad, down_a, down_b, up_a, up_b, attn_terms[0]),
        log_total,
        seg_col,
        seg_row,
        low_block,
        high_block,
    )
    query_grad = after(
        query_grad,
        up_next_a[1],
        up_next_b[1],
        down_next_a[1],
        down_next_b[1],
        attn_terms[1],
    )
    with jax.named_scope("reduce_mlp"):
        mlp_sum = jnp.concatenate(
            [
                jnp.concatenate(
                    [
                        added(up_next_a[0], after(up_next_a[1], query_grad)),
                        added(up_next_b[0], after(up_next_b[1], query_grad)),
                    ],
                    1,
                ),
                added(down_next_a[0], after(down_next_a[1], query_grad)),
                added(down_next_b[0], after(down_next_b[1], query_grad)),
            ],
            2,
        )
        mlp_ring = ring_start(mlp_sum, "z")
    with jax.named_scope("reduce_attn"):
        attn_terms = halve(added(attn_terms[0], after(attn_terms[1], query_grad)), "x", 1)
    qkv_grad = jnp.concatenate(
        [query_grad * jnp.asarray(HEAD_DIM ** (-0.5), BF), key_grad, value_grad], axis=1
    )
    with jax.named_scope("reduce_qkv"):
        qkv_terms = dot_tn(first_in, after(qkv_grad, mlp_sum)).astype(BF)
        qkv_a, qkv_b = pairs_of(qkv_terms)
        qkv_a, qkv_b = halve(qkv_a, "y", 1), halve(qkv_b, "x", 2)
    first_grad = both_cores(dot_nt(after(qkv_grad, qkv_terms), qkv_half))
    gain_one_part = jnp.sum(first_grad * normed_one, axis=0)
    bias_one_part = jnp.sum(first_grad, axis=0)
    hidden_zero_grad = (
        hidden_one_grad + norm_back(first_grad, gain_one, normed_one, inverse_one)
    ).astype(BF)
    embed_grad = input_scale * dot_nt(hidden_zero_grad, input_full)
    token_grad = (
        embed_grad + (own_term * width ** (-0.5))[:, None] * outputs.astype(F32)
    ).astype(BF)
    token_own = pick(token_grad.reshape(2, half, width), c, 0)
    with jax.named_scope("token_pair"):
        token_moved = swap(token_own, "x")
    with jax.named_scope("reduce_mlp"):
        mlp_ring = ring_up(ring_next(mlp_sum, after(mlp_ring, token_own), 1, "z").astype(BF), "z")
    with jax.named_scope("token_pair"):
        token_grad_two = jnp.concatenate([token_grad, token_moved, swap(token_moved, "c")], 0)
        slots_two = slots_here.reshape(2, length)
        other_slots = pick(slots_two, 1 - x, 0).reshape(2, half)
        token_slots = jnp.concatenate(
            [pick(slots_two, x, 0), pick(other_slots, c, 0), pick(other_slots, 1 - c, 0)]
        )[None, :]
    with jax.named_scope("reduce_qkv"):
        qkv_a = halve(added(qkv_a[0], after(qkv_a[1], token_moved)), "x", 1)
        qkv_b = halve(added(qkv_b[0], after(qkv_b[1], token_moved)), "y", 1)

    input_w_grad = dot_tn(inputs, hidden_zero_grad)
    input_rows = input_proj.shape[0]
    with jax.named_scope("reduce_small"):
        vector_grad = jnp.concatenate(
            [
                pick(part.reshape(zy + (2, 2, rows_here)), c, 2)
                for part in (gain_one_part, bias_one_part, gain_two_part, bias_two_part)
            ]
            + [up_bias_part.reshape(zy + (2, -1))],
            axis=-1,
        ).reshape(zy + (2, -1, 128))
        small_grad = jnp.concatenate(
            [
                pick(input_w_grad.reshape(zy + (2, 2, input_rows, D)), c, 2).reshape(
                    zy + (2, rows_here, width)
                ),
                pick(output_w_grad.reshape(zy + (2, 2, rows_here, width)), c, 2),
                jnp.pad(
                    vector_grad,
                    ((0, 0),) * 3 + ((0, rows_here - vector_grad.shape[3]), (0, 128)),
                ),
            ],
            axis=-1,
        ).astype(BF)
        small_terms = halve(small_grad, "y", 1)

    with jax.named_scope("reduce_small"):
        small_terms = halve(added(small_terms[0], after(small_terms[1], token_moved)), "x", 1)
    with jax.named_scope("reduce_attn"):
        attn_sum = added(attn_terms[0], after(attn_terms[1], token_moved))
    with jax.named_scope("reduce_mlp"):
        mlp_ring = ring_up(ring_next(mlp_sum, after(mlp_ring, token_moved), 2, "z").astype(BF), "z")
    with jax.named_scope("reduce_rest"):
        rest_sum = jnp.concatenate(
            [
                jnp.concatenate(
                    [
                        added(qkv_a[0], after(qkv_a[1], token_grad_two)),
                        added(qkv_b[0], after(qkv_b[1], token_grad_two)),
                    ],
                    1,
                ),
                added(small_terms[0], after(small_terms[1], token_grad_two))
                .reshape(zn, rows_here, 2, -1)
                .transpose(0, 2, 1, 3)
                .reshape(zn, 2 * rows_here, -1),
                attn_sum.reshape(zn, rows_here, 2, D // 2)
                .transpose(0, 2, 1, 3)
                .reshape(zn, 2 * rows_here, D // 2),
            ],
            2,
        )
        rest_ring = ring_start(rest_sum, "z")
    table_terms = table_add(table_sums, token_slots, after(token_grad_two, rest_sum))
    table_terms = after(table_terms, mlp_ring, rest_ring)
    with jax.named_scope("reduce_table"):
        terms = table_terms.reshape(2, zn, block_len, width)
        terms_a, terms_b = terms[:, :, :table_cut], terms[:, :, table_cut:]
        early = table_cut // 32 * 16
        moved_early = swap(terms_a[1, :, :early], "y")
        moved_late = swap(terms_a[1, :, early:], "y")
        moved_b = ring_up(terms_b[:, zn - 1], "z")
    with jax.named_scope("reduce_rest"):
        rest_own = ring_next(rest_sum, after(rest_ring, table_terms), 1, "z")
        rest_ring = ring_up(rest_own.astype(BF), "z")
    moved_b, rest_ring, moved_early = lax.optimization_barrier((moved_b, rest_ring, moved_early))
    for step in range(1, zn):
        with jax.named_scope("reduce_table"):
            total_b = terms_b[:, zn - 1 - step].astype(F32) + moved_b.astype(F32)
            if step < zn - 1:
                moved_b = ring_up(total_b.astype(BF), "z")
            else:
                moved_b = swap(total_b[1].astype(BF), "y")
        if step < zn - 1:
            with jax.named_scope("reduce_rest"):
                rest_own = ring_next(rest_sum, rest_ring, step + 1, "z")
                if step < zn - 2:
                    rest_ring = ring_up(rest_own.astype(BF), "z")
        if step == zn - 2:
            with jax.named_scope("reduce_table"):
                moved_a = jnp.concatenate([moved_early, moved_late], 1)
                sum_a = added(terms_a[0], after(moved_a, total_b))
                moving_a = ring_up(sum_a[zn - 1], "z")
            moved_b, moving_a = lax.optimization_barrier((moved_b, moving_a))
        elif step < zn - 2:
            moved_b, rest_ring, moved_late = lax.optimization_barrier(
                (moved_b, rest_ring, moved_late)
            )
    with jax.named_scope("reduce_table"):
        for step in range(2, zn):
            total_a = sum_a[zn - step].astype(F32) + moving_a.astype(F32)
            moving_a = ring_up(total_a.astype(BF), "z")
            if step == 2:
                moved_b, moving_a = lax.optimization_barrier((moved_b, moving_a))
        total_b = total_b[0] + moved_b.astype(F32)
        total_a = sum_a[0].astype(F32) + moving_a.astype(F32)
    with jax.named_scope("reduce_mlp"):
        mlp_own = ring_next(mlp_sum, after(mlp_ring, rest_sum), 3, "z")

    up_total = mlp_own[:, : ff // 2].reshape(2, rows_here, ff // 2)
    down_own = jnp.concatenate([mlp_own[:, ff // 2 : ff // 2 + D], mlp_own[:, ff // 2 + D :]], 0)
    qkv_total = rest_own[:, :qkv_cols].reshape(2, rows_here, qkv_cols)
    small_end = rest_own.shape[1] - D // 2
    small_own = rest_own[:, qkv_cols:small_end]
    small_own = jnp.concatenate([small_own[:rows_here], small_own[rows_here:]], 1)
    attn_own = rest_own[:, small_end:]
    attn_own = jnp.concatenate([attn_own[:rows_here], attn_own[rows_here:]], 1)

    unit_grad = jnp.concatenate([total_a, total_b], axis=0)
    own_rows = embed_table.astype(F32)
    inverse = lax.rsqrt(jnp.mean(own_rows * own_rows, axis=1, keepdims=True) + 1e-06)
    along = jnp.mean(own_rows * unit_grad, axis=1, keepdims=True)
    table_grad = inverse * unit_grad - own_rows * (inverse * inverse * inverse * along)

    input_own = small_own[:, :width].reshape(input_rows, D)
    output_own = small_own[:, width : 2 * width]
    vector_own = small_own[: vector.size // 128, 2 * width : 2 * width + 128].reshape(-1)
    gains = [vector_own[k * rows_here : (k + 1) * rows_here] for k in range(4)]

    def columns_back(sums, split_shape, axis):
        mine_rows, other_rows = pick(sums, c, 0), pick(sums, 1 - c, 0)
        other_cols = swap(other_rows, "c")
        return ordered(
            mine_rows.reshape(split_shape), other_cols.reshape(split_shape), c, axis
        ).reshape(rows_here, -1)

    qkv_own = columns_back(qkv_total, (rows_here, 3 * heads // 2, HEAD_DIM), 2)
    up_own = columns_back(up_total, (rows_here, groups, ff_block), 2)
    return (
        token_loss,
        table_grad,
        input_own,
        gains[0],
        gains[1],
        qkv_own,
        attn_own,
        gains[2],
        gains[3],
        up_own,
        vector_own[4 * rows_here :],
        down_own,
        output_own,
    )


def combined_all(shard, axis, combine):
    everything = jax.tree.map(lambda part: lax.all_gather(part, axis), shard)
    first = jax.tree.map(lambda part: part[0], everything)

    def step(k, so_far):
        return combine(so_far, jax.tree.map(lambda part: part[k], everything))

    return lax.fori_loop(1, lax.axis_size(axis), step, first)


def product(left, right):
    return jnp.dot(left, right, preferred_element_type=jnp.float32)


def product_left(left, right):
    return lax.dot_general(
        left, right, (((0,), (0,)), ((), ())), preferred_element_type=jnp.float32
    )


def product_right(left, right):
    return lax.dot_general(
        left, right, (((1,), (1,)), ((), ())), preferred_element_type=jnp.float32
    )


def normalize_rows(matrix):
    return matrix * lax.rsqrt(jnp.mean(matrix * matrix, axis=1, keepdims=True) + 1e-06)


def layer_norm(hidden, norm_gain, norm_bias):
    centre = hidden - jnp.mean(hidden, axis=-1, keepdims=True)
    spread = jnp.mean(centre * centre, axis=-1, keepdims=True)
    return centre * lax.rsqrt(spread + 1e-05) * norm_gain + norm_bias


def exact_gelu(pre_act):
    return jax.nn.gelu(pre_act, approximate=False)


def noise_rows(row_seeds, positions, channel_count):
    channel = lax.iota(jnp.int32, channel_count)
    mixed_once = (
        row_seeds[:, None, None] + 7919 * positions[None, :, None] + 104729 * channel[None, None, :]
    ) % 65521
    mixed_twice = (mixed_once * (mixed_once % 32719) + 31 * channel[None, None, :]) % 65521
    return (mixed_twice.astype(jnp.float32) / 32760.5 - 1.0) * 1.7320508


def time_terms(time_steps):
    fraction = time_steps.astype(jnp.float32) / (TSTEPS - 1)
    noise_level = 0.3 * jnp.exp(fraction * math.log(30.0))
    return (noise_level, lax.rsqrt(1.0 + noise_level * noise_level), 0.5 + fraction)


def masked_scores(query_block, key_rows, segment_block, segment_row):
    scores = jnp.einsum("qhd,khd->hqk", query_block, key_rows, preferred_element_type=jnp.float32)
    same_doc = segment_block[:, None] == segment_row[None, :]
    return jnp.where(same_doc[None], scores, -1e30)


def attend_row(operands):
    queries, key_rows, value_rows, segment_row = operands
    length = queries.shape[0]
    block_rows = math.gcd(length, 512)
    block_count = length // block_rows

    def attend_block(pieces):
        query_block, segment_block = pieces
        scores = masked_scores(query_block, key_rows, segment_block, segment_row)
        row_max = jnp.max(scores, axis=-1, keepdims=True)
        raised = jnp.exp(scores - row_max)
        summed = jnp.sum(raised, axis=-1, keepdims=True)
        probs_low = (raised / summed).astype(jnp.bfloat16)
        attended = jnp.einsum(
            "hqk,khd->qhd", probs_low, value_rows, preferred_element_type=jnp.float32
        )
        return (attended.astype(jnp.bfloat16), (row_max + jnp.log(summed))[..., 0])

    attended, log_total = lax.map(
        attend_block,
        (
            queries.reshape((block_count, block_rows) + queries.shape[1:]),
            segment_row.reshape(block_count, block_rows),
        ),
    )
    return (attended.reshape(queries.shape), log_total)


def attend_back_row(operands):
    queries, key_rows, value_rows, segment_row, grad_rows, log_total = operands
    length = queries.shape[0]
    block_rows = math.gcd(length, 512)
    block_count = length // block_rows

    def back_block(carry, pieces):
        key_sum, value_sum = carry
        query_block, segment_block, grad_block, total_block = pieces
        scores = masked_scores(query_block, key_rows, segment_block, segment_row)
        probs = jnp.exp(scores - total_block[:, :, None])
        prob_grad = jnp.einsum(
            "qhd,khd->hqk", grad_block, value_rows, preferred_element_type=jnp.float32
        )
        score_grad = (
            probs * (prob_grad - jnp.sum(probs * prob_grad, axis=-1, keepdims=True))
        ).astype(jnp.bfloat16)
        query_grad = jnp.einsum(
            "hqk,khd->qhd", score_grad, key_rows, preferred_element_type=jnp.float32
        )
        key_sum = key_sum + jnp.einsum(
            "hqk,qhd->khd", score_grad, query_block, preferred_element_type=jnp.float32
        )
        value_sum = value_sum + jnp.einsum(
            "hqk,qhd->khd",
            probs.astype(jnp.bfloat16),
            grad_block,
            preferred_element_type=jnp.float32,
        )
        return ((key_sum, value_sum), query_grad.astype(jnp.bfloat16))

    block_shape = (block_count, block_rows) + queries.shape[1:]
    start_sums = (jnp.zeros(key_rows.shape, jnp.float32), jnp.zeros(value_rows.shape, jnp.float32))
    (key_sum, value_sum), query_grad = lax.scan(
        back_block,
        start_sums,
        (
            queries.reshape(block_shape),
            segment_row.reshape(block_count, block_rows),
            grad_rows.reshape(block_shape),
            log_total,
        ),
    )
    return (
        query_grad.reshape(queries.shape),
        key_sum.astype(jnp.bfloat16),
        value_sum.astype(jnp.bfloat16),
    )


def join_parts(first, second):
    top = jnp.maximum(first[0], second[0])
    total = first[1] * jnp.exp(first[0] - top) + second[1] * jnp.exp(second[0] - top)
    return (top, total, first[2] + second[2], first[3] + second[3])


def local(
    token_ids,
    segment_ids,
    time_steps,
    row_seeds,
    loss_weights,
    embed_table,
    input_proj,
    attn_gain,
    attn_bias,
    qkv_proj,
    attn_proj,
    mlp_gain,
    mlp_bias,
    up_proj,
    up_bias,
    down_proj,
    output_proj,
):
    seq_count = lax.axis_size("seq")
    seq_place = lax.axis_index("seq")
    dp_count = lax.axis_size("dp")
    row_count, length = token_ids.shape
    local_len = length // seq_count
    tok_count = row_count * local_len
    start_pos = seq_place * local_len
    own_ids = lax.dynamic_slice_in_dim(token_ids, start_pos, local_len, 1)
    positions = start_pos + lax.iota(jnp.int32, local_len)
    gathered = (
        lax.all_gather(embed_table, ("dp", "seq"), axis=0, tiled=True),
        lax.all_gather(input_proj, ("dp", "seq"), axis=0, tiled=True),
        lax.all_gather(attn_gain, ("dp", "seq"), axis=0, tiled=True),
        lax.all_gather(attn_bias, ("dp", "seq"), axis=0, tiled=True),
        lax.all_gather(qkv_proj, ("dp", "seq"), axis=0, tiled=True),
        lax.all_gather(attn_proj, ("dp", "seq"), axis=0, tiled=True),
        lax.all_gather(mlp_gain, ("dp", "seq"), axis=0, tiled=True),
        lax.all_gather(mlp_bias, ("dp", "seq"), axis=0, tiled=True),
        lax.all_gather(up_proj, ("dp", "seq"), axis=0, tiled=True),
        lax.all_gather(up_bias, ("dp", "seq"), axis=0, tiled=True),
        lax.all_gather(down_proj, ("dp", "seq"), axis=0, tiled=True),
        lax.all_gather(output_proj, ("dp", "seq"), axis=0, tiled=True),
    )
    (
        table_full,
        input_full,
        gain_one,
        bias_one,
        qkv_full,
        attn_full,
        gain_two,
        bias_two,
        up_full,
        upbias_full,
        down_full,
        output_full,
    ) = gathered
    vocab_size, embed_width = table_full.shape
    block_len = vocab_size // (dp_count * seq_count)
    unit, unit_back = jax.vjp(normalize_rows, table_full.astype(jnp.float32))
    sub_table = lax.dynamic_slice_in_dim(
        table_full.reshape(dp_count, seq_count, block_len, embed_width), seq_place, 1, 1
    ).reshape(dp_count * block_len, embed_width)
    sub_unit = lax.dynamic_slice_in_dim(
        unit.reshape(dp_count, seq_count, block_len, embed_width), seq_place, 1, 1
    ).reshape(dp_count * block_len, embed_width)
    scaled = (sub_unit * embed_width ** (-0.5)).astype(jnp.bfloat16)
    local_rows = lax.iota(jnp.int32, dp_count * block_len)
    vocab_index = (
        local_rows // block_len * seq_count + seq_place
    ) * block_len + local_rows % block_len
    noise_level, input_scale, residual_scale = time_terms(time_steps)
    noise = noise_rows(row_seeds, positions, embed_width)
    embedded = jnp.take(unit, own_ids, axis=0)
    inputs = (
        (input_scale[:, None, None] * (embedded + noise_level[:, None, None] * noise))
        .astype(jnp.bfloat16)
        .reshape(tok_count, embed_width)
    )
    token_scale = jnp.repeat(residual_scale, local_len)[:, None]
    token_input_scale = jnp.repeat(input_scale, local_len)[:, None]
    hidden_zero = product(inputs, input_full)
    first_norm, first_back = jax.vjp(
        layer_norm, hidden_zero, gain_one.astype(jnp.float32), bias_one.astype(jnp.float32)
    )
    first_in = first_norm.astype(jnp.bfloat16)
    qkv = product(first_in, qkv_full)
    query_tok = (
        (qkv[:, :D] * HEAD_DIM ** (-0.5)).astype(jnp.bfloat16).reshape(row_count, local_len, D)
    )
    key_tok = qkv[:, D : 2 * D].astype(jnp.bfloat16).reshape(row_count, local_len, D)
    value_tok = qkv[:, 2 * D :].astype(jnp.bfloat16).reshape(row_count, local_len, D)
    head_q, head_k, head_v = (
        lax.all_to_all(query_tok, "seq", split_axis=2, concat_axis=1, tiled=True),
        lax.all_to_all(key_tok, "seq", split_axis=2, concat_axis=1, tiled=True),
        lax.all_to_all(value_tok, "seq", split_axis=2, concat_axis=1, tiled=True),
    )
    heads_here = head_q.shape[2] // HEAD_DIM
    head_shape = (row_count, length, heads_here, HEAD_DIM)
    head_q = head_q.reshape(head_shape)
    head_k = head_k.reshape(head_shape)
    head_v = head_v.reshape(head_shape)
    attended, log_total = lax.map(attend_row, (head_q, head_k, head_v, segment_ids))
    attended = attended.reshape(row_count, length, heads_here * HEAD_DIM)
    mixed = lax.all_to_all(attended, "seq", split_axis=1, concat_axis=2, tiled=True).reshape(
        tok_count, D
    )
    hidden_one = hidden_zero + token_scale * product(mixed, attn_full)
    second_norm, second_back = jax.vjp(
        layer_norm, hidden_one, gain_two.astype(jnp.float32), bias_two.astype(jnp.float32)
    )
    second_in = second_norm.astype(jnp.bfloat16)
    pre_act = product(second_in, up_full) + upbias_full.astype(jnp.float32)
    activated, gelu_back = jax.vjp(exact_gelu, pre_act)
    act_low = activated.astype(jnp.bfloat16)
    hidden_two = hidden_one + token_scale * product(act_low, down_full)
    final_in = hidden_two.astype(jnp.bfloat16)
    outputs = product(final_in, output_full).astype(jnp.bfloat16)
    group_tok = seq_count * tok_count
    group_out = lax.all_gather(outputs, "seq", axis=0, tiled=True)
    group_ids = (
        token_ids.reshape(row_count, seq_count, local_len).transpose(1, 0, 2).reshape(group_tok)
    )
    spread = jnp.where(
        lax.iota(jnp.int32, seq_count)[:, None] == seq_place,
        loss_weights.reshape(1, tok_count),
        0.0,
    )
    tile_rows = math.gcd(group_tok, 512)
    tile_count = group_tok // tile_rows
    out_tiles = group_out.reshape(tile_count, tile_rows, embed_width)
    id_tiles = group_ids.reshape(tile_count, tile_rows)

    def part_tile(pieces):
        out_block, target_block = pieces
        logits = product_right(out_block, scaled)
        row_max = jnp.max(logits, axis=1)
        exp_sum = jnp.sum(jnp.exp(logits - row_max[:, None]), axis=1)
        picked = jnp.sum(
            jnp.where(vocab_index[None, :] == target_block[:, None], logits, 0.0), axis=1
        )
        return (row_max, exp_sum, picked)

    part_max, part_sum, part_pick = lax.map(part_tile, (out_tiles, id_tiles))
    top, total, pick, weight_tiles = combined_all(
        (part_max, part_sum, part_pick, spread), "seq", join_parts
    )
    log_tiles = top + jnp.log(total)
    all_loss = log_tiles - pick
    token_loss = lax.dynamic_slice_in_dim(all_loss, seq_place, 1, 0)

    def back_tile(scaled_sum, pieces):
        out_block, target_block, log_block, weight_block = pieces
        logits = product_right(out_block, scaled)
        probs = jnp.exp(logits - log_block[:, None])
        onehot = (vocab_index[None, :] == target_block[:, None]).astype(jnp.float32)
        grad_logits = (weight_block[:, None] * (probs - onehot)).astype(jnp.bfloat16)
        scaled_sum = scaled_sum + product_left(grad_logits, out_block)
        return (scaled_sum, product(grad_logits, scaled))

    scaled_grad, out_terms = lax.scan(
        back_tile,
        jnp.zeros(scaled.shape, jnp.float32),
        (out_tiles, id_tiles, log_tiles, weight_tiles),
    )
    out_terms = out_terms.reshape(tile_count * tile_rows, embed_width)
    out_grad = lax.psum_scatter(out_terms, "seq", scatter_dimension=0, tiled=True).astype(
        jnp.bfloat16
    )
    output_w_grad = product_left(final_in, out_grad)
    hidden_two_grad = product_right(out_grad, output_full)
    branch_grad = (token_scale * hidden_two_grad).astype(jnp.bfloat16)
    down_w_grad = product_left(act_low, branch_grad)
    pre_grad = gelu_back(product_right(branch_grad, down_full))[0].astype(jnp.bfloat16)
    up_w_grad = product_left(second_in, pre_grad)
    upbias_grad = jnp.sum(pre_grad, axis=0, dtype=jnp.float32)
    hidden_one_part, gain_two_grad, bias_two_grad = second_back(product_right(pre_grad, up_full))
    hidden_one_grad = hidden_two_grad + hidden_one_part
    attn_grad = (token_scale * hidden_one_grad).astype(jnp.bfloat16)
    attn_w_grad = product_left(mixed, attn_grad)
    mixed_grad = (
        product_right(attn_grad, attn_full).astype(jnp.bfloat16).reshape(row_count, local_len, D)
    )
    head_grad = lax.all_to_all(mixed_grad, "seq", split_axis=2, concat_axis=1, tiled=True).reshape(
        head_shape
    )
    query_grad, key_grad, value_grad = lax.map(
        attend_back_row, (head_q, head_k, head_v, segment_ids, head_grad, log_total)
    )
    merged_shape = (row_count, length, heads_here * HEAD_DIM)
    query_back, key_back, value_back = (
        lax.all_to_all(
            query_grad.reshape(merged_shape), "seq", split_axis=1, concat_axis=2, tiled=True
        ),
        lax.all_to_all(
            key_grad.reshape(merged_shape), "seq", split_axis=1, concat_axis=2, tiled=True
        ),
        lax.all_to_all(
            value_grad.reshape(merged_shape), "seq", split_axis=1, concat_axis=2, tiled=True
        ),
    )
    qkv_grad = jnp.concatenate(
        [query_back * HEAD_DIM ** (-0.5), key_back, value_back], axis=2
    ).reshape(tok_count, 3 * D)
    qkv_w_grad = product_left(first_in, qkv_grad)
    hidden_zero_part, gain_one_grad, bias_one_grad = first_back(product_right(qkv_grad, qkv_full))
    hidden_zero_grad = (hidden_one_grad + hidden_zero_part).astype(jnp.bfloat16)
    input_w_grad = product_left(inputs, hidden_zero_grad)
    embedded_grad = token_input_scale * product_right(hidden_zero_grad, input_full)
    scaled_part = scaled_grad * embed_width ** (-0.5)
    group_grad = lax.all_gather(
        embedded_grad.astype(jnp.bfloat16), "seq", axis=0, tiled=True
    ).astype(embedded_grad.dtype)
    block_id = group_ids // block_len
    owned = block_id % seq_count == seq_place
    local_slot = jnp.where(
        owned, block_id // seq_count * block_len + group_ids % block_len, scaled.shape[0]
    )
    unit_grad = scaled_part.at[local_slot].add(group_grad, mode="drop")
    table_term = jax.vjp(normalize_rows, sub_table.astype(jnp.float32))[1](unit_grad)[0]
    table_grad = lax.psum_scatter(
        table_term.astype(jnp.bfloat16), "dp", scatter_dimension=0, tiled=True
    ).astype(jnp.float32)
    summed = (
        lax.psum_scatter(input_w_grad, ("dp", "seq"), scatter_dimension=0, tiled=True),
        lax.psum_scatter(gain_one_grad, ("dp", "seq"), scatter_dimension=0, tiled=True),
        lax.psum_scatter(bias_one_grad, ("dp", "seq"), scatter_dimension=0, tiled=True),
        lax.psum_scatter(qkv_w_grad, ("dp", "seq"), scatter_dimension=0, tiled=True),
        lax.psum_scatter(attn_w_grad, ("dp", "seq"), scatter_dimension=0, tiled=True),
        lax.psum_scatter(gain_two_grad, ("dp", "seq"), scatter_dimension=0, tiled=True),
        lax.psum_scatter(bias_two_grad, ("dp", "seq"), scatter_dimension=0, tiled=True),
        lax.psum_scatter(up_w_grad, ("dp", "seq"), scatter_dimension=0, tiled=True),
        lax.psum_scatter(upbias_grad, ("dp", "seq"), scatter_dimension=0, tiled=True),
        lax.psum_scatter(down_w_grad, ("dp", "seq"), scatter_dimension=0, tiled=True),
        lax.psum_scatter(output_w_grad, ("dp", "seq"), scatter_dimension=0, tiled=True),
    )
    return (token_loss.reshape(row_count, local_len), table_grad) + tuple(summed)


def solution(mesh):
    dp, seq = mesh.shape["dp"], mesh.shape["seq"]
    if (dp, seq) == (16, 2):
        inner = Mesh(mesh.devices.reshape(dp // 4, 2, 2, seq), ("z", "y", "c", "x"))
        dp_names, seq_names, body = ("z", "y", "c"), ("x",), paired
    else:
        inner, dp_names, seq_names, body = mesh, ("dp",), ("seq",), local
    every = dp_names + seq_names
    in_specs = (
        P(dp_names, None),
        P(dp_names, None),
        P(dp_names),
        P(dp_names),
        P(dp_names, seq_names),
        P(every, None),
        P(every, None),
        P(every),
        P(every),
        P(every, None),
        P(every, None),
        P(every),
        P(every),
        P(every, None),
        P(every),
        P(every, None),
        P(every, None),
    )
    out_specs = (
        P(dp_names, seq_names),
        P(every, None),
        P(every, None),
        P(every),
        P(every),
        P(every, None),
        P(every, None),
        P(every),
        P(every),
        P(every, None),
        P(every),
        P(every, None),
        P(every, None),
    )
    return jax.shard_map(body, mesh=inner, in_specs=in_specs, out_specs=out_specs, check_vma=False)
```

```python
import math

import jax
import jax.numpy as jnp
from jax import lax
from jax.experimental import pallas as pl
from jax.experimental.pallas import tpu as pltpu
from jax.sharding import Mesh
from jax.sharding import PartitionSpec as P

D = 1024
HEAD_DIM = 64
TSTEPS = 1000
SWAP = ((0, 1), (1, 0))
BF = jnp.bfloat16
F32 = jnp.float32
NEG = -1e30
LIMIT = 70.0
MIB = 1 << 20


def dot_nn(left, right):
    return lax.dot_general(left, right, (((1,), (0,)), ((), ())), preferred_element_type=F32)


def dot_nt(left, right):
    return lax.dot_general(left, right, (((1,), (1,)), ((), ())), preferred_element_type=F32)


def dot_tn(left, right):
    return lax.dot_general(left, right, (((0,), (0,)), ((), ())), preferred_element_type=F32)


def swap(value, axis):
    return lax.ppermute(value, axis, SWAP)


def ring_down(value, axis):
    n = lax.axis_size(axis)
    return lax.ppermute(value, axis, [(i, (i - 1) % n) for i in range(n)])


def ring_up(value, axis):
    n = lax.axis_size(axis)
    return lax.ppermute(value, axis, [(i, (i + 1) % n) for i in range(n)])


def ordered(own, other, place, axis):
    return jnp.where(
        place == 0, jnp.stack([own, other], axis), jnp.stack([other, own], axis)
    )


def pick(value, index, axis):
    return lax.dynamic_index_in_dim(value, index, axis, keepdims=False)


def after(value, *others):
    return lax.optimization_barrier((value,) + others)[0]


def ring_blocks(value, axis):
    parts = [value]
    for _ in range(lax.axis_size(axis) - 1):
        parts.append(ring_down(parts[-1], axis))
    return parts


def joined_swap(held, axis):
    return jnp.concatenate([held, swap(held, axis)], 0)


def apart(value, axis, distance):
    n = lax.axis_size(axis)
    return lax.ppermute(value, axis, [(i, i ^ distance) for i in range(n)])


def joined_apart(value, axis):
    held, distance = value[None], 1
    while distance < lax.axis_size(axis):
        held = jnp.concatenate([held, apart(held, axis, distance)], 0)
        distance *= 2
    return held


def halve(value, axis, at):
    here = lax.axis_index(axis)
    return pick(value, here, at), swap(pick(value, 1 - here, at), axis)


def added(kept, moved):
    return (kept.astype(F32) + moved.astype(F32)).astype(BF)


def ring_start(value, axis):
    n, here = lax.axis_size(axis), lax.axis_index(axis)
    return ring_up(pick(value, (here - 1) % n, 0), axis)


def ring_next(value, moved, step, axis):
    n, here = lax.axis_size(axis), lax.axis_index(axis)
    return pick(value, (here - 1 - step) % n, 0).astype(F32) + moved.astype(F32)


def place_blocks(places, halves, outs):
    flat = halves[0] + halves[1]

    def body(places_ref, *refs):
        ins, results, block = refs[: len(flat)], refs[len(flat) :], 0
        for number, piece in enumerate(ins):
            for k in range(piece.shape[0]):
                p, h = places_ref[block], number // len(halves[0])
                block += 1
                for (low, high, _, index), result in zip(outs, results):
                    result[index(p, h)] = piece[k, :, low:high]

    return pl.pallas_call(
        body,
        out_shape=tuple(jax.ShapeDtypeStruct(shape, BF) for _, _, shape, _ in outs),
        in_specs=[pl.BlockSpec(memory_space=pltpu.SMEM)]
        + [pl.BlockSpec(memory_space=pltpu.VMEM)] * len(flat),
        out_specs=tuple(pl.BlockSpec(memory_space=pltpu.VMEM) for _ in outs),
        compiler_params=pltpu.CompilerParams(vmem_limit_bytes=32 * MIB),
        name="place_blocks",
    )(places, *flat)


def for_each_window(lo, hi, blocks, run):
    for count in range(1, blocks + 1):

        @pl.when(hi - lo == count)
        def _():
            run(lo, count)


def attend_body(
    lo_ref, hi_ref, q_ref, k_ref, v_ref, seg_col_ref, seg_row_ref, o_ref, lse_ref, v_ones
):
    length = q_ref.shape[0]
    blk = min(256, length)
    lane = lax.broadcasted_iota(jnp.int32, (1, 128), 1)
    masks = (lane < HEAD_DIM, lane >= HEAD_DIM)
    v = v_ref[...]
    for h in range(2):
        v_ones[h] = jnp.where(masks[h], v, jnp.ones_like(v))

    def largest(ref):
        rows = ref[...].astype(F32)
        return jnp.max(jnp.sum(rows * rows, axis=1, keepdims=True))

    small = largest(q_ref) * largest(k_ref) <= LIMIT * LIMIT

    def finish(rows, accs):
        totals = [pltpu.roll(acc, HEAD_DIM, axis=1) for acc in accs]
        o_ref[rows, :] = (
            jnp.where(masks[0], accs[0], accs[1]) / jnp.where(masks[0], totals[0], totals[1])
        ).astype(BF)
        return [accs[0].T[HEAD_DIM : HEAD_DIM + 1], accs[1].T[0:1]]

    def each(qi, _):
        rows = pl.ds(pl.multiple_of(qi * blk, blk), blk)
        q = q_ref[rows, :]
        q_heads = [jnp.where(m, q, jnp.zeros_like(q)) for m in masks]

        def run(first, count):
            at = pl.ds(pl.multiple_of(first * blk, blk), count * blk)
            k = k_ref[at, :]
            same = seg_col_ref[rows, :] == seg_row_ref[:, at]
            accs = []
            for h in range(2):
                e = jnp.exp(jnp.where(same, dot_nt(q_heads[h], k), NEG)).astype(BF)
                accs.append(dot_nn(e, v_ones[h, at, :]))
            for h, total in enumerate(finish(rows, accs)):
                lse_ref[0, h : h + 1, rows] = jnp.log(total)

        @pl.when(small)
        def _():
            for_each_window(lo_ref[qi], hi_ref[qi], length // blk, run)

        @pl.when(jnp.logical_not(small))
        def _():
            def scores(kb, h):
                at = pl.ds(pl.multiple_of(kb * blk, blk), blk)
                same = seg_col_ref[at, :] == seg_row_ref[:, rows]
                return jnp.where(same, dot_nt(k_ref[at, :], q_heads[h]), NEG)

            def highest(kb, tops):
                return tuple(
                    jnp.maximum(tops[h], jnp.max(scores(kb, h), axis=0, keepdims=True))
                    for h in range(2)
                )

            tops = lax.fori_loop(
                lo_ref[qi], hi_ref[qi], highest, (jnp.full((1, blk), NEG, F32),) * 2
            )

            def gather(kb, accs):
                at = pl.ds(pl.multiple_of(kb * blk, blk), blk)
                return tuple(
                    accs[h]
                    + dot_tn(jnp.exp(scores(kb, h) - tops[h]).astype(BF), v_ones[h, at, :])
                    for h in range(2)
                )

            accs = lax.fori_loop(
                lo_ref[qi], hi_ref[qi], gather, (jnp.zeros((blk, 128), F32),) * 2
            )
            for h, total in enumerate(finish(rows, accs)):
                lse_ref[0, h : h + 1, rows] = tops[h] + jnp.log(total)

        return 0

    lax.fori_loop(0, length // blk, each, 0)


def attend(q, k, v, seg_col, seg_row, lo, hi):
    length, width = q.shape
    pairs = width // 128
    spec = pl.BlockSpec((length, 128), lambda i, *_: (0, i))
    return pl.pallas_call(
        attend_body,
        out_shape=(
            jax.ShapeDtypeStruct((length, width), BF),
            jax.ShapeDtypeStruct((pairs, 2, length), F32),
        ),
        grid_spec=pltpu.PrefetchScalarGridSpec(
            num_scalar_prefetch=2,
            grid=(pairs,),
            in_specs=[
                spec,
                spec,
                spec,
                pl.BlockSpec((length, 1), lambda i, *_: (0, 0)),
                pl.BlockSpec((1, length), lambda i, *_: (0, 0)),
            ],
            out_specs=(spec, pl.BlockSpec((1, 2, length), lambda i, *_: (i, 0, 0))),
            scratch_shapes=[pltpu.VMEM((2, length, 128), BF)],
        ),
        compiler_params=pltpu.CompilerParams(vmem_limit_bytes=32 * MIB),
        cost_estimate=pl.CostEstimate(
            flops=16 * length * length * width,
            bytes_accessed=8 * length * width,
            transcendentals=length * length * width // HEAD_DIM,
        ),
        name="attend",
    )(lo, hi, q, k, v, seg_col, seg_row)


def attend_back_body(
    lo_ref,
    hi_ref,
    q_ref,
    k_ref,
    v_ref,
    o_ref,
    g_ref,
    lse_ref,
    seg_col_ref,
    seg_row_ref,
    dq_ref,
    dk_ref,
    dv_ref,
    dk_sum,
    dv_sum,
    k_t,
):
    length = q_ref.shape[0]
    blk = min(256, length)
    lane = lax.broadcasted_iota(jnp.int32, (1, 128), 1)
    masks = (lane < HEAD_DIM, lane >= HEAD_DIM)
    dk_sum[...] = jnp.zeros_like(dk_sum)
    dv_sum[...] = jnp.zeros_like(dv_sum)
    k_t[...] = k_ref[...].astype(F32).T.astype(BF)
    def each(qi, _):
        rows = pl.ds(pl.multiple_of(qi * blk, blk), blk)

        def run(first, count):
            q, g = q_ref[rows, :], g_ref[rows, :]
            mixed = (g.astype(F32) * o_ref[rows, :].astype(F32)).T
            at = pl.ds(pl.multiple_of(first * blk, blk), count * blk)
            k, v = k_ref[at, :], v_ref[at, :]
            same = seg_col_ref[at, :] == seg_row_ref[:, rows]
            dq = []
            dk, dv = dk_sum[at, :], dv_sum[at, :]
            for h in range(2):
                q_head = jnp.where(masks[h], q, jnp.zeros_like(q))
                g_head = jnp.where(masks[h], g, jnp.zeros_like(g))
                delta = jnp.sum(mixed[h * HEAD_DIM : (h + 1) * HEAD_DIM], axis=0, keepdims=True)
                s = dot_nt(k, q_head)
                p = jnp.exp(jnp.where(same, s - lse_ref[0, h : h + 1, rows], NEG))
                dp = dot_nt(v, g_head)
                ds = (p * (dp - delta)).astype(BF)
                dv = dv + dot_nn(p.astype(BF), g_head)
                dk = dk + dot_nn(ds, q_head)
                dq.append(dot_nn(k_t[h * HEAD_DIM : (h + 1) * HEAD_DIM, at], ds))
            dk_sum[at, :] = dk
            dv_sum[at, :] = dv
            dq_ref[rows, :] = jnp.concatenate(dq, axis=0).T.astype(BF)

        for_each_window(lo_ref[qi], hi_ref[qi], length // blk, run)
        return 0

    lax.fori_loop(0, length // blk, each, 0)
    dk_ref[...] = dk_sum[...].astype(BF)
    dv_ref[...] = dv_sum[...].astype(BF)


def attend_back(q, k, v, o, g, lse, seg_col, seg_row, lo, hi):
    length, width = q.shape
    pairs = width // 128
    spec = pl.BlockSpec((length, 128), lambda i, *_: (0, i))
    shape = jax.ShapeDtypeStruct((length, width), BF)
    return pl.pallas_call(
        attend_back_body,
        out_shape=(shape, shape, shape),
        grid_spec=pltpu.PrefetchScalarGridSpec(
            num_scalar_prefetch=2,
            grid=(pairs,),
            in_specs=[
                spec,
                spec,
                spec,
                spec,
                spec,
                pl.BlockSpec((1, 2, length), lambda i, *_: (i, 0, 0)),
                pl.BlockSpec((length, 1), lambda i, *_: (0, 0)),
                pl.BlockSpec((1, length), lambda i, *_: (0, 0)),
            ],
            out_specs=(spec, spec, spec),
            scratch_shapes=[
                pltpu.VMEM((length, 128), F32),
                pltpu.VMEM((length, 128), F32),
                pltpu.VMEM((128, length), BF),
            ],
        ),
        compiler_params=pltpu.CompilerParams(vmem_limit_bytes=32 * MIB),
        cost_estimate=pl.CostEstimate(
            flops=32 * length * length * width,
            bytes_accessed=16 * length * width,
            transcendentals=length * length * width // HEAD_DIM,
        ),
        name="attend_back",
    )(lo, hi, q, k, v, o, g, lse, seg_col, seg_row)


def score_body(
    norm_ref, out_ref, table_ref, slot_ref, raised_ref, tops_ref, acc_ref, total_ref, top, fast
):
    j = pl.program_id(0)
    tokens, width = out_ref.shape
    count = table_ref.shape[1]
    rows = table_ref[0].astype(F32)
    unit = rows * lax.rsqrt(jnp.mean(rows * rows, axis=1, keepdims=True) + 1e-06)
    low = unit * width ** (-0.5)
    scaled, scaled_t = low.astype(BF), low.T.astype(BF)
    row = lax.broadcasted_iota(jnp.int32, (count, 1), 0) + j * count

    @pl.when(j == 0)
    def _():
        acc_ref[...] = jnp.zeros_like(acc_ref)
        total_ref[...] = jnp.zeros_like(total_ref)
        some = scaled[: min(count, 128)]
        first = jnp.max(dot_nt(some, out_ref[...]), axis=0, keepdims=True)
        floor = norm_ref[...] - LIMIT
        kept = jnp.max(floor - first) <= LIMIT
        top[...] = jnp.where(kept, jnp.maximum(first, floor), NEG)
        fast[0] = kept.astype(jnp.int32)

    @pl.when(fast[0] == 1)
    def _():
        e = jnp.exp(dot_nt(scaled, out_ref[...]) - top[...])
        total_ref[...] += jnp.sum(e, axis=0, keepdims=True)
        raised_ref[0] = jnp.where(row == slot_ref[...], 0.0, e).astype(BF)
        acc_ref[...] += dot_nn(scaled_t, raised_ref[0])
        tops_ref[0] = top[...]

    @pl.when(fast[0] == 0)
    def _():
        part = math.gcd(tokens, 512)

        def each(n, _):
            at = pl.ds(pl.multiple_of(n * part, part), part)
            logits = dot_nt(scaled, out_ref[at, :])
            new_top = jnp.maximum(top[:, at], jnp.max(logits, axis=0, keepdims=True))
            keep = jnp.exp(top[:, at] - new_top)
            e = jnp.exp(logits - new_top)
            total_ref[:, at] = total_ref[:, at] * keep + jnp.sum(e, axis=0, keepdims=True)
            raised_ref[0, :, at] = jnp.where(row == slot_ref[:, at], 0.0, e).astype(BF)
            acc_ref[:, at] = acc_ref[:, at] * keep + dot_nn(scaled_t, raised_ref[0, :, at])
            tops_ref[0, :, at] = new_top
            top[:, at] = new_top
            return 0

        lax.fori_loop(0, tokens // part, each, 0)


def score(outputs, table, slots):
    tokens, width = outputs.shape
    blocks, rows, _ = table.shape
    squares = jnp.square(outputs.astype(F32))
    norms = 1.01 * jnp.sqrt(dot_nt(jnp.ones((8, width), BF), squares.astype(BF))[:1])
    return pl.pallas_call(
        score_body,
        out_shape=(
            jax.ShapeDtypeStruct((blocks, rows, tokens), BF),
            jax.ShapeDtypeStruct((blocks, 1, tokens), F32),
            jax.ShapeDtypeStruct((width, tokens), F32),
            jax.ShapeDtypeStruct((1, tokens), F32),
        ),
        grid=(blocks,),
        in_specs=[
            pl.BlockSpec((1, tokens), lambda j: (0, 0)),
            pl.BlockSpec((tokens, width), lambda j: (0, 0)),
            pl.BlockSpec((1, rows, width), lambda j: (j, 0, 0)),
            pl.BlockSpec((1, tokens), lambda j: (0, 0)),
        ],
        out_specs=(
            pl.BlockSpec((1, rows, tokens), lambda j: (j, 0, 0)),
            pl.BlockSpec((1, 1, tokens), lambda j: (j, 0, 0)),
            pl.BlockSpec((width, tokens), lambda j: (0, 0)),
            pl.BlockSpec((1, tokens), lambda j: (0, 0)),
        ),
        scratch_shapes=[pltpu.VMEM((1, tokens), F32), pltpu.SMEM((1,), jnp.int32)],
        compiler_params=pltpu.CompilerParams(vmem_limit_bytes=48 * MIB),
        cost_estimate=pl.CostEstimate(
            flops=4 * blocks * rows * tokens * width,
            bytes_accessed=2 * blocks * rows * tokens,
            transcendentals=blocks * rows * tokens,
        ),
        name="score",
    )(norms, outputs, table, slots)


def table_product_body(raised_ref, out_ref, coef_ref, sum_ref):
    j = pl.program_id(0)
    lane = lax.broadcasted_iota(jnp.int32, coef_ref.shape, 1)
    coef = jnp.sum(jnp.where(lane == j, coef_ref[...], 0.0), axis=1, keepdims=True)
    weighted = (out_ref[...].astype(F32) * coef).astype(BF)
    sum_ref[0] = dot_nn(raised_ref[0], weighted)


def table_product(raised, outputs, coef):
    blocks, rows, tokens = raised.shape
    width = outputs.shape[1]
    return pl.pallas_call(
        table_product_body,
        out_shape=jax.ShapeDtypeStruct((blocks, rows, width), F32),
        grid=(blocks,),
        in_specs=[
            pl.BlockSpec((1, rows, tokens), lambda j: (j, 0, 0)),
            pl.BlockSpec((tokens, width), lambda j: (0, 0)),
            pl.BlockSpec((tokens, blocks), lambda j: (0, 0)),
        ],
        out_specs=pl.BlockSpec((1, rows, width), lambda j: (j, 0, 0)),
        compiler_params=pltpu.CompilerParams(vmem_limit_bytes=48 * MIB),
        cost_estimate=pl.CostEstimate(
            flops=2 * blocks * rows * tokens * width,
            bytes_accessed=2 * blocks * rows * tokens,
            transcendentals=0,
        ),
        name="table_product",
    )(raised, outputs, coef)


def table_add_body(sum_ref, slot_ref, grad_ref, out_ref):
    j = pl.program_id(0)
    rows = sum_ref.shape[1]
    row = lax.broadcasted_iota(jnp.int32, (rows, 1), 0) + j * rows
    chosen = (row == slot_ref[...]).astype(F32).astype(BF)
    out_ref[0] = (sum_ref[0] + dot_nn(chosen, grad_ref[...])).astype(BF)


def table_add(sums, slots, grads):
    blocks, rows, width = sums.shape
    tokens = grads.shape[0]
    return pl.pallas_call(
        table_add_body,
        out_shape=jax.ShapeDtypeStruct(sums.shape, BF),
        grid=(blocks,),
        in_specs=[
            pl.BlockSpec((1, rows, width), lambda j: (j, 0, 0)),
            pl.BlockSpec((1, tokens), lambda j: (0, 0)),
            pl.BlockSpec((tokens, width), lambda j: (0, 0)),
        ],
        out_specs=pl.BlockSpec((1, rows, width), lambda j: (j, 0, 0)),
        compiler_params=pltpu.CompilerParams(vmem_limit_bytes=48 * MIB),
        cost_estimate=pl.CostEstimate(
            flops=2 * blocks * rows * tokens * width,
            bytes_accessed=6 * blocks * rows * width,
            transcendentals=0,
        ),
        name="table_add",
    )(sums, slots, grads)


def norm_parts(hidden):
    centre = hidden - jnp.mean(hidden, axis=-1, keepdims=True)
    spread = jnp.mean(centre * centre, axis=-1, keepdims=True)
    inverse = lax.rsqrt(spread + 1e-05)
    return centre * inverse, inverse


def norm_back(grad, gain, normed, inverse):
    grad_normed = grad * gain
    first = jnp.mean(grad_normed, axis=-1, keepdims=True)
    second = jnp.mean(grad_normed * normed, axis=-1, keepdims=True)
    return inverse * (grad_normed - first - normed * second)


def noise_field(row_seed, length, channel_count):
    position = lax.iota(jnp.int32, length)[:, None]
    channel = lax.iota(jnp.int32, channel_count)[None, :]
    mixed_once = (row_seed + 7919 * position + 104729 * channel) % 65521
    mixed_twice = (mixed_once * (mixed_once % 32719) + 31 * channel) % 65521
    return (mixed_twice.astype(F32) / 32760.5 - 1.0) * 1.7320508


def paired(
    token_ids,
    segment_ids,
    time_steps,
    row_seeds,
    loss_weights,
    embed_table,
    input_proj,
    attn_gain,
    attn_bias,
    qkv_proj,
    attn_proj,
    mlp_gain,
    mlp_bias,
    up_proj,
    up_bias,
    down_proj,
    output_proj,
):
    z, y, c, x = (lax.axis_index(a) for a in ("z", "y", "c", "x"))
    zn = lax.axis_size("z")
    groups = zn * lax.axis_size("y")
    length = token_ids.shape[1]
    half = length // 2
    block_len, width = embed_table.shape
    ff = up_proj.shape[1]
    rows_here = qkv_proj.shape[0]
    heads = D // HEAD_DIM
    ff_block = down_proj.shape[0] * 2

    meta = jnp.concatenate([token_ids[0], segment_ids[0], time_steps, row_seeds])
    meta_two = ordered(meta, swap(meta, "c"), c, 0)
    weight_c = ordered(loss_weights[0], swap(loss_weights[0], "c"), c, 0)
    weight_two = ordered(weight_c, swap(weight_c, "x"), x, 1).reshape(2, length)
    ids_two = meta_two[:, :length]
    own_meta = pick(meta_two, x, 0)
    segments = own_meta[length : 2 * length]
    weight_row = pick(weight_two, x, 0)
    fraction = own_meta[2 * length].astype(F32) / (TSTEPS - 1)
    noise_level = 0.3 * jnp.exp(fraction * math.log(30.0))
    input_scale = lax.rsqrt(1.0 + noise_level * noise_level)
    residual_scale = 0.5 + fraction
    noise = noise_field(own_meta[2 * length + 1], length, width)

    small_width = 2 * width + 128
    vector = jnp.concatenate([attn_gain, attn_bias, mlp_gain, mlp_bias, up_bias])
    small = jnp.concatenate(
        [
            input_proj.reshape(rows_here, width),
            output_proj,
            jnp.pad(vector.reshape(-1, 128), ((0, rows_here - vector.size // 128), (0, 0))),
        ],
        axis=1,
    )
    qkv_split = qkv_proj.reshape(rows_here, 3 * heads // 2, 2, HEAD_DIM)
    up_split = up_proj.reshape(rows_here, groups, 2, ff_block)

    def packed(core):
        return jnp.concatenate(
            [
                pick(qkv_split, core, 2).reshape(rows_here, -1),
                small,
                pick(up_split, core, 2).reshape(rows_here, -1),
            ],
            axis=1,
        )

    pair = ordered(packed(c), swap(packed(1 - c), "c"), c, 0).reshape(2 * rows_here, -1)
    qkv_cols, small_cols = 3 * D // 2, 3 * D // 2 + small_width
    first_cols = small_cols + D // 2
    first_shard = jnp.concatenate(
        [
            pair[:, :small_cols],
            jnp.concatenate([attn_proj[:, : D // 2], attn_proj[:, D // 2 :]], axis=0),
        ],
        axis=1,
    )
    up_shard = pair[:, small_cols:]

    def places(order, ring):
        block, found = jnp.arange(2 * groups, dtype=jnp.int32), {}
        for axis in order:
            n, here = lax.axis_size(axis), lax.axis_index(axis)
            found[axis] = (block + here) % n if ring else (block % n) ^ here
            block = block // n
        return (found["z"] * 2 + found["y"]) * 2 + found["x"]

    def both_places(ring):
        return jnp.concatenate([places(("z", "y", "x"), ring), places(("z", "x", "y"), ring)])

    def over_one(blocks):
        rows = blocks.shape[1] // 2
        return joined_swap(blocks[:, :rows], "y"), joined_swap(blocks[:, rows:], "x")

    def over_one_start(blocks):
        rows = blocks.shape[1] // 2
        first, second = blocks[:, :rows], blocks[:, rows:]
        return (first, swap(first, "y")), (second, swap(second, "x"))

    def over_other(held):
        return [[held[0], swap(held[0], "x")], [held[1], swap(held[1], "y")]]

    cut = block_len // 32 * 16
    with jax.named_scope("gather_table"):
        table_a = [embed_table[None, :cut]]
        table_a.append(ring_down(table_a[-1], "z"))
        table_b = [joined_swap(embed_table[None, cut:], "y")]
        table_b.append(ring_down(table_b[-1], "z"))
    with jax.named_scope("gather_first"):
        first_z = [first_shard[None]]
        first_z.append(ring_down(first_z[-1], "z"))
    with jax.named_scope("gather_table"):
        for _ in range(2, zn):
            table_a.append(ring_down(table_a[-1], "z"))
    for step in range(2, zn):
        with jax.named_scope("gather_first"):
            first_z.append(ring_down(after(first_z[-1], table_a[step - 1]), "z"))
        with jax.named_scope("gather_table"):
            table_b.append(ring_down(after(table_b[-1], table_a[-1]), "z"))
    with jax.named_scope("gather_table"):
        table_z = table_b[-1]
        table_a = joined_swap(jnp.concatenate(table_a, 0), "y")
        table_b = jnp.stack(table_b, 1).reshape(groups, block_len - cut, width)
    with jax.named_scope("gather_first"):
        first_held = over_one(jnp.concatenate(first_z, 0))
        first_pieces = over_other(first_held)
    with jax.named_scope("gather_up"):
        up_first = after(up_shard[None], table_z, first_z[-1])
        up_moved = apart(up_first, "z", 1)
        up_two = jnp.concatenate([up_first, up_moved], 0)
        up_far = apart(up_two, "z", 2)
    with jax.named_scope("gather_down"):
        down_first = after(down_proj[None], up_far)
        down_moved = apart(down_first, "z", 1)
        down_two = jnp.concatenate([down_first, down_moved], 0)

    flat_ids = ids_two.reshape(-1)
    owner = flat_ids // block_len
    within = flat_ids % block_len
    home = {"z": owner // 8, "y": owner // 4 % 2}
    mine = owner % 4 == c * 2 + x
    table_rows = jnp.concatenate([after(table_a, *first_held, up_moved), table_b], axis=1)
    relative_y, relative_z = (home["y"] - y) % 2, (home["z"] - z) % zn
    slot = (relative_y * zn + relative_z) * block_len + within
    found = jnp.take(
        table_rows.reshape(groups * block_len, width), jnp.where(mine, slot, 0), axis=0
    )
    found = jnp.where(mine[:, None], found, jnp.zeros_like(found)).reshape(2, length, width)

    def to_rows(terms, kind, others):
        split = terms.reshape(2, 2, half, width)
        moved = swap(pick(split, 1 - c, 1).astype(kind), "c")
        both = pick(split, c, 1).astype(F32) + moved.astype(F32)
        both = after(both, *others)
        moved = swap(pick(both, 1 - x, 0).astype(kind), "x")
        own = (pick(both, x, 0).astype(F32) + moved.astype(F32)).astype(kind)
        return ordered(own, swap(own, "c"), c, 0).reshape(length, width)

    def to_pair(row):
        own = pick(row.reshape(2, half, width), c, 0)
        moved = swap(own, "x")
        other = ordered(moved, swap(moved, "c"), c, 0).reshape(length, width)
        return ordered(row, other, x, 0)

    raw = to_rows(found, BF, (first_pieces[0][1], first_pieces[1][1], up_far))
    raw_low = after(raw, down_moved)
    raw = raw_low.astype(F32)
    with jax.named_scope("gather_up"):
        up_z = after(jnp.concatenate([up_two, up_far], 0), first_pieces[0][1], first_pieces[1][1])
        up_moved = over_one_start(up_z)
    paired_shape = (groups, 2, 2, rows_here)

    def in_pairs(p, h):
        return (p // 2, h, p % 2)

    def held_back(pieces, *values):
        return [[after(piece, *values) for piece in half_pieces] for half_pieces in pieces]

    qkv_half, small_full, attn_half = place_blocks(
        both_places(True),
        held_back(first_pieces, found),
        [
            (0, qkv_cols, paired_shape + (qkv_cols,), in_pairs),
            (qkv_cols, small_cols, paired_shape + (small_width,), in_pairs),
            (
                small_cols,
                first_cols,
                (2 * groups, rows_here, D),
                lambda p, h: (p, slice(None), slice(h * D // 2, (h + 1) * D // 2)),
            ),
        ],
    )
    qkv_half, small_full = qkv_half.reshape(D, qkv_cols), small_full.reshape(D, small_width)
    attn_half = attn_half.reshape(D // 2, D)
    input_full = small_full[:, :width].reshape(width, D)
    output_full = small_full[:, width : 2 * width]
    vectors = small_full[:, 2 * width :].reshape(groups, 2, 2, rows_here, 128)
    vectors = vectors[..., : vector.size // 128, :].reshape(groups, 2, 2, vector.size)
    gain_one, bias_one, gain_two, bias_two = (
        vectors[..., k * rows_here : (k + 1) * rows_here].reshape(1, D).astype(F32)
        for k in range(4)
    )
    up_bias_half = pick(vectors[..., 4 * rows_here :], c, 1).reshape(1, ff // 2).astype(F32)
    unit = raw * lax.rsqrt(jnp.mean(raw * raw, axis=1, keepdims=True) + 1e-06)
    target = (unit * width ** (-0.5)).astype(BF)
    inputs = (input_scale * (unit + noise_level * noise)).astype(BF)

    hidden_zero = dot_nn(inputs, input_full)
    normed_one, inverse_one = norm_parts(hidden_zero)
    first_in = (normed_one * gain_one + bias_one).astype(BF)
    first_in = after(first_in, up_moved[0][1], up_moved[1][1])
    with jax.named_scope("gather_up"):
        up_held = [
            jnp.concatenate([own, after(got, first_in)], 0) for own, got in up_moved
        ]
        up_pieces = over_other(up_held)
    with jax.named_scope("gather_down"):
        down_far = apart(after(down_two, raw_low), "z", 2)
    qkv = dot_nn(first_in, qkv_half)
    split = D // 2
    queries = (qkv[:, :split] * HEAD_DIM ** (-0.5)).astype(BF)
    keys = qkv[:, split : 2 * split].astype(BF)
    values = qkv[:, 2 * split :].astype(BF)
    seg_col, seg_row = segments[:, None], segments[None, :]
    blk = min(256, length)
    edges = segments.reshape(length // blk, blk)
    before = jnp.sum(seg_row < edges[:, :1], axis=1, dtype=jnp.int32)
    through = jnp.sum(seg_row <= edges[:, -1:], axis=1, dtype=jnp.int32)
    low_block, high_block = before // blk, (through + blk - 1) // blk
    with jax.named_scope("gather_down"):
        down_z = jnp.concatenate([down_two, down_far], 0)
        down_moved = over_one_start(down_z)
    attended, log_total = attend(
        after(queries, down_z, *up_held), keys, values, seg_col, seg_row, low_block, high_block
    )
    attended = after(
        attended, up_pieces[0][1], up_pieces[1][1], down_moved[0][1], down_moved[1][1]
    )
    with jax.named_scope("gather_down"):
        down_held = [jnp.concatenate([own, after(got, attended)], 0) for own, got in down_moved]
        down_pieces = over_other(down_held)

    def both_cores(part):
        return part + swap(part.astype(BF), "c").astype(F32)

    hidden_one = hidden_zero + residual_scale * both_cores(dot_nn(attended, attn_half))
    normed_two, inverse_two = norm_parts(hidden_one)
    second_in = (normed_two * gain_two + bias_two).astype(BF)
    (up_half,) = place_blocks(
        both_places(False),
        held_back(up_pieces, queries),
        [(0, ff // 2, paired_shape + (ff // 2,), in_pairs)],
    )
    up_half = up_half.reshape(D, ff // 2)
    pre_act = dot_nn(second_in, up_half) + up_bias_half
    below = 0.5 * (1.0 + lax.erf(pre_act * math.sqrt(0.5)))
    activated = (pre_act * below).astype(BF)
    slope = (
        below + pre_act * (jnp.exp(-0.5 * pre_act * pre_act) * (1.0 / math.sqrt(2.0 * math.pi)))
    ).astype(BF)
    (down_half,) = place_blocks(
        both_places(False),
        held_back(down_pieces, activated),
        [
            (
                0,
                D,
                (2 * groups, 2, down_proj.shape[0] // 2, D),
                lambda p, h: (p, h),
            )
        ],
    )
    down_half = down_half.reshape(ff // 2, D)
    hidden_two = hidden_one + residual_scale * both_cores(dot_nn(activated, down_half))
    final_in = hidden_two.astype(BF)
    outputs = dot_nn(final_in, output_full).astype(BF)

    outputs_two = to_pair(outputs).reshape(2 * length, width)
    slots_here = jnp.where(mine, slot, -1)[None, :]
    raised, tops, reached, total = score(outputs_two, table_rows, slots_here)
    ends = jnp.concatenate([tops[-1], total])

    def joined(first, second):
        top = jnp.maximum(first[0], second[0])
        scale_first, scale_second = jnp.exp(first[0] - top), jnp.exp(second[0] - top)
        return jnp.stack([top, first[1] * scale_first + second[1] * scale_second])

    def own_half(value):
        parts = [value[:, k * half : (k + 1) * half] for k in range(4)]
        low, high = jnp.concatenate(parts[::2], 1), jnp.concatenate(parts[1::2], 1)
        return jnp.where(c == 0, low, high), jnp.where(c == 0, high, low)

    def own_row(value):
        first, second = value[:, :half], value[:, half:]
        return jnp.where(x == 0, first, second), jnp.where(x == 0, second, first)

    ends_c = swap(ends, "c")
    kept, sent = own_half(reached)
    moved = swap(sent.astype(BF), "c").astype(F32)
    all_ends = joined(ends, ends_c)
    ends_x = swap(all_ends, "x")
    kept_top, _ = own_half(all_ends[:1])
    both = kept * jnp.exp(own_half(ends[:1])[0] - kept_top) + moved * jnp.exp(
        own_half(ends_c[:1])[0] - kept_top
    )
    kept, sent = own_row(both)
    moved = swap(sent.astype(BF), "x").astype(F32)
    last_ends = joined(all_ends, ends_x)
    log_sum = last_ends[0] + jnp.log(last_ends[1])
    own_log = own_row(own_half(log_sum[None])[0])[0]
    here_top = own_row(own_half(all_ends[:1])[0])[0]
    there_top = own_row(own_half(ends_x[:1])[0])[0]
    own = (kept * jnp.exp(here_top - own_log) + moved * jnp.exp(there_top - own_log)).astype(BF)
    moved = swap(own, "c")
    expected = jnp.concatenate(
        [jnp.where(c == 0, own, moved), jnp.where(c == 0, moved, own)], 1
    ).astype(F32).T
    log_row = pick(log_sum.reshape(2, length), x, 0)
    chosen = jnp.sum(outputs.astype(F32) * target.astype(F32), axis=1)
    loss_row = log_row - chosen
    loss_two = ordered(loss_row, swap(loss_row, "x"), x, 0)
    token_loss = pick(pick(loss_two, c, 0).reshape(2, half), x, 0)[None]

    own_term = weight_row * (jnp.exp(chosen - log_row) - 1.0)
    out_grad = (
        weight_row[:, None] * expected + own_term[:, None] * target.astype(F32)
    ).astype(BF)
    coef = (
        (weight_two.reshape(-1) * width ** (-0.5))[None, :] * jnp.exp(tops[:, 0] - log_sum[None, :])
    ).T

    zy = (zn, lax.axis_size("y"))
    table_cut = block_len * 9 // 256 * 16

    def rows_of(grad):
        rows = grad.shape[0] // (2 * groups)
        return grad.astype(BF).reshape(zy + (2, rows, grad.shape[1]))

    def pairs_of(grad):
        rows = grad.shape[0] // (4 * groups)
        shaped = grad.astype(BF).reshape(zy + (2, 2, rows, grad.shape[1]))
        return shaped[:, :, 0], shaped[:, :, 1]

    output_w_grad = dot_tn(final_in, out_grad)
    hidden_two_grad = dot_nt(out_grad, output_full)
    branch_grad = (residual_scale * hidden_two_grad).astype(BF)
    with jax.named_scope("reduce_down"):
        down_terms = rows_of(dot_tn(activated, branch_grad))
        rows = down_terms.shape[3] // 2
        down_a = halve(down_terms[..., :rows, :], "x", 2)
        down_b = halve(down_terms[..., rows:, :], "y", 1)
    pre_grad = (
        dot_nt(after(branch_grad, down_terms), down_half) * slope.astype(F32)
    ).astype(BF)
    with jax.named_scope("reduce_up"):
        up_terms = dot_tn(second_in, pre_grad).astype(BF)
        up_a, up_b = pairs_of(up_terms)
        up_a, up_b = halve(up_a, "y", 1), halve(up_b, "x", 2)
    up_bias_part = jnp.sum(pre_grad, axis=0, dtype=F32)
    second_part = dot_nt(after(pre_grad, up_terms, down_a[1], down_b[1]), up_half)
    table_sums = table_product(raised, after(outputs_two, second_part), coef)
    second_grad = after(both_cores(second_part), table_sums)
    gain_two_part = jnp.sum(second_grad * normed_two, axis=0)
    bias_two_part = jnp.sum(second_grad, axis=0)
    hidden_one_grad = hidden_two_grad + norm_back(second_grad, gain_two, normed_two, inverse_two)
    attn_grad = after((residual_scale * hidden_one_grad).astype(BF), up_a[1], up_b[1])
    with jax.named_scope("reduce_attn"):
        attn_terms = halve(rows_of(dot_tn(attended, attn_grad)), "y", 1)
    attended_grad = dot_nt(attn_grad, attn_half).astype(BF)
    with jax.named_scope("reduce_down"):
        down_a = added(down_a[0], after(down_a[1], up_terms))
        down_b = added(down_b[0], after(down_b[1], up_terms))
        down_next_a, down_next_b = halve(down_a, "y", 1), halve(down_b, "x", 1)
    with jax.named_scope("reduce_up"):
        up_a = added(up_a[0], after(up_a[1], attn_grad))
        up_b = added(up_b[0], after(up_b[1], attn_grad))
        up_next_a, up_next_b = halve(up_a, "x", 1), halve(up_b, "y", 1)
    query_grad, key_grad, value_grad = attend_back(
        queries,
        keys,
        values,
        attended,
        after(attended_grad, down_a, down_b, up_a, up_b, attn_terms[0]),
        log_total,
        seg_col,
        seg_row,
        low_block,
        high_block,
    )
    query_grad = after(
        query_grad,
        up_next_a[1],
        up_next_b[1],
        down_next_a[1],
        down_next_b[1],
        attn_terms[1],
    )
    with jax.named_scope("reduce_mlp"):
        mlp_sum = jnp.concatenate(
            [
                jnp.concatenate(
                    [
                        added(up_next_a[0], after(up_next_a[1], query_grad)),
                        added(up_next_b[0], after(up_next_b[1], query_grad)),
                    ],
                    1,
                ),
                added(down_next_a[0], after(down_next_a[1], query_grad)),
                added(down_next_b[0], after(down_next_b[1], query_grad)),
            ],
            2,
        )
        mlp_ring = ring_start(mlp_sum, "z")
    with jax.named_scope("reduce_attn"):
        attn_terms = halve(added(attn_terms[0], after(attn_terms[1], query_grad)), "x", 1)
    qkv_grad = jnp.concatenate(
        [query_grad * jnp.asarray(HEAD_DIM ** (-0.5), BF), key_grad, value_grad], axis=1
    )
    with jax.named_scope("reduce_qkv"):
        qkv_terms = dot_tn(first_in, after(qkv_grad, mlp_sum)).astype(BF)
        qkv_a, qkv_b = pairs_of(qkv_terms)
        qkv_a, qkv_b = halve(qkv_a, "y", 1), halve(qkv_b, "x", 2)
    first_grad = both_cores(dot_nt(after(qkv_grad, qkv_terms), qkv_half))
    gain_one_part = jnp.sum(first_grad * normed_one, axis=0)
    bias_one_part = jnp.sum(first_grad, axis=0)
    hidden_zero_grad = (
        hidden_one_grad + norm_back(first_grad, gain_one, normed_one, inverse_one)
    ).astype(BF)
    embed_grad = input_scale * dot_nt(hidden_zero_grad, input_full)
    token_grad = (
        embed_grad + (own_term * width ** (-0.5))[:, None] * outputs.astype(F32)
    ).astype(BF)
    token_own = pick(token_grad.reshape(2, half, width), c, 0)
    with jax.named_scope("token_pair"):
        token_moved = swap(token_own, "x")
    with jax.named_scope("reduce_mlp"):
        mlp_ring = ring_up(ring_next(mlp_sum, after(mlp_ring, token_own), 1, "z").astype(BF), "z")
    with jax.named_scope("token_pair"):
        token_grad_two = jnp.concatenate([token_grad, token_moved, swap(token_moved, "c")], 0)
        slots_two = slots_here.reshape(2, length)
        other_slots = pick(slots_two, 1 - x, 0).reshape(2, half)
        token_slots = jnp.concatenate(
            [pick(slots_two, x, 0), pick(other_slots, c, 0), pick(other_slots, 1 - c, 0)]
        )[None, :]
    with jax.named_scope("reduce_qkv"):
        qkv_a = halve(added(qkv_a[0], after(qkv_a[1], token_moved)), "x", 1)
        qkv_b = halve(added(qkv_b[0], after(qkv_b[1], token_moved)), "y", 1)

    input_w_grad = dot_tn(inputs, hidden_zero_grad)
    input_rows = input_proj.shape[0]
    with jax.named_scope("reduce_small"):
        vector_grad = jnp.concatenate(
            [
                pick(part.reshape(zy + (2, 2, rows_here)), c, 2)
                for part in (gain_one_part, bias_one_part, gain_two_part, bias_two_part)
            ]
            + [up_bias_part.reshape(zy + (2, -1))],
            axis=-1,
        ).reshape(zy + (2, -1, 128))
        small_grad = jnp.concatenate(
            [
                pick(input_w_grad.reshape(zy + (2, 2, input_rows, D)), c, 2).reshape(
                    zy + (2, rows_here, width)
                ),
                pick(output_w_grad.reshape(zy + (2, 2, rows_here, width)), c, 2),
                jnp.pad(
                    vector_grad,
                    ((0, 0),) * 3 + ((0, rows_here - vector_grad.shape[3]), (0, 128)),
                ),
            ],
            axis=-1,
        ).astype(BF)
        small_terms = halve(small_grad, "y", 1)

    with jax.named_scope("reduce_small"):
        small_terms = halve(added(small_terms[0], after(small_terms[1], token_moved)), "x", 1)
    with jax.named_scope("reduce_attn"):
        attn_sum = added(attn_terms[0], after(attn_terms[1], token_moved))
    with jax.named_scope("reduce_mlp"):
        mlp_ring = ring_up(ring_next(mlp_sum, after(mlp_ring, token_moved), 2, "z").astype(BF), "z")
    with jax.named_scope("reduce_rest"):
        rest_sum = jnp.concatenate(
            [
                jnp.concatenate(
                    [
                        added(qkv_a[0], after(qkv_a[1], token_grad_two)),
                        added(qkv_b[0], after(qkv_b[1], token_grad_two)),
                    ],
                    1,
                ),
                added(small_terms[0], after(small_terms[1], token_grad_two))
                .reshape(zn, rows_here, 2, -1)
                .transpose(0, 2, 1, 3)
                .reshape(zn, 2 * rows_here, -1),
                attn_sum.reshape(zn, rows_here, 2, D // 2)
                .transpose(0, 2, 1, 3)
                .reshape(zn, 2 * rows_here, D // 2),
            ],
            2,
        )
        rest_ring = ring_start(rest_sum, "z")
    table_terms = table_add(table_sums, token_slots, after(token_grad_two, rest_sum))
    table_terms = after(table_terms, mlp_ring, rest_ring)
    with jax.named_scope("reduce_table"):
        terms = table_terms.reshape(2, zn, block_len, width)
        terms_a, terms_b = terms[:, :, :table_cut], terms[:, :, table_cut:]
        early = table_cut // 32 * 16
        moved_early = swap(terms_a[1, :, :early], "y")
        moved_late = swap(terms_a[1, :, early:], "y")
        moved_b = ring_up(terms_b[:, zn - 1], "z")
    with jax.named_scope("reduce_rest"):
        rest_own = ring_next(rest_sum, after(rest_ring, table_terms), 1, "z")
        rest_ring = ring_up(rest_own.astype(BF), "z")
    moved_b, rest_ring, moved_early = lax.optimization_barrier((moved_b, rest_ring, moved_early))
    for step in range(1, zn):
        with jax.named_scope("reduce_table"):
            total_b = terms_b[:, zn - 1 - step].astype(F32) + moved_b.astype(F32)
            if step < zn - 1:
                moved_b = ring_up(total_b.astype(BF), "z")
            else:
                moved_b = swap(total_b[1].astype(BF), "y")
        if step < zn - 1:
            with jax.named_scope("reduce_rest"):
                rest_own = ring_next(rest_sum, rest_ring, step + 1, "z")
                if step < zn - 2:
                    rest_ring = ring_up(rest_own.astype(BF), "z")
        if step == zn - 2:
            with jax.named_scope("reduce_table"):
                moved_a = jnp.concatenate([moved_early, moved_late], 1)
                sum_a = added(terms_a[0], after(moved_a, total_b))
                moving_a = ring_up(sum_a[zn - 1], "z")
            moved_b, moving_a = lax.optimization_barrier((moved_b, moving_a))
        elif step < zn - 2:
            moved_b, rest_ring, moved_late = lax.optimization_barrier(
                (moved_b, rest_ring, moved_late)
            )
    with jax.named_scope("reduce_table"):
        for step in range(2, zn):
            total_a = sum_a[zn - step].astype(F32) + moving_a.astype(F32)
            moving_a = ring_up(total_a.astype(BF), "z")
            if step == 2:
                moved_b, moving_a = lax.optimization_barrier((moved_b, moving_a))
        total_b = total_b[0] + moved_b.astype(F32)
        total_a = sum_a[0].astype(F32) + moving_a.astype(F32)
    with jax.named_scope("reduce_mlp"):
        mlp_own = ring_next(mlp_sum, after(mlp_ring, rest_sum), 3, "z")

    up_total = mlp_own[:, : ff // 2].reshape(2, rows_here, ff // 2)
    down_own = jnp.concatenate([mlp_own[:, ff // 2 : ff // 2 + D], mlp_own[:, ff // 2 + D :]], 0)
    qkv_total = rest_own[:, :qkv_cols].reshape(2, rows_here, qkv_cols)
    small_end = rest_own.shape[1] - D // 2
    small_own = rest_own[:, qkv_cols:small_end]
    small_own = jnp.concatenate([small_own[:rows_here], small_own[rows_here:]], 1)
    attn_own = rest_own[:, small_end:]
    attn_own = jnp.concatenate([attn_own[:rows_here], attn_own[rows_here:]], 1)

    unit_grad = jnp.concatenate([total_a, total_b], axis=0)
    own_rows = embed_table.astype(F32)
    inverse = lax.rsqrt(jnp.mean(own_rows * own_rows, axis=1, keepdims=True) + 1e-06)
    along = jnp.mean(own_rows * unit_grad, axis=1, keepdims=True)
    table_grad = inverse * unit_grad - own_rows * (inverse * inverse * inverse * along)

    input_own = small_own[:, :width].reshape(input_rows, D)
    output_own = small_own[:, width : 2 * width]
    vector_own = small_own[: vector.size // 128, 2 * width : 2 * width + 128].reshape(-1)
    gains = [vector_own[k * rows_here : (k + 1) * rows_here] for k in range(4)]

    def columns_back(sums, split_shape, axis):
        mine_rows, other_rows = pick(sums, c, 0), pick(sums, 1 - c, 0)
        other_cols = swap(other_rows, "c")
        return ordered(
            mine_rows.reshape(split_shape), other_cols.reshape(split_shape), c, axis
        ).reshape(rows_here, -1)

    qkv_own = columns_back(qkv_total, (rows_here, 3 * heads // 2, HEAD_DIM), 2)
    up_own = columns_back(up_total, (rows_here, groups, ff_block), 2)
    return (
        token_loss,
        table_grad,
        input_own,
        gains[0],
        gains[1],
        qkv_own,
        attn_own,
        gains[2],
        gains[3],
        up_own,
        vector_own[4 * rows_here :],
        down_own,
        output_own,
    )


def combined_all(shard, axis, combine):
    everything = jax.tree.map(lambda part: lax.all_gather(part, axis), shard)
    first = jax.tree.map(lambda part: part[0], everything)

    def step(k, so_far):
        return combine(so_far, jax.tree.map(lambda part: part[k], everything))

    return lax.fori_loop(1, lax.axis_size(axis), step, first)


def product(left, right):
    return jnp.dot(left, right, preferred_element_type=jnp.float32)


def product_left(left, right):
    return lax.dot_general(
        left, right, (((0,), (0,)), ((), ())), preferred_element_type=jnp.float32
    )


def product_right(left, right):
    return lax.dot_general(
        left, right, (((1,), (1,)), ((), ())), preferred_element_type=jnp.float32
    )


def normalize_rows(matrix):
    return matrix * lax.rsqrt(jnp.mean(matrix * matrix, axis=1, keepdims=True) + 1e-06)


def layer_norm(hidden, norm_gain, norm_bias):
    centre = hidden - jnp.mean(hidden, axis=-1, keepdims=True)
    spread = jnp.mean(centre * centre, axis=-1, keepdims=True)
    return centre * lax.rsqrt(spread + 1e-05) * norm_gain + norm_bias


def exact_gelu(pre_act):
    return jax.nn.gelu(pre_act, approximate=False)


def noise_rows(row_seeds, positions, channel_count):
    channel = lax.iota(jnp.int32, channel_count)
    mixed_once = (
        row_seeds[:, None, None] + 7919 * positions[None, :, None] + 104729 * channel[None, None, :]
    ) % 65521
    mixed_twice = (mixed_once * (mixed_once % 32719) + 31 * channel[None, None, :]) % 65521
    return (mixed_twice.astype(jnp.float32) / 32760.5 - 1.0) * 1.7320508


def time_terms(time_steps):
    fraction = time_steps.astype(jnp.float32) / (TSTEPS - 1)
    noise_level = 0.3 * jnp.exp(fraction * math.log(30.0))
    return (noise_level, lax.rsqrt(1.0 + noise_level * noise_level), 0.5 + fraction)


def masked_scores(query_block, key_rows, segment_block, segment_row):
    scores = jnp.einsum("qhd,khd->hqk", query_block, key_rows, preferred_element_type=jnp.float32)
    same_doc = segment_block[:, None] == segment_row[None, :]
    return jnp.where(same_doc[None], scores, -1e30)


def attend_row(operands):
    queries, key_rows, value_rows, segment_row = operands
    length = queries.shape[0]
    block_rows = math.gcd(length, 512)
    block_count = length // block_rows

    def attend_block(pieces):
        query_block, segment_block = pieces
        scores = masked_scores(query_block, key_rows, segment_block, segment_row)
        row_max = jnp.max(scores, axis=-1, keepdims=True)
        raised = jnp.exp(scores - row_max)
        summed = jnp.sum(raised, axis=-1, keepdims=True)
        probs_low = (raised / summed).astype(jnp.bfloat16)
        attended = jnp.einsum(
            "hqk,khd->qhd", probs_low, value_rows, preferred_element_type=jnp.float32
        )
        return (attended.astype(jnp.bfloat16), (row_max + jnp.log(summed))[..., 0])

    attended, log_total = lax.map(
        attend_block,
        (
            queries.reshape((block_count, block_rows) + queries.shape[1:]),
            segment_row.reshape(block_count, block_rows),
        ),
    )
    return (attended.reshape(queries.shape), log_total)


def attend_back_row(operands):
    queries, key_rows, value_rows, segment_row, grad_rows, log_total = operands
    length = queries.shape[0]
    block_rows = math.gcd(length, 512)
    block_count = length // block_rows

    def back_block(carry, pieces):
        key_sum, value_sum = carry
        query_block, segment_block, grad_block, total_block = pieces
        scores = masked_scores(query_block, key_rows, segment_block, segment_row)
        probs = jnp.exp(scores - total_block[:, :, None])
        prob_grad = jnp.einsum(
            "qhd,khd->hqk", grad_block, value_rows, preferred_element_type=jnp.float32
        )
        score_grad = (
            probs * (prob_grad - jnp.sum(probs * prob_grad, axis=-1, keepdims=True))
        ).astype(jnp.bfloat16)
        query_grad = jnp.einsum(
            "hqk,khd->qhd", score_grad, key_rows, preferred_element_type=jnp.float32
        )
        key_sum = key_sum + jnp.einsum(
            "hqk,qhd->khd", score_grad, query_block, preferred_element_type=jnp.float32
        )
        value_sum = value_sum + jnp.einsum(
            "hqk,qhd->khd",
            probs.astype(jnp.bfloat16),
            grad_block,
            preferred_element_type=jnp.float32,
        )
        return ((key_sum, value_sum), query_grad.astype(jnp.bfloat16))

    block_shape = (block_count, block_rows) + queries.shape[1:]
    start_sums = (jnp.zeros(key_rows.shape, jnp.float32), jnp.zeros(value_rows.shape, jnp.float32))
    (key_sum, value_sum), query_grad = lax.scan(
        back_block,
        start_sums,
        (
            queries.reshape(block_shape),
            segment_row.reshape(block_count, block_rows),
            grad_rows.reshape(block_shape),
            log_total,
        ),
    )
    return (
        query_grad.reshape(queries.shape),
        key_sum.astype(jnp.bfloat16),
        value_sum.astype(jnp.bfloat16),
    )


def join_parts(first, second):
    top = jnp.maximum(first[0], second[0])
    total = first[1] * jnp.exp(first[0] - top) + second[1] * jnp.exp(second[0] - top)
    return (top, total, first[2] + second[2], first[3] + second[3])


def local(
    token_ids,
    segment_ids,
    time_steps,
    row_seeds,
    loss_weights,
    embed_table,
    input_proj,
    attn_gain,
    attn_bias,
    qkv_proj,
    attn_proj,
    mlp_gain,
    mlp_bias,
    up_proj,
    up_bias,
    down_proj,
    output_proj,
):
    seq_count = lax.axis_size("seq")
    seq_place = lax.axis_index("seq")
    dp_count = lax.axis_size("dp")
    row_count, length = token_ids.shape
    local_len = length // seq_count
    tok_count = row_count * local_len
    start_pos = seq_place * local_len
    own_ids = lax.dynamic_slice_in_dim(token_ids, start_pos, local_len, 1)
    positions = start_pos + lax.iota(jnp.int32, local_len)
    gathered = (
        lax.all_gather(embed_table, ("dp", "seq"), axis=0, tiled=True),
        lax.all_gather(input_proj, ("dp", "seq"), axis=0, tiled=True),
        lax.all_gather(attn_gain, ("dp", "seq"), axis=0, tiled=True),
        lax.all_gather(attn_bias, ("dp", "seq"), axis=0, tiled=True),
        lax.all_gather(qkv_proj, ("dp", "seq"), axis=0, tiled=True),
        lax.all_gather(attn_proj, ("dp", "seq"), axis=0, tiled=True),
        lax.all_gather(mlp_gain, ("dp", "seq"), axis=0, tiled=True),
        lax.all_gather(mlp_bias, ("dp", "seq"), axis=0, tiled=True),
        lax.all_gather(up_proj, ("dp", "seq"), axis=0, tiled=True),
        lax.all_gather(up_bias, ("dp", "seq"), axis=0, tiled=True),
        lax.all_gather(down_proj, ("dp", "seq"), axis=0, tiled=True),
        lax.all_gather(output_proj, ("dp", "seq"), axis=0, tiled=True),
    )
    (
        table_full,
        input_full,
        gain_one,
        bias_one,
        qkv_full,
        attn_full,
        gain_two,
        bias_two,
        up_full,
        upbias_full,
        down_full,
        output_full,
    ) = gathered
    vocab_size, embed_width = table_full.shape
    block_len = vocab_size // (dp_count * seq_count)
    unit, unit_back = jax.vjp(normalize_rows, table_full.astype(jnp.float32))
    sub_table = lax.dynamic_slice_in_dim(
        table_full.reshape(dp_count, seq_count, block_len, embed_width), seq_place, 1, 1
    ).reshape(dp_count * block_len, embed_width)
    sub_unit = lax.dynamic_slice_in_dim(
        unit.reshape(dp_count, seq_count, block_len, embed_width), seq_place, 1, 1
    ).reshape(dp_count * block_len, embed_width)
    scaled = (sub_unit * embed_width ** (-0.5)).astype(jnp.bfloat16)
    local_rows = lax.iota(jnp.int32, dp_count * block_len)
    vocab_index = (
        local_rows // block_len * seq_count + seq_place
    ) * block_len + local_rows % block_len
    noise_level, input_scale, residual_scale = time_terms(time_steps)
    noise = noise_rows(row_seeds, positions, embed_width)
    embedded = jnp.take(unit, own_ids, axis=0)
    inputs = (
        (input_scale[:, None, None] * (embedded + noise_level[:, None, None] * noise))
        .astype(jnp.bfloat16)
        .reshape(tok_count, embed_width)
    )
    token_scale = jnp.repeat(residual_scale, local_len)[:, None]
    token_input_scale = jnp.repeat(input_scale, local_len)[:, None]
    hidden_zero = product(inputs, input_full)
    first_norm, first_back = jax.vjp(
        layer_norm, hidden_zero, gain_one.astype(jnp.float32), bias_one.astype(jnp.float32)
    )
    first_in = first_norm.astype(jnp.bfloat16)
    qkv = product(first_in, qkv_full)
    query_tok = (
        (qkv[:, :D] * HEAD_DIM ** (-0.5)).astype(jnp.bfloat16).reshape(row_count, local_len, D)
    )
    key_tok = qkv[:, D : 2 * D].astype(jnp.bfloat16).reshape(row_count, local_len, D)
    value_tok = qkv[:, 2 * D :].astype(jnp.bfloat16).reshape(row_count, local_len, D)
    head_q, head_k, head_v = (
        lax.all_to_all(query_tok, "seq", split_axis=2, concat_axis=1, tiled=True),
        lax.all_to_all(key_tok, "seq", split_axis=2, concat_axis=1, tiled=True),
        lax.all_to_all(value_tok, "seq", split_axis=2, concat_axis=1, tiled=True),
    )
    heads_here = head_q.shape[2] // HEAD_DIM
    head_shape = (row_count, length, heads_here, HEAD_DIM)
    head_q = head_q.reshape(head_shape)
    head_k = head_k.reshape(head_shape)
    head_v = head_v.reshape(head_shape)
    attended, log_total = lax.map(attend_row, (head_q, head_k, head_v, segment_ids))
    attended = attended.reshape(row_count, length, heads_here * HEAD_DIM)
    mixed = lax.all_to_all(attended, "seq", split_axis=1, concat_axis=2, tiled=True).reshape(
        tok_count, D
    )
    hidden_one = hidden_zero + token_scale * product(mixed, attn_full)
    second_norm, second_back = jax.vjp(
        layer_norm, hidden_one, gain_two.astype(jnp.float32), bias_two.astype(jnp.float32)
    )
    second_in = second_norm.astype(jnp.bfloat16)
    pre_act = product(second_in, up_full) + upbias_full.astype(jnp.float32)
    activated, gelu_back = jax.vjp(exact_gelu, pre_act)
    act_low = activated.astype(jnp.bfloat16)
    hidden_two = hidden_one + token_scale * product(act_low, down_full)
    final_in = hidden_two.astype(jnp.bfloat16)
    outputs = product(final_in, output_full).astype(jnp.bfloat16)
    group_tok = seq_count * tok_count
    group_out = lax.all_gather(outputs, "seq", axis=0, tiled=True)
    group_ids = (
        token_ids.reshape(row_count, seq_count, local_len).transpose(1, 0, 2).reshape(group_tok)
    )
    spread = jnp.where(
        lax.iota(jnp.int32, seq_count)[:, None] == seq_place,
        loss_weights.reshape(1, tok_count),
        0.0,
    )
    tile_rows = math.gcd(group_tok, 512)
    tile_count = group_tok // tile_rows
    out_tiles = group_out.reshape(tile_count, tile_rows, embed_width)
    id_tiles = group_ids.reshape(tile_count, tile_rows)

    def part_tile(pieces):
        out_block, target_block = pieces
        logits = product_right(out_block, scaled)
        row_max = jnp.max(logits, axis=1)
        exp_sum = jnp.sum(jnp.exp(logits - row_max[:, None]), axis=1)
        picked = jnp.sum(
            jnp.where(vocab_index[None, :] == target_block[:, None], logits, 0.0), axis=1
        )
        return (row_max, exp_sum, picked)

    part_max, part_sum, part_pick = lax.map(part_tile, (out_tiles, id_tiles))
    top, total, pick, weight_tiles = combined_all(
        (part_max, part_sum, part_pick, spread), "seq", join_parts
    )
    log_tiles = top + jnp.log(total)
    all_loss = log_tiles - pick
    token_loss = lax.dynamic_slice_in_dim(all_loss, seq_place, 1, 0)

    def back_tile(scaled_sum, pieces):
        out_block, target_block, log_block, weight_block = pieces
        logits = product_right(out_block, scaled)
        probs = jnp.exp(logits - log_block[:, None])
        onehot = (vocab_index[None, :] == target_block[:, None]).astype(jnp.float32)
        grad_logits = (weight_block[:, None] * (probs - onehot)).astype(jnp.bfloat16)
        scaled_sum = scaled_sum + product_left(grad_logits, out_block)
        return (scaled_sum, product(grad_logits, scaled))

    scaled_grad, out_terms = lax.scan(
        back_tile,
        jnp.zeros(scaled.shape, jnp.float32),
        (out_tiles, id_tiles, log_tiles, weight_tiles),
    )
    out_terms = out_terms.reshape(tile_count * tile_rows, embed_width)
    out_grad = lax.psum_scatter(out_terms, "seq", scatter_dimension=0, tiled=True).astype(
        jnp.bfloat16
    )
    output_w_grad = product_left(final_in, out_grad)
    hidden_two_grad = product_right(out_grad, output_full)
    branch_grad = (token_scale * hidden_two_grad).astype(jnp.bfloat16)
    down_w_grad = product_left(act_low, branch_grad)
    pre_grad = gelu_back(product_right(branch_grad, down_full))[0].astype(jnp.bfloat16)
    up_w_grad = product_left(second_in, pre_grad)
    upbias_grad = jnp.sum(pre_grad, axis=0, dtype=jnp.float32)
    hidden_one_part, gain_two_grad, bias_two_grad = second_back(product_right(pre_grad, up_full))
    hidden_one_grad = hidden_two_grad + hidden_one_part
    attn_grad = (token_scale * hidden_one_grad).astype(jnp.bfloat16)
    attn_w_grad = product_left(mixed, attn_grad)
    mixed_grad = (
        product_right(attn_grad, attn_full).astype(jnp.bfloat16).reshape(row_count, local_len, D)
    )
    head_grad = lax.all_to_all(mixed_grad, "seq", split_axis=2, concat_axis=1, tiled=True).reshape(
        head_shape
    )
    query_grad, key_grad, value_grad = lax.map(
        attend_back_row, (head_q, head_k, head_v, segment_ids, head_grad, log_total)
    )
    merged_shape = (row_count, length, heads_here * HEAD_DIM)
    query_back, key_back, value_back = (
        lax.all_to_all(
            query_grad.reshape(merged_shape), "seq", split_axis=1, concat_axis=2, tiled=True
        ),
        lax.all_to_all(
            key_grad.reshape(merged_shape), "seq", split_axis=1, concat_axis=2, tiled=True
        ),
        lax.all_to_all(
            value_grad.reshape(merged_shape), "seq", split_axis=1, concat_axis=2, tiled=True
        ),
    )
    qkv_grad = jnp.concatenate(
        [query_back * HEAD_DIM ** (-0.5), key_back, value_back], axis=2
    ).reshape(tok_count, 3 * D)
    qkv_w_grad = product_left(first_in, qkv_grad)
    hidden_zero_part, gain_one_grad, bias_one_grad = first_back(product_right(qkv_grad, qkv_full))
    hidden_zero_grad = (hidden_one_grad + hidden_zero_part).astype(jnp.bfloat16)
    input_w_grad = product_left(inputs, hidden_zero_grad)
    embedded_grad = token_input_scale * product_right(hidden_zero_grad, input_full)
    scaled_part = scaled_grad * embed_width ** (-0.5)
    group_grad = lax.all_gather(
        embedded_grad.astype(jnp.bfloat16), "seq", axis=0, tiled=True
    ).astype(embedded_grad.dtype)
    block_id = group_ids // block_len
    owned = block_id % seq_count == seq_place
    local_slot = jnp.where(
        owned, block_id // seq_count * block_len + group_ids % block_len, scaled.shape[0]
    )
    unit_grad = scaled_part.at[local_slot].add(group_grad, mode="drop")
    table_term = jax.vjp(normalize_rows, sub_table.astype(jnp.float32))[1](unit_grad)[0]
    table_grad = lax.psum_scatter(
        table_term.astype(jnp.bfloat16), "dp", scatter_dimension=0, tiled=True
    ).astype(jnp.float32)
    summed = (
        lax.psum_scatter(input_w_grad, ("dp", "seq"), scatter_dimension=0, tiled=True),
        lax.psum_scatter(gain_one_grad, ("dp", "seq"), scatter_dimension=0, tiled=True),
        lax.psum_scatter(bias_one_grad, ("dp", "seq"), scatter_dimension=0, tiled=True),
        lax.psum_scatter(qkv_w_grad, ("dp", "seq"), scatter_dimension=0, tiled=True),
        lax.psum_scatter(attn_w_grad, ("dp", "seq"), scatter_dimension=0, tiled=True),
        lax.psum_scatter(gain_two_grad, ("dp", "seq"), scatter_dimension=0, tiled=True),
        lax.psum_scatter(bias_two_grad, ("dp", "seq"), scatter_dimension=0, tiled=True),
        lax.psum_scatter(up_w_grad, ("dp", "seq"), scatter_dimension=0, tiled=True),
        lax.psum_scatter(upbias_grad, ("dp", "seq"), scatter_dimension=0, tiled=True),
        lax.psum_scatter(down_w_grad, ("dp", "seq"), scatter_dimension=0, tiled=True),
        lax.psum_scatter(output_w_grad, ("dp", "seq"), scatter_dimension=0, tiled=True),
    )
    return (token_loss.reshape(row_count, local_len), table_grad) + tuple(summed)


def solution(mesh):
    dp, seq = mesh.shape["dp"], mesh.shape["seq"]
    if (dp, seq) == (16, 2):
        inner = Mesh(mesh.devices.reshape(dp // 4, 2, 2, seq), ("z", "y", "c", "x"))
        dp_names, seq_names, body = ("z", "y", "c"), ("x",), paired
    else:
        inner, dp_names, seq_names, body = mesh, ("dp",), ("seq",), local
    every = dp_names + seq_names
    in_specs = (
        P(dp_names, None),
        P(dp_names, None),
        P(dp_names),
        P(dp_names),
        P(dp_names, seq_names),
        P(every, None),
        P(every, None),
        P(every),
        P(every),
        P(every, None),
        P(every, None),
        P(every),
        P(every),
        P(every, None),
        P(every),
        P(every, None),
        P(every, None),
    )
    out_specs = (
        P(dp_names, seq_names),
        P(every, None),
        P(every, None),
        P(every),
        P(every),
        P(every, None),
        P(every, None),
        P(every),
        P(every),
        P(every, None),
        P(every),
        P(every, None),
        P(every, None),
    )
    return jax.shard_map(body, mesh=inner, in_specs=in_specs, out_specs=out_specs, check_vma=False)
```

```python
import math

import jax
import jax.numpy as jnp
from jax import lax
from jax.experimental import pallas as pl
from jax.experimental.pallas import tpu as pltpu
from jax.sharding import Mesh
from jax.sharding import PartitionSpec as P

D = 1024
HEAD_DIM = 64
TSTEPS = 1000
SWAP = ((0, 1), (1, 0))
BF = jnp.bfloat16
F32 = jnp.float32
NEG = -1e30
LIMIT = 70.0
MIB = 1 << 20


def dot_nn(left, right):
    return lax.dot_general(left, right, (((1,), (0,)), ((), ())), preferred_element_type=F32)


def dot_nt(left, right):
    return lax.dot_general(left, right, (((1,), (1,)), ((), ())), preferred_element_type=F32)


def dot_tn(left, right):
    return lax.dot_general(left, right, (((0,), (0,)), ((), ())), preferred_element_type=F32)


def swap(value, axis):
    return lax.ppermute(value, axis, SWAP)


def ring_down(value, axis):
    n = lax.axis_size(axis)
    return lax.ppermute(value, axis, [(i, (i - 1) % n) for i in range(n)])


def ring_up(value, axis):
    n = lax.axis_size(axis)
    return lax.ppermute(value, axis, [(i, (i + 1) % n) for i in range(n)])


def ordered(own, other, place, axis):
    return jnp.where(
        place == 0, jnp.stack([own, other], axis), jnp.stack([other, own], axis)
    )


def pick(value, index, axis):
    return lax.dynamic_index_in_dim(value, index, axis, keepdims=False)


def after(value, *others):
    return lax.optimization_barrier((value,) + others)[0]


def ring_blocks(value, axis):
    parts = [value]
    for _ in range(lax.axis_size(axis) - 1):
        parts.append(ring_down(parts[-1], axis))
    return parts


def joined_swap(held, axis):
    return jnp.concatenate([held, swap(held, axis)], 0)


def apart(value, axis, distance):
    n = lax.axis_size(axis)
    return lax.ppermute(value, axis, [(i, i ^ distance) for i in range(n)])


def joined_apart(value, axis):
    held, distance = value[None], 1
    while distance < lax.axis_size(axis):
        held = jnp.concatenate([held, apart(held, axis, distance)], 0)
        distance *= 2
    return held


def halve(value, axis, at):
    here = lax.axis_index(axis)
    return pick(value, here, at), swap(pick(value, 1 - here, at), axis)


def added(kept, moved):
    return (kept.astype(F32) + moved.astype(F32)).astype(BF)


def ring_start(value, axis):
    n, here = lax.axis_size(axis), lax.axis_index(axis)
    return ring_up(pick(value, (here - 1) % n, 0), axis)


def ring_next(value, moved, step, axis):
    n, here = lax.axis_size(axis), lax.axis_index(axis)
    return pick(value, (here - 1 - step) % n, 0).astype(F32) + moved.astype(F32)


def place_blocks(places, halves, outs):
    flat = halves[0] + halves[1]

    def body(places_ref, *refs):
        ins, results, block = refs[: len(flat)], refs[len(flat) :], 0
        for number, piece in enumerate(ins):
            for k in range(piece.shape[0]):
                p, h = places_ref[block], number // len(halves[0])
                block += 1
                for (low, high, _, index), result in zip(outs, results):
                    result[index(p, h)] = piece[k, :, low:high]

    return pl.pallas_call(
        body,
        out_shape=tuple(jax.ShapeDtypeStruct(shape, BF) for _, _, shape, _ in outs),
        in_specs=[pl.BlockSpec(memory_space=pltpu.SMEM)]
        + [pl.BlockSpec(memory_space=pltpu.VMEM)] * len(flat),
        out_specs=tuple(pl.BlockSpec(memory_space=pltpu.VMEM) for _ in outs),
        compiler_params=pltpu.CompilerParams(vmem_limit_bytes=32 * MIB),
        name="place_blocks",
    )(places, *flat)


def for_each_window(lo, hi, blocks, run):
    for count in range(1, blocks + 1):

        @pl.when(hi - lo == count)
        def _():
            run(lo, count)


def attend_body(
    lo_ref, hi_ref, q_ref, k_ref, v_ref, seg_col_ref, seg_row_ref, o_ref, lse_ref, v_ones
):
    length = q_ref.shape[0]
    blk = min(256, length)
    lane = lax.broadcasted_iota(jnp.int32, (1, 128), 1)
    masks = (lane < HEAD_DIM, lane >= HEAD_DIM)
    v = v_ref[...]
    for h in range(2):
        v_ones[h] = jnp.where(masks[h], v, jnp.ones_like(v))

    def largest(ref):
        rows = ref[...].astype(F32)
        return jnp.max(jnp.sum(rows * rows, axis=1, keepdims=True))

    small = largest(q_ref) * largest(k_ref) <= LIMIT * LIMIT

    def finish(rows, accs):
        totals = [pltpu.roll(acc, HEAD_DIM, axis=1) for acc in accs]
        o_ref[rows, :] = (
            jnp.where(masks[0], accs[0], accs[1]) / jnp.where(masks[0], totals[0], totals[1])
        ).astype(BF)
        return [accs[0].T[HEAD_DIM : HEAD_DIM + 1], accs[1].T[0:1]]

    def each(qi, _):
        rows = pl.ds(pl.multiple_of(qi * blk, blk), blk)
        q = q_ref[rows, :]
        q_heads = [jnp.where(m, q, jnp.zeros_like(q)) for m in masks]

        def run(first, count):
            at = pl.ds(pl.multiple_of(first * blk, blk), count * blk)
            k = k_ref[at, :]
            same = seg_col_ref[rows, :] == seg_row_ref[:, at]
            accs = []
            for h in range(2):
                e = jnp.exp(jnp.where(same, dot_nt(q_heads[h], k), NEG)).astype(BF)
                accs.append(dot_nn(e, v_ones[h, at, :]))
            for h, total in enumerate(finish(rows, accs)):
                lse_ref[0, h : h + 1, rows] = jnp.log(total)

        @pl.when(small)
        def _():
            for_each_window(lo_ref[qi], hi_ref[qi], length // blk, run)

        @pl.when(jnp.logical_not(small))
        def _():
            def scores(kb, h):
                at = pl.ds(pl.multiple_of(kb * blk, blk), blk)
                same = seg_col_ref[at, :] == seg_row_ref[:, rows]
                return jnp.where(same, dot_nt(k_ref[at, :], q_heads[h]), NEG)

            def highest(kb, tops):
                return tuple(
                    jnp.maximum(tops[h], jnp.max(scores(kb, h), axis=0, keepdims=True))
                    for h in range(2)
                )

            tops = lax.fori_loop(
                lo_ref[qi], hi_ref[qi], highest, (jnp.full((1, blk), NEG, F32),) * 2
            )

            def gather(kb, accs):
                at = pl.ds(pl.multiple_of(kb * blk, blk), blk)
                return tuple(
                    accs[h]
                    + dot_tn(jnp.exp(scores(kb, h) - tops[h]).astype(BF), v_ones[h, at, :])
                    for h in range(2)
                )

            accs = lax.fori_loop(
                lo_ref[qi], hi_ref[qi], gather, (jnp.zeros((blk, 128), F32),) * 2
            )
            for h, total in enumerate(finish(rows, accs)):
                lse_ref[0, h : h + 1, rows] = tops[h] + jnp.log(total)

        return 0

    lax.fori_loop(0, length // blk, each, 0)


def attend(q, k, v, seg_col, seg_row, lo, hi):
    length, width = q.shape
    pairs = width // 128
    spec = pl.BlockSpec((length, 128), lambda i, *_: (0, i))
    return pl.pallas_call(
        attend_body,
        out_shape=(
            jax.ShapeDtypeStruct((length, width), BF),
            jax.ShapeDtypeStruct((pairs, 2, length), F32),
        ),
        grid_spec=pltpu.PrefetchScalarGridSpec(
            num_scalar_prefetch=2,
            grid=(pairs,),
            in_specs=[
                spec,
                spec,
                spec,
                pl.BlockSpec((length, 1), lambda i, *_: (0, 0)),
                pl.BlockSpec((1, length), lambda i, *_: (0, 0)),
            ],
            out_specs=(spec, pl.BlockSpec((1, 2, length), lambda i, *_: (i, 0, 0))),
            scratch_shapes=[pltpu.VMEM((2, length, 128), BF)],
        ),
        compiler_params=pltpu.CompilerParams(vmem_limit_bytes=32 * MIB),
        cost_estimate=pl.CostEstimate(
            flops=16 * length * length * width,
            bytes_accessed=8 * length * width,
            transcendentals=length * length * width // HEAD_DIM,
        ),
        name="attend",
    )(lo, hi, q, k, v, seg_col, seg_row)


def attend_back_body(
    lo_ref,
    hi_ref,
    q_ref,
    k_ref,
    v_ref,
    o_ref,
    g_ref,
    lse_ref,
    seg_col_ref,
    seg_row_ref,
    dq_ref,
    dk_ref,
    dv_ref,
    dk_sum,
    dv_sum,
    k_t,
):
    length = q_ref.shape[0]
    blk = min(256, length)
    lane = lax.broadcasted_iota(jnp.int32, (1, 128), 1)
    masks = (lane < HEAD_DIM, lane >= HEAD_DIM)
    dk_sum[...] = jnp.zeros_like(dk_sum)
    dv_sum[...] = jnp.zeros_like(dv_sum)
    k_t[...] = k_ref[...].astype(F32).T.astype(BF)
    def each(qi, _):
        rows = pl.ds(pl.multiple_of(qi * blk, blk), blk)

        def run(first, count):
            q, g = q_ref[rows, :], g_ref[rows, :]
            mixed = (g.astype(F32) * o_ref[rows, :].astype(F32)).T
            at = pl.ds(pl.multiple_of(first * blk, blk), count * blk)
            k, v = k_ref[at, :], v_ref[at, :]
            same = seg_col_ref[at, :] == seg_row_ref[:, rows]
            dq = []
            dk, dv = dk_sum[at, :], dv_sum[at, :]
            for h in range(2):
                q_head = jnp.where(masks[h], q, jnp.zeros_like(q))
                g_head = jnp.where(masks[h], g, jnp.zeros_like(g))
                delta = jnp.sum(mixed[h * HEAD_DIM : (h + 1) * HEAD_DIM], axis=0, keepdims=True)
                s = dot_nt(k, q_head)
                p = jnp.exp(jnp.where(same, s - lse_ref[0, h : h + 1, rows], NEG))
                dp = dot_nt(v, g_head)
                ds = (p * (dp - delta)).astype(BF)
                dv = dv + dot_nn(p.astype(BF), g_head)
                dk = dk + dot_nn(ds, q_head)
                dq.append(dot_nn(k_t[h * HEAD_DIM : (h + 1) * HEAD_DIM, at], ds))
            dk_sum[at, :] = dk
            dv_sum[at, :] = dv
            dq_ref[rows, :] = jnp.concatenate(dq, axis=0).T.astype(BF)

        for_each_window(lo_ref[qi], hi_ref[qi], length // blk, run)
        return 0

    lax.fori_loop(0, length // blk, each, 0)
    dk_ref[...] = dk_sum[...].astype(BF)
    dv_ref[...] = dv_sum[...].astype(BF)


def attend_back(q, k, v, o, g, lse, seg_col, seg_row, lo, hi):
    length, width = q.shape
    pairs = width // 128
    spec = pl.BlockSpec((length, 128), lambda i, *_: (0, i))
    shape = jax.ShapeDtypeStruct((length, width), BF)
    return pl.pallas_call(
        attend_back_body,
        out_shape=(shape, shape, shape),
        grid_spec=pltpu.PrefetchScalarGridSpec(
            num_scalar_prefetch=2,
            grid=(pairs,),
            in_specs=[
                spec,
                spec,
                spec,
                spec,
                spec,
                pl.BlockSpec((1, 2, length), lambda i, *_: (i, 0, 0)),
                pl.BlockSpec((length, 1), lambda i, *_: (0, 0)),
                pl.BlockSpec((1, length), lambda i, *_: (0, 0)),
            ],
            out_specs=(spec, spec, spec),
            scratch_shapes=[
                pltpu.VMEM((length, 128), F32),
                pltpu.VMEM((length, 128), F32),
                pltpu.VMEM((128, length), BF),
            ],
        ),
        compiler_params=pltpu.CompilerParams(vmem_limit_bytes=32 * MIB),
        cost_estimate=pl.CostEstimate(
            flops=32 * length * length * width,
            bytes_accessed=16 * length * width,
            transcendentals=length * length * width // HEAD_DIM,
        ),
        name="attend_back",
    )(lo, hi, q, k, v, o, g, lse, seg_col, seg_row)


def score_body(
    norm_ref, out_ref, table_ref, slot_ref, raised_ref, tops_ref, acc_ref, total_ref, top, fast
):
    j = pl.program_id(0)
    tokens, width = out_ref.shape
    count = table_ref.shape[1]
    rows = table_ref[0].astype(F32)
    unit = rows * lax.rsqrt(jnp.mean(rows * rows, axis=1, keepdims=True) + 1e-06)
    low = unit * width ** (-0.5)
    scaled, scaled_t = low.astype(BF), low.T.astype(BF)
    row = lax.broadcasted_iota(jnp.int32, (count, 1), 0) + j * count

    @pl.when(j == 0)
    def _():
        acc_ref[...] = jnp.zeros_like(acc_ref)
        total_ref[...] = jnp.zeros_like(total_ref)
        some = scaled[: min(count, 128)]
        first = jnp.max(dot_nt(some, out_ref[...]), axis=0, keepdims=True)
        floor = norm_ref[...] - LIMIT
        kept = jnp.max(floor - first) <= LIMIT
        top[...] = jnp.where(kept, jnp.maximum(first, floor), NEG)
        fast[0] = kept.astype(jnp.int32)

    @pl.when(fast[0] == 1)
    def _():
        e = jnp.exp(dot_nt(scaled, out_ref[...]) - top[...])
        total_ref[...] += jnp.sum(e, axis=0, keepdims=True)
        raised_ref[0] = jnp.where(row == slot_ref[...], 0.0, e).astype(BF)
        acc_ref[...] += dot_nn(scaled_t, raised_ref[0])
        tops_ref[0] = top[...]

    @pl.when(fast[0] == 0)
    def _():
        part = math.gcd(tokens, 512)

        def each(n, _):
            at = pl.ds(pl.multiple_of(n * part, part), part)
            logits = dot_nt(scaled, out_ref[at, :])
            new_top = jnp.maximum(top[:, at], jnp.max(logits, axis=0, keepdims=True))
            keep = jnp.exp(top[:, at] - new_top)
            e = jnp.exp(logits - new_top)
            total_ref[:, at] = total_ref[:, at] * keep + jnp.sum(e, axis=0, keepdims=True)
            raised_ref[0, :, at] = jnp.where(row == slot_ref[:, at], 0.0, e).astype(BF)
            acc_ref[:, at] = acc_ref[:, at] * keep + dot_nn(scaled_t, raised_ref[0, :, at])
            tops_ref[0, :, at] = new_top
            top[:, at] = new_top
            return 0

        lax.fori_loop(0, tokens // part, each, 0)


def score(outputs, table, slots):
    tokens, width = outputs.shape
    blocks, rows, _ = table.shape
    squares = jnp.square(outputs.astype(F32))
    norms = 1.01 * jnp.sqrt(dot_nt(jnp.ones((8, width), BF), squares.astype(BF))[:1])
    return pl.pallas_call(
        score_body,
        out_shape=(
            jax.ShapeDtypeStruct((blocks, rows, tokens), BF),
            jax.ShapeDtypeStruct((blocks, 1, tokens), F32),
            jax.ShapeDtypeStruct((width, tokens), F32),
            jax.ShapeDtypeStruct((1, tokens), F32),
        ),
        grid=(blocks,),
        in_specs=[
            pl.BlockSpec((1, tokens), lambda j: (0, 0)),
            pl.BlockSpec((tokens, width), lambda j: (0, 0)),
            pl.BlockSpec((1, rows, width), lambda j: (j, 0, 0)),
            pl.BlockSpec((1, tokens), lambda j: (0, 0)),
        ],
        out_specs=(
            pl.BlockSpec((1, rows, tokens), lambda j: (j, 0, 0)),
            pl.BlockSpec((1, 1, tokens), lambda j: (j, 0, 0)),
            pl.BlockSpec((width, tokens), lambda j: (0, 0)),
            pl.BlockSpec((1, tokens), lambda j: (0, 0)),
        ),
        scratch_shapes=[pltpu.VMEM((1, tokens), F32), pltpu.SMEM((1,), jnp.int32)],
        compiler_params=pltpu.CompilerParams(vmem_limit_bytes=48 * MIB),
        cost_estimate=pl.CostEstimate(
            flops=4 * blocks * rows * tokens * width,
            bytes_accessed=2 * blocks * rows * tokens,
            transcendentals=blocks * rows * tokens,
        ),
        name="score",
    )(norms, outputs, table, slots)


def table_product_body(raised_ref, out_ref, coef_ref, sum_ref):
    j = pl.program_id(0)
    lane = lax.broadcasted_iota(jnp.int32, coef_ref.shape, 1)
    coef = jnp.sum(jnp.where(lane == j, coef_ref[...], 0.0), axis=1, keepdims=True)
    weighted = (out_ref[...].astype(F32) * coef).astype(BF)
    sum_ref[0] = dot_nn(raised_ref[0], weighted)


def table_product(raised, outputs, coef):
    blocks, rows, tokens = raised.shape
    width = outputs.shape[1]
    return pl.pallas_call(
        table_product_body,
        out_shape=jax.ShapeDtypeStruct((blocks, rows, width), F32),
        grid=(blocks,),
        in_specs=[
            pl.BlockSpec((1, rows, tokens), lambda j: (j, 0, 0)),
            pl.BlockSpec((tokens, width), lambda j: (0, 0)),
            pl.BlockSpec((tokens, blocks), lambda j: (0, 0)),
        ],
        out_specs=pl.BlockSpec((1, rows, width), lambda j: (j, 0, 0)),
        compiler_params=pltpu.CompilerParams(vmem_limit_bytes=48 * MIB),
        cost_estimate=pl.CostEstimate(
            flops=2 * blocks * rows * tokens * width,
            bytes_accessed=2 * blocks * rows * tokens,
            transcendentals=0,
        ),
        name="table_product",
    )(raised, outputs, coef)


def table_add_body(sum_ref, slot_ref, grad_ref, out_ref):
    j = pl.program_id(0)
    rows = sum_ref.shape[1]
    row = lax.broadcasted_iota(jnp.int32, (rows, 1), 0) + j * rows
    chosen = (row == slot_ref[...]).astype(F32).astype(BF)
    out_ref[0] = (sum_ref[0] + dot_nn(chosen, grad_ref[...])).astype(BF)


def table_add(sums, slots, grads):
    blocks, rows, width = sums.shape
    tokens = grads.shape[0]
    return pl.pallas_call(
        table_add_body,
        out_shape=jax.ShapeDtypeStruct(sums.shape, BF),
        grid=(blocks,),
        in_specs=[
            pl.BlockSpec((1, rows, width), lambda j: (j, 0, 0)),
            pl.BlockSpec((1, tokens), lambda j: (0, 0)),
            pl.BlockSpec((tokens, width), lambda j: (0, 0)),
        ],
        out_specs=pl.BlockSpec((1, rows, width), lambda j: (j, 0, 0)),
        compiler_params=pltpu.CompilerParams(vmem_limit_bytes=48 * MIB),
        cost_estimate=pl.CostEstimate(
            flops=2 * blocks * rows * tokens * width,
            bytes_accessed=6 * blocks * rows * width,
            transcendentals=0,
        ),
        name="table_add",
    )(sums, slots, grads)


def norm_parts(hidden):
    centre = hidden - jnp.mean(hidden, axis=-1, keepdims=True)
    spread = jnp.mean(centre * centre, axis=-1, keepdims=True)
    inverse = lax.rsqrt(spread + 1e-05)
    return centre * inverse, inverse


def norm_back(grad, gain, normed, inverse):
    grad_normed = grad * gain
    first = jnp.mean(grad_normed, axis=-1, keepdims=True)
    second = jnp.mean(grad_normed * normed, axis=-1, keepdims=True)
    return inverse * (grad_normed - first - normed * second)


def noise_field(row_seed, length, channel_count):
    position = lax.iota(jnp.int32, length)[:, None]
    channel = lax.iota(jnp.int32, channel_count)[None, :]
    mixed_once = (row_seed + 7919 * position + 104729 * channel) % 65521
    mixed_twice = (mixed_once * (mixed_once % 32719) + 31 * channel) % 65521
    return (mixed_twice.astype(F32) / 32760.5 - 1.0) * 1.7320508


def paired(
    token_ids,
    segment_ids,
    time_steps,
    row_seeds,
    loss_weights,
    embed_table,
    input_proj,
    attn_gain,
    attn_bias,
    qkv_proj,
    attn_proj,
    mlp_gain,
    mlp_bias,
    up_proj,
    up_bias,
    down_proj,
    output_proj,
):
    z, y, c, x = (lax.axis_index(a) for a in ("z", "y", "c", "x"))
    zn = lax.axis_size("z")
    groups = zn * lax.axis_size("y")
    length = token_ids.shape[1]
    half = length // 2
    block_len, width = embed_table.shape
    ff = up_proj.shape[1]
    rows_here = qkv_proj.shape[0]
    heads = D // HEAD_DIM
    ff_block = down_proj.shape[0] * 2

    meta = jnp.concatenate([token_ids[0], segment_ids[0], time_steps, row_seeds])
    meta_two = ordered(meta, swap(meta, "c"), c, 0)
    weight_c = ordered(loss_weights[0], swap(loss_weights[0], "c"), c, 0)
    weight_two = ordered(weight_c, swap(weight_c, "x"), x, 1).reshape(2, length)
    ids_two = meta_two[:, :length]
    own_meta = pick(meta_two, x, 0)
    segments = own_meta[length : 2 * length]
    weight_row = pick(weight_two, x, 0)
    fraction = own_meta[2 * length].astype(F32) / (TSTEPS - 1)
    noise_level = 0.3 * jnp.exp(fraction * math.log(30.0))
    input_scale = lax.rsqrt(1.0 + noise_level * noise_level)
    residual_scale = 0.5 + fraction
    noise = noise_field(own_meta[2 * length + 1], length, width)

    small_width = 2 * width + 128
    vector = jnp.concatenate([attn_gain, attn_bias, mlp_gain, mlp_bias, up_bias])
    small = jnp.concatenate(
        [
            input_proj.reshape(rows_here, width),
            output_proj,
            jnp.pad(vector.reshape(-1, 128), ((0, rows_here - vector.size // 128), (0, 0))),
        ],
        axis=1,
    )
    qkv_split = qkv_proj.reshape(rows_here, 3 * heads // 2, 2, HEAD_DIM)
    up_split = up_proj.reshape(rows_here, groups, 2, ff_block)

    def packed(core):
        return jnp.concatenate(
            [
                pick(qkv_split, core, 2).reshape(rows_here, -1),
                small,
                pick(up_split, core, 2).reshape(rows_here, -1),
            ],
            axis=1,
        )

    pair = ordered(packed(c), swap(packed(1 - c), "c"), c, 0).reshape(2 * rows_here, -1)
    qkv_cols, small_cols = 3 * D // 2, 3 * D // 2 + small_width
    first_cols = small_cols + D // 2
    first_shard = jnp.concatenate(
        [
            pair[:, :small_cols],
            jnp.concatenate([attn_proj[:, : D // 2], attn_proj[:, D // 2 :]], axis=0),
        ],
        axis=1,
    )
    up_shard = pair[:, small_cols:]

    def places(order, ring):
        block, found = jnp.arange(2 * groups, dtype=jnp.int32), {}
        for axis in order:
            n, here = lax.axis_size(axis), lax.axis_index(axis)
            found[axis] = (block + here) % n if ring else (block % n) ^ here
            block = block // n
        return (found["z"] * 2 + found["y"]) * 2 + found["x"]

    def both_places(ring):
        return jnp.concatenate([places(("z", "y", "x"), ring), places(("z", "x", "y"), ring)])

    def over_one(blocks):
        rows = blocks.shape[1] // 2
        return joined_swap(blocks[:, :rows], "y"), joined_swap(blocks[:, rows:], "x")

    def over_one_start(blocks):
        rows = blocks.shape[1] // 2
        first, second = blocks[:, :rows], blocks[:, rows:]
        return (first, swap(first, "y")), (second, swap(second, "x"))

    def over_other(held):
        return [[held[0], swap(held[0], "x")], [held[1], swap(held[1], "y")]]

    cut = block_len // 32 * 16
    with jax.named_scope("gather_table"):
        table_a = [embed_table[None, :cut]]
        table_a.append(ring_down(table_a[-1], "z"))
        table_b = [joined_swap(embed_table[None, cut:], "y")]
        table_b.append(ring_down(table_b[-1], "z"))
    with jax.named_scope("gather_first"):
        first_z = [first_shard[None]]
        first_z.append(ring_down(first_z[-1], "z"))
    with jax.named_scope("gather_table"):
        for _ in range(2, zn):
            table_a.append(ring_down(table_a[-1], "z"))
    for step in range(2, zn):
        with jax.named_scope("gather_first"):
            first_z.append(ring_down(after(first_z[-1], table_a[step - 1]), "z"))
        with jax.named_scope("gather_table"):
            table_b.append(ring_down(after(table_b[-1], table_a[-1]), "z"))
    with jax.named_scope("gather_table"):
        table_z = table_b[-1]
        table_a = joined_swap(jnp.concatenate(table_a, 0), "y")
        table_b = jnp.stack(table_b, 1).reshape(groups, block_len - cut, width)
    with jax.named_scope("gather_first"):
        first_held = over_one(jnp.concatenate(first_z, 0))
        first_pieces = over_other(first_held)
    with jax.named_scope("gather_up"):
        up_first = after(up_shard[None], table_z, first_z[-1])
        up_moved = apart(up_first, "z", 1)
        up_two = jnp.concatenate([up_first, up_moved], 0)
        up_far = apart(up_two, "z", 2)
    with jax.named_scope("gather_down"):
        down_first = after(down_proj[None], up_far)
        down_moved = apart(down_first, "z", 1)
        down_two = jnp.concatenate([down_first, down_moved], 0)

    flat_ids = ids_two.reshape(-1)
    owner = flat_ids // block_len
    within = flat_ids % block_len
    home = {"z": owner // 8, "y": owner // 4 % 2}
    mine = owner % 4 == c * 2 + x
    table_rows = jnp.concatenate([after(table_a, *first_held, up_moved), table_b], axis=1)
    relative_y, relative_z = (home["y"] - y) % 2, (home["z"] - z) % zn
    slot = (relative_y * zn + relative_z) * block_len + within
    found = jnp.take(
        table_rows.reshape(groups * block_len, width), jnp.where(mine, slot, 0), axis=0
    )
    found = jnp.where(mine[:, None], found, jnp.zeros_like(found)).reshape(2, length, width)

    def to_rows(terms, kind, others):
        split = terms.reshape(2, 2, half, width)
        moved = swap(pick(split, 1 - c, 1).astype(kind), "c")
        both = pick(split, c, 1).astype(F32) + moved.astype(F32)
        both = after(both, *others)
        moved = swap(pick(both, 1 - x, 0).astype(kind), "x")
        own = (pick(both, x, 0).astype(F32) + moved.astype(F32)).astype(kind)
        return ordered(own, swap(own, "c"), c, 0).reshape(length, width)

    def to_pair(row):
        own = pick(row.reshape(2, half, width), c, 0)
        moved = swap(own, "x")
        other = ordered(moved, swap(moved, "c"), c, 0).reshape(length, width)
        return ordered(row, other, x, 0)

    raw = to_rows(found, BF, (first_pieces[0][1], first_pieces[1][1], up_far))
    raw_low = after(raw, down_moved)
    raw = raw_low.astype(F32)
    with jax.named_scope("gather_up"):
        up_z = after(jnp.concatenate([up_two, up_far], 0), first_pieces[0][1], first_pieces[1][1])
        up_moved = over_one_start(up_z)
    paired_shape = (groups, 2, 2, rows_here)

    def in_pairs(p, h):
        return (p // 2, h, p % 2)

    def held_back(pieces, *values):
        return [[after(piece, *values) for piece in half_pieces] for half_pieces in pieces]

    qkv_half, small_full, attn_half = place_blocks(
        both_places(True),
        held_back(first_pieces, found),
        [
            (0, qkv_cols, paired_shape + (qkv_cols,), in_pairs),
            (qkv_cols, small_cols, paired_shape + (small_width,), in_pairs),
            (
                small_cols,
                first_cols,
                (2 * groups, rows_here, D),
                lambda p, h: (p, slice(None), slice(h * D // 2, (h + 1) * D // 2)),
            ),
        ],
    )
    qkv_half, small_full = qkv_half.reshape(D, qkv_cols), small_full.reshape(D, small_width)
    attn_half = attn_half.reshape(D // 2, D)
    input_full = small_full[:, :width].reshape(width, D)
    output_full = small_full[:, width : 2 * width]
    vectors = small_full[:, 2 * width :].reshape(groups, 2, 2, rows_here, 128)
    vectors = vectors[..., : vector.size // 128, :].reshape(groups, 2, 2, vector.size)
    gain_one, bias_one, gain_two, bias_two = (
        vectors[..., k * rows_here : (k + 1) * rows_here].reshape(1, D).astype(F32)
        for k in range(4)
    )
    up_bias_half = pick(vectors[..., 4 * rows_here :], c, 1).reshape(1, ff // 2).astype(F32)
    unit = raw * lax.rsqrt(jnp.mean(raw * raw, axis=1, keepdims=True) + 1e-06)
    target = (unit * width ** (-0.5)).astype(BF)
    inputs = (input_scale * (unit + noise_level * noise)).astype(BF)

    hidden_zero = dot_nn(inputs, input_full)
    normed_one, inverse_one = norm_parts(hidden_zero)
    first_in = (normed_one * gain_one + bias_one).astype(BF)
    first_in = after(first_in, up_moved[0][1], up_moved[1][1])
    with jax.named_scope("gather_up"):
        up_held = [
            jnp.concatenate([own, after(got, first_in)], 0) for own, got in up_moved
        ]
        up_pieces = over_other(up_held)
    with jax.named_scope("gather_down"):
        down_far = apart(after(down_two, raw_low), "z", 2)
    qkv = dot_nn(first_in, qkv_half)
    split = D // 2
    queries = (qkv[:, :split] * HEAD_DIM ** (-0.5)).astype(BF)
    keys = qkv[:, split : 2 * split].astype(BF)
    values = qkv[:, 2 * split :].astype(BF)
    seg_col, seg_row = segments[:, None], segments[None, :]
    blk = min(256, length)
    edges = segments.reshape(length // blk, blk)
    before = jnp.sum(seg_row < edges[:, :1], axis=1, dtype=jnp.int32)
    through = jnp.sum(seg_row <= edges[:, -1:], axis=1, dtype=jnp.int32)
    low_block, high_block = before // blk, (through + blk - 1) // blk
    with jax.named_scope("gather_down"):
        down_z = jnp.concatenate([down_two, down_far], 0)
        down_moved = over_one_start(down_z)
    attended, log_total = attend(
        after(queries, down_z, *up_held), keys, values, seg_col, seg_row, low_block, high_block
    )
    attended = after(
        attended, up_pieces[0][1], up_pieces[1][1], down_moved[0][1], down_moved[1][1]
    )
    with jax.named_scope("gather_down"):
        down_held = [jnp.concatenate([own, after(got, attended)], 0) for own, got in down_moved]
        down_pieces = over_other(down_held)

    def both_cores(part):
        return part + swap(part.astype(BF), "c").astype(F32)

    hidden_one = hidden_zero + residual_scale * both_cores(dot_nn(attended, attn_half))
    normed_two, inverse_two = norm_parts(hidden_one)
    second_in = (normed_two * gain_two + bias_two).astype(BF)
    (up_half,) = place_blocks(
        both_places(False),
        held_back(up_pieces, queries),
        [(0, ff // 2, paired_shape + (ff // 2,), in_pairs)],
    )
    up_half = up_half.reshape(D, ff // 2)
    pre_act = dot_nn(second_in, up_half) + up_bias_half
    below = 0.5 * (1.0 + lax.erf(pre_act * math.sqrt(0.5)))
    activated = (pre_act * below).astype(BF)
    slope = (
        below + pre_act * (jnp.exp(-0.5 * pre_act * pre_act) * (1.0 / math.sqrt(2.0 * math.pi)))
    ).astype(BF)
    (down_half,) = place_blocks(
        both_places(False),
        held_back(down_pieces, activated),
        [
            (
                0,
                D,
                (2 * groups, 2, down_proj.shape[0] // 2, D),
                lambda p, h: (p, h),
            )
        ],
    )
    down_half = down_half.reshape(ff // 2, D)
    hidden_two = hidden_one + residual_scale * both_cores(dot_nn(activated, down_half))
    final_in = hidden_two.astype(BF)
    outputs = dot_nn(final_in, output_full).astype(BF)

    outputs_two = to_pair(outputs).reshape(2 * length, width)
    slots_here = jnp.where(mine, slot, -1)[None, :]
    raised, tops, reached, total = score(outputs_two, table_rows, slots_here)
    ends = jnp.concatenate([tops[-1], total])

    def joined(first, second):
        top = jnp.maximum(first[0], second[0])
        scale_first, scale_second = jnp.exp(first[0] - top), jnp.exp(second[0] - top)
        return jnp.stack([top, first[1] * scale_first + second[1] * scale_second])

    def own_half(value):
        parts = [value[:, k * half : (k + 1) * half] for k in range(4)]
        low, high = jnp.concatenate(parts[::2], 1), jnp.concatenate(parts[1::2], 1)
        return jnp.where(c == 0, low, high), jnp.where(c == 0, high, low)

    def own_row(value):
        first, second = value[:, :half], value[:, half:]
        return jnp.where(x == 0, first, second), jnp.where(x == 0, second, first)

    ends_c = swap(ends, "c")
    kept, sent = own_half(reached)
    moved = swap(sent.astype(BF), "c").astype(F32)
    all_ends = joined(ends, ends_c)
    ends_x = swap(all_ends, "x")
    kept_top, _ = own_half(all_ends[:1])
    both = kept * jnp.exp(own_half(ends[:1])[0] - kept_top) + moved * jnp.exp(
        own_half(ends_c[:1])[0] - kept_top
    )
    kept, sent = own_row(both)
    moved = swap(sent.astype(BF), "x").astype(F32)
    last_ends = joined(all_ends, ends_x)
    log_sum = last_ends[0] + jnp.log(last_ends[1])
    own_log = own_row(own_half(log_sum[None])[0])[0]
    here_top = own_row(own_half(all_ends[:1])[0])[0]
    there_top = own_row(own_half(ends_x[:1])[0])[0]
    own = (kept * jnp.exp(here_top - own_log) + moved * jnp.exp(there_top - own_log)).astype(BF)
    moved = swap(own, "c")
    expected = jnp.concatenate(
        [jnp.where(c == 0, own, moved), jnp.where(c == 0, moved, own)], 1
    ).astype(F32).T
    log_row = pick(log_sum.reshape(2, length), x, 0)
    chosen = jnp.sum(outputs.astype(F32) * target.astype(F32), axis=1)
    loss_row = log_row - chosen
    loss_two = ordered(loss_row, swap(loss_row, "x"), x, 0)
    token_loss = pick(pick(loss_two, c, 0).reshape(2, half), x, 0)[None]

    own_term = weight_row * (jnp.exp(chosen - log_row) - 1.0)
    out_grad = (
        weight_row[:, None] * expected + own_term[:, None] * target.astype(F32)
    ).astype(BF)
    coef = (
        (weight_two.reshape(-1) * width ** (-0.5))[None, :] * jnp.exp(tops[:, 0] - log_sum[None, :])
    ).T

    zy = (zn, lax.axis_size("y"))
    table_cut = block_len // 32 * 16

    def rows_of(grad):
        rows = grad.shape[0] // (2 * groups)
        return grad.astype(BF).reshape(zy + (2, rows, grad.shape[1]))

    def pairs_of(grad):
        rows = grad.shape[0] // (4 * groups)
        shaped = grad.astype(BF).reshape(zy + (2, 2, rows, grad.shape[1]))
        return shaped[:, :, 0], shaped[:, :, 1]

    output_w_grad = dot_tn(final_in, out_grad)
    hidden_two_grad = dot_nt(out_grad, output_full)
    branch_grad = (residual_scale * hidden_two_grad).astype(BF)
    with jax.named_scope("reduce_down"):
        down_terms = rows_of(dot_tn(activated, branch_grad))
        rows = down_terms.shape[3] // 2
        down_a = halve(down_terms[..., :rows, :], "x", 2)
        down_b = halve(down_terms[..., rows:, :], "y", 1)
    pre_grad = (
        dot_nt(after(branch_grad, down_terms), down_half) * slope.astype(F32)
    ).astype(BF)
    with jax.named_scope("reduce_up"):
        up_terms = dot_tn(second_in, pre_grad).astype(BF)
        up_a, up_b = pairs_of(up_terms)
        up_a, up_b = halve(up_a, "y", 1), halve(up_b, "x", 2)
    up_bias_part = jnp.sum(pre_grad, axis=0, dtype=F32)
    second_part = dot_nt(after(pre_grad, up_terms, down_a[1], down_b[1]), up_half)
    table_sums = table_product(raised, after(outputs_two, second_part), coef)
    second_grad = after(both_cores(second_part), table_sums)
    gain_two_part = jnp.sum(second_grad * normed_two, axis=0)
    bias_two_part = jnp.sum(second_grad, axis=0)
    hidden_one_grad = hidden_two_grad + norm_back(second_grad, gain_two, normed_two, inverse_two)
    attn_grad = after((residual_scale * hidden_one_grad).astype(BF), up_a[1], up_b[1])
    with jax.named_scope("reduce_attn"):
        attn_terms = halve(rows_of(dot_tn(attended, attn_grad)), "y", 1)
    attended_grad = dot_nt(attn_grad, attn_half).astype(BF)
    with jax.named_scope("reduce_down"):
        down_a = added(down_a[0], after(down_a[1], up_terms))
        down_b = added(down_b[0], after(down_b[1], up_terms))
        down_next_a, down_next_b = halve(down_a, "y", 1), halve(down_b, "x", 1)
    with jax.named_scope("reduce_up"):
        up_a = added(up_a[0], after(up_a[1], attn_grad))
        up_b = added(up_b[0], after(up_b[1], attn_grad))
        up_next_a, up_next_b = halve(up_a, "x", 1), halve(up_b, "y", 1)
    query_grad, key_grad, value_grad = attend_back(
        queries,
        keys,
        values,
        attended,
        after(attended_grad, down_a, down_b, up_a, up_b, attn_terms[0]),
        log_total,
        seg_col,
        seg_row,
        low_block,
        high_block,
    )
    query_grad = after(
        query_grad,
        up_next_a[1],
        up_next_b[1],
        down_next_a[1],
        down_next_b[1],
        attn_terms[1],
    )
    with jax.named_scope("reduce_mlp"):
        mlp_sum = jnp.concatenate(
            [
                jnp.concatenate(
                    [
                        added(up_next_a[0], after(up_next_a[1], query_grad)),
                        added(up_next_b[0], after(up_next_b[1], query_grad)),
                    ],
                    1,
                ),
                added(down_next_a[0], after(down_next_a[1], query_grad)),
                added(down_next_b[0], after(down_next_b[1], query_grad)),
            ],
            2,
        )
        mlp_ring = ring_start(mlp_sum, "z")
    with jax.named_scope("reduce_attn"):
        attn_terms = halve(added(attn_terms[0], after(attn_terms[1], query_grad)), "x", 1)
    qkv_grad = jnp.concatenate(
        [query_grad * jnp.asarray(HEAD_DIM ** (-0.5), BF), key_grad, value_grad], axis=1
    )
    with jax.named_scope("reduce_qkv"):
        qkv_terms = dot_tn(first_in, after(qkv_grad, mlp_sum)).astype(BF)
        qkv_a, qkv_b = pairs_of(qkv_terms)
        qkv_a, qkv_b = halve(qkv_a, "y", 1), halve(qkv_b, "x", 2)
    first_grad = both_cores(dot_nt(after(qkv_grad, qkv_terms), qkv_half))
    gain_one_part = jnp.sum(first_grad * normed_one, axis=0)
    bias_one_part = jnp.sum(first_grad, axis=0)
    hidden_zero_grad = (
        hidden_one_grad + norm_back(first_grad, gain_one, normed_one, inverse_one)
    ).astype(BF)
    embed_grad = input_scale * dot_nt(hidden_zero_grad, input_full)
    token_grad = (
        embed_grad + (own_term * width ** (-0.5))[:, None] * outputs.astype(F32)
    ).astype(BF)
    token_own = pick(token_grad.reshape(2, half, width), c, 0)
    with jax.named_scope("token_pair"):
        token_moved = swap(token_own, "x")
    with jax.named_scope("reduce_mlp"):
        mlp_ring = ring_up(ring_next(mlp_sum, after(mlp_ring, token_own), 1, "z").astype(BF), "z")
    with jax.named_scope("token_pair"):
        token_grad_two = jnp.concatenate([token_grad, token_moved, swap(token_moved, "c")], 0)
        slots_two = slots_here.reshape(2, length)
        other_slots = pick(slots_two, 1 - x, 0).reshape(2, half)
        token_slots = jnp.concatenate(
            [pick(slots_two, x, 0), pick(other_slots, c, 0), pick(other_slots, 1 - c, 0)]
        )[None, :]
    with jax.named_scope("reduce_qkv"):
        qkv_a = halve(added(qkv_a[0], after(qkv_a[1], token_moved)), "x", 1)
        qkv_b = halve(added(qkv_b[0], after(qkv_b[1], token_moved)), "y", 1)

    input_w_grad = dot_tn(inputs, hidden_zero_grad)
    input_rows = input_proj.shape[0]
    with jax.named_scope("reduce_small"):
        vector_grad = jnp.concatenate(
            [
                pick(part.reshape(zy + (2, 2, rows_here)), c, 2)
                for part in (gain_one_part, bias_one_part, gain_two_part, bias_two_part)
            ]
            + [up_bias_part.reshape(zy + (2, -1))],
            axis=-1,
        ).reshape(zy + (2, -1, 128))
        small_grad = jnp.concatenate(
            [
                pick(input_w_grad.reshape(zy + (2, 2, input_rows, D)), c, 2).reshape(
                    zy + (2, rows_here, width)
                ),
                pick(output_w_grad.reshape(zy + (2, 2, rows_here, width)), c, 2),
                jnp.pad(
                    vector_grad,
                    ((0, 0),) * 3 + ((0, rows_here - vector_grad.shape[3]), (0, 128)),
                ),
            ],
            axis=-1,
        ).astype(BF)
        small_terms = halve(small_grad, "y", 1)

    with jax.named_scope("reduce_small"):
        small_terms = halve(added(small_terms[0], after(small_terms[1], token_moved)), "x", 1)
    with jax.named_scope("reduce_attn"):
        attn_sum = added(attn_terms[0], after(attn_terms[1], token_moved))
    with jax.named_scope("reduce_mlp"):
        mlp_ring = ring_up(ring_next(mlp_sum, after(mlp_ring, token_moved), 2, "z").astype(BF), "z")
    with jax.named_scope("reduce_rest"):
        rest_sum = jnp.concatenate(
            [
                jnp.concatenate(
                    [
                        added(qkv_a[0], after(qkv_a[1], token_grad_two)),
                        added(qkv_b[0], after(qkv_b[1], token_grad_two)),
                    ],
                    1,
                ),
                added(small_terms[0], after(small_terms[1], token_grad_two))
                .reshape(zn, rows_here, 2, -1)
                .transpose(0, 2, 1, 3)
                .reshape(zn, 2 * rows_here, -1),
                attn_sum.reshape(zn, rows_here, 2, D // 2)
                .transpose(0, 2, 1, 3)
                .reshape(zn, 2 * rows_here, D // 2),
            ],
            2,
        )
        rest_ring = ring_start(rest_sum, "z")
    table_terms = table_add(table_sums, token_slots, after(token_grad_two, rest_sum))
    table_terms = after(table_terms, mlp_ring, rest_ring)
    with jax.named_scope("reduce_table"):
        terms = table_terms.reshape(2, zn, block_len, width)
        terms_a, terms_b = terms[:, :, :table_cut], terms[:, :, table_cut:]
        early = table_cut // 32 * 16
        moved_early = swap(terms_a[1, :, :early], "y")
        moved_late = swap(terms_a[1, :, early:], "y")
        moved_b = ring_up(terms_b[:, zn - 1], "z")
    with jax.named_scope("reduce_rest"):
        rest_own = ring_next(rest_sum, after(rest_ring, table_terms), 1, "z")
        rest_ring = ring_up(rest_own.astype(BF), "z")
    moved_b, rest_ring, moved_early = lax.optimization_barrier((moved_b, rest_ring, moved_early))
    for step in range(1, zn):
        with jax.named_scope("reduce_table"):
            total_b = terms_b[:, zn - 1 - step].astype(F32) + moved_b.astype(F32)
            if step < zn - 1:
                moved_b = ring_up(total_b.astype(BF), "z")
            else:
                moved_b = swap(total_b[1].astype(BF), "y")
        if step < zn - 1:
            with jax.named_scope("reduce_rest"):
                rest_own = ring_next(rest_sum, rest_ring, step + 1, "z")
                if step < zn - 2:
                    rest_ring = ring_up(rest_own.astype(BF), "z")
        if step == zn - 2:
            with jax.named_scope("reduce_table"):
                moved_a = jnp.concatenate([moved_early, moved_late], 1)
                sum_a = added(terms_a[0], after(moved_a, total_b))
                moving_a = ring_up(sum_a[zn - 1], "z")
            moved_b, moving_a = lax.optimization_barrier((moved_b, moving_a))
        elif step < zn - 2:
            moved_b, rest_ring, moved_late = lax.optimization_barrier(
                (moved_b, rest_ring, moved_late)
            )
    with jax.named_scope("reduce_table"):
        for step in range(2, zn):
            total_a = sum_a[zn - step].astype(F32) + moving_a.astype(F32)
            moving_a = ring_up(total_a.astype(BF), "z")
            if step == 2:
                moved_b, moving_a = lax.optimization_barrier((moved_b, moving_a))
        total_b = total_b[0] + moved_b.astype(F32)
        total_a = sum_a[0].astype(F32) + moving_a.astype(F32)
    with jax.named_scope("reduce_mlp"):
        mlp_own = ring_next(mlp_sum, after(mlp_ring, rest_sum), 3, "z")

    up_total = mlp_own[:, : ff // 2].reshape(2, rows_here, ff // 2)
    down_own = jnp.concatenate([mlp_own[:, ff // 2 : ff // 2 + D], mlp_own[:, ff // 2 + D :]], 0)
    qkv_total = rest_own[:, :qkv_cols].reshape(2, rows_here, qkv_cols)
    small_end = rest_own.shape[1] - D // 2
    small_own = rest_own[:, qkv_cols:small_end]
    small_own = jnp.concatenate([small_own[:rows_here], small_own[rows_here:]], 1)
    attn_own = rest_own[:, small_end:]
    attn_own = jnp.concatenate([attn_own[:rows_here], attn_own[rows_here:]], 1)

    unit_grad = jnp.concatenate([total_a, total_b], axis=0)
    own_rows = embed_table.astype(F32)
    inverse = lax.rsqrt(jnp.mean(own_rows * own_rows, axis=1, keepdims=True) + 1e-06)
    along = jnp.mean(own_rows * unit_grad, axis=1, keepdims=True)
    table_grad = inverse * unit_grad - own_rows * (inverse * inverse * inverse * along)

    input_own = small_own[:, :width].reshape(input_rows, D)
    output_own = small_own[:, width : 2 * width]
    vector_own = small_own[: vector.size // 128, 2 * width : 2 * width + 128].reshape(-1)
    gains = [vector_own[k * rows_here : (k + 1) * rows_here] for k in range(4)]

    def columns_back(sums, split_shape, axis):
        mine_rows, other_rows = pick(sums, c, 0), pick(sums, 1 - c, 0)
        other_cols = swap(other_rows, "c")
        return ordered(
            mine_rows.reshape(split_shape), other_cols.reshape(split_shape), c, axis
        ).reshape(rows_here, -1)

    qkv_own = columns_back(qkv_total, (rows_here, 3 * heads // 2, HEAD_DIM), 2)
    up_own = columns_back(up_total, (rows_here, groups, ff_block), 2)
    return (
        token_loss,
        table_grad,
        input_own,
        gains[0],
        gains[1],
        qkv_own,
        attn_own,
        gains[2],
        gains[3],
        up_own,
        vector_own[4 * rows_here :],
        down_own,
        output_own,
    )


def combined_all(shard, axis, combine):
    everything = jax.tree.map(lambda part: lax.all_gather(part, axis), shard)
    first = jax.tree.map(lambda part: part[0], everything)

    def step(k, so_far):
        return combine(so_far, jax.tree.map(lambda part: part[k], everything))

    return lax.fori_loop(1, lax.axis_size(axis), step, first)


def product(left, right):
    return jnp.dot(left, right, preferred_element_type=jnp.float32)


def product_left(left, right):
    return lax.dot_general(
        left, right, (((0,), (0,)), ((), ())), preferred_element_type=jnp.float32
    )


def product_right(left, right):
    return lax.dot_general(
        left, right, (((1,), (1,)), ((), ())), preferred_element_type=jnp.float32
    )


def normalize_rows(matrix):
    return matrix * lax.rsqrt(jnp.mean(matrix * matrix, axis=1, keepdims=True) + 1e-06)


def layer_norm(hidden, norm_gain, norm_bias):
    centre = hidden - jnp.mean(hidden, axis=-1, keepdims=True)
    spread = jnp.mean(centre * centre, axis=-1, keepdims=True)
    return centre * lax.rsqrt(spread + 1e-05) * norm_gain + norm_bias


def exact_gelu(pre_act):
    return jax.nn.gelu(pre_act, approximate=False)


def noise_rows(row_seeds, positions, channel_count):
    channel = lax.iota(jnp.int32, channel_count)
    mixed_once = (
        row_seeds[:, None, None] + 7919 * positions[None, :, None] + 104729 * channel[None, None, :]
    ) % 65521
    mixed_twice = (mixed_once * (mixed_once % 32719) + 31 * channel[None, None, :]) % 65521
    return (mixed_twice.astype(jnp.float32) / 32760.5 - 1.0) * 1.7320508


def time_terms(time_steps):
    fraction = time_steps.astype(jnp.float32) / (TSTEPS - 1)
    noise_level = 0.3 * jnp.exp(fraction * math.log(30.0))
    return (noise_level, lax.rsqrt(1.0 + noise_level * noise_level), 0.5 + fraction)


def masked_scores(query_block, key_rows, segment_block, segment_row):
    scores = jnp.einsum("qhd,khd->hqk", query_block, key_rows, preferred_element_type=jnp.float32)
    same_doc = segment_block[:, None] == segment_row[None, :]
    return jnp.where(same_doc[None], scores, -1e30)


def attend_row(operands):
    queries, key_rows, value_rows, segment_row = operands
    length = queries.shape[0]
    block_rows = math.gcd(length, 512)
    block_count = length // block_rows

    def attend_block(pieces):
        query_block, segment_block = pieces
        scores = masked_scores(query_block, key_rows, segment_block, segment_row)
        row_max = jnp.max(scores, axis=-1, keepdims=True)
        raised = jnp.exp(scores - row_max)
        summed = jnp.sum(raised, axis=-1, keepdims=True)
        probs_low = (raised / summed).astype(jnp.bfloat16)
        attended = jnp.einsum(
            "hqk,khd->qhd", probs_low, value_rows, preferred_element_type=jnp.float32
        )
        return (attended.astype(jnp.bfloat16), (row_max + jnp.log(summed))[..., 0])

    attended, log_total = lax.map(
        attend_block,
        (
            queries.reshape((block_count, block_rows) + queries.shape[1:]),
            segment_row.reshape(block_count, block_rows),
        ),
    )
    return (attended.reshape(queries.shape), log_total)


def attend_back_row(operands):
    queries, key_rows, value_rows, segment_row, grad_rows, log_total = operands
    length = queries.shape[0]
    block_rows = math.gcd(length, 512)
    block_count = length // block_rows

    def back_block(carry, pieces):
        key_sum, value_sum = carry
        query_block, segment_block, grad_block, total_block = pieces
        scores = masked_scores(query_block, key_rows, segment_block, segment_row)
        probs = jnp.exp(scores - total_block[:, :, None])
        prob_grad = jnp.einsum(
            "qhd,khd->hqk", grad_block, value_rows, preferred_element_type=jnp.float32
        )
        score_grad = (
            probs * (prob_grad - jnp.sum(probs * prob_grad, axis=-1, keepdims=True))
        ).astype(jnp.bfloat16)
        query_grad = jnp.einsum(
            "hqk,khd->qhd", score_grad, key_rows, preferred_element_type=jnp.float32
        )
        key_sum = key_sum + jnp.einsum(
            "hqk,qhd->khd", score_grad, query_block, preferred_element_type=jnp.float32
        )
        value_sum = value_sum + jnp.einsum(
            "hqk,qhd->khd",
            probs.astype(jnp.bfloat16),
            grad_block,
            preferred_element_type=jnp.float32,
        )
        return ((key_sum, value_sum), query_grad.astype(jnp.bfloat16))

    block_shape = (block_count, block_rows) + queries.shape[1:]
    start_sums = (jnp.zeros(key_rows.shape, jnp.float32), jnp.zeros(value_rows.shape, jnp.float32))
    (key_sum, value_sum), query_grad = lax.scan(
        back_block,
        start_sums,
        (
            queries.reshape(block_shape),
            segment_row.reshape(block_count, block_rows),
            grad_rows.reshape(block_shape),
            log_total,
        ),
    )
    return (
        query_grad.reshape(queries.shape),
        key_sum.astype(jnp.bfloat16),
        value_sum.astype(jnp.bfloat16),
    )


def join_parts(first, second):
    top = jnp.maximum(first[0], second[0])
    total = first[1] * jnp.exp(first[0] - top) + second[1] * jnp.exp(second[0] - top)
    return (top, total, first[2] + second[2], first[3] + second[3])


def local(
    token_ids,
    segment_ids,
    time_steps,
    row_seeds,
    loss_weights,
    embed_table,
    input_proj,
    attn_gain,
    attn_bias,
    qkv_proj,
    attn_proj,
    mlp_gain,
    mlp_bias,
    up_proj,
    up_bias,
    down_proj,
    output_proj,
):
    seq_count = lax.axis_size("seq")
    seq_place = lax.axis_index("seq")
    dp_count = lax.axis_size("dp")
    row_count, length = token_ids.shape
    local_len = length // seq_count
    tok_count = row_count * local_len
    start_pos = seq_place * local_len
    own_ids = lax.dynamic_slice_in_dim(token_ids, start_pos, local_len, 1)
    positions = start_pos + lax.iota(jnp.int32, local_len)
    gathered = (
        lax.all_gather(embed_table, ("dp", "seq"), axis=0, tiled=True),
        lax.all_gather(input_proj, ("dp", "seq"), axis=0, tiled=True),
        lax.all_gather(attn_gain, ("dp", "seq"), axis=0, tiled=True),
        lax.all_gather(attn_bias, ("dp", "seq"), axis=0, tiled=True),
        lax.all_gather(qkv_proj, ("dp", "seq"), axis=0, tiled=True),
        lax.all_gather(attn_proj, ("dp", "seq"), axis=0, tiled=True),
        lax.all_gather(mlp_gain, ("dp", "seq"), axis=0, tiled=True),
        lax.all_gather(mlp_bias, ("dp", "seq"), axis=0, tiled=True),
        lax.all_gather(up_proj, ("dp", "seq"), axis=0, tiled=True),
        lax.all_gather(up_bias, ("dp", "seq"), axis=0, tiled=True),
        lax.all_gather(down_proj, ("dp", "seq"), axis=0, tiled=True),
        lax.all_gather(output_proj, ("dp", "seq"), axis=0, tiled=True),
    )
    (
        table_full,
        input_full,
        gain_one,
        bias_one,
        qkv_full,
        attn_full,
        gain_two,
        bias_two,
        up_full,
        upbias_full,
        down_full,
        output_full,
    ) = gathered
    vocab_size, embed_width = table_full.shape
    block_len = vocab_size // (dp_count * seq_count)
    unit, unit_back = jax.vjp(normalize_rows, table_full.astype(jnp.float32))
    sub_table = lax.dynamic_slice_in_dim(
        table_full.reshape(dp_count, seq_count, block_len, embed_width), seq_place, 1, 1
    ).reshape(dp_count * block_len, embed_width)
    sub_unit = lax.dynamic_slice_in_dim(
        unit.reshape(dp_count, seq_count, block_len, embed_width), seq_place, 1, 1
    ).reshape(dp_count * block_len, embed_width)
    scaled = (sub_unit * embed_width ** (-0.5)).astype(jnp.bfloat16)
    local_rows = lax.iota(jnp.int32, dp_count * block_len)
    vocab_index = (
        local_rows // block_len * seq_count + seq_place
    ) * block_len + local_rows % block_len
    noise_level, input_scale, residual_scale = time_terms(time_steps)
    noise = noise_rows(row_seeds, positions, embed_width)
    embedded = jnp.take(unit, own_ids, axis=0)
    inputs = (
        (input_scale[:, None, None] * (embedded + noise_level[:, None, None] * noise))
        .astype(jnp.bfloat16)
        .reshape(tok_count, embed_width)
    )
    token_scale = jnp.repeat(residual_scale, local_len)[:, None]
    token_input_scale = jnp.repeat(input_scale, local_len)[:, None]
    hidden_zero = product(inputs, input_full)
    first_norm, first_back = jax.vjp(
        layer_norm, hidden_zero, gain_one.astype(jnp.float32), bias_one.astype(jnp.float32)
    )
    first_in = first_norm.astype(jnp.bfloat16)
    qkv = product(first_in, qkv_full)
    query_tok = (
        (qkv[:, :D] * HEAD_DIM ** (-0.5)).astype(jnp.bfloat16).reshape(row_count, local_len, D)
    )
    key_tok = qkv[:, D : 2 * D].astype(jnp.bfloat16).reshape(row_count, local_len, D)
    value_tok = qkv[:, 2 * D :].astype(jnp.bfloat16).reshape(row_count, local_len, D)
    head_q, head_k, head_v = (
        lax.all_to_all(query_tok, "seq", split_axis=2, concat_axis=1, tiled=True),
        lax.all_to_all(key_tok, "seq", split_axis=2, concat_axis=1, tiled=True),
        lax.all_to_all(value_tok, "seq", split_axis=2, concat_axis=1, tiled=True),
    )
    heads_here = head_q.shape[2] // HEAD_DIM
    head_shape = (row_count, length, heads_here, HEAD_DIM)
    head_q = head_q.reshape(head_shape)
    head_k = head_k.reshape(head_shape)
    head_v = head_v.reshape(head_shape)
    attended, log_total = lax.map(attend_row, (head_q, head_k, head_v, segment_ids))
    attended = attended.reshape(row_count, length, heads_here * HEAD_DIM)
    mixed = lax.all_to_all(attended, "seq", split_axis=1, concat_axis=2, tiled=True).reshape(
        tok_count, D
    )
    hidden_one = hidden_zero + token_scale * product(mixed, attn_full)
    second_norm, second_back = jax.vjp(
        layer_norm, hidden_one, gain_two.astype(jnp.float32), bias_two.astype(jnp.float32)
    )
    second_in = second_norm.astype(jnp.bfloat16)
    pre_act = product(second_in, up_full) + upbias_full.astype(jnp.float32)
    activated, gelu_back = jax.vjp(exact_gelu, pre_act)
    act_low = activated.astype(jnp.bfloat16)
    hidden_two = hidden_one + token_scale * product(act_low, down_full)
    final_in = hidden_two.astype(jnp.bfloat16)
    outputs = product(final_in, output_full).astype(jnp.bfloat16)
    group_tok = seq_count * tok_count
    group_out = lax.all_gather(outputs, "seq", axis=0, tiled=True)
    group_ids = (
        token_ids.reshape(row_count, seq_count, local_len).transpose(1, 0, 2).reshape(group_tok)
    )
    spread = jnp.where(
        lax.iota(jnp.int32, seq_count)[:, None] == seq_place,
        loss_weights.reshape(1, tok_count),
        0.0,
    )
    tile_rows = math.gcd(group_tok, 512)
    tile_count = group_tok // tile_rows
    out_tiles = group_out.reshape(tile_count, tile_rows, embed_width)
    id_tiles = group_ids.reshape(tile_count, tile_rows)

    def part_tile(pieces):
        out_block, target_block = pieces
        logits = product_right(out_block, scaled)
        row_max = jnp.max(logits, axis=1)
        exp_sum = jnp.sum(jnp.exp(logits - row_max[:, None]), axis=1)
        picked = jnp.sum(
            jnp.where(vocab_index[None, :] == target_block[:, None], logits, 0.0), axis=1
        )
        return (row_max, exp_sum, picked)

    part_max, part_sum, part_pick = lax.map(part_tile, (out_tiles, id_tiles))
    top, total, pick, weight_tiles = combined_all(
        (part_max, part_sum, part_pick, spread), "seq", join_parts
    )
    log_tiles = top + jnp.log(total)
    all_loss = log_tiles - pick
    token_loss = lax.dynamic_slice_in_dim(all_loss, seq_place, 1, 0)

    def back_tile(scaled_sum, pieces):
        out_block, target_block, log_block, weight_block = pieces
        logits = product_right(out_block, scaled)
        probs = jnp.exp(logits - log_block[:, None])
        onehot = (vocab_index[None, :] == target_block[:, None]).astype(jnp.float32)
        grad_logits = (weight_block[:, None] * (probs - onehot)).astype(jnp.bfloat16)
        scaled_sum = scaled_sum + product_left(grad_logits, out_block)
        return (scaled_sum, product(grad_logits, scaled))

    scaled_grad, out_terms = lax.scan(
        back_tile,
        jnp.zeros(scaled.shape, jnp.float32),
        (out_tiles, id_tiles, log_tiles, weight_tiles),
    )
    out_terms = out_terms.reshape(tile_count * tile_rows, embed_width)
    out_grad = lax.psum_scatter(out_terms, "seq", scatter_dimension=0, tiled=True).astype(
        jnp.bfloat16
    )
    output_w_grad = product_left(final_in, out_grad)
    hidden_two_grad = product_right(out_grad, output_full)
    branch_grad = (token_scale * hidden_two_grad).astype(jnp.bfloat16)
    down_w_grad = product_left(act_low, branch_grad)
    pre_grad = gelu_back(product_right(branch_grad, down_full))[0].astype(jnp.bfloat16)
    up_w_grad = product_left(second_in, pre_grad)
    upbias_grad = jnp.sum(pre_grad, axis=0, dtype=jnp.float32)
    hidden_one_part, gain_two_grad, bias_two_grad = second_back(product_right(pre_grad, up_full))
    hidden_one_grad = hidden_two_grad + hidden_one_part
    attn_grad = (token_scale * hidden_one_grad).astype(jnp.bfloat16)
    attn_w_grad = product_left(mixed, attn_grad)
    mixed_grad = (
        product_right(attn_grad, attn_full).astype(jnp.bfloat16).reshape(row_count, local_len, D)
    )
    head_grad = lax.all_to_all(mixed_grad, "seq", split_axis=2, concat_axis=1, tiled=True).reshape(
        head_shape
    )
    query_grad, key_grad, value_grad = lax.map(
        attend_back_row, (head_q, head_k, head_v, segment_ids, head_grad, log_total)
    )
    merged_shape = (row_count, length, heads_here * HEAD_DIM)
    query_back, key_back, value_back = (
        lax.all_to_all(
            query_grad.reshape(merged_shape), "seq", split_axis=1, concat_axis=2, tiled=True
        ),
        lax.all_to_all(
            key_grad.reshape(merged_shape), "seq", split_axis=1, concat_axis=2, tiled=True
        ),
        lax.all_to_all(
            value_grad.reshape(merged_shape), "seq", split_axis=1, concat_axis=2, tiled=True
        ),
    )
    qkv_grad = jnp.concatenate(
        [query_back * HEAD_DIM ** (-0.5), key_back, value_back], axis=2
    ).reshape(tok_count, 3 * D)
    qkv_w_grad = product_left(first_in, qkv_grad)
    hidden_zero_part, gain_one_grad, bias_one_grad = first_back(product_right(qkv_grad, qkv_full))
    hidden_zero_grad = (hidden_one_grad + hidden_zero_part).astype(jnp.bfloat16)
    input_w_grad = product_left(inputs, hidden_zero_grad)
    embedded_grad = token_input_scale * product_right(hidden_zero_grad, input_full)
    scaled_part = scaled_grad * embed_width ** (-0.5)
    group_grad = lax.all_gather(
        embedded_grad.astype(jnp.bfloat16), "seq", axis=0, tiled=True
    ).astype(embedded_grad.dtype)
    block_id = group_ids // block_len
    owned = block_id % seq_count == seq_place
    local_slot = jnp.where(
        owned, block_id // seq_count * block_len + group_ids % block_len, scaled.shape[0]
    )
    unit_grad = scaled_part.at[local_slot].add(group_grad, mode="drop")
    table_term = jax.vjp(normalize_rows, sub_table.astype(jnp.float32))[1](unit_grad)[0]
    table_grad = lax.psum_scatter(
        table_term.astype(jnp.bfloat16), "dp", scatter_dimension=0, tiled=True
    ).astype(jnp.float32)
    summed = (
        lax.psum_scatter(input_w_grad, ("dp", "seq"), scatter_dimension=0, tiled=True),
        lax.psum_scatter(gain_one_grad, ("dp", "seq"), scatter_dimension=0, tiled=True),
        lax.psum_scatter(bias_one_grad, ("dp", "seq"), scatter_dimension=0, tiled=True),
        lax.psum_scatter(qkv_w_grad, ("dp", "seq"), scatter_dimension=0, tiled=True),
        lax.psum_scatter(attn_w_grad, ("dp", "seq"), scatter_dimension=0, tiled=True),
        lax.psum_scatter(gain_two_grad, ("dp", "seq"), scatter_dimension=0, tiled=True),
        lax.psum_scatter(bias_two_grad, ("dp", "seq"), scatter_dimension=0, tiled=True),
        lax.psum_scatter(up_w_grad, ("dp", "seq"), scatter_dimension=0, tiled=True),
        lax.psum_scatter(upbias_grad, ("dp", "seq"), scatter_dimension=0, tiled=True),
        lax.psum_scatter(down_w_grad, ("dp", "seq"), scatter_dimension=0, tiled=True),
        lax.psum_scatter(output_w_grad, ("dp", "seq"), scatter_dimension=0, tiled=True),
    )
    return (token_loss.reshape(row_count, local_len), table_grad) + tuple(summed)


def solution(mesh):
    dp, seq = mesh.shape["dp"], mesh.shape["seq"]
    if (dp, seq) == (16, 2):
        inner = Mesh(mesh.devices.reshape(dp // 4, 2, 2, seq), ("z", "y", "c", "x"))
        dp_names, seq_names, body = ("z", "y", "c"), ("x",), paired
    else:
        inner, dp_names, seq_names, body = mesh, ("dp",), ("seq",), local
    every = dp_names + seq_names
    in_specs = (
        P(dp_names, None),
        P(dp_names, None),
        P(dp_names),
        P(dp_names),
        P(dp_names, seq_names),
        P(every, None),
        P(every, None),
        P(every),
        P(every),
        P(every, None),
        P(every, None),
        P(every),
        P(every),
        P(every, None),
        P(every),
        P(every, None),
        P(every, None),
    )
    out_specs = (
        P(dp_names, seq_names),
        P(every, None),
        P(every, None),
        P(every),
        P(every),
        P(every, None),
        P(every, None),
        P(every),
        P(every),
        P(every, None),
        P(every),
        P(every, None),
        P(every, None),
    )
    return jax.shard_map(body, mesh=inner, in_specs=in_specs, out_specs=out_specs, check_vma=False)
```
